32 devices in a mesh: shard: 4 (over x, core), seq: 8 (over z, y).
Axes of the slice: x: 2, y: 2, z: 4, core: 2. Of those that a mesh axis runs over, the one named last changes fastest.
Arguments:
- hidden: bfloat16 [16384, 1536], P(('shard', 'seq')), may hold values from -6 to 6
- cotangent: bfloat16 [16384, 1536], P(('shard', 'seq')), may hold values from -6 to 6
- seg_ids: int32 [16384], replicated, may hold values from 0 to 7, never falling along the last dimension, each value on 1 to 4096 neighbouring positions
- norm_gain: bfloat16 [1536], P('shard'), may hold values from 0.5 to 1.5
- in_weight: bfloat16 [1536, 6448], P('shard'), may hold values from -0.15625 to 0.15625
- conv_weight: bfloat16 [4, 3328], P(None, 'shard'), may hold values from -3 to 3
- conv_bias: bfloat16 [3328], P('shard'), may hold values from -3 to 3
- dt_bias: bfloat16 [48], replicated, may hold values from -8 to -2
- a_log: bfloat16 [48], replicated, may hold values from 0 to 2.6875
- d_skip: bfloat16 [48], replicated, may hold values from 0.5 to 1.5
- out_gain: bfloat16 [3072], P('shard'), may hold values from 0.5 to 1.5
- out_weight: bfloat16 [3072, 1536], P('shard'), may hold values from -0.109375 to 0.109375
Outputs:
- block_out: bfloat16 [16384, 1536], P(('shard', 'seq'))
- grad_hidden: float32 [16384, 1536], P(('shard', 'seq'))
- grad_norm_gain: float32 [1536], P(('shard', 'seq'))
- grad_in_weight: float32 [1536, 6448], P(('shard', 'seq'))
- grad_conv_weight: float32 [4, 3328], P(None, ('shard', 'seq'))
- grad_conv_bias: float32 [3328], P(('shard', 'seq'))
- grad_dt_bias: float32 [48], replicated
- grad_a_log: float32 [48], replicated
- grad_d_skip: float32 [48], replicated
- grad_out_gain: float32 [3072], P(('shard', 'seq'))
- grad_out_weight: float32 [3072, 1536], P(('shard', 'seq'))
The draws below stay inside these ranges and needn't reach their ends.
Inputs may be any that keep to these rules, and one draw needn't show every extreme that they name: seg_ids never falls along the tokens; every value occurs; each document holds 1 to 4096 tokens and one holds exactly 4096.
All inputs are finite; a program needn't handle non-finite values.
Results may differ from the reference program's by a relative error of at most 0.02.
Values may be sent and summed in bfloat16 or wider, within the bound.
No kernel may reach another device: no remote copies, remote signals or barrier semaphores. Data moves between devices by JAX's collectives and lax.ppermute only.
A program may use at most 384 MiB of HBM per device.

```python
import math
import jax
import jax.numpy as jnp
import numpy as np
from jax import lax

D = 1536
HEADS = 48
HEAD_DIM = 64
STATE = 128
CONV = 4
BLOCK = 256
DOC_MAX = 4096
INNER = 3072
CHANNELS = 3328
PROJ = 6448
TOKENS = 16384
DOCS = 8


def block_scale(own_key, dims, cuts, smallest, high):
    level = 1.0
    for axis_at, blocks in cuts:
        heights = jax.random.uniform(jax.random.fold_in(jax.random.fold_in(own_key, 6), axis_at), (blocks,), jnp.float32, smallest / len(cuts), high / len(cuts))
        level = level * jnp.repeat(jnp.exp(heights), dims[axis_at] // blocks).reshape((-1,) + (1,) * (len(dims) - 1 - axis_at))
    return level


def length_profile(count, total, most, lean):
    portions = [(1 << 20) // math.isqrt(rank ** lean) + 1 for rank in range(2, count + 1)]
    surplus, given = total - most - (count - 1), [1] * (count - 1)
    while surplus > 0:
        movable = [i for i in range(count - 1) if given[i] < most]
        mass, left = sum([portions[i] for i in movable]), surplus
        for i in movable:
            extra = min(most - given[i], max(1, left * portions[i] // mass), surplus)
            given[i] = given[i] + extra
            surplus = surplus - extra
    return np.array([most] + given)


def ragged_sizes(stream_key, amount, total, reach, lean):
    if amount == 2:
        one = jax.random.randint(stream_key, (), max(1, total - reach), min(reach, total - 1) + 1)
        return jnp.stack([one, total - one])
    tallies = jnp.asarray(length_profile(amount, total, reach, lean), jnp.int32)
    couples = (amount - 1) // 2
    giver, receiver = tallies[1:1 + 2 * couples:2], tallies[2:2 + 2 * couples:2]
    slack = jnp.minimum(giver - 1, reach - receiver)
    shifted = jax.random.randint(jax.random.fold_in(stream_key, 1), (couples,), 0, 1 << 20) % (slack + 1)
    tallies = tallies.at[1:1 + 2 * couples:2].set(giver - shifted).at[2:2 + 2 * couples:2].set(receiver + shifted)
    return tallies[jax.random.permutation(jax.random.fold_in(stream_key, 2), amount)]


def gaussian(rng, extent, width, reach, split=(), held_as=jnp.bfloat16):
    entries = jax.random.normal(rng, extent, jnp.float32) * width
    if len(split) > 0:
        entries = block_scale(rng, extent, split, -0.22, 0.18) * entries
    return jnp.clip(entries, min=-reach, max=reach).astype(held_as)


def setup_inputs(seed: int = 0) -> dict:
    seeds = jax.random.split(jax.random.key(seed), 13)
    return {
        "hidden": gaussian(seeds[0], (TOKENS, D), 1.0, 6.0, ((0, 32),)),
        "cotangent": gaussian(seeds[1], (TOKENS, D), 1.0, 6.0, ((0, 32),)),
        "seg_ids": jnp.searchsorted(jnp.cumsum(ragged_sizes(seeds[2], DOCS, TOKENS, DOC_MAX, 2)), jnp.arange(TOKENS), side="right").astype(jnp.int32),
        "norm_gain": jnp.clip(1.0 + 0.1 * jax.random.normal(seeds[3], (D,), jnp.float32), 0.5, 1.5).astype(jnp.bfloat16),
        "in_weight": gaussian(seeds[4], (D, PROJ), D ** -0.5, 0.15625, ((0, 4),)),
        "conv_weight": gaussian(seeds[5], (CONV, CHANNELS), CONV ** -0.5, 3.0, ((1, 4),)),
        "conv_bias": gaussian(seeds[6], (CHANNELS,), 0.5, 3.0, ((0, 4),)),
        "dt_bias": jnp.clip(jax.random.uniform(seeds[7], (HEADS,), jnp.float32, -8.0, -2.0), -8.0, -2.0).astype(jnp.bfloat16),
        "a_log": jnp.clip(jax.random.uniform(seeds[8], (HEADS,), jnp.float32, 0.0, 2.6875), 0.0, 2.6875).astype(jnp.bfloat16),
        "d_skip": jnp.clip(jax.random.uniform(seeds[9], (HEADS,), jnp.float32, 0.5, 1.5), 0.5, 1.5).astype(jnp.bfloat16),
        "out_gain": jnp.clip(1.0 + 0.1 * jax.random.normal(seeds[10], (INNER,), jnp.float32), 0.5, 1.5).astype(jnp.bfloat16),
        "out_weight": gaussian(seeds[11], (INNER, D), INNER ** -0.5, 0.109375, ((0, 4),)),
    }


@jax.custom_vjp
def low(v):
    return lax.optimization_barrier(v.astype(jnp.bfloat16)).astype(jnp.float32)

@jax.custom_vjp
def low_back(v):
    return v

def low_keep(v):
    return (low(v), None)

def low_pass(kept, grad):
    return (grad,)

def back_keep(v):
    return (v, None)

def back_low(kept, grad):
    return (low(grad),)
low.defvjp(low_keep, low_pass)
low_back.defvjp(back_keep, back_low)
HIGH = lax.Precision.HIGHEST
EPS = 1e-05

def conv_mixing(xbc, seg_ids, conv_weight, conv_bias):
    length = xbc.shape[0]
    lead = jnp.zeros((CONV - 1, xbc.shape[1]), jnp.float32)
    padded = jnp.concatenate([lead, xbc], 0)
    seg_pad = jnp.concatenate([jnp.full((CONV - 1,), -1, jnp.int32), seg_ids], 0)
    summed = jnp.zeros_like(xbc) + conv_bias[None, :]
    for tap in range(CONV):
        same_doc = (seg_pad[tap:tap + length] == seg_ids).astype(jnp.float32)
        summed = summed + conv_weight[tap][None, :] * padded[tap:tap + length] * same_doc[:, None]
    return jax.nn.silu(summed)

def block_step(state, inputs):
    x_block, b_block, c_block, decay_block, seg_block, seg_prior = inputs
    cum_decay = jnp.cumsum(decay_block, axis=0)
    positions = jnp.arange(BLOCK, dtype=jnp.int32)
    same_doc = (seg_block[:, None] == seg_block[None, :]) & (positions[:, None] >= positions[None, :])
    log_gap = cum_decay.T[:, :, None] - cum_decay.T[:, None, :]
    weights = jnp.exp(jnp.where(same_doc[None], log_gap, -jnp.inf))
    scores = jnp.dot(c_block, b_block.T, precision=HIGH)
    inside = jnp.einsum('hts,shp->thp', weights * scores[None], x_block, precision=HIGH)
    enter_block = jnp.exp(cum_decay) * (seg_block == seg_prior).astype(jnp.float32)[:, None]
    from_state = jnp.einsum('tn,hpn->thp', c_block, state, precision=HIGH) * enter_block[:, :, None]
    keep_tail = jnp.exp(jnp.where((seg_block == seg_block[BLOCK - 1])[:, None], cum_decay[BLOCK - 1][None, :] - cum_decay, -jnp.inf))
    added = jnp.einsum('shp,sn->hpn', x_block * keep_tail[:, :, None], b_block, precision=HIGH)
    new_state = enter_block[BLOCK - 1][:, None, None] * state + added
    return (new_state, inside + from_state)

def forward(seg_ids, hidden, norm_gain, in_weight, conv_weight, conv_bias, dt_bias, a_log, d_skip, out_gain, out_weight):
    scale_in = lax.rsqrt(lax.optimization_barrier(jnp.mean(hidden * hidden, axis=1, keepdims=True)) + EPS)
    normed_in = low(hidden * scale_in * norm_gain[None, :])
    projected = low(low_back(jnp.dot(normed_in, in_weight, precision=HIGH)))
    gate_z = projected[:, :INNER]
    x_raw = low_back(projected[:, INNER:2 * INNER])
    remaining = projected[:, 2 * INNER:]
    mixed = conv_mixing(jnp.concatenate([x_raw, remaining[:, :2 * STATE]], 1), seg_ids, conv_weight, conv_bias)
    x_conv = mixed[:, :INNER].reshape(TOKENS, HEADS, HEAD_DIM)
    b_mat = mixed[:, INNER:INNER + STATE]
    c_mat = mixed[:, INNER + STATE:]
    step_size = jax.nn.softplus(remaining[:, 2 * STATE:] + dt_bias[None, :])
    log_decay = -step_size * jnp.exp(a_log)[None, :]
    x_step = x_conv * step_size[:, :, None]
    n_blocks = TOKENS // BLOCK
    seg_before = jnp.concatenate([jnp.full((1,), -1, jnp.int32), seg_ids[:-1]]).reshape(n_blocks, BLOCK)[:, 0]
    inputs = (x_step.reshape(n_blocks, BLOCK, HEADS, HEAD_DIM), b_mat.reshape(n_blocks, BLOCK, STATE), c_mat.reshape(n_blocks, BLOCK, STATE), log_decay.reshape(n_blocks, BLOCK, HEADS), seg_ids.reshape(n_blocks, BLOCK), seg_before)
    initial = jnp.zeros((HEADS, HEAD_DIM, STATE), jnp.float32)
    _, block_out = lax.scan(jax.checkpoint(block_step), initial, inputs)
    mixer_out = block_out.reshape(TOKENS, HEADS, HEAD_DIM) + x_conv * d_skip[None, :, None]
    mixer_out = low(low_back(mixer_out.reshape(TOKENS, INNER)))
    gated = mixer_out * jax.nn.silu(gate_z)
    scale_out = lax.rsqrt(lax.optimization_barrier(jnp.mean(gated * gated, axis=1, keepdims=True)) + EPS)
    normed_out = low(gated * scale_out * out_gain[None, :])
    return hidden + jnp.dot(normed_out, out_weight, precision=HIGH)

def reference(hidden, cotangent, seg_ids, norm_gain, in_weight, conv_weight, conv_bias, dt_bias, a_log, d_skip, out_gain, out_weight):
    params = tuple((value.astype(jnp.float32) for value in (hidden, norm_gain, in_weight, conv_weight, conv_bias, dt_bias, a_log, d_skip, out_gain, out_weight)))

    def wrapped(*values):
        return forward(seg_ids, *values)
    result, pullback = jax.vjp(wrapped, *params)
    grads = pullback(cotangent.astype(jnp.float32))
    return (result.astype(jnp.bfloat16), grads[0], grads[1], grads[2], grads[3], grads[4], grads[5], grads[6], grads[7], grads[8], grads[9])
```

```python
import jax
import jax.numpy as jnp
from jax import lax
from jax.experimental import pallas as pl
from jax.experimental.pallas import tpu as pltpu
from jax.sharding import PartitionSpec as P

HEAD_DIM = 64
CONV = 4
EPS = 1e-05
HALO = 8
GROUP = 4
WIDE = GROUP * HEAD_DIM
TILE = 128
HIGH = lax.Precision.HIGHEST
ALL = ("shard", "seq")
f32 = jnp.float32
bf16 = jnp.bfloat16


def mm(a, b):
    return jnp.dot(a, b, preferred_element_type=f32)


def mm_nt(a, b):
    return lax.dot_general(a, b, (((1,), (1,)), ((), ())), preferred_element_type=f32)


def mm_tn(a, b):
    return lax.dot_general(a, b, (((0,), (0,)), ((), ())), preferred_element_type=f32)


def spread(columns, first, stride):
    rows = columns.shape[0]
    lane = lax.broadcasted_iota(jnp.int32, (rows, 2 * HEAD_DIM), 1)
    out = []
    for pair in range(GROUP // 2):
        at = first + 2 * pair * stride
        low = columns[:, at : at + 1]
        top = columns[:, at + stride : at + stride + 1]
        out.append(jnp.where(lane < HEAD_DIM, low, top))
    return jnp.concatenate(out, axis=1)


def conv_rows(wide, taps, masks, start, rows):
    pre = taps[CONV : CONV + 1, :] + taps[CONV - 1 : CONV, :] * wide[pl.ds(HALO + start, rows), :]
    for tap in range(CONV - 1):
        shifted = wide[pl.ds(HALO - CONV + 1 + tap + start, rows), :]
        pre = pre + taps[tap : tap + 1, :] * shifted * masks[pl.ds(start, rows), tap : tap + 1]
    return pre


def forward_kernel(
    raw, taps, masks, seg_row, aux, aux_row, y_out, state_out, bc_out, ct_out, wide, score, bt, xs
):
    length = y_out.shape[0]
    n_state = bt.shape[0]
    step = pl.program_id(0)
    wide[...] = raw[...].astype(f32)

    @pl.when(step == 0)
    def _():
        for start in range(0, length, TILE):
            rows = pl.ds(start, TILE)
            pre = conv_rows(wide, taps, masks, start, TILE)
            both = pre * jax.nn.sigmoid(pre)
            bc_out[rows, :] = both.astype(bf16)
            bt[:, rows] = both[:, :n_state].T.astype(bf16)
            ct_out[:, rows] = both[:, n_state:].T.astype(bf16)
        for start in range(0, length, TILE):
            rows = pl.ds(start, TILE)
            product = mm(bc_out[rows, n_state:], bt[...])
            here = lax.broadcasted_iota(jnp.int32, (TILE, length), 0) + start
            there = lax.broadcasted_iota(jnp.int32, (TILE, length), 1)
            seen = (masks[rows, 6:7] == seg_row[0:1, :]) & (here >= there)
            score[rows, :] = jnp.where(seen, product, 0.0)

    @pl.when(step > 0)
    def _():
        for start in range(0, length, TILE):
            rows = pl.ds(start, TILE)
            pre = conv_rows(wide, taps, masks, start, TILE)
            x = pre * jax.nn.sigmoid(pre)
            columns = aux[0, rows, :]
            scaled = (x * spread(columns, 1, 4)).astype(bf16)
            xs[rows, :] = scaled
            y_out[rows, :] = x * taps[5:6, :]
        for start in range(0, length, TILE):
            rows = pl.ds(start, TILE)
            seen = start + TILE
            columns = aux[0, rows, :]
            for head in range(GROUP):
                lanes = slice(head * HEAD_DIM, (head + 1) * HEAD_DIM)
                gap = columns[:, 4 * head : 4 * head + 1] - aux_row[0, head : head + 1, :seen]
                weight = jnp.exp(jnp.minimum(gap, 0.0)) * score[rows, :seen]
                y_out[rows, lanes] += mm(weight.astype(bf16), xs[:seen, lanes])
        kept = []
        for start in range(0, length, TILE):
            rows = pl.ds(start, TILE)
            kept.append((xs[rows, :].astype(f32) * spread(aux[0, rows, :], 2, 4)).astype(bf16))
        state_out[...] = mm(bt[...], jnp.concatenate(kept, 0)).astype(bf16)


def gate_kernel(
    y_in, z_in, dn_in, bc, ct, enter, state, gain, mo_out, norm_out, dz_out, dy_out, ds_out,
    dc_out, dg_out, gated_s, silu_s, ds_acc
):
    rows = y_in.shape[0]
    width = y_in.shape[1]
    n_state = state.shape[0]
    step = pl.program_id(0)
    lane = lax.broadcasted_iota(jnp.int32, (rows, 2 * HEAD_DIM), 1)
    c_mat = bc[:, n_state:]

    @pl.when(step == 0)
    def _():
        ds_acc[...] = jnp.zeros_like(ds_acc)
        dg_out[...] = jnp.zeros_like(dg_out)

    def entering(block):
        low = enter[:, 2 * block : 2 * block + 1]
        top = enter[:, 2 * block + 1 : 2 * block + 2]
        return jnp.where(lane < HEAD_DIM, low, top)

    square = jnp.zeros((rows, 2 * HEAD_DIM), f32)
    cross = jnp.zeros((rows, 2 * HEAD_DIM), f32)
    for block in range(width // (2 * HEAD_DIM)):
        lanes = slice(block * 2 * HEAD_DIM, (block + 1) * 2 * HEAD_DIM)
        mo = y_in[:, lanes] + entering(block) * mm(c_mat, state[:, lanes])
        mo_out[:, lanes] = mo
        z = z_in[:, lanes].astype(f32)
        silu = z * jax.nn.sigmoid(z)
        gated = mo.astype(bf16).astype(f32) * silu
        gated_s[:, lanes] = gated
        silu_s[:, lanes] = silu
        square = square + gated * gated
        cross = cross + gated * (dn_in[:, lanes] * gain[0:1, lanes])
    scale = lax.rsqrt(jnp.sum(square, axis=1, keepdims=True) * (1.0 / width) + EPS)
    pull = scale * scale * scale * (jnp.sum(cross, axis=1, keepdims=True) * (1.0 / width))
    dc = jnp.zeros((rows, n_state), f32)
    for block in range(width // (2 * HEAD_DIM)):
        lanes = slice(block * 2 * HEAD_DIM, (block + 1) * 2 * HEAD_DIM)
        gated = gated_s[:, lanes]
        silu = silu_s[:, lanes]
        dn = dn_in[:, lanes]
        hat = gated * scale
        norm_out[:, lanes] = (hat * gain[0:1, lanes]).astype(bf16)
        part = dn * hat
        total = part[0:8, :]
        for at in range(8, rows, 8):
            total = total + part[at : at + 8, :]
        dg_out[:, lanes] += total
        d_gated = scale * (dn * gain[0:1, lanes]) - gated * pull
        dy = (d_gated * silu).astype(bf16)
        dy_out[:, lanes] = dy
        z = z_in[:, lanes].astype(f32)
        sig = jax.nn.sigmoid(z)
        mo = mo_out[:, lanes].astype(bf16).astype(f32)
        dz_out[:, lanes] = (d_gated * mo * (sig + silu * (1.0 - sig))).astype(bf16)
        weighted = (dy.astype(f32) * entering(block)).astype(bf16)
        ds_acc[:, lanes] += mm(ct[...], weighted)
        dc = dc + mm_nt(weighted, state[:, lanes])
    dc_out[...] = dc

    @pl.when(step == pl.num_programs(0) - 1)
    def _():
        ds_out[...] = ds_acc[...].astype(bf16)


def inside_kernel(
    raw, taps, masks, seg_row, aux, aux_row, bc, ct, dy, dxs_out, db_out, dc_out, wide, score, pair,
    xs
):
    length = dxs_out.shape[0]
    n_state = ct.shape[0]
    step = pl.program_id(0)
    wide[...] = raw[...].astype(f32)

    @pl.when(step == 0)
    def _():
        pair[...] = jnp.zeros_like(pair)
        for start in range(0, length, TILE):
            rows = pl.ds(start, TILE)
            product = mm(bc[rows, :n_state], ct[...])
            here = lax.broadcasted_iota(jnp.int32, (TILE, length), 0) + start
            there = lax.broadcasted_iota(jnp.int32, (TILE, length), 1)
            seen = (masks[rows, 6:7] == seg_row[0:1, :]) & (here <= there)
            score[rows, :] = jnp.where(seen, product, 0.0)

    for start in range(0, length, TILE):
        rows = pl.ds(start, TILE)
        pre = conv_rows(wide, taps, masks, start, TILE)
        x = pre * jax.nn.sigmoid(pre)
        xs[rows, :] = (x * spread(aux[0, rows, :], 1, 4)).astype(bf16)
    for start in range(0, length, TILE):
        rows = pl.ds(start, TILE)
        columns = aux[0, rows, :]
        gathered = None
        for head in range(GROUP):
            lanes = slice(head * HEAD_DIM, (head + 1) * HEAD_DIM)
            gap = aux_row[0, head : head + 1, start:] - columns[:, 4 * head : 4 * head + 1]
            decay = jnp.exp(jnp.minimum(gap, 0.0))
            weight = (decay * score[rows, start:]).astype(bf16)
            dxs_out[rows, lanes] = mm(weight, dy[start:, lanes])
            crossed = decay * mm_nt(xs[rows, lanes], dy[start:, lanes])
            gathered = crossed if gathered is None else gathered + crossed
        pair[rows, start:] += gathered

    @pl.when(step == pl.num_programs(0) - 1)
    def _():
        for start in range(0, length, TILE):
            rows = pl.ds(start, TILE)
            here = lax.broadcasted_iota(jnp.int32, (TILE, length), 0) + start
            there = lax.broadcasted_iota(jnp.int32, (TILE, length), 1)
            seen = (masks[rows, 6:7] == seg_row[0:1, :]) & (here <= there)
            part = jnp.where(seen, pair[rows, :], 0.0).astype(bf16)
            db_out[rows, :] = mm(part, bc[:, n_state:])
            if start == 0:
                dc_out[...] = mm_tn(part, bc[rows, :n_state])
            else:
                dc_out[...] += mm_tn(part, bc[rows, :n_state])


def outside_kernel(
    raw, taps, masks, aux, bc, dy, mo, dxs_in, d_state, state, db_in, dc_in, dc_more,
    d_out, first_out, last_out, sums_out, red_out, wide, d_pre, db_acc
):
    length = d_out.shape[0]
    n_state = bc.shape[1] // 2
    step = pl.program_id(0)
    last_step = pl.num_programs(0) - 1
    wide[...] = raw[...].astype(f32)

    @pl.when(step == 0)
    def _():
        db_acc[...] = jnp.zeros_like(db_acc)

    d_pre[pl.ds(length, HALO), :] = jnp.zeros((HALO, d_pre.shape[1]), f32)
    zero = jnp.zeros((1, d_pre.shape[1]), f32)

    @pl.when(step < last_step)
    def _():
        skip_sum, keep_sum = (zero, zero)
        ds = d_state[...]
        lane = lax.broadcasted_iota(jnp.int32, (TILE, 2 * HEAD_DIM), 1)
        for start in range(0, length, TILE):
            rows = pl.ds(start, TILE)
            columns = aux[0, rows, :]
            pre = conv_rows(wide, taps, masks, start, TILE)
            sig = jax.nn.sigmoid(pre)
            x = pre * sig
            stepped = spread(columns, 1, 4)
            scaled = (x * stepped).astype(bf16)
            keep = spread(columns, 2, 4)
            carried = keep * mm(bc[rows, :n_state], ds)
            dxs = dxs_in[rows, :] + carried
            kept = (scaled.astype(f32) * keep).astype(bf16)
            db_acc[rows, :] += mm_nt(kept, ds)
            grad = dy[rows, :].astype(f32)
            keep_sum = keep_sum + jnp.sum(scaled.astype(f32) * carried, 0, keepdims=True)
            skip_sum = skip_sum + jnp.sum(grad * x, 0, keepdims=True)
            change = grad * (mo[rows, :] - taps[5:6, :] * x) - scaled.astype(f32) * dxs
            direct = x * dxs
            found = jnp.zeros((TILE, 2 * HEAD_DIM), f32)
            for head in range(GROUP):
                lanes = slice(head * HEAD_DIM, (head + 1) * HEAD_DIM)
                one = jnp.sum(change[:, lanes], 1, keepdims=True)
                two = jnp.sum(direct[:, lanes], 1, keepdims=True)
                found = jnp.where(lane == head, one, found)
                found = jnp.where(lane == GROUP + head, two, found)
            red_out[0, rows, :] = found[:, : red_out.shape[2]]
            d_x = taps[5:6, :] * grad + stepped * dxs
            d_pre[rows, :] = d_x * (sig + x * (1.0 - sig))
        met = jnp.sum(ds.astype(f32) * state[...].astype(f32), 0, keepdims=True)
        sums_out[5:6, :] = skip_sum
        sums_out[6:7, :] = keep_sum
        sums_out[7:8, :] = met

    @pl.when(step == last_step)
    def _():
        for start in range(0, length, TILE):
            rows = pl.ds(start, TILE)
            pre = conv_rows(wide, taps, masks, start, TILE)
            sig = jax.nn.sigmoid(pre)
            slope = sig + pre * sig * (1.0 - sig)
            d_b = db_in[rows, :] + db_acc[rows, :]
            d_c = dc_in[rows, :] + dc_more[rows, :]
            d_pre[rows, :] = jnp.concatenate([d_b, d_c], 1) * slope
        sums_out[5:8, :] = jnp.zeros((3, d_pre.shape[1]), f32)

    totals = [zero] * (CONV + 1)
    for start in range(0, length, TILE):
        rows = pl.ds(start, TILE)
        grad = d_pre[rows, :]
        totals[CONV] = totals[CONV] + jnp.sum(grad, 0, keepdims=True)
        here = wide[pl.ds(HALO + start, TILE), :]
        totals[CONV - 1] = totals[CONV - 1] + jnp.sum(grad * here, 0, keepdims=True)
        back = taps[CONV - 1 : CONV, :] * grad
        for tap in range(CONV - 1):
            shifted = wide[pl.ds(HALO - CONV + 1 + tap + start, TILE), :]
            masked = grad * masks[rows, tap : tap + 1]
            totals[tap] = totals[tap] + jnp.sum(masked * shifted, 0, keepdims=True)
            ahead = d_pre[pl.ds(start + CONV - 1 - tap, TILE), :]
            back = back + taps[tap : tap + 1, :] * ahead * masks[rows, 3 + tap : 4 + tap]
        d_out[rows, :] = back.astype(bf16)
        if start + TILE == length:
            last_out[...] = back[TILE - HALO :, :]
    first_out[...] = d_pre[pl.ds(0, HALO), :]
    for tap in range(CONV + 1):
        sums_out[tap : tap + 1, :] = totals[tap]


def scan_devices(local, decay, backward):
    shards, places = (lax.axis_size("shard"), lax.axis_size("seq"))
    shard, place = (lax.axis_index("shard"), lax.axis_index("seq"))
    n_state, inner = local.shape
    width = inner // places
    split = local.reshape(n_state, places, width).transpose(1, 0, 2)
    mine = lax.all_to_all(split, "seq", split_axis=0, concat_axis=0, tiled=True).astype(f32)
    decay = lax.dynamic_slice_in_dim(decay.reshape(shards, places, inner), place * width, width, 2)
    own = lax.dynamic_index_in_dim(decay, shard, 0, False)
    order = range(places - 1, -1, -1) if backward else range(places)
    state = jnp.zeros((n_state, width), f32)
    for at in order:
        state = own[at][None, :] * state + mine[at]
    parts = lax.all_gather(state.astype(bf16), "shard").astype(f32)
    whole = jnp.prod(decay, axis=1)
    state = jnp.zeros((n_state, width), f32)
    for at in range(shards - 1, -1, -1) if backward else range(shards):
        counted = (at > shard) if backward else (at < shard)
        state = jnp.where(counted, whole[at][None, :] * state + parts[at], state)
    entering = [None] * places
    for at in order:
        entering[at] = state.astype(bf16)
        state = own[at][None, :] * state + mine[at]
    back = lax.all_to_all(jnp.stack(entering), "seq", split_axis=0, concat_axis=0, tiled=True)
    return back.transpose(1, 0, 2).reshape(n_state, inner)


def on_device(
    hidden,
    cotangent,
    seg_ids,
    norm_gain,
    in_weight,
    conv_weight,
    conv_bias,
    dt_bias,
    a_log,
    d_skip,
    out_gain,
    out_weight,
):
    shards, places = (lax.axis_size("shard"), lax.axis_size("seq"))
    shard, place = (lax.axis_index("shard"), lax.axis_index("seq"))
    devices = shards * places
    me = shard * places + place
    length, width = hidden.shape
    heads = dt_bias.shape[0]
    inner = out_weight.shape[0] * shards
    channels = conv_bias.shape[0] * shards
    n_state = (channels - inner) // 2
    groups = inner // WIDE
    start = me * length

    small = jnp.concatenate(
        [norm_gain, conv_weight.reshape(-1), conv_bias, out_gain]
    )
    small = lax.all_gather(small, "shard")
    at = 0
    gain_in = small[:, at : at + norm_gain.shape[0]].reshape(-1).astype(f32)
    at += norm_gain.shape[0]
    taps = small[:, at : at + conv_weight.size].reshape(shards, CONV, -1)
    taps = taps.transpose(1, 0, 2).reshape(CONV, channels).astype(f32)
    at += conv_weight.size
    bias = small[:, at : at + conv_bias.shape[0]].reshape(-1).astype(f32)
    at += conv_bias.shape[0]
    gain_out = small[:, at:].reshape(-1).astype(f32)
    w_x = lax.all_gather(in_weight[:, inner:], "shard", axis=0, tiled=True)
    w_z = lax.all_gather(in_weight[:, :inner], "shard", axis=0, tiled=True)
    w_out = lax.all_gather(out_weight, "shard", axis=0, tiled=True)
    skip_wide = jnp.repeat(d_skip.astype(f32), HEAD_DIM)
    rows = jnp.concatenate([skip_wide, jnp.zeros((channels - inner,), f32)])
    taps8 = jnp.concatenate([taps, bias[None], rows[None], jnp.zeros((2, channels), f32)], 0)

    edge = jnp.full((HALO,), -1, jnp.int32)
    padded = jnp.concatenate([edge, seg_ids, edge - 1])
    near = lax.dynamic_slice_in_dim(padded, start, length + 2 * HALO)
    seg = near[HALO : HALO + length]
    fwd_masks = [near[HALO - CONV + 1 + k : HALO - CONV + 1 + k + length] == seg for k in range(3)]
    spot = jnp.arange(length, dtype=jnp.int32)
    bwd_masks = [
        (near[HALO + CONV - 1 - k : HALO + CONV - 1 - k + length] == seg)
        & (spot + CONV - 1 - k < length)
        for k in range(3)
    ]
    masks = jnp.stack(
        [m.astype(f32) for m in fwd_masks + bwd_masks] + [seg.astype(f32), jnp.zeros((length,), f32)],
        1,
    )
    seg_row = jnp.broadcast_to(seg.astype(f32)[None, :], (8, length))
    from_before = seg == near[HALO - 1]
    to_last = seg == seg[length - 1]

    behind = lax.ppermute(
        hidden[length - HALO :], ALL, [(i, i + 1) for i in range(devices - 1)]
    )
    hidden_f = jnp.concatenate([behind, hidden], 0).astype(f32)
    scale_in = lax.rsqrt(jnp.mean(hidden_f * hidden_f, axis=1, keepdims=True) + EPS)
    normed_ext = (hidden_f * scale_in * gain_in[None, :]).astype(bf16)
    normed_in = normed_ext[HALO:]
    proj = mm(normed_ext, w_x).astype(bf16)
    dt_raw = proj[HALO:, channels:].astype(f32)
    shifted = dt_raw + dt_bias.astype(f32)[None, :]
    step_size = jax.nn.softplus(shifted)
    rate = jnp.exp(a_log.astype(f32))
    log_decay = -step_size * rate[None, :]
    lower = (spot[:, None] >= spot[None, :]).astype(f32)
    cum = jnp.dot(lower, log_decay, precision=HIGH)
    keep = jnp.where(to_last[:, None], jnp.exp(cum[length - 1][None, :] - cum), 0.0)
    enter = jnp.where(from_before[:, None], jnp.exp(cum), 0.0)
    aux = jnp.stack([cum, step_size, keep, enter], -1).reshape(length, groups, 4 * GROUP)
    aux = aux.transpose(1, 0, 2)
    aux_row = cum.T.reshape(groups, GROUP, length)
    decays = lax.all_gather(enter[length - 1], ALL)
    decays = jnp.repeat(decays.reshape(devices, heads), HEAD_DIM, axis=1)

    big = pltpu.CompilerParams(vmem_limit_bytes=56 * 1024 * 1024)

    def whole(shape):
        return pl.BlockSpec(shape, lambda g: (0,) * len(shape))

    def group_of(g):
        return jnp.maximum(g - 1, 0)

    order = lambda g: jnp.where(g == 0, groups, g - 1)
    y_local, state_local, bc, ct = pl.pallas_call(
        forward_kernel,
        grid=(groups + 1,),
        in_specs=[
            pl.BlockSpec((length + HALO, WIDE), lambda g: (0, order(g))),
            pl.BlockSpec((8, WIDE), lambda g: (0, order(g))),
            whole((length, 8)),
            whole((8, length)),
            pl.BlockSpec((1, length, 4 * GROUP), lambda g: (group_of(g), 0, 0)),
            pl.BlockSpec((1, GROUP, length), lambda g: (group_of(g), 0, 0)),
        ],
        out_specs=[
            pl.BlockSpec((length, WIDE), lambda g: (0, group_of(g))),
            pl.BlockSpec((n_state, WIDE), lambda g: (0, group_of(g))),
            whole((length, 2 * n_state)),
            whole((n_state, length)),
        ],
        out_shape=[
            jax.ShapeDtypeStruct((length, inner), f32),
            jax.ShapeDtypeStruct((n_state, inner), bf16),
            jax.ShapeDtypeStruct((length, 2 * n_state), bf16),
            jax.ShapeDtypeStruct((n_state, length), bf16),
        ],
        scratch_shapes=[
            pltpu.VMEM((length + HALO, WIDE), f32),
            pltpu.VMEM((length, length), f32),
            pltpu.VMEM((n_state, length), bf16),
            pltpu.VMEM((length, WIDE), bf16),
        ],
        compiler_params=big,
        cost_estimate=pl.CostEstimate(
            flops=4 * length * length * inner, bytes_accessed=10 * length * inner, transcendentals=0
        ),
        name="mixer_forward",
    )(proj, taps8, masks, seg_row, aux, aux_row)

    state_in = scan_devices(state_local, decays, False)
    gate_z = mm(normed_in, w_z).astype(bf16)
    d_normed = mm_nt(cotangent, w_out)

    block = TILE
    tall = lambda dim: pl.BlockSpec((block, dim), lambda g: (g, 0))
    mo, normed_out, d_z, d_y, d_state_local, dc_more, d_gain = pl.pallas_call(
        gate_kernel,
        grid=(length // block,),
        in_specs=[
            tall(inner),
            tall(inner),
            tall(inner),
            tall(2 * n_state),
            pl.BlockSpec((n_state, block), lambda g: (0, g)),
            tall(heads),
            whole((n_state, inner)),
            whole((1, inner)),
        ],
        out_specs=[
            tall(inner),
            tall(inner),
            tall(inner),
            tall(inner),
            whole((n_state, inner)),
            tall(n_state),
            whole((8, inner)),
        ],
        out_shape=[
            jax.ShapeDtypeStruct((length, inner), f32),
            jax.ShapeDtypeStruct((length, inner), bf16),
            jax.ShapeDtypeStruct((length, inner), bf16),
            jax.ShapeDtypeStruct((length, inner), bf16),
            jax.ShapeDtypeStruct((n_state, inner), bf16),
            jax.ShapeDtypeStruct((length, n_state), f32),
            jax.ShapeDtypeStruct((8, inner), f32),
        ],
        scratch_shapes=[
            pltpu.VMEM((block, inner), f32),
            pltpu.VMEM((block, inner), f32),
            pltpu.VMEM((n_state, inner), f32),
        ],
        compiler_params=big,
        cost_estimate=pl.CostEstimate(
            flops=8 * length * n_state * inner, bytes_accessed=22 * length * inner, transcendentals=0
        ),
        name="mixer_gate",
    )(y_local, gate_z, d_normed, bc, ct, enter, state_in, gain_out[None, :])

    block_out = (hidden.astype(f32) + mm(normed_out, w_out)).astype(bf16)
    grad_out_w = mm_tn(normed_out, cotangent).astype(bf16)
    grad_z_w = mm_tn(normed_in, d_z).astype(bf16)
    d_state = scan_devices(d_state_local, decays, True)

    dxs, db_in, dc_in = pl.pallas_call(
        inside_kernel,
        grid=(groups,),
        in_specs=[
            pl.BlockSpec((length + HALO, WIDE), lambda g: (0, g)),
            pl.BlockSpec((8, WIDE), lambda g: (0, g)),
            whole((length, 8)),
            whole((8, length)),
            pl.BlockSpec((1, length, 4 * GROUP), lambda g: (g, 0, 0)),
            pl.BlockSpec((1, GROUP, length), lambda g: (g, 0, 0)),
            whole((length, 2 * n_state)),
            whole((n_state, length)),
            pl.BlockSpec((length, WIDE), lambda g: (0, g)),
        ],
        out_specs=[
            pl.BlockSpec((length, WIDE), lambda g: (0, g)),
            whole((length, n_state)),
            whole((length, n_state)),
        ],
        out_shape=[
            jax.ShapeDtypeStruct((length, inner), f32),
            jax.ShapeDtypeStruct((length, n_state), f32),
            jax.ShapeDtypeStruct((length, n_state), f32),
        ],
        scratch_shapes=[
            pltpu.VMEM((length + HALO, WIDE), f32),
            pltpu.VMEM((length, length), f32),
            pltpu.VMEM((length, length), f32),
            pltpu.VMEM((length, WIDE), bf16),
        ],
        compiler_params=big,
        cost_estimate=pl.CostEstimate(
            flops=8 * length * length * inner, bytes_accessed=10 * length * inner, transcendentals=0
        ),
        name="mixer_inside",
    )(proj, taps8, masks, seg_row, aux, aux_row, bc, ct, d_y)

    kept = lambda g: jnp.minimum(g, groups - 1)
    d_xbc, first, last, sums, reduced = pl.pallas_call(
        outside_kernel,
        grid=(groups + 1,),
        in_specs=[
            pl.BlockSpec((length + HALO, WIDE), lambda g: (0, g)),
            pl.BlockSpec((8, WIDE), lambda g: (0, g)),
            whole((length, 8)),
            pl.BlockSpec((1, length, 4 * GROUP), lambda g: (kept(g), 0, 0)),
            whole((length, 2 * n_state)),
            pl.BlockSpec((length, WIDE), lambda g: (0, kept(g))),
            pl.BlockSpec((length, WIDE), lambda g: (0, kept(g))),
            pl.BlockSpec((length, WIDE), lambda g: (0, kept(g))),
            pl.BlockSpec((n_state, WIDE), lambda g: (0, kept(g))),
            pl.BlockSpec((n_state, WIDE), lambda g: (0, kept(g))),
            whole((length, n_state)),
            whole((length, n_state)),
            whole((length, n_state)),
        ],
        out_specs=[
            pl.BlockSpec((length, WIDE), lambda g: (0, g)),
            pl.BlockSpec((HALO, WIDE), lambda g: (0, g)),
            pl.BlockSpec((HALO, WIDE), lambda g: (0, g)),
            pl.BlockSpec((8, WIDE), lambda g: (0, g)),
            pl.BlockSpec((1, length, 2 * GROUP), lambda g: (kept(g), 0, 0)),
        ],
        out_shape=[
            jax.ShapeDtypeStruct((length, channels), bf16),
            jax.ShapeDtypeStruct((HALO, channels), f32),
            jax.ShapeDtypeStruct((HALO, channels), f32),
            jax.ShapeDtypeStruct((8, channels), f32),
            jax.ShapeDtypeStruct((groups, length, 2 * GROUP), f32),
        ],
        scratch_shapes=[
            pltpu.VMEM((length + HALO, WIDE), f32),
            pltpu.VMEM((length + HALO, WIDE), f32),
            pltpu.VMEM((length, n_state), f32),
        ],
        compiler_params=big,
        cost_estimate=pl.CostEstimate(
            flops=8 * length * n_state * inner, bytes_accessed=16 * length * inner, transcendentals=0
        ),
        name="mixer_outside",
    )(proj, taps8, masks, aux, bc, d_y, mo, dxs, d_state, state_in, db_in, dc_in, dc_more)

    ahead = lax.ppermute(first, ALL, [(i + 1, i) for i in range(devices - 1)])
    joined = jnp.concatenate([jnp.zeros((HALO, channels), f32), ahead], 0)
    seg_end = near[length : length + 2 * HALO]
    for tap in range(CONV - 1):
        lead = CONV - 1 - tap
        same = (seg_end[lead : lead + HALO] == seg_end[:HALO]).astype(f32)[:, None]
        last = last + taps[tap][None, :] * joined[lead : lead + HALO] * same
    d_xbc = lax.dynamic_update_slice_in_dim(d_xbc, last.astype(bf16), length - HALO, 0)

    reduced = reduced.reshape(groups, length, 2, GROUP).transpose(2, 1, 0, 3).reshape(2, length, heads)
    to_head = lambda row: row[:inner].reshape(heads, HEAD_DIM).sum(1)
    tail = to_head(sums[6]) + enter[length - 1] * to_head(sums[7])
    d_cum = reduced[0].at[length - 1].add(tail)
    d_log = jnp.dot(lower.T, d_cum, precision=HIGH)
    d_step = reduced[1] - rate[None, :] * d_log
    d_dt = d_step * jax.nn.sigmoid(shifted)
    grad_a = jnp.sum(d_log * log_decay, 0)
    grad_dt = jnp.sum(d_dt, 0)
    grad_skip = to_head(sums[5])

    d_proj = jnp.concatenate([d_xbc, d_dt.astype(bf16)], 1)
    grad_x_w = mm_tn(normed_in, d_proj).astype(bf16)
    d_normed_in = mm_nt(d_z, w_z) + mm_nt(d_proj, w_x)
    base = hidden_f[HALO:]
    scale = scale_in[HALO:]
    d_hat = d_normed_in * gain_in[None, :]
    mean = jnp.mean(d_hat * base, axis=1, keepdims=True)
    grad_hidden = cotangent.astype(f32) + scale * d_hat - base * (scale * scale * scale * mean)
    grad_gain_in = jnp.sum(d_normed_in * base * scale, 0)
    grad_gain_out = jnp.sum(d_gain, 0)

    scatter = lambda a: lax.psum_scatter(a, ALL, scatter_dimension=0, tiled=True)
    out_w = scatter(grad_out_w).astype(f32)
    z_w = scatter(grad_z_w).astype(f32)
    x_w = scatter(grad_x_w).astype(f32)
    pieces = [
        grad_gain_in,
        sums[:CONV].reshape(-1),
        sums[CONV],
        grad_gain_out,
        grad_dt,
        grad_a,
        grad_skip,
    ]
    total = lax.psum(jnp.concatenate(pieces), ALL)
    found, at = ([], 0)
    for piece in pieces:
        found.append(total[at : at + piece.shape[0]])
        at += piece.shape[0]

    def part(vector):
        size = vector.shape[-1] // devices
        return lax.dynamic_slice_in_dim(vector, me * size, size, vector.ndim - 1)

    return (
        block_out,
        grad_hidden,
        part(found[0]),
        jnp.concatenate([z_w, x_w], 1),
        part(found[1].reshape(CONV, channels)),
        part(found[2]),
        found[4],
        found[5],
        found[6],
        part(found[3]),
        out_w,
    )


def solution(mesh):
    return jax.shard_map(
        on_device,
        mesh=mesh,
        in_specs=(
            P(ALL, None),
            P(ALL, None),
            P(),
            P("shard"),
            P("shard", None),
            P(None, "shard"),
            P("shard"),
            P(),
            P(),
            P(),
            P("shard"),
            P("shard", None),
        ),
        out_specs=(
            P(ALL, None),
            P(ALL, None),
            P(ALL),
            P(ALL, None),
            P(None, ALL),
            P(ALL),
            P(),
            P(),
            P(),
            P(ALL),
            P(ALL, None),
        ),
        check_vma=False,
    )
```

```python
import jax
import jax.numpy as jnp
from jax import lax
from jax.experimental import pallas as pl
from jax.experimental.pallas import tpu as pltpu
from jax.sharding import PartitionSpec as P

HEAD_DIM = 64
CONV = 4
EPS = 1e-05
HALO = 8
GROUP = 4
WIDE = GROUP * HEAD_DIM
TILE = 128
HIGH = lax.Precision.HIGHEST
ALL = ("shard", "seq")
f32 = jnp.float32
bf16 = jnp.bfloat16


def mm(a, b):
    return jnp.dot(a, b, preferred_element_type=f32)


def mm_nt(a, b):
    return lax.dot_general(a, b, (((1,), (1,)), ((), ())), preferred_element_type=f32)


def mm_tn(a, b):
    return lax.dot_general(a, b, (((0,), (0,)), ((), ())), preferred_element_type=f32)


def sigmoid(value):
    return 0.5 * jnp.tanh(0.5 * value) + 0.5


def group_columns(value, group):
    lanes = value.shape[1]
    return pltpu.roll(value, lax.rem(lanes - GROUP * group, lanes), 1)


def spread(columns):
    rows = columns.shape[0]
    lane = lax.broadcasted_iota(jnp.int32, (rows, 2 * HEAD_DIM), 1)
    out = []
    for pair in range(GROUP // 2):
        low = columns[:, 2 * pair : 2 * pair + 1]
        top = columns[:, 2 * pair + 1 : 2 * pair + 2]
        out.append(jnp.where(lane < HEAD_DIM, low, top))
    return jnp.concatenate(out, axis=1)


def conv_rows(wide, taps, masks, start, rows):
    pre = taps[CONV : CONV + 1, :] + taps[CONV - 1 : CONV, :] * wide[pl.ds(HALO + start, rows), :]
    for tap in range(CONV - 1):
        shifted = wide[pl.ds(HALO - CONV + 1 + tap + start, rows), :]
        pre = pre + taps[tap : tap + 1, :] * shifted * masks[pl.ds(start, rows), tap : tap + 1]
    return pre


def prepare_kernel(edge, rates, masks, out, row_out):
    length = out.shape[1]
    shifted = edge[...].astype(f32) + rates[0:1, :]
    step = jax.nn.softplus(shifted)
    here = lax.broadcasted_iota(jnp.int32, (length, length), 0)
    there = lax.broadcasted_iota(jnp.int32, (length, length), 1)
    lower = jnp.where(here >= there, 1.0, 0.0)
    log_decay = -step * jnp.exp(rates[1:2, :])
    cum = lax.dot_general(
        lower, log_decay, (((1,), (0,)), ((), ())), precision=HIGH, preferred_element_type=f32
    )
    out[0] = cum
    out[1] = step
    out[2] = jnp.exp(cum[length - 1 : length, :] - cum) * masks[:, 8:9]
    out[3] = jnp.exp(cum) * masks[:, 7:8]
    out[4] = sigmoid(shifted)
    turned = cum.T
    for group in range(row_out.shape[0]):
        row_out[group] = turned[GROUP * group : GROUP * (group + 1), :]


def state_kernel(raw, raw_bc, taps, masks, heads, x_out, state_out, bc_out, bt_out, ct_out, wide, bt):
    length = x_out.shape[0]
    n_state = bt.shape[0]
    step = pl.program_id(0)

    @pl.when(step == 0)
    def _():
        wide[...] = raw_bc[...].astype(f32)
        for start in range(0, length, TILE):
            rows = pl.ds(start, TILE)
            pre = conv_rows(wide, taps, masks, start, TILE)
            both = pre * sigmoid(pre)
            bc_out[rows, :] = both.astype(bf16)
            turned = both[:, :n_state].T.astype(bf16)
            bt[:, rows] = turned
            bt_out[:, rows] = turned
            ct_out[:, rows] = both[:, n_state:].T.astype(bf16)

    @pl.when(step > 0)
    def _():
        wide[...] = raw[...].astype(f32)
        kept = []
        for start in range(0, length, TILE):
            rows = pl.ds(start, TILE)
            pre = conv_rows(wide, taps, masks, start, TILE)
            x = (pre * sigmoid(pre)).astype(bf16)
            x_out[rows, :] = x
            stepped = spread(group_columns(heads[1, rows, :], step - 1))
            scaled = (x.astype(f32) * stepped).astype(bf16)
            keep = spread(group_columns(heads[2, rows, :], step - 1))
            kept.append((scaled.astype(f32) * keep).astype(bf16))
        state_out[...] = mm(bt[...], jnp.concatenate(kept, 0)).astype(bf16)


def scored(first, second, masks, seg_row, score, later):
    length = score.shape[0]
    for start in range(0, length, TILE):
        rows = pl.ds(start, TILE)
        product = mm(first(rows), second[...])
        here = lax.broadcasted_iota(jnp.int32, (TILE, length), 0) + start
        there = lax.broadcasted_iota(jnp.int32, (TILE, length), 1)
        order = (here >= there) if later else (here <= there)
        seen = (masks[rows, 6:7] == seg_row[0:1, :]) & order
        score[rows, :] = jnp.where(seen, product, 0.0)


def scale_by_step(x_in, heads, xs, group):
    for start in range(0, x_in.shape[0], TILE):
        rows = pl.ds(start, TILE)
        stepped = spread(group_columns(heads[1, rows, :], group))
        xs[rows, :] = (x_in[rows, :].astype(f32) * stepped).astype(bf16)


def forward_kernel(x_in, masks, seg_row, heads, sums_row, bc, bt, y_out, score, xs, weights):
    length = y_out.shape[0]
    n_state = bt.shape[0]
    group = pl.program_id(0)
    big = 2 * TILE

    @pl.when(group == 0)
    def _():
        scored(lambda rows: bc[rows, n_state:], bt, masks, seg_row, score, True)
        weights[...] = jnp.zeros_like(weights)

    scale_by_step(x_in, heads, xs, group)
    columns = [group_columns(heads[0, pl.ds(at, TILE), :], group) for at in range(0, length, TILE)]
    for head in range(GROUP):
        lanes = slice(head * HEAD_DIM, (head + 1) * HEAD_DIM)
        for start in range(0, length, TILE):
            rows = pl.ds(start, TILE)
            seen = start + TILE
            gap = columns[start // TILE][:, head : head + 1] - sums_row[0, head : head + 1, :seen]
            weight = jnp.exp(jnp.minimum(gap, 0.0)) * score[rows, :seen]
            weights[rows, :seen] = weight.astype(bf16)
        for cut in range(0, length, big):
            part = mm(weights[cut:, cut : cut + big], xs[cut : cut + big, lanes])
            if cut == 0:
                y_out[:, lanes] = part
            else:
                y_out[cut:, lanes] += part


def gate_kernel(
    y_in, x_in, z_in, dn_in, bc, ct, enter, state, gain, ssm_out, norm_out, dz_out, dy_out,
    ds_out, dc_out, dg_out, gated_s, sig_s, mo_s, ds_acc
):
    rows = y_in.shape[0]
    width = y_in.shape[1]
    n_state = state.shape[0]
    step = pl.program_id(0)
    lane = lax.broadcasted_iota(jnp.int32, (rows, 2 * HEAD_DIM), 1)
    c_mat = bc[:, n_state:]

    @pl.when(step == 0)
    def _():
        ds_acc[...] = jnp.zeros_like(ds_acc)
        dg_out[...] = jnp.zeros_like(dg_out)

    def entering(block):
        low = enter[:, 2 * block : 2 * block + 1]
        top = enter[:, 2 * block + 1 : 2 * block + 2]
        return jnp.where(lane < HEAD_DIM, low, top)

    square = jnp.zeros((rows, 2 * HEAD_DIM), f32)
    cross = jnp.zeros((rows, 2 * HEAD_DIM), f32)
    for block in range(width // (2 * HEAD_DIM)):
        lanes = slice(block * 2 * HEAD_DIM, (block + 1) * 2 * HEAD_DIM)
        ssm = y_in[:, lanes] + entering(block) * mm(c_mat, state[:, lanes])
        ssm_out[:, lanes] = ssm
        mo = (ssm + gain[1:2, lanes] * x_in[:, lanes].astype(f32)).astype(bf16)
        mo_s[:, lanes] = mo
        z = z_in[:, lanes].astype(f32)
        sig = sigmoid(z)
        gated = mo.astype(f32) * (z * sig)
        gated_s[:, lanes] = gated
        sig_s[:, lanes] = sig
        square = square + gated * gated
        cross = cross + gated * (dn_in[:, lanes] * gain[0:1, lanes])
    scale = lax.rsqrt(jnp.sum(square, axis=1, keepdims=True) * (1.0 / width) + EPS)
    pull = scale * scale * scale * (jnp.sum(cross, axis=1, keepdims=True) * (1.0 / width))
    dc = jnp.zeros((rows, n_state), f32)
    for block in range(width // (2 * HEAD_DIM)):
        lanes = slice(block * 2 * HEAD_DIM, (block + 1) * 2 * HEAD_DIM)
        gated = gated_s[:, lanes]
        sig = sig_s[:, lanes]
        silu = z_in[:, lanes].astype(f32) * sig
        dn = dn_in[:, lanes]
        hat = gated * scale
        norm_out[:, lanes] = (hat * gain[0:1, lanes]).astype(bf16)
        part = dn * hat
        total = part[0:8, :]
        for at in range(8, rows, 8):
            total = total + part[at : at + 8, :]
        dg_out[:, lanes] += total
        d_gated = scale * (dn * gain[0:1, lanes]) - gated * pull
        dy = (d_gated * silu).astype(bf16)
        dy_out[:, lanes] = dy
        mo = mo_s[:, lanes].astype(f32)
        dz_out[:, lanes] = (d_gated * mo * (sig + silu * (1.0 - sig))).astype(bf16)
        weighted = (dy.astype(f32) * entering(block)).astype(bf16)
        ds_acc[:, lanes] += mm(ct[...], weighted)
        dc = dc + mm_nt(weighted, state[:, lanes])
    dc_out[...] = dc

    @pl.when(step == pl.num_programs(0) - 1)
    def _():
        ds_out[...] = ds_acc[...].astype(bf16)


def inside_kernel(
    x_in, masks, seg_row, heads, sums_row, bc, ct, dy, dxs_out, db_out, dc_out, score, pair, xs,
    weights, crossed
):
    length = dxs_out.shape[0]
    n_state = ct.shape[0]
    group = pl.program_id(0)
    big = 2 * TILE

    @pl.when(group == 0)
    def _():
        pair[...] = jnp.zeros_like(pair)
        weights[...] = jnp.zeros_like(weights)
        scored(lambda rows: bc[rows, :n_state], ct, masks, seg_row, score, False)

    scale_by_step(x_in, heads, xs, group)
    columns = [group_columns(heads[0, pl.ds(at, TILE), :], group) for at in range(0, length, TILE)]
    for head in range(GROUP):
        lanes = slice(head * HEAD_DIM, (head + 1) * HEAD_DIM)
        for cut in range(0, length, big):
            stop = cut + big
            crossed[:stop, cut:stop] = mm_nt(xs[:stop, lanes], dy[cut:stop, lanes])
        for start in range(0, length, TILE):
            rows = pl.ds(start, TILE)
            gap = sums_row[0, head : head + 1, start:] - columns[start // TILE][:, head : head + 1]
            decay = jnp.exp(jnp.minimum(gap, 0.0))
            weights[rows, start:] = (decay * score[rows, start:]).astype(bf16)
            pair[rows, start:] += decay * crossed[rows, start:]
        for cut in range(length - big, -1, -big):
            stop = cut + big
            part = mm(weights[:stop, cut:stop], dy[cut:stop, lanes])
            if stop == length:
                dxs_out[:, lanes] = part
            else:
                dxs_out[:stop, lanes] += part

    @pl.when(group == pl.num_programs(0) - 1)
    def _():
        for start in range(0, length, TILE):
            rows = pl.ds(start, TILE)
            here = lax.broadcasted_iota(jnp.int32, (TILE, length), 0) + start
            there = lax.broadcasted_iota(jnp.int32, (TILE, length), 1)
            seen = (masks[rows, 6:7] == seg_row[0:1, :]) & (here <= there)
            part = jnp.where(seen, pair[rows, :], 0.0).astype(bf16)
            db_out[rows, :] = mm(part, bc[:, n_state:])
            if start == 0:
                dc_out[...] = mm_tn(part, bc[rows, :n_state])
            else:
                dc_out[...] += mm_tn(part, bc[rows, :n_state])


def split_mm(value, chosen):
    high = value.astype(bf16)
    low = (value - high.astype(f32)).astype(bf16)
    return mm(high, chosen) + mm(low, chosen)


def outside_kernel(
    raw, raw_bc, taps, masks, heads, rates, bc, dy, ssm, dxs_in, d_state, state, db_in, dc_in,
    dc_more, d_out, first_out, last_out, sums_out, head_out, wide, d_pre, db_acc, found, totals_s
):
    length = d_out.shape[0]
    n_state = bc.shape[1] // 2
    step = pl.program_id(0)
    bc_step = pl.num_programs(0) - 2

    @pl.when(step == 0)
    def _():
        db_acc[...] = jnp.zeros_like(db_acc)
        found[...] = jnp.zeros_like(found)
        totals_s[...] = jnp.zeros_like(totals_s)

    d_pre[pl.ds(length, HALO), :] = jnp.zeros((HALO, d_pre.shape[1]), f32)
    zero = jnp.zeros((1, d_pre.shape[1]), f32)

    @pl.when(step < bc_step)
    def _():
        wide[...] = raw[...].astype(f32)
        skip_sum, keep_sum = (zero, zero)
        ds = d_state[...]
        owner = lax.broadcasted_iota(jnp.int32, (WIDE, TILE), 0) // HEAD_DIM + GROUP * step
        chosen = (owner == lax.broadcasted_iota(jnp.int32, (WIDE, TILE), 1)).astype(f32)
        chosen_b = chosen.astype(bf16)
        for start in range(0, length, TILE):
            rows = pl.ds(start, TILE)
            pre = conv_rows(wide, taps, masks, start, TILE)
            sig = sigmoid(pre)
            x = pre * sig
            stepped = spread(group_columns(heads[1, rows, :], step))
            scaled = (x.astype(bf16).astype(f32) * stepped).astype(bf16)
            keep = spread(group_columns(heads[2, rows, :], step))
            carried = keep * mm(bc[rows, :n_state], ds)
            dxs = dxs_in[rows, :] + carried
            scaled = scaled.astype(f32)
            db_acc[rows, :] += mm_nt((scaled * keep).astype(bf16), ds)
            grad = dy[rows, :].astype(f32)
            keep_sum = keep_sum + jnp.sum(scaled * carried, 0, keepdims=True)
            skip_sum = skip_sum + jnp.sum(grad * x, 0, keepdims=True)
            found[0, rows, :] += split_mm(grad * ssm[rows, :] - scaled * dxs, chosen_b)
            found[1, rows, :] += split_mm(x * dxs, chosen_b)
            d_x = taps[5:6, :] * grad + stepped * dxs
            d_pre[rows, :] = d_x * (sig + x * (1.0 - sig))
        met = jnp.sum(ds.astype(f32) * state[...].astype(f32), 0, keepdims=True)
        rest = jnp.zeros((5, WIDE), f32)
        totals_s[...] += lax.dot_general(
            jnp.concatenate([skip_sum, keep_sum, met, rest], 0),
            chosen,
            (((1,), (0,)), ((), ())),
            precision=HIGH,
            preferred_element_type=f32,
        )

    @pl.when(step == bc_step)
    def _():
        wide[...] = raw_bc[...].astype(f32)
        for start in range(0, length, TILE):
            rows = pl.ds(start, TILE)
            pre = conv_rows(wide, taps, masks, start, TILE)
            sig = sigmoid(pre)
            slope = sig + pre * sig * (1.0 - sig)
            d_b = db_in[rows, :] + db_acc[rows, :]
            d_c = dc_in[rows, :] + dc_more[rows, :]
            d_pre[rows, :] = jnp.concatenate([d_b, d_c], 1) * slope

    @pl.when(step <= bc_step)
    def _():
        totals = [zero] * (CONV + 1)
        for start in range(0, length, TILE):
            rows = pl.ds(start, TILE)
            grad = d_pre[rows, :]
            totals[CONV] = totals[CONV] + jnp.sum(grad, 0, keepdims=True)
            here = wide[pl.ds(HALO + start, TILE), :]
            totals[CONV - 1] = totals[CONV - 1] + jnp.sum(grad * here, 0, keepdims=True)
            back = taps[CONV - 1 : CONV, :] * grad
            for tap in range(CONV - 1):
                shifted = wide[pl.ds(HALO - CONV + 1 + tap + start, TILE), :]
                masked = grad * masks[rows, tap : tap + 1]
                totals[tap] = totals[tap] + jnp.sum(masked * shifted, 0, keepdims=True)
                ahead = d_pre[pl.ds(start + CONV - 1 - tap, TILE), :]
                back = back + taps[tap : tap + 1, :] * ahead * masks[rows, 3 + tap : 4 + tap]
            d_out[rows, :] = back.astype(bf16)
            if start + TILE == length:
                last_out[...] = back[TILE - HALO :, :]
        first_out[...] = d_pre[pl.ds(0, HALO), :]
        for tap in range(CONV + 1):
            sums_out[tap : tap + 1, :] = totals[tap]
        sums_out[CONV + 1 : 8, :] = jnp.zeros((7 - CONV, d_pre.shape[1]), f32)

    @pl.when(step == bc_step + 1)
    def _():
        first_out[...] = jnp.zeros_like(first_out)
        last_out[...] = jnp.zeros_like(last_out)
        sums_out[...] = jnp.zeros_like(sums_out)
        rate = jnp.exp(rates[1:2, :])
        end = totals_s[1:2, :] + heads[3, pl.ds(length - 1, 1), :] * totals_s[2:3, :]
        here = lax.broadcasted_iota(jnp.int32, (length, length), 0)
        there = lax.broadcasted_iota(jnp.int32, (length, length), 1)
        upper = jnp.where(here <= there, 1.0, 0.0)
        d_log = lax.dot_general(
            upper, found[0], (((1,), (0,)), ((), ())), precision=HIGH, preferred_element_type=f32
        )
        d_log = d_log + end
        d_dt = (found[1] - rate * d_log) * heads[4]
        d_out[:, :TILE] = d_dt.astype(bf16)
        d_out[:, TILE:] = jnp.zeros((length, WIDE - TILE), bf16)
        head_out[0:1, :] = jnp.sum(d_dt, 0, keepdims=True)
        head_out[1:2, :] = jnp.sum(d_log * (-heads[1] * rate), 0, keepdims=True)
        head_out[2:3, :] = totals_s[0:1, :]
        head_out[3:8, :] = jnp.zeros((5, TILE), f32)


def pack_kernel(sizes, sums, gain_in, gain_out, head, out):
    devices = out.shape[0]
    wide, channels, inner, heads = sizes
    gains = jnp.sum(gain_out[...], 0, keepdims=True)
    for at in range(devices):
        pieces = [gain_in[:, at * wide : (at + 1) * wide]]
        for tap in range(CONV + 1):
            pieces.append(sums[tap : tap + 1, at * channels : (at + 1) * channels])
        pieces.append(gains[:, at * inner : (at + 1) * inner])
        for row in range(3):
            pieces.append(head[row : row + 1, :heads])
        begin = 0
        for piece in pieces:
            out[at, :, begin : begin + piece.shape[1]] = piece
            begin += piece.shape[1]
        if begin < out.shape[2]:
            out[at, :, begin:] = jnp.zeros((1, out.shape[2] - begin), f32)


def scan_kernel(backward, mine, decay, out):
    count = mine.shape[0]

    def one(index, state):
        at = count - 1 - index if backward else index
        out[at] = state.astype(bf16)
        return decay[pl.ds(at, 1), :] * state + mine[at].astype(f32)

    lax.fori_loop(0, count, one, jnp.zeros(mine.shape[1:], f32))


def to_slices(value, devices):
    n_state, inner = value.shape
    across = max(1, devices // 16)
    rows = n_state * across // devices
    value = value.reshape(n_state // rows, rows, across, inner // across)
    return value.transpose(0, 2, 1, 3).reshape(devices, rows, inner // across)


def from_slices(slices, n_state, inner):
    devices, rows, columns = slices.shape
    value = slices.reshape(n_state // rows, inner // columns, rows, columns)
    return value.transpose(0, 2, 1, 3).reshape(n_state, inner)


def send_slices(local, devices):
    return lax.all_to_all(to_slices(local, devices), ALL, split_axis=0, concat_axis=0, tiled=True)


def return_slices(states, n_state, inner):
    back = lax.all_to_all(states, ALL, split_axis=0, concat_axis=0, tiled=True)
    return from_slices(back, n_state, inner)


def scan_devices(mine, decay, me, backward):
    devices, heads = decay.shape
    across = max(1, devices // 16)
    wide = jnp.repeat(decay, HEAD_DIM, axis=1).reshape(devices, across, heads * HEAD_DIM // across)
    wide = lax.dynamic_index_in_dim(wide, me % across, 1, False)
    return pl.pallas_call(
        lambda *refs: scan_kernel(backward, *refs),
        out_shape=jax.ShapeDtypeStruct(mine.shape, bf16),
        name="scan_backward" if backward else "scan_forward",
    )(mine, wide)


def flip(axis, bit):
    count = lax.axis_size(axis)
    return [(i, i ^ bit) for i in range(count)]


def other_core(value):
    return lax.ppermute(value, "shard", flip("shard", 1))


class Gather:
    def __init__(self, own, other, base, size, chunks):
        self.own, self.other, self.base, self.size = (own, other, base, size)
        self.other_base = base
        self.mine = lax.axis_index("seq") % 2
        self.blocks = []
        for chunk in range(chunks):
            self.blocks += [2 * chunk + self.mine, 2 * chunk + 1 - self.mine]
        self.direct = [None] * chunks
        self.parts = [None] * (2 * chunks)

    def fetch(self, chunk, *wait):
        start = self.base + (2 * chunk + self.mine) * self.size
        send = lax.dynamic_slice_in_dim(self.own, start, self.size, 0)
        if wait:
            send = after(send, *wait)
        self.direct[chunk] = lax.ppermute(send, "shard", flip("shard", 2))

    def share(self, chunk, *wait):
        direct = self.direct[chunk]
        if wait:
            direct = after(direct, *wait)
        passed = lax.ppermute(direct, "seq", flip("seq", 1))
        self.parts[2 * chunk] = (direct, other_core(direct))
        self.parts[2 * chunk + 1] = (passed, other_core(passed))


def project_kernel(table, a0, a1, a2, a3, w0, w1, w2, w3, *rest):
    left = rest[-1]
    out = rest[-2]

    @pl.when(pl.program_id(0) == 0)
    def _():
        left[...] = jnp.concatenate([a0[...], a1[...], a2[...], a3[...]], 1)

    weight = jnp.concatenate([w0[...], w1[...], w2[...], w3[...]], 1)
    out[...] = mm_nt(left[...], weight).astype(bf16)


def project(value, gather, number, shard, result):
    rows = value.shape[0]
    deep = gather.own.shape[1]
    steps = gather.size // WIDE
    first = gather.blocks[number] * steps
    table = jnp.stack([shard, shard ^ 1, shard ^ 2, shard ^ 3, first]).astype(jnp.int32)
    base = gather.base // WIDE
    a_spec = lambda k: pl.BlockSpec((rows, deep), lambda j, t: (0, t[k]))
    other_base = gather.other_base // WIDE
    near = pl.BlockSpec((WIDE, deep), lambda j, t: (base + t[4] + j, 0))
    near_other = pl.BlockSpec((WIDE, deep), lambda j, t: (other_base + t[4] + j, 0))
    far = pl.BlockSpec((WIDE, deep), lambda j, t: (j, 0))
    columns = len(gather.blocks) * gather.size
    direct, crossed = gather.parts[number]
    operands = [table, value, value, value, value, gather.own, gather.other, direct, crossed]
    in_specs = [a_spec(k) for k in range(4)] + [near, near_other, far, far]
    aliases = {}
    if result is not None:
        operands.append(result)
        in_specs.append(pl.BlockSpec(memory_space=pl.ANY))
        aliases = {len(operands) - 1: 0}
    return pl.pallas_call(
        project_kernel,
        grid_spec=pltpu.PrefetchScalarGridSpec(
            num_scalar_prefetch=1,
            grid=(steps,),
            in_specs=in_specs,
            out_specs=pl.BlockSpec((rows, WIDE), lambda j, t: (0, t[4] + j)),
            scratch_shapes=[pltpu.VMEM((rows, 4 * deep), bf16)],
        ),
        out_shape=jax.ShapeDtypeStruct((rows, columns), bf16),
        input_output_aliases=aliases,
        compiler_params=pltpu.CompilerParams(vmem_limit_bytes=40 * 1024 * 1024),
        cost_estimate=pl.CostEstimate(
            flops=8 * rows * deep * gather.size, bytes_accessed=8 * deep * gather.size, transcendentals=0
        ),
        name="project",
    )(*operands)


def back_kernel(count, extra, table, d, own, other, *rest):
    pieces = rest[: 2 * count]
    rest = rest[2 * count :]
    step = pl.program_id(0)
    out, total = rest[-2:]
    deep = own.shape[1]

    @pl.when(step == 0)
    def _():
        for k in range(4):
            if extra:
                total[k] = mm(rest[0][...], rest[1 + k][...])
            else:
                total[k] = jnp.zeros(total.shape[1:], f32)

    value = d[...]
    total[0] += mm(value, own[...])
    total[1] += mm(value, other[...])
    for number in range(count):

        @pl.when(step == number)
        def _(number=number):
            total[2] += mm(value, pieces[2 * number][...])
            total[3] += mm(value, pieces[2 * number + 1][...])

    @pl.when(step == count - 1)
    def _():
        for k in range(4):
            at = pl.multiple_of(table[count + k] * deep, deep)
            out[:, pl.ds(at, deep)] = total[k]


def back(value, gather, shard, extra=()):
    rows = value.shape[0]
    deep = gather.own.shape[1]
    count = len(gather.blocks)
    size = gather.size
    base = gather.base // size
    table = jnp.stack(gather.blocks + [shard, shard ^ 1, shard ^ 2, shard ^ 3]).astype(jnp.int32)
    fixed = lambda shape: pl.BlockSpec(shape, lambda g, t: (0, 0))
    other_base = gather.other_base // size
    near = pl.BlockSpec((size, deep), lambda g, t: (base + t[g], 0))
    near_other = pl.BlockSpec((size, deep), lambda g, t: (other_base + t[g], 0))
    operands = [table, value, gather.own, gather.other]
    in_specs = [pl.BlockSpec((rows, size), lambda g, t: (0, t[g])), near, near_other]
    for part in gather.parts:
        operands += list(part)
        in_specs += [fixed((size, deep))] * 2
    operands += list(extra)
    in_specs += [fixed(e.shape) for e in extra]
    return pl.pallas_call(
        lambda *refs: back_kernel(count, len(extra) > 0, *refs),
        grid_spec=pltpu.PrefetchScalarGridSpec(
            num_scalar_prefetch=1,
            grid=(count,),
            in_specs=in_specs,
            out_specs=fixed((rows, 4 * deep)),
            scratch_shapes=[pltpu.VMEM((4, rows, deep), f32)],
        ),
        out_shape=jax.ShapeDtypeStruct((rows, 4 * deep), f32),
        compiler_params=pltpu.CompilerParams(vmem_limit_bytes=56 * 1024 * 1024),
        cost_estimate=pl.CostEstimate(
            flops=8 * rows * deep * size * count, bytes_accessed=8 * deep * size * count, transcendentals=0
        ),
        name="back",
    )(*operands)


def stacked_project_kernel(value, *rest):
    weight = jnp.concatenate([w[...] for w in rest[:-1]], 1)
    rest[-1][...] = mm_nt(value[...], weight).astype(bf16)


def stacked_project(value, stack, base, count):
    rows = value.shape[0]
    shards, _, deep = stack.shape
    first = base // WIDE
    specs = [
        pl.BlockSpec((None, WIDE, deep), lambda j, k=k: (k, first + j, 0)) for k in range(shards)
    ]
    return pl.pallas_call(
        stacked_project_kernel,
        grid=(count // WIDE,),
        in_specs=[pl.BlockSpec((rows, shards * deep), lambda j: (0, 0))] + specs,
        out_specs=pl.BlockSpec((rows, WIDE), lambda j: (0, j)),
        out_shape=jax.ShapeDtypeStruct((rows, count), bf16),
        compiler_params=pltpu.CompilerParams(vmem_limit_bytes=40 * 1024 * 1024),
        cost_estimate=pl.CostEstimate(
            flops=2 * rows * shards * deep * count,
            bytes_accessed=2 * shards * deep * count,
            transcendentals=0,
        ),
        name="stacked_project",
    )(value, *([stack] * shards))


def stacked_back_kernel(value, *rest):
    out, total = rest[-2:]
    step = pl.program_id(0)

    @pl.when(step == 0)
    def _():
        total[...] = jnp.zeros_like(total)

    weight = jnp.concatenate([w[...] for w in rest[:-2]], 1)
    total[...] += mm(value[...], weight)

    @pl.when(step == pl.num_programs(0) - 1)
    def _():
        out[...] = total[...]


def stacked_back(value, stack, base):
    rows, count = value.shape
    shards, _, deep = stack.shape
    size = 2 * WIDE
    first = base // size
    specs = [
        pl.BlockSpec((None, size, deep), lambda j, k=k: (k, first + j, 0)) for k in range(shards)
    ]
    return pl.pallas_call(
        stacked_back_kernel,
        grid=(count // size,),
        in_specs=[pl.BlockSpec((rows, size), lambda j: (0, j))] + specs,
        out_specs=pl.BlockSpec((rows, shards * deep), lambda j: (0, 0)),
        out_shape=jax.ShapeDtypeStruct((rows, shards * deep), f32),
        scratch_shapes=[pltpu.VMEM((rows, shards * deep), f32)],
        compiler_params=pltpu.CompilerParams(vmem_limit_bytes=40 * 1024 * 1024),
        cost_estimate=pl.CostEstimate(
            flops=2 * rows * shards * deep * count,
            bytes_accessed=2 * shards * deep * count,
            transcendentals=0,
        ),
        name="stacked_back",
    )(value, *([stack] * shards))


def rows_of(gather):
    shard = lax.axis_index("shard")
    direct, passed = gather.parts
    own = 2 * shard
    return [
        (gather.own, own, 2),
        (gather.other, own ^ 2, 2),
        (direct[0], (own ^ 4) + gather.blocks[0], 1),
        (direct[1], (own ^ 6) + gather.blocks[0], 1),
        (passed[0], (own ^ 4) + gather.blocks[1], 1),
        (passed[1], (own ^ 6) + gather.blocks[1], 1),
    ]


def out_specs_of(gather):
    width = gather.own.shape[1]
    size = gather.size
    operands, specs, owners, table = ([], [], [], [])
    for piece, block, count in rows_of(gather):
        begin = len(table)
        for at in range(count):
            owners.append(len(operands))
            table.append(block + at)
        operands.append(piece)
        specs.append(
            pl.BlockSpec(
                (size, width),
                lambda g, t, begin=begin, count=count: (jnp.clip(g - begin, 0, count - 1), 0),
            )
        )
    return operands, specs, owners, jnp.stack(table).astype(jnp.int32)


def out_back_kernel(owners, table, value, *rest):
    step = pl.program_id(0)
    out = rest[-1]
    for at, owner in enumerate(owners):

        @pl.when(step == at)
        def _(owner=owner):
            out[...] = mm_nt(value[...], rest[owner][...])


def out_back(value, gather):
    rows, width = value.shape
    operands, specs, owners, table = out_specs_of(gather)
    size = gather.size
    return pl.pallas_call(
        lambda *refs: out_back_kernel(owners, *refs),
        grid_spec=pltpu.PrefetchScalarGridSpec(
            num_scalar_prefetch=1,
            grid=(len(owners),),
            in_specs=[pl.BlockSpec((rows, width), lambda g, t: (0, 0))] + specs,
            out_specs=pl.BlockSpec((rows, size), lambda g, t: (0, t[g])),
        ),
        out_shape=jax.ShapeDtypeStruct((rows, len(owners) * size), f32),
        compiler_params=pltpu.CompilerParams(vmem_limit_bytes=56 * 1024 * 1024),
        cost_estimate=pl.CostEstimate(
            flops=16 * rows * width * size, bytes_accessed=16 * width * size, transcendentals=0
        ),
        name="out_back",
    )(table, value, *operands)


def out_forward_kernel(owners, table, value, base, *rest):
    step = pl.program_id(0)
    out, total = rest[-2:]

    @pl.when(step == 0)
    def _():
        total[...] = base[...].astype(f32)

    for at, owner in enumerate(owners):

        @pl.when(step == at)
        def _(owner=owner):
            total[...] += mm(value[...], rest[owner][...])

    @pl.when(step == len(owners) - 1)
    def _():
        out[...] = total[...].astype(bf16)


def out_forward(value, base, gather):
    rows = value.shape[0]
    operands, specs, owners, table = out_specs_of(gather)
    size = gather.size
    width = gather.own.shape[1]
    fixed = pl.BlockSpec((rows, width), lambda g, t: (0, 0))
    return pl.pallas_call(
        lambda *refs: out_forward_kernel(owners, *refs),
        grid_spec=pltpu.PrefetchScalarGridSpec(
            num_scalar_prefetch=1,
            grid=(len(owners),),
            in_specs=[pl.BlockSpec((rows, size), lambda g, t: (0, t[g])), fixed] + specs,
            out_specs=fixed,
            scratch_shapes=[pltpu.VMEM((rows, width), f32)],
        ),
        out_shape=jax.ShapeDtypeStruct((rows, width), bf16),
        compiler_params=pltpu.CompilerParams(vmem_limit_bytes=56 * 1024 * 1024),
        cost_estimate=pl.CostEstimate(
            flops=16 * rows * width * size, bytes_accessed=16 * width * size, transcendentals=0
        ),
        name="out_forward",
    )(table, value, base, *operands)


def halve(value, dim, axis, bit, mine):
    shape = value.shape
    value = value.reshape(shape[:dim] + (shape[dim] // 2, 2) + shape[dim + 1 :])
    send = lax.dynamic_index_in_dim(value, 1 - mine, dim + 1, False)
    kept = lax.dynamic_index_in_dim(value, mine, dim + 1, False)
    came = lax.ppermute(send, axis, flip(axis, bit))
    return (kept.astype(f32) + came.astype(f32)).astype(bf16)


class RowSum:
    def __init__(self, partial, far_first):
        shards, places = (lax.axis_size("shard"), lax.axis_size("seq"))
        shard, place = (lax.axis_index("shard"), lax.axis_index("seq"))
        rows, columns = partial.shape
        chips = shards // 2
        self.value = partial.reshape(chips, places, rows // (chips * places), columns)
        far = [(0, "shard", 2 << k, (shard >> (k + 1)) & 1) for k in range(chips.bit_length() - 1)]
        near = [(1, "seq", 1 << k, (place >> k) & 1) for k in range(places.bit_length() - 1)]
        self.order = far + near if far_first else near[:1] + far + near[1:]

    def step(self, *wait):
        if not self.order:
            return
        dim, axis, bit, mine = self.order.pop(0)
        value = after(self.value, *wait) if wait else self.value
        self.value = halve(value, dim, axis, bit, mine)

    def rows(self):
        return self.value.reshape(self.value.shape[2:])


def core_rows(value, core):
    shards = lax.axis_size("shard")
    size = value.shape[1] // shards
    even = [value[:, at * size : (at + 1) * size] for at in range(0, shards, 2)]
    odd = [value[:, at * size : (at + 1) * size] for at in range(1, shards, 2)]
    own = [jnp.where(core == 0, a, b) for a, b in zip(even, odd)]
    rest = [jnp.where(core == 0, b, a) for a, b in zip(even, odd)]
    return jnp.concatenate(own, 1), jnp.concatenate(rest, 1)


def after(value, *others):
    return lax.optimization_barrier((value,) + others)[0]


def turn_blocks(value, shard):
    shards = lax.axis_size("shard")
    size = value.shape[1] // shards
    blocks = [
        lax.dynamic_slice_in_dim(value, (at ^ shard) * size, size, 1) for at in range(shards)
    ]
    return jnp.concatenate(blocks, 1)


def on_device(
    hidden,
    cotangent,
    seg_ids,
    norm_gain,
    in_weight,
    conv_weight,
    conv_bias,
    dt_bias,
    a_log,
    d_skip,
    out_gain,
    out_weight,
):
    shards, places = (lax.axis_size("shard"), lax.axis_size("seq"))
    shard, place = (lax.axis_index("shard"), lax.axis_index("seq"))
    devices = shards * places
    me = shard * places + place
    length, width = hidden.shape
    heads = dt_bias.shape[0]
    inner = out_weight.shape[0] * shards
    channels = conv_bias.shape[0] * shards
    n_state = (channels - inner) // 2
    groups = inner // WIDE
    start = me * length

    small = jnp.concatenate(
        [norm_gain, conv_weight.reshape(-1), conv_bias, out_gain]
    )
    small = jnp.pad(small, (0, -small.shape[0] % 128))[None, None]
    small = jnp.broadcast_to(small, (shards, 1, small.shape[2]))
    small = lax.all_to_all(small, "shard", split_axis=0, concat_axis=0, tiled=True)[:, 0]
    at = 0
    gain_in = small[:, at : at + norm_gain.shape[0]].reshape(-1).astype(f32)
    at += norm_gain.shape[0]
    taps = small[:, at : at + conv_weight.size].reshape(shards, CONV, -1)
    taps = taps.transpose(1, 0, 2).reshape(CONV, channels).astype(f32)
    at += conv_weight.size
    bias = small[:, at : at + conv_bias.shape[0]].reshape(-1).astype(f32)
    at += conv_bias.shape[0]
    gain_out = small[:, at : at + out_gain.shape[0]].reshape(-1).astype(f32)
    core = shard % 2
    w_in = in_weight.T
    spare = -(w_in.shape[0] - 2 * inner) % TILE
    edge_w = jnp.pad(w_in[2 * inner :], ((0, spare), (0, 0)))
    by_hand = shards == 4 and places % 2 == 0
    if by_hand:
        edge_far = lax.ppermute(edge_w, "shard", flip("shard", 2))
        g_x = Gather(w_in, None, inner, inner // 4, 2)
        g_x.fetch(0)
        edge_other = other_core(edge_w)
        g_x.fetch(1)
        x_other = other_core(w_in[inner : 2 * inner])
        g_x.other, g_x.other_base = (x_other, 0)
        g_x.share(0)
        g_out = Gather(out_weight, other_core(out_weight), 0, out_weight.shape[0] // 2, 1)
        g_out.fetch(0, g_x.direct[0])
        g_x.share(1)
        edges = [edge_w, edge_other, edge_far, other_core(edge_far)]
        stack_z = lax.all_gather(after(w_in[:inner], g_x.direct[0]), "shard")
    else:
        stack_z = lax.all_gather(w_in[:inner], "shard")
        stack_x = lax.all_gather(w_in[inner : 2 * inner], "shard")
        w_edge = lax.all_gather(edge_w, "shard").transpose(1, 0, 2).reshape(-1, width)
        w_out = lax.all_gather(out_weight, "shard", axis=0, tiled=True)
    skip_wide = jnp.repeat(d_skip.astype(f32), HEAD_DIM)
    rows = jnp.concatenate([skip_wide, jnp.zeros((channels - inner,), f32)])
    taps8 = jnp.concatenate([taps, bias[None], rows[None], jnp.zeros((2, channels), f32)], 0)

    edge = jnp.full((HALO,), -1, jnp.int32)
    padded = jnp.concatenate([edge, seg_ids, edge - 1])
    near = lax.dynamic_slice_in_dim(padded, start, length + 2 * HALO)
    seg = near[HALO : HALO + length]
    fwd_masks = [near[HALO - CONV + 1 + k : HALO - CONV + 1 + k + length] == seg for k in range(3)]
    spot = jnp.arange(length, dtype=jnp.int32)
    bwd_masks = [
        (near[HALO + CONV - 1 - k : HALO + CONV - 1 - k + length] == seg)
        & (spot + CONV - 1 - k < length)
        for k in range(3)
    ]
    from_before = seg == near[HALO - 1]
    to_last = seg == seg[length - 1]
    masks = jnp.stack(
        [m.astype(f32) for m in fwd_masks + bwd_masks + [seg, from_before, to_last]], 1
    )
    masks = jnp.pad(masks, ((0, 0), (0, 16 - masks.shape[1])))
    seg_row = jnp.broadcast_to(seg.astype(f32)[None, :], (8, length))

    behind = lax.ppermute(
        hidden[length - HALO :], ALL, [(i, i + 1) for i in range(devices - 1)]
    )
    hidden_f = jnp.concatenate([behind, hidden], 0).astype(f32)
    scale_in = lax.rsqrt(jnp.mean(hidden_f * hidden_f, axis=1, keepdims=True) + EPS)
    normed_ext = (hidden_f * scale_in * gain_in[None, :]).astype(bf16)
    normed_in = normed_ext[HALO:]
    if by_hand:
        w_edge = jnp.concatenate(edges, 1)
        proj_edge = mm_nt(turn_blocks(normed_ext, shard), w_edge).astype(bf16)
    else:
        proj_edge = mm_nt(normed_ext, w_edge).astype(bf16)
    proj_bc = proj_edge[:, : 2 * n_state]
    rates = jnp.stack([dt_bias, a_log]).astype(f32)
    rates = jnp.pad(rates, ((0, 6), (0, TILE - heads)))
    big = pltpu.CompilerParams(vmem_limit_bytes=56 * 1024 * 1024)
    by_head, sums_row = pl.pallas_call(
        prepare_kernel,
        out_shape=[
            jax.ShapeDtypeStruct((5, length, TILE), f32),
            jax.ShapeDtypeStruct((groups, GROUP, length), f32),
        ],
        compiler_params=big,
        name="prepare",
    )(proj_edge[HALO:, 2 * n_state :], rates, masks)
    end = by_head[3, length - 1, :heads]
    decays = jnp.broadcast_to(end[None, None, :], (devices, 1, heads))
    decays = lax.all_to_all(decays, ALL, split_axis=0, concat_axis=0, tiled=True)[:, 0, :]
    if by_hand:
        proj = None
        for number in range(4):
            proj = project(after(normed_ext, by_head), g_x, number, shard, proj)
    else:
        proj = stacked_project(normed_ext, stack_x, 0, inner)

    def whole(shape):
        return pl.BlockSpec(shape, lambda g: (0,) * len(shape))

    def group_of(g):
        return jnp.maximum(g - 1, 0)

    order = lambda g: jnp.where(g == 0, groups, g - 1)
    x_conv, state_local, bc, bt, ct = pl.pallas_call(
        state_kernel,
        grid=(groups + 1,),
        in_specs=[
            pl.BlockSpec((length + HALO, WIDE), lambda g: (0, group_of(g))),
            whole((length + HALO, WIDE)),
            pl.BlockSpec((8, WIDE), lambda g: (0, order(g))),
            whole(masks.shape),
            whole(by_head.shape),
        ],
        out_specs=[
            pl.BlockSpec((length, WIDE), lambda g: (0, group_of(g))),
            pl.BlockSpec((n_state, WIDE), lambda g: (0, group_of(g))),
            whole((length, 2 * n_state)),
            whole((n_state, length)),
            whole((n_state, length)),
        ],
        out_shape=[
            jax.ShapeDtypeStruct((length, inner), bf16),
            jax.ShapeDtypeStruct((n_state, inner), bf16),
            jax.ShapeDtypeStruct((length, 2 * n_state), bf16),
            jax.ShapeDtypeStruct((n_state, length), bf16),
            jax.ShapeDtypeStruct((n_state, length), bf16),
        ],
        scratch_shapes=[
            pltpu.VMEM((length + HALO, WIDE), f32),
            pltpu.VMEM((n_state, length), bf16),
        ],
        compiler_params=big,
        cost_estimate=pl.CostEstimate(
            flops=20 * length * inner * n_state, bytes_accessed=10 * length * inner, transcendentals=0
        ),
        name="mixer_state",
    )(proj, proj_bc, taps8, masks, by_head)

    sent = send_slices(state_local, devices)
    if by_hand:
        g_out.share(0, state_local)
    gate_z = stacked_project(after(normed_in, state_local), stack_z, 0, inner)
    states = scan_devices(after(sent, gate_z), decays, me, False)
    state_in = return_slices(states, n_state, inner)
    x_conv = after(x_conv, states)
    y_local = pl.pallas_call(
        forward_kernel,
        grid=(groups,),
        in_specs=[
            pl.BlockSpec((length, WIDE), lambda g: (0, g)),
            whole(masks.shape),
            whole((8, length)),
            whole(by_head.shape),
            pl.BlockSpec((1, GROUP, length), lambda g: (g, 0, 0)),
            whole((length, 2 * n_state)),
            whole((n_state, length)),
        ],
        out_specs=pl.BlockSpec((length, WIDE), lambda g: (0, g)),
        out_shape=jax.ShapeDtypeStruct((length, inner), f32),
        scratch_shapes=[
            pltpu.VMEM((length, length), f32),
            pltpu.VMEM((length, WIDE), bf16),
            pltpu.VMEM((length, length), bf16),
        ],
        compiler_params=big,
        cost_estimate=pl.CostEstimate(
            flops=16 * length * length * inner, bytes_accessed=10 * length * inner, transcendentals=0
        ),
        name="mixer_forward",
    )(x_conv, masks, seg_row, by_head, sums_row, bc, bt)
    if by_hand:
        d_normed = out_back(after(cotangent, y_local), g_out)
    else:
        d_normed = mm_nt(cotangent, w_out)
    block = TILE
    tall = lambda dim: pl.BlockSpec((block, dim), lambda g: (g, 0))
    gains = jnp.stack([gain_out, skip_wide], 0)
    ssm, normed_out, d_z, d_y, d_state_local, dc_more, d_gain = pl.pallas_call(
        gate_kernel,
        grid=(length // block,),
        in_specs=[
            tall(inner),
            tall(inner),
            tall(inner),
            tall(inner),
            tall(2 * n_state),
            pl.BlockSpec((n_state, block), lambda g: (0, g)),
            tall(TILE),
            whole((n_state, inner)),
            whole((2, inner)),
        ],
        out_specs=[
            tall(inner),
            tall(inner),
            tall(inner),
            tall(inner),
            whole((n_state, inner)),
            tall(n_state),
            whole((8, inner)),
        ],
        out_shape=[
            jax.ShapeDtypeStruct((length, inner), f32),
            jax.ShapeDtypeStruct((length, inner), bf16),
            jax.ShapeDtypeStruct((length, inner), bf16),
            jax.ShapeDtypeStruct((length, inner), bf16),
            jax.ShapeDtypeStruct((n_state, inner), bf16),
            jax.ShapeDtypeStruct((length, n_state), f32),
            jax.ShapeDtypeStruct((8, inner), f32),
        ],
        scratch_shapes=[
            pltpu.VMEM((block, inner), f32),
            pltpu.VMEM((block, inner), f32),
            pltpu.VMEM((block, inner), bf16),
            pltpu.VMEM((n_state, inner), f32),
        ],
        compiler_params=big,
        cost_estimate=pl.CostEstimate(
            flops=8 * length * n_state * inner, bytes_accessed=22 * length * inner, transcendentals=0
        ),
        name="mixer_gate",
    )(y_local, x_conv, gate_z, d_normed, bc, ct, by_head[3], state_in, gains)

    sent = send_slices(d_state_local, devices)

    def both(value):
        return jnp.concatenate([value, other_core(value)], 0)

    def both_rows(value):
        own, rest = core_rows(value, core)
        return jnp.concatenate([own, other_core(rest)], 0)

    normed_pair = both_rows(normed_in)
    cot_pair = both(cotangent)
    out_pair = both_rows(normed_out)
    z_pair = both(d_z)
    if by_hand:
        block_out = out_forward(normed_out, hidden, g_out)
    else:
        block_out = (hidden.astype(f32) + mm(normed_out, w_out)).astype(bf16)
    d_normed_z = stacked_back(after(d_z, block_out), stack_z, 0)
    grad_o = mm_tn(after(out_pair, block_out), cot_pair).astype(bf16)
    states = scan_devices(after(sent, grad_o, d_normed_z), decays, me, True)
    d_state = return_slices(states, n_state, inner)
    grad_z = mm_tn(normed_pair, after(z_pair, states)).astype(bf16)
    half_o, half_z = (width // 2, inner // 2)
    sums_o = [RowSum(grad_o[:, :half_o], True), RowSum(grad_o[:, half_o:], False)]
    sums_z = [RowSum(grad_z[:, :half_z], True), RowSum(grad_z[:, half_z:], False)]
    x_conv = after(x_conv, states, grad_z)

    dxs, db_in, dc_in = pl.pallas_call(
        inside_kernel,
        grid=(groups,),
        in_specs=[
            pl.BlockSpec((length, WIDE), lambda g: (0, g)),
            whole(masks.shape),
            whole((8, length)),
            whole(by_head.shape),
            pl.BlockSpec((1, GROUP, length), lambda g: (g, 0, 0)),
            whole((length, 2 * n_state)),
            whole((n_state, length)),
            pl.BlockSpec((length, WIDE), lambda g: (0, g)),
        ],
        out_specs=[
            pl.BlockSpec((length, WIDE), lambda g: (0, g)),
            whole((length, n_state)),
            whole((length, n_state)),
        ],
        out_shape=[
            jax.ShapeDtypeStruct((length, inner), f32),
            jax.ShapeDtypeStruct((length, n_state), f32),
            jax.ShapeDtypeStruct((length, n_state), f32),
        ],
        scratch_shapes=[
            pltpu.VMEM((length, length), f32),
            pltpu.VMEM((length, length), f32),
            pltpu.VMEM((length, WIDE), bf16),
            pltpu.VMEM((length, length), bf16),
            pltpu.VMEM((length, length), f32),
        ],
        compiler_params=big,
        cost_estimate=pl.CostEstimate(
            flops=8 * length * length * inner, bytes_accessed=10 * length * inner, transcendentals=0
        ),
        name="mixer_inside",
    )(x_conv, masks, seg_row, by_head, sums_row, bc, ct, d_y)

    for chain in sums_o + sums_z:
        chain.step()
    d_y = after(d_y, *[chain.value for chain in sums_o + sums_z])
    for chain in sums_o + sums_z:
        chain.step(dxs)

    kept = lambda g: jnp.minimum(g, groups - 1)
    taps8 = jnp.pad(taps8, ((0, 0), (0, WIDE)))
    d_out, first, last, sums, head_sums = pl.pallas_call(
        outside_kernel,
        grid=(groups + 2,),
        in_specs=[
            pl.BlockSpec((length + HALO, WIDE), lambda g: (0, kept(g))),
            whole((length + HALO, WIDE)),
            pl.BlockSpec((8, WIDE), lambda g: (0, g)),
            whole(masks.shape),
            whole(by_head.shape),
            whole(rates.shape),
            whole((length, 2 * n_state)),
            pl.BlockSpec((length, WIDE), lambda g: (0, kept(g))),
            pl.BlockSpec((length, WIDE), lambda g: (0, kept(g))),
            pl.BlockSpec((length, WIDE), lambda g: (0, kept(g))),
            pl.BlockSpec((n_state, WIDE), lambda g: (0, kept(g))),
            pl.BlockSpec((n_state, WIDE), lambda g: (0, kept(g))),
            whole((length, n_state)),
            whole((length, n_state)),
            whole((length, n_state)),
        ],
        out_specs=[
            pl.BlockSpec((length, WIDE), lambda g: (0, g)),
            pl.BlockSpec((HALO, WIDE), lambda g: (0, g)),
            pl.BlockSpec((HALO, WIDE), lambda g: (0, g)),
            pl.BlockSpec((8, WIDE), lambda g: (0, g)),
            whole((8, TILE)),
        ],
        out_shape=[
            jax.ShapeDtypeStruct((length, channels + WIDE), bf16),
            jax.ShapeDtypeStruct((HALO, channels + WIDE), f32),
            jax.ShapeDtypeStruct((HALO, channels + WIDE), f32),
            jax.ShapeDtypeStruct((8, channels + WIDE), f32),
            jax.ShapeDtypeStruct((8, TILE), f32),
        ],
        scratch_shapes=[
            pltpu.VMEM((length + HALO, WIDE), f32),
            pltpu.VMEM((length + HALO, WIDE), f32),
            pltpu.VMEM((length, n_state), f32),
            pltpu.VMEM((2, length, TILE), f32),
            pltpu.VMEM((8, TILE), f32),
        ],
        compiler_params=big,
        cost_estimate=pl.CostEstimate(
            flops=8 * length * n_state * inner, bytes_accessed=16 * length * inner, transcendentals=0
        ),
        name="mixer_outside",
    )(proj, proj_bc, taps8, masks, by_head, rates, bc, d_y, ssm, dxs, d_state, state_in, db_in,
      dc_in, dc_more)

    ahead = lax.ppermute(first, ALL, [(i + 1, i) for i in range(devices - 1)])
    joined = jnp.concatenate([jnp.zeros_like(first), ahead], 0)
    seg_end = near[length : length + 2 * HALO]
    for tap in range(CONV - 1):
        lead = CONV - 1 - tap
        same = (seg_end[lead : lead + HALO] == seg_end[:HALO]).astype(f32)[:, None]
        last = last + taps8[tap][None, :] * joined[lead : lead + HALO] * same
    fixed_rows = last[:, :channels].astype(bf16)
    d_out = lax.dynamic_update_slice(d_out, fixed_rows, (length - HALO, 0))

    x_pair = both(d_out)
    half = d_out.shape[1] // 2
    grad_x = mm_tn(normed_pair, x_pair[:, :half]).astype(bf16)
    grad_y = mm_tn(normed_pair, x_pair[:, half:]).astype(bf16)
    sums_x = [RowSum(grad_x, True), RowSum(grad_y, False)]
    d_edge = d_out[:, inner : inner + w_edge.shape[0]]
    d_edge = after(d_edge, grad_x, grad_y)
    if by_hand:
        d_normed_in = d_normed_z + back(after(d_out, grad_x, grad_y), g_x, shard, (d_edge, *edges))
    else:
        d_normed_in = d_normed_z + stacked_back(d_out[:, :inner], stack_x, 0) + mm(d_edge, w_edge)
    for chain in sums_o + sums_z:
        chain.step(grad_x)
    for chain in sums_x:
        chain.step()
        chain.step(d_normed_in)
    for chain in sums_o + sums_z + sums_x:
        while chain.order:
            chain.step(d_normed_in)
    base = hidden_f[HALO:]
    scale = scale_in[HALO:]
    d_hat = d_normed_in * gain_in[None, :]
    mean = jnp.mean(d_hat * base, axis=1, keepdims=True)
    grad_hidden = cotangent.astype(f32) + scale * d_hat - base * (scale * scale * scale * mean)
    grad_gain_in = jnp.sum(d_normed_in * base * scale, 0)
    counts = [width // devices] + [channels // devices] * (CONV + 1) + [inner // devices]
    counts += [heads] * 3
    total = sum(counts)
    if by_hand:
        sizes = (width // devices, channels // devices, inner // devices, heads)
        packed = pl.pallas_call(
            lambda *refs: pack_kernel(sizes, *refs),
            out_shape=jax.ShapeDtypeStruct((devices, 1, total + -total % TILE), f32),
            name="pack",
        )(sums[:, :channels], grad_gain_in[None], d_gain, head_sums)
    else:
        slots = lambda v: v.reshape(-1, devices, v.shape[-1] // devices).transpose(1, 0, 2)
        same = jnp.broadcast_to(head_sums[:3, :heads].reshape(1, -1), (devices, 3 * heads))
        pieces = [slots(grad_gain_in), slots(sums[: CONV + 1, :channels])]
        pieces += [slots(jnp.sum(d_gain, 0)), same]
        packed = jnp.concatenate([p.reshape(devices, -1) for p in pieces], 1)[:, None]
    packed = lax.all_to_all(packed, ALL, split_axis=0, concat_axis=0, tiled=True).sum((0, 1))
    found, at = ([], 0)
    for size in counts:
        found.append(packed[at : at + size])
        at += size

    grads = jnp.concatenate([c.rows() for c in sums_z + sums_x], 1)
    return (
        block_out,
        grad_hidden,
        found[0],
        grads[:, : 2 * inner + 2 * n_state + heads].astype(f32),
        jnp.stack(found[1 : CONV + 1]),
        found[CONV + 1],
        found[CONV + 3],
        found[CONV + 4],
        found[CONV + 5],
        found[CONV + 2],
        jnp.concatenate([c.rows() for c in sums_o], 1).astype(f32),
    )


def solution(mesh):
    return jax.shard_map(
        on_device,
        mesh=mesh,
        in_specs=(
            P(ALL, None),
            P(ALL, None),
            P(),
            P("shard"),
            P("shard", None),
            P(None, "shard"),
            P("shard"),
            P(),
            P(),
            P(),
            P("shard"),
            P("shard", None),
        ),
        out_specs=(
            P(ALL, None),
            P(ALL, None),
            P(ALL),
            P(ALL, None),
            P(None, ALL),
            P(ALL),
            P(),
            P(),
            P(),
            P(ALL),
            P(ALL, None),
        ),
        check_vma=False,
    )
```

```python
import jax
import jax.numpy as jnp
from jax import lax
from jax.experimental import pallas as pl
from jax.experimental.pallas import tpu as pltpu
from jax.sharding import PartitionSpec as P

HEAD_DIM = 64
CONV = 4
EPS = 1e-05
HALO = 8
GROUP = 4
WIDE = GROUP * HEAD_DIM
TILE = 128
PIECE = 3 * WIDE
HIGH = lax.Precision.HIGHEST
ALL = ("shard", "seq")
f32 = jnp.float32
bf16 = jnp.bfloat16


def mm(a, b):
    return jnp.dot(a, b, preferred_element_type=f32)


def mm_nt(a, b):
    return lax.dot_general(a, b, (((1,), (1,)), ((), ())), preferred_element_type=f32)


def mm_tn(a, b):
    return lax.dot_general(a, b, (((0,), (0,)), ((), ())), preferred_element_type=f32)


def sigmoid(value):
    return 0.5 * jnp.tanh(0.5 * value) + 0.5


def head_lanes(group):
    lane = lax.rem(lax.broadcasted_iota(jnp.int32, (2 * TILE, WIDE), 0), TILE)
    owner = lax.broadcasted_iota(jnp.int32, (2 * TILE, WIDE), 1) // HEAD_DIM + GROUP * group
    return jnp.where(lane == owner, 1.0, 0.0).astype(bf16)


def two_parts(value):
    high = value.astype(bf16)
    low = (value - high.astype(f32)).astype(bf16)
    return high, low


def twice(value):
    return jnp.concatenate([value, value], 1)


def conv_rows(wide, taps, masks, start, rows):
    pre = taps[CONV : CONV + 1, :] + taps[CONV - 1 : CONV, :] * wide[pl.ds(HALO + start, rows), :]
    for tap in range(CONV - 1):
        shifted = wide[pl.ds(HALO - CONV + 1 + tap + start, rows), :]
        pre = pre + taps[tap : tap + 1, :] * shifted * twice(masks[tap, pl.ds(start, rows), :])
    return pre


def prepare_kernel(edge, rates, flags, out, spread_out, cum_out, row_out, masks_out):
    length = out.shape[1]
    shifted = edge[...].astype(f32) + rates[0:1, :]
    step = jax.nn.softplus(shifted)
    here = lax.broadcasted_iota(jnp.int32, (length, length), 0)
    there = lax.broadcasted_iota(jnp.int32, (length, length), 1)
    lower = jnp.where(here >= there, 1.0, 0.0)
    log_decay = -step * jnp.exp(rates[1:2, :])
    cum = lax.dot_general(
        lower, log_decay, (((1,), (0,)), ((), ())), precision=HIGH, preferred_element_type=f32
    )
    keep = jnp.exp(cum[length - 1 : length, :] - cum) * flags[:, 8:9]
    out[0] = cum
    out[1] = step
    out[2] = keep
    out[3] = jnp.exp(cum) * flags[:, 7:8]
    out[4] = sigmoid(shifted)
    for at, value in enumerate((step, keep)):
        high, low = two_parts(value)
        spread_out[at, :, :TILE] = high
        spread_out[at, :, TILE:] = low
    turned = cum.T
    for group in range(row_out.shape[0]):
        heads = slice(GROUP * group, GROUP * (group + 1))
        row_out[group] = turned[heads, :]
        cum_out[group] = cum[:, heads]
    for at in range(2 * (CONV - 1)):
        masks_out[at] = jnp.broadcast_to(flags[:, at : at + 1], (length, TILE))


def state_kernel(raw, raw_bc, taps, masks, spreads, x_out, state_out, bc_out, bt_out, ct_out, wide, bt):
    length = x_out.shape[0]
    n_state = bt.shape[0]
    step = pl.program_id(0)

    @pl.when(step == 0)
    def _():
        wide[...] = raw_bc[...].astype(f32)
        for start in range(0, length, TILE):
            rows = pl.ds(start, TILE)
            pre = conv_rows(wide, taps, masks, start, TILE)
            both = pre * sigmoid(pre)
            bc_out[rows, :] = both.astype(bf16)
            turned = both[:, :n_state].T.astype(bf16)
            bt[:, rows] = turned
            bt_out[:, rows] = turned
            ct_out[:, rows] = both[:, n_state:].T.astype(bf16)

    @pl.when(step > 0)
    def _():
        wide[...] = raw[...].astype(f32)
        lanes = head_lanes(step - 1)
        kept = []
        for start in range(0, length, TILE):
            rows = pl.ds(start, TILE)
            pre = conv_rows(wide, taps, masks, start, TILE)
            x = (pre * sigmoid(pre)).astype(bf16)
            x_out[rows, :] = x
            scaled = (x.astype(f32) * mm(spreads[0, rows, :], lanes)).astype(bf16)
            kept.append((scaled.astype(f32) * mm(spreads[1, rows, :], lanes)).astype(bf16))
        state_out[...] = mm(bt[...], jnp.concatenate(kept, 0)).astype(bf16)


def scored(first, second, flags, seg_row, score, later):
    length = score.shape[0]
    for start in range(0, length, TILE):
        rows = pl.ds(start, TILE)
        product = mm(first(rows), second[...])
        here = lax.broadcasted_iota(jnp.int32, (TILE, length), 0) + start
        there = lax.broadcasted_iota(jnp.int32, (TILE, length), 1)
        order = (here >= there) if later else (here <= there)
        seen = (flags[rows, 6:7] == seg_row[0:1, :]) & order
        score[rows, :] = jnp.where(seen, product, 0.0)


def by_head(value):
    owner = lax.broadcasted_iota(jnp.int32, value.shape, 1) // HEAD_DIM
    zero = jnp.zeros_like(value)
    return [jnp.where(owner == head, value, zero) for head in range(GROUP)]


def forward_kernel(x_in, flags, seg_row, spreads, cum, sums_row, bc, bt, y_out, score, apart, weights):
    length = y_out.shape[0]
    n_state = bt.shape[0]
    group = pl.program_id(0)
    big = weights.shape[2] // GROUP

    @pl.when(group == 0)
    def _():
        scored(lambda rows: bc[rows, n_state:], bt, flags, seg_row, score, True)
        weights[...] = jnp.zeros_like(weights)

    lanes = head_lanes(group)
    for start in range(0, length, TILE):
        rows = pl.ds(start, TILE)
        scaled = x_in[rows, :].astype(f32) * mm(spreads[0, rows, :], lanes)
        for head, value in enumerate(by_head(scaled)):
            apart[start // big, pl.ds(head * big + start % big, TILE), :] = value.astype(bf16)
    for head in range(GROUP):
        for start in range(0, length, TILE):
            rows = pl.ds(start, TILE)
            for at in range(0, start + TILE, big):
                end = min(at + big, start + TILE)
                gap = cum[0, rows, head : head + 1] - sums_row[0, head : head + 1, at:end]
                weight = jnp.exp(jnp.minimum(gap, 0.0)) * score[rows, at:end]
                weights[at // big, rows, head * big : head * big + end - at] = weight.astype(bf16)
    for at in range(0, length, big):
        part = mm(weights[at // big, at:, :], apart[at // big])
        if at == 0:
            y_out[...] = part
        else:
            y_out[at:, :] += part


def gate_kernel(
    y_in, x_in, z_in, dn_in, bc, ct, enter, state, gain, ssm_out, norm_out, dz_out, dy_out,
    ds_out, dc_out, dg_out, gated_s, sig_s, mo_s, ds_acc
):
    rows = y_in.shape[0]
    width = y_in.shape[1]
    n_state = state.shape[0]
    step = pl.program_id(0)
    lane = lax.broadcasted_iota(jnp.int32, (rows, 2 * HEAD_DIM), 1)
    c_mat = bc[:, n_state:]

    @pl.when(step == 0)
    def _():
        ds_acc[...] = jnp.zeros_like(ds_acc)
        dg_out[...] = jnp.zeros_like(dg_out)

    def entering(block):
        low = enter[:, 2 * block : 2 * block + 1]
        top = enter[:, 2 * block + 1 : 2 * block + 2]
        return jnp.where(lane < HEAD_DIM, low, top)

    square = jnp.zeros((rows, 2 * HEAD_DIM), f32)
    cross = jnp.zeros((rows, 2 * HEAD_DIM), f32)
    for block in range(width // (2 * HEAD_DIM)):
        lanes = slice(block * 2 * HEAD_DIM, (block + 1) * 2 * HEAD_DIM)
        ssm = y_in[:, lanes] + entering(block) * mm(c_mat, state[:, lanes])
        ssm_out[:, lanes] = ssm
        mo = (ssm + gain[1:2, lanes] * x_in[:, lanes].astype(f32)).astype(bf16)
        mo_s[:, lanes] = mo
        z = z_in[:, lanes].astype(f32)
        sig = sigmoid(z)
        gated = mo.astype(f32) * (z * sig)
        gated_s[:, lanes] = gated
        sig_s[:, lanes] = sig
        square = square + gated * gated
        cross = cross + gated * (dn_in[:, lanes] * gain[0:1, lanes])
    scale = lax.rsqrt(jnp.sum(square, axis=1, keepdims=True) * (1.0 / width) + EPS)
    pull = scale * scale * scale * (jnp.sum(cross, axis=1, keepdims=True) * (1.0 / width))
    dc = jnp.zeros((rows, n_state), f32)
    for block in range(width // (2 * HEAD_DIM)):
        lanes = slice(block * 2 * HEAD_DIM, (block + 1) * 2 * HEAD_DIM)
        gated = gated_s[:, lanes]
        sig = sig_s[:, lanes]
        silu = z_in[:, lanes].astype(f32) * sig
        dn = dn_in[:, lanes]
        hat = gated * scale
        norm_out[:, lanes] = (hat * gain[0:1, lanes]).astype(bf16)
        part = dn * hat
        total = part[0:8, :]
        for at in range(8, rows, 8):
            total = total + part[at : at + 8, :]
        dg_out[:, lanes] += total
        d_gated = scale * (dn * gain[0:1, lanes]) - gated * pull
        dy = (d_gated * silu).astype(bf16)
        dy_out[:, lanes] = dy
        mo = mo_s[:, lanes].astype(f32)
        dz_out[:, lanes] = (d_gated * mo * (sig + silu * (1.0 - sig))).astype(bf16)
        weighted = (dy.astype(f32) * entering(block)).astype(bf16)
        ds_acc[:, lanes] += mm(ct[...], weighted)
        dc = dc + mm_nt(weighted, state[:, lanes])
    dc_out[...] = dc

    @pl.when(step == pl.num_programs(0) - 1)
    def _():
        ds_out[...] = ds_acc[...].astype(bf16)


def inside_kernel(
    x_in, flags, seg_row, spreads, cum, sums_row, bc, ct, dy, dxs_out, db_out, dc_out, score, pair,
    apart, weights, xs, crossed
):
    length = dxs_out.shape[0]
    n_state = ct.shape[0]
    group = pl.program_id(0)
    big = weights.shape[2] // GROUP

    @pl.when(group == 0)
    def _():
        pair[...] = jnp.zeros_like(pair)
        weights[...] = jnp.zeros_like(weights)
        scored(lambda rows: bc[rows, :n_state], ct, flags, seg_row, score, False)

    lanes = head_lanes(group)
    for start in range(0, length, TILE):
        rows = pl.ds(start, TILE)
        scaled = x_in[rows, :].astype(f32) * mm(spreads[0, rows, :], lanes)
        for head, value in enumerate(by_head(scaled)):
            xs[head, rows, :] = value.astype(bf16)
        for head, value in enumerate(by_head(dy[rows, :].astype(f32))):
            apart[start // big, pl.ds(head * big + start % big, TILE), :] = value.astype(bf16)
    for head in range(GROUP):
        for at in range(0, length, big):
            end = at + big
            crossed[head % 2, :end, at:end] = mm_nt(xs[head, :end, :], dy[at:end, :])
        for start in range(0, length, TILE):
            rows = pl.ds(start, TILE)
            for at in range(start // big * big, length, big):
                first = max(at, start)
                end = at + big
                gap = sums_row[0, head : head + 1, first:end] - cum[0, rows, head : head + 1]
                decay = jnp.exp(jnp.minimum(gap, 0.0))
                weight = (decay * score[rows, first:end]).astype(bf16)
                weights[at // big, rows, head * big + first - at : (head + 1) * big] = weight
                pair[rows, first:end] += decay * crossed[head % 2, rows, first:end]
    for at in range(length - big, -1, -big):
        end = at + big
        part = mm(weights[at // big, :end, :], apart[at // big])
        if end == length:
            dxs_out[...] = part
        else:
            dxs_out[:end, :] += part

    @pl.when(group == pl.num_programs(0) - 1)
    def _():
        for start in range(0, length, TILE):
            rows = pl.ds(start, TILE)
            here = lax.broadcasted_iota(jnp.int32, (TILE, length), 0) + start
            there = lax.broadcasted_iota(jnp.int32, (TILE, length), 1)
            seen = (flags[rows, 6:7] == seg_row[0:1, :]) & (here <= there)
            part = jnp.where(seen, pair[rows, :], 0.0).astype(bf16)
            db_out[rows, :] = mm(part, bc[:, n_state:])
            if start == 0:
                dc_out[...] = mm_tn(part, bc[rows, :n_state])
            else:
                dc_out[...] += mm_tn(part, bc[rows, :n_state])


def split_mm(value, chosen):
    high, low = two_parts(value)
    return mm(high, chosen) + mm(low, chosen)


def outside_kernel(first_group, count, final, *refs):
    (raw, raw_bc, taps, masks, spreads, heads, rates, bc, dy, ssm, dxs_in, d_state, state, db_in,
     dc_in, dc_more, db_start, found_start, totals_start, d_out, first_out, last_out, sums_out,
     head_out, db_acc, found, totals_s, wide, d_pre) = refs
    length = d_out.shape[0]
    n_state = bc.shape[1] // 2
    step = pl.program_id(0)
    bc_step = count

    @pl.when(step == 0)
    def _():
        db_acc[...] = db_start[...]
        found[...] = found_start[...]
        totals_s[...] = totals_start[...]

    d_pre[pl.ds(length, HALO), :] = jnp.zeros((HALO, d_pre.shape[1]), f32)
    zero = jnp.zeros((1, d_pre.shape[1]), f32)

    @pl.when(step < bc_step)
    def _():
        wide[...] = raw[...].astype(f32)
        skip_sum, keep_sum = (zero, zero)
        ds = d_state[...]
        group = step + first_group
        lanes = head_lanes(group)
        owner = lax.broadcasted_iota(jnp.int32, (WIDE, TILE), 0) // HEAD_DIM + GROUP * group
        chosen = (owner == lax.broadcasted_iota(jnp.int32, (WIDE, TILE), 1)).astype(f32)
        chosen_b = chosen.astype(bf16)
        for start in range(0, length, TILE):
            rows = pl.ds(start, TILE)
            pre = conv_rows(wide, taps, masks, start, TILE)
            sig = sigmoid(pre)
            x = pre * sig
            stepped = mm(spreads[0, rows, :], lanes)
            scaled = (x.astype(bf16).astype(f32) * stepped).astype(bf16)
            keep = mm(spreads[1, rows, :], lanes)
            carried = keep * mm(bc[rows, :n_state], ds)
            dxs = dxs_in[rows, :] + carried
            scaled = scaled.astype(f32)
            db_acc[rows, :] += mm_nt((scaled * keep).astype(bf16), ds)
            grad = dy[rows, :].astype(f32)
            keep_sum = keep_sum + jnp.sum(scaled * carried, 0, keepdims=True)
            skip_sum = skip_sum + jnp.sum(grad * x, 0, keepdims=True)
            found[0, rows, :] += split_mm(grad * ssm[rows, :] - scaled * dxs, chosen_b)
            found[1, rows, :] += split_mm(x * dxs, chosen_b)
            d_x = taps[5:6, :] * grad + stepped * dxs
            d_pre[rows, :] = d_x * (sig + x * (1.0 - sig))
        met = jnp.sum(ds.astype(f32) * state[...].astype(f32), 0, keepdims=True)
        rest = jnp.zeros((5, WIDE), f32)
        totals_s[...] += lax.dot_general(
            jnp.concatenate([skip_sum, keep_sum, met, rest], 0),
            chosen,
            (((1,), (0,)), ((), ())),
            precision=HIGH,
            preferred_element_type=f32,
        )

    if final:

        @pl.when(step == bc_step)
        def _():
            wide[...] = raw_bc[...].astype(f32)
            for start in range(0, length, TILE):
                rows = pl.ds(start, TILE)
                pre = conv_rows(wide, taps, masks, start, TILE)
                sig = sigmoid(pre)
                slope = sig + pre * sig * (1.0 - sig)
                d_b = db_in[rows, :] + db_acc[rows, :]
                d_c = dc_in[rows, :] + dc_more[rows, :]
                d_pre[rows, :] = jnp.concatenate([d_b, d_c], 1) * slope

    @pl.when(step <= bc_step)
    def _():
        totals = [zero] * (CONV + 1)
        for start in range(0, length, TILE):
            rows = pl.ds(start, TILE)
            grad = d_pre[rows, :]
            totals[CONV] = totals[CONV] + jnp.sum(grad, 0, keepdims=True)
            here = wide[pl.ds(HALO + start, TILE), :]
            totals[CONV - 1] = totals[CONV - 1] + jnp.sum(grad * here, 0, keepdims=True)
            back = taps[CONV - 1 : CONV, :] * grad
            for tap in range(CONV - 1):
                shifted = wide[pl.ds(HALO - CONV + 1 + tap + start, TILE), :]
                masked = grad * twice(masks[tap, rows, :])
                totals[tap] = totals[tap] + jnp.sum(masked * shifted, 0, keepdims=True)
                ahead = d_pre[pl.ds(start + CONV - 1 - tap, TILE), :]
                back = back + taps[tap : tap + 1, :] * ahead * twice(masks[3 + tap, rows, :])
            d_out[rows, :] = back.astype(bf16)
            if start + TILE == length:
                last_out[...] = back[TILE - HALO :, :]
        first_out[...] = d_pre[pl.ds(0, HALO), :]
        for tap in range(CONV + 1):
            sums_out[tap : tap + 1, :] = totals[tap]
        sums_out[CONV + 1 : 8, :] = jnp.zeros((7 - CONV, d_pre.shape[1]), f32)

    if not final:
        head_out[...] = jnp.zeros_like(head_out)
        return

    @pl.when(step == bc_step + 1)
    def _():
        first_out[...] = jnp.zeros_like(first_out)
        last_out[...] = jnp.zeros_like(last_out)
        sums_out[...] = jnp.zeros_like(sums_out)
        rate = jnp.exp(rates[1:2, :])
        end = totals_s[1:2, :] + heads[3, pl.ds(length - 1, 1), :] * totals_s[2:3, :]
        here = lax.broadcasted_iota(jnp.int32, (length, length), 0)
        there = lax.broadcasted_iota(jnp.int32, (length, length), 1)
        upper = jnp.where(here <= there, 1.0, 0.0)
        d_log = lax.dot_general(
            upper, found[0], (((1,), (0,)), ((), ())), precision=HIGH, preferred_element_type=f32
        )
        d_log = d_log + end
        d_dt = (found[1] - rate * d_log) * heads[4]
        d_out[:, :TILE] = d_dt.astype(bf16)
        d_out[:, TILE:] = jnp.zeros((length, WIDE - TILE), bf16)
        head_out[0:1, :] = jnp.sum(d_dt, 0, keepdims=True)
        head_out[1:2, :] = jnp.sum(d_log * (-heads[1] * rate), 0, keepdims=True)
        head_out[2:3, :] = totals_s[0:1, :]
        head_out[3:8, :] = jnp.zeros((5, TILE), f32)


def pack_kernel(sizes, sums, gain_in, gain_out, head, out):
    devices = out.shape[0]
    wide, channels, inner, heads = sizes
    gains = jnp.sum(gain_out[...], 0, keepdims=True)
    for at in range(devices):
        pieces = [gain_in[:, at * wide : (at + 1) * wide]]
        for tap in range(CONV + 1):
            pieces.append(sums[tap : tap + 1, at * channels : (at + 1) * channels])
        pieces.append(gains[:, at * inner : (at + 1) * inner])
        for row in range(3):
            pieces.append(head[row : row + 1, :heads])
        begin = 0
        for piece in pieces:
            out[at, :, begin : begin + piece.shape[1]] = piece
            begin += piece.shape[1]
        if begin < out.shape[2]:
            out[at, :, begin:] = jnp.zeros((1, out.shape[2] - begin), f32)


def scan_kernel(backward, mine, decay, out):
    count = mine.shape[0]

    def one(index, state):
        at = count - 1 - index if backward else index
        out[at] = state.astype(bf16)
        return decay[pl.ds(at, 1), :] * state + mine[at].astype(f32)

    lax.fori_loop(0, count, one, jnp.zeros(mine.shape[1:], f32))


def to_slices(value, devices):
    n_state, inner = value.shape
    across = max(1, devices // 16)
    rows = n_state * across // devices
    value = value.reshape(n_state // rows, rows, across, inner // across)
    return value.transpose(0, 2, 1, 3).reshape(devices, rows, inner // across)


def from_slices(slices, n_state, inner):
    devices, rows, columns = slices.shape
    value = slices.reshape(n_state // rows, inner // columns, rows, columns)
    return value.transpose(0, 2, 1, 3).reshape(n_state, inner)


def exchange(slices):
    return lax.all_to_all(slices, ALL, split_axis=0, concat_axis=0, tiled=True)


def return_slices(states, n_state, inner):
    return from_slices(exchange(states), n_state, inner)


def scan_devices(mine, decay, me, backward):
    devices, heads = decay.shape
    across = max(1, devices // 16)
    wide = jnp.repeat(decay, HEAD_DIM, axis=1).reshape(devices, across, heads * HEAD_DIM // across)
    wide = lax.dynamic_index_in_dim(wide, me % across, 1, False)
    return pl.pallas_call(
        lambda *refs: scan_kernel(backward, *refs),
        out_shape=jax.ShapeDtypeStruct(mine.shape, bf16),
        name="scan_backward" if backward else "scan_forward",
    )(mine, wide)


def flip(axis, bit):
    count = lax.axis_size(axis)
    return [(i, i ^ bit) for i in range(count)]


def other_core(value):
    return lax.ppermute(value, "shard", flip("shard", 1))


class Gather:
    def __init__(self, own, other, base, half, *wait):
        self.own, self.other, self.base, self.half = (own, other, base, half)
        self.mine = lax.axis_index("seq") % 2
        send = lax.dynamic_slice_in_dim(own, base + self.mine * half, half, 0)
        if wait:
            send = after(send, *wait)
        self.send = send
        self.direct = lax.ppermute(send, "shard", flip("shard", 2))

    def share(self, *wait):
        if wait:
            self.direct = after(self.direct, *wait)
        self.passed = lax.ppermute(self.direct, "seq", flip("seq", 1))

    def cross(self, *wait):
        direct, passed = (self.direct, self.passed)
        if wait:
            direct, passed = lax.optimization_barrier((direct, passed) + wait)[:2]
        self.parts = [direct, other_core(direct), passed, other_core(passed)]

    def turns(self):
        shard = lax.axis_index("shard")
        return [shard, shard ^ 1, shard ^ 2, shard ^ 3]


def project_kernel(table, *refs):
    lefts, (own, other, direct, direct_o, passed, passed_o, out, left) = (refs[:4], refs[4:])
    step = pl.program_id(0)

    @pl.when(step == 0)
    def _():
        left[...] = jnp.concatenate([a[...] for a in lefts], 1)

    def product(far, far_o):
        weight = jnp.concatenate([own[...], other[...], far[...], far_o[...]], 1)
        out[...] = mm_nt(left[...], weight).astype(bf16)

    near = pl.num_programs(0) // 2
    pl.when(step < near)(lambda: product(direct, direct_o))
    pl.when(step >= near)(lambda: product(passed, passed_o))


def project(value, gather):
    rows = value.shape[0]
    deep = gather.own.shape[1]
    near = gather.half // PIECE
    base = gather.base // PIECE
    order = [near * gather.mine + at for at in range(near)]
    order += [near * (1 - gather.mine) + at for at in range(near)]
    table = jnp.stack(gather.turns() + order).astype(jnp.int32)
    block = lambda index: pl.BlockSpec((PIECE, deep), index)
    left = lambda k: pl.BlockSpec((rows, deep), lambda j, t: (0, t[k]))
    own = block(lambda j, t: (base + t[4 + j], 0))
    first = block(lambda j, t: (jnp.minimum(j, near - 1), 0))
    second = block(lambda j, t: (jnp.maximum(j - near, 0), 0))
    return pl.pallas_call(
        project_kernel,
        grid_spec=pltpu.PrefetchScalarGridSpec(
            num_scalar_prefetch=1,
            grid=(2 * near,),
            in_specs=[left(k) for k in range(4)] + [own, own, first, first, second, second],
            out_specs=pl.BlockSpec((rows, PIECE), lambda j, t: (0, t[4 + j])),
            scratch_shapes=[pltpu.VMEM((rows, 4 * deep), bf16)],
        ),
        out_shape=jax.ShapeDtypeStruct((rows, 2 * gather.half), bf16),
        compiler_params=pltpu.CompilerParams(vmem_limit_bytes=58 * 1024 * 1024),
        cost_estimate=pl.CostEstimate(
            flops=16 * rows * deep * gather.half,
            bytes_accessed=16 * deep * gather.half,
            transcendentals=0,
        ),
        name="project",
    )(table, *([value] * 4), gather.own, gather.other, *gather.parts)


def back_kernel(values, table, *refs):
    (own, other, direct, direct_o, passed, passed_o, out, total) = refs[-8:]
    start = refs[values : len(refs) - 8]
    step = pl.program_id(0)
    last = pl.num_programs(0) - 1
    deep = own.shape[1]
    place = lambda k: pl.ds(pl.multiple_of(table[k] * deep, deep), deep)

    @pl.when(step == 0)
    def _():
        if start:
            for k in range(4):
                total[:, k * deep : (k + 1) * deep] = start[0][:, place(k)]
        else:
            total[...] = jnp.zeros_like(total)

    def product(value, far, far_o):
        weight = jnp.concatenate([own[...], other[...], far[...], far_o[...]], 1)
        total[...] += mm(value[...], weight)

    near = table[4 + step] == 1
    for at in range(values):
        mine = (step * values // (last + 1)) == at
        pl.when(mine & near)(lambda at=at: product(refs[at], direct, direct_o))
        pl.when(mine & jnp.logical_not(near))(lambda at=at: product(refs[at], passed, passed_o))

    @pl.when(step == last)
    def _():
        for k in range(4):
            out[:, place(k)] = total[:, k * deep : (k + 1) * deep]


def back(values, gather, start):
    rows = values[0].shape[0]
    deep = gather.own.shape[1]
    count = 2 * gather.half // PIECE
    share = count // len(values)
    near = gather.half // PIECE
    base = gather.base // PIECE
    mine = gather.mine
    flags, direct, passed = ([], [], [])
    for at in range(count):
        half, place = (at // near, at % near)
        is_near = mine == half
        ends = lambda own: jnp.where(own > half, 0, near - 1)
        flags.append(is_near)
        direct.append(jnp.where(is_near, place, ends(mine)))
        passed.append(jnp.where(is_near, ends(1 - mine), place))
    table = jnp.stack([jnp.asarray(v, jnp.int32) for v in gather.turns() + flags + direct + passed])
    block = lambda index: pl.BlockSpec((PIECE, deep), index)
    whole = pl.BlockSpec((rows, 4 * deep), lambda j, t: (0, 0))
    own = block(lambda j, t: (base + j, 0))
    one = block(lambda j, t: (t[4 + count + j], 0))
    two = block(lambda j, t: (t[4 + 2 * count + j], 0))
    in_specs = [
        pl.BlockSpec((rows, PIECE), lambda j, t, k=k: (0, jnp.clip(j - k * share, 0, share - 1)))
        for k in range(len(values))
    ]
    started = [] if start is None else [start]
    in_specs += [whole] * len(started) + [own, own, one, one, two, two]
    return pl.pallas_call(
        lambda *refs: back_kernel(len(values), *refs),
        grid_spec=pltpu.PrefetchScalarGridSpec(
            num_scalar_prefetch=1,
            grid=(count,),
            in_specs=in_specs,
            out_specs=whole,
            scratch_shapes=[pltpu.VMEM((rows, 4 * deep), f32)],
        ),
        out_shape=jax.ShapeDtypeStruct((rows, 4 * deep), f32),
        compiler_params=pltpu.CompilerParams(vmem_limit_bytes=58 * 1024 * 1024),
        cost_estimate=pl.CostEstimate(
            flops=16 * rows * deep * gather.half,
            bytes_accessed=16 * deep * gather.half,
            transcendentals=0,
        ),
        name="back",
    )(table, *values, *started, gather.own, gather.other, *gather.parts)


def by_shard(gather):
    half, width = (gather.half, gather.own.shape[1])
    whole = pl.BlockSpec((2 * half, width), lambda g, t: (0, 0))
    part = pl.BlockSpec((half, width), lambda g, t: (0, 0))
    direct, direct_o, passed, passed_o = gather.parts
    operands = [gather.own, gather.other, direct, passed, direct_o, passed_o]
    table = jnp.stack(gather.turns() + [gather.mine]).astype(jnp.int32)
    return operands, [whole] * 2 + [part] * 4, table


def out_back_kernel(table, value, own, other, direct, passed, direct_o, passed_o, out):
    step = pl.program_id(0)
    half = direct.shape[0]

    def two(near, far):
        out[:, pl.ds(pl.multiple_of(table[4] * half, half), half)] = mm_nt(value[...], near[...])
        far_at = pl.multiple_of((1 - table[4]) * half, half)
        out[:, pl.ds(far_at, half)] = mm_nt(value[...], far[...])

    for at, piece in enumerate((own, other)):

        @pl.when(step == at)
        def _(piece=piece):
            out[...] = mm_nt(value[...], piece[...])

    pl.when(step == 2)(lambda: two(direct, passed))
    pl.when(step == 3)(lambda: two(direct_o, passed_o))


def out_back(value, gather):
    rows, width = value.shape
    operands, specs, table = by_shard(gather)
    size = 2 * gather.half
    return pl.pallas_call(
        out_back_kernel,
        grid_spec=pltpu.PrefetchScalarGridSpec(
            num_scalar_prefetch=1,
            grid=(4,),
            in_specs=[pl.BlockSpec((rows, width), lambda g, t: (0, 0))] + specs,
            out_specs=pl.BlockSpec((rows, size), lambda g, t: (0, t[g])),
        ),
        out_shape=jax.ShapeDtypeStruct((rows, 4 * size), f32),
        compiler_params=pltpu.CompilerParams(vmem_limit_bytes=58 * 1024 * 1024),
        cost_estimate=pl.CostEstimate(
            flops=8 * rows * width * size, bytes_accessed=8 * width * size, transcendentals=0
        ),
        name="out_back",
    )(table, value, *operands)


def out_forward_kernel(table, value, base, own, other, direct, passed, direct_o, passed_o, out, total):
    step = pl.program_id(0)
    half = direct.shape[0]

    def two(near, far):
        near_at = pl.multiple_of(table[4] * half, half)
        far_at = pl.multiple_of((1 - table[4]) * half, half)
        total[...] += mm(value[:, pl.ds(near_at, half)], near[...])
        total[...] += mm(value[:, pl.ds(far_at, half)], far[...])

    @pl.when(step == 0)
    def _():
        total[...] = base[...].astype(f32) + mm(value[...], own[...])

    @pl.when(step == 1)
    def _():
        total[...] += mm(value[...], other[...])

    pl.when(step == 2)(lambda: two(direct, passed))

    @pl.when(step == 3)
    def _():
        two(direct_o, passed_o)
        out[...] = total[...].astype(bf16)


def out_forward(value, base, gather):
    rows = value.shape[0]
    operands, specs, table = by_shard(gather)
    size = 2 * gather.half
    width = gather.own.shape[1]
    fixed = pl.BlockSpec((rows, width), lambda g, t: (0, 0))
    return pl.pallas_call(
        out_forward_kernel,
        grid_spec=pltpu.PrefetchScalarGridSpec(
            num_scalar_prefetch=1,
            grid=(4,),
            in_specs=[pl.BlockSpec((rows, size), lambda g, t: (0, t[g])), fixed] + specs,
            out_specs=fixed,
            scratch_shapes=[pltpu.VMEM((rows, width), f32)],
        ),
        out_shape=jax.ShapeDtypeStruct((rows, width), bf16),
        compiler_params=pltpu.CompilerParams(vmem_limit_bytes=58 * 1024 * 1024),
        cost_estimate=pl.CostEstimate(
            flops=8 * rows * width * size, bytes_accessed=8 * width * size, transcendentals=0
        ),
        name="out_forward",
    )(table, value, base, *operands)


def stacked_project_kernel(value, *rest):
    weight = jnp.concatenate([w[...] for w in rest[:-1]], 1)
    rest[-1][...] = mm_nt(value[...], weight).astype(bf16)


def stacked_project(value, stack, base, count):
    rows = value.shape[0]
    shards, _, deep = stack.shape
    first = base // WIDE
    specs = [
        pl.BlockSpec((None, WIDE, deep), lambda j, k=k: (k, first + j, 0)) for k in range(shards)
    ]
    return pl.pallas_call(
        stacked_project_kernel,
        grid=(count // WIDE,),
        in_specs=[pl.BlockSpec((rows, shards * deep), lambda j: (0, 0))] + specs,
        out_specs=pl.BlockSpec((rows, WIDE), lambda j: (0, j)),
        out_shape=jax.ShapeDtypeStruct((rows, count), bf16),
        compiler_params=pltpu.CompilerParams(vmem_limit_bytes=58 * 1024 * 1024),
        cost_estimate=pl.CostEstimate(
            flops=2 * rows * shards * deep * count,
            bytes_accessed=2 * shards * deep * count,
            transcendentals=0,
        ),
        name="stacked_project",
    )(value, *([stack] * shards))


def stacked_back_kernel(value, *rest):
    out, total = rest[-2:]
    step = pl.program_id(0)

    @pl.when(step == 0)
    def _():
        total[...] = jnp.zeros_like(total)

    weight = jnp.concatenate([w[...] for w in rest[:-2]], 1)
    total[...] += mm(value[...], weight)

    @pl.when(step == pl.num_programs(0) - 1)
    def _():
        out[...] = total[...]


def stacked_back(value, stack, base):
    rows, count = value.shape
    shards, _, deep = stack.shape
    size = WIDE
    first = base // size
    specs = [
        pl.BlockSpec((None, size, deep), lambda j, k=k: (k, first + j, 0)) for k in range(shards)
    ]
    return pl.pallas_call(
        stacked_back_kernel,
        grid=(count // size,),
        in_specs=[pl.BlockSpec((rows, size), lambda j: (0, j))] + specs,
        out_specs=pl.BlockSpec((rows, shards * deep), lambda j: (0, 0)),
        out_shape=jax.ShapeDtypeStruct((rows, shards * deep), f32),
        scratch_shapes=[pltpu.VMEM((rows, shards * deep), f32)],
        compiler_params=pltpu.CompilerParams(vmem_limit_bytes=58 * 1024 * 1024),
        cost_estimate=pl.CostEstimate(
            flops=2 * rows * shards * deep * count,
            bytes_accessed=2 * shards * deep * count,
            transcendentals=0,
        ),
        name="stacked_back",
    )(value, *([stack] * shards))


def halve(value, dim, axis, bit, mine, wait):
    shape = value.shape
    value = value.reshape(shape[:dim] + (shape[dim] // 2, 2) + shape[dim + 1 :])
    send = lax.dynamic_index_in_dim(value, 1 - mine, dim + 1, False)
    kept = lax.dynamic_index_in_dim(value, mine, dim + 1, False)
    came = lax.ppermute(send, axis, flip(axis, bit))
    if wait:
        came = after(came, *wait)
    return (kept.astype(f32) + came.astype(f32)).astype(bf16), send


class RowSum:
    def __init__(self, partial, far_first):
        shards, places = (lax.axis_size("shard"), lax.axis_size("seq"))
        shard, place = (lax.axis_index("shard"), lax.axis_index("seq"))
        rows, columns = partial.shape
        chips = shards // 2
        self.value = partial.reshape(chips, places, rows // (chips * places), columns)
        far = [(0, "shard", 2 << k, (shard >> (k + 1)) & 1) for k in range(chips.bit_length() - 1)]
        near = [(1, "seq", 1 << k, (place >> k) & 1) for k in range(places.bit_length() - 1)]
        self.order = far + near if far_first else near[:1] + far + near[1:]

    def step(self, *wait):
        if not self.order:
            return
        dim, axis, bit, mine = self.order.pop(0)
        self.value, self.send = halve(self.value, dim, axis, bit, mine, wait)

    def rows(self):
        return self.value.reshape(self.value.shape[2:])


def core_rows(value, core):
    shards = lax.axis_size("shard")
    size = value.shape[1] // shards
    even = [value[:, at * size : (at + 1) * size] for at in range(0, shards, 2)]
    odd = [value[:, at * size : (at + 1) * size] for at in range(1, shards, 2)]
    own = [jnp.where(core == 0, a, b) for a, b in zip(even, odd)]
    rest = [jnp.where(core == 0, b, a) for a, b in zip(even, odd)]
    return jnp.concatenate(own, 1), jnp.concatenate(rest, 1)


def after(value, *others):
    return lax.optimization_barrier((value,) + others)[0]


def turn_blocks(value, shard):
    shards = lax.axis_size("shard")
    size = value.shape[1] // shards
    blocks = [
        lax.dynamic_slice_in_dim(value, (at ^ shard) * size, size, 1) for at in range(shards)
    ]
    return jnp.concatenate(blocks, 1)


def on_device(
    hidden,
    cotangent,
    seg_ids,
    norm_gain,
    in_weight,
    conv_weight,
    conv_bias,
    dt_bias,
    a_log,
    d_skip,
    out_gain,
    out_weight,
):
    shards, places = (lax.axis_size("shard"), lax.axis_size("seq"))
    shard, place = (lax.axis_index("shard"), lax.axis_index("seq"))
    devices = shards * places
    me = shard * places + place
    length, width = hidden.shape
    heads = dt_bias.shape[0]
    inner = out_weight.shape[0] * shards
    channels = conv_bias.shape[0] * shards
    n_state = (channels - inner) // 2
    groups = inner // WIDE
    start = me * length

    core = shard % 2
    w_in = in_weight.T
    by_hand = shards == 4 and places % 2 == 0
    edge_rows = w_in.shape[0] - 2 * inner
    small = jnp.concatenate([norm_gain, conv_weight.reshape(-1), conv_bias, out_gain])
    small_rows = pl.cdiv(small.shape[0], w_in.shape[1])
    small_rows += -(small_rows + edge_rows) % 16
    small = jnp.pad(small, (0, small_rows * w_in.shape[1] - small.shape[0]))
    edges = jnp.concatenate([w_in[2 * inner :], small.reshape(small_rows, w_in.shape[1])], 0)
    if by_hand:
        in_other = other_core(w_in)
        g_x = Gather(w_in, in_other, inner, inner // 2)
        edges = after(edges, g_x.send)
    edges = jnp.broadcast_to(edges[None], (shards, *edges.shape))
    edges = lax.all_to_all(edges, "shard", split_axis=0, concat_axis=0, tiled=True)
    w_edge = edges[:, :edge_rows].transpose(1, 0, 2).reshape(edge_rows, width)
    w_edge = jnp.pad(w_edge, ((0, -edge_rows % TILE), (0, 0)))
    small = edges[:, edge_rows:].reshape(shards, -1)
    if by_hand:
        g_x.share()
        g_x.cross()
        g_z = Gather(w_in, in_other, 0, inner // 2, g_x.direct)
        g_z.share()
        out_other = other_core(after(out_weight, g_x.direct))
        g_out = Gather(out_weight, out_other, 0, out_weight.shape[0] // 2, g_z.direct)
    else:
        stack_x = lax.all_gather(w_in[inner : 2 * inner], "shard")
        stack_z = lax.all_gather(w_in[:inner], "shard")
        w_out = lax.all_gather(out_weight, "shard", axis=0, tiled=True)
    at = 0
    gain_in = small[:, at : at + norm_gain.shape[0]].reshape(-1).astype(f32)
    at += norm_gain.shape[0]
    taps = small[:, at : at + conv_weight.size].reshape(shards, CONV, -1)
    taps = taps.transpose(1, 0, 2).reshape(CONV, channels).astype(f32)
    at += conv_weight.size
    bias = small[:, at : at + conv_bias.shape[0]].reshape(-1).astype(f32)
    at += conv_bias.shape[0]
    gain_out = small[:, at : at + out_gain.shape[0]].reshape(-1).astype(f32)
    skip_wide = jnp.repeat(d_skip.astype(f32), HEAD_DIM)
    rows = jnp.concatenate([skip_wide, jnp.zeros((channels - inner,), f32)])
    taps8 = jnp.concatenate([taps, bias[None], rows[None], jnp.zeros((2, channels), f32)], 0)

    edge = jnp.full((HALO,), -1, jnp.int32)
    padded = jnp.concatenate([edge, seg_ids, edge - 1])
    near = lax.dynamic_slice_in_dim(padded, start, length + 2 * HALO)
    seg = near[HALO : HALO + length]
    fwd_masks = [near[HALO - CONV + 1 + k : HALO - CONV + 1 + k + length] == seg for k in range(3)]
    spot = jnp.arange(length, dtype=jnp.int32)
    bwd_masks = [
        (near[HALO + CONV - 1 - k : HALO + CONV - 1 - k + length] == seg)
        & (spot + CONV - 1 - k < length)
        for k in range(3)
    ]
    from_before = seg == near[HALO - 1]
    to_last = seg == seg[length - 1]
    flags = jnp.stack(
        [m.astype(f32) for m in fwd_masks + bwd_masks + [seg, from_before, to_last]], 1
    )
    flags = jnp.pad(flags, ((0, 0), (0, 16 - flags.shape[1])))
    seg_row = jnp.broadcast_to(seg.astype(f32)[None, :], (8, length))

    behind = lax.ppermute(
        hidden[length - HALO :], ALL, [(i, i + 1) for i in range(devices - 1)]
    )
    hidden_f = jnp.concatenate([behind, hidden], 0).astype(f32)
    scale_in = lax.rsqrt(jnp.mean(hidden_f * hidden_f, axis=1, keepdims=True) + EPS)
    normed_ext = (hidden_f * scale_in * gain_in[None, :]).astype(bf16)
    normed_in = normed_ext[HALO:]
    proj_edge = mm_nt(normed_ext, w_edge).astype(bf16)
    proj_bc = proj_edge[:, : 2 * n_state]
    rates = jnp.stack([dt_bias, a_log]).astype(f32)
    rates = jnp.pad(rates, ((0, 6), (0, TILE - heads)))
    big = pltpu.CompilerParams(vmem_limit_bytes=56 * 1024 * 1024)
    per_head, spreads, cum, sums_row, masks = pl.pallas_call(
        prepare_kernel,
        out_shape=[
            jax.ShapeDtypeStruct((5, length, TILE), f32),
            jax.ShapeDtypeStruct((2, length, 2 * TILE), bf16),
            jax.ShapeDtypeStruct((groups, length, GROUP), f32),
            jax.ShapeDtypeStruct((groups, GROUP, length), f32),
            jax.ShapeDtypeStruct((2 * (CONV - 1), length, TILE), f32),
        ],
        compiler_params=big,
        name="prepare",
    )(proj_edge[HALO:, 2 * n_state :], rates, flags)
    end = per_head[3, length - 1, :heads]
    decays = jnp.broadcast_to(end[None, None, :], (devices, 1, heads))
    decays = lax.all_to_all(decays, ALL, split_axis=0, concat_axis=0, tiled=True)[:, 0, :]
    if by_hand:
        proj = project(after(normed_ext, g_z.direct, decays), g_x)
    else:
        proj = stacked_project(normed_ext, stack_x, 0, inner)

    def whole(shape):
        return pl.BlockSpec(shape, lambda g: (0,) * len(shape))

    def group_of(g):
        return jnp.maximum(g - 1, 0)

    order = lambda g: jnp.where(g == 0, groups, g - 1)
    x_conv, state_local, bc, bt, ct = pl.pallas_call(
        state_kernel,
        grid=(groups + 1,),
        in_specs=[
            pl.BlockSpec((length + HALO, WIDE), lambda g: (0, group_of(g))),
            whole((length + HALO, WIDE)),
            pl.BlockSpec((8, WIDE), lambda g: (0, order(g))),
            whole(masks.shape),
            whole(spreads.shape),
        ],
        out_specs=[
            pl.BlockSpec((length, WIDE), lambda g: (0, group_of(g))),
            pl.BlockSpec((n_state, WIDE), lambda g: (0, group_of(g))),
            whole((length, 2 * n_state)),
            whole((n_state, length)),
            whole((n_state, length)),
        ],
        out_shape=[
            jax.ShapeDtypeStruct((length, inner), bf16),
            jax.ShapeDtypeStruct((n_state, inner), bf16),
            jax.ShapeDtypeStruct((length, 2 * n_state), bf16),
            jax.ShapeDtypeStruct((n_state, length), bf16),
            jax.ShapeDtypeStruct((n_state, length), bf16),
        ],
        scratch_shapes=[
            pltpu.VMEM((length + HALO, WIDE), f32),
            pltpu.VMEM((n_state, length), bf16),
        ],
        compiler_params=big,
        cost_estimate=pl.CostEstimate(
            flops=20 * length * inner * n_state, bytes_accessed=10 * length * inner, transcendentals=0
        ),
        name="mixer_state",
    )(proj, proj_bc, taps8, masks, spreads)

    if by_hand:
        slices = after(to_slices(state_local, devices), g_out.direct)
        g_out.share(slices)
        sent = exchange(slices)
        g_z.cross(slices)
        gate_z = project(after(normed_in, slices), g_z)
        states = scan_devices(after(sent, gate_z), decays, me, False)
    else:
        sent = exchange(to_slices(state_local, devices))
        gate_z = stacked_project(normed_in, stack_z, 0, inner)
        states = scan_devices(sent, decays, me, False)
    state_in = return_slices(states, n_state, inner)
    x_conv = after(x_conv, states)
    half_t = 2 * TILE
    y_local = pl.pallas_call(
        forward_kernel,
        grid=(groups,),
        in_specs=[
            pl.BlockSpec((length, WIDE), lambda g: (0, g)),
            whole(flags.shape),
            whole((8, length)),
            whole(spreads.shape),
            pl.BlockSpec((1, length, GROUP), lambda g: (g, 0, 0)),
            pl.BlockSpec((1, GROUP, length), lambda g: (g, 0, 0)),
            whole((length, 2 * n_state)),
            whole((n_state, length)),
        ],
        out_specs=pl.BlockSpec((length, WIDE), lambda g: (0, g)),
        out_shape=jax.ShapeDtypeStruct((length, inner), f32),
        scratch_shapes=[
            pltpu.VMEM((length, length), f32),
            pltpu.VMEM((length // half_t, GROUP * half_t, WIDE), bf16),
            pltpu.VMEM((length // half_t, length, GROUP * half_t), bf16),
        ],
        compiler_params=big,
        cost_estimate=pl.CostEstimate(
            flops=16 * length * length * inner, bytes_accessed=10 * length * inner, transcendentals=0
        ),
        name="mixer_forward",
    )(x_conv, flags, seg_row, spreads, cum, sums_row, bc, bt)
    if by_hand:
        g_out.cross(y_local)
        d_normed = out_back(after(cotangent, y_local), g_out)
    else:
        d_normed = mm_nt(cotangent, w_out)
    block = TILE
    tall = lambda dim: pl.BlockSpec((block, dim), lambda g: (g, 0))
    gains = jnp.stack([gain_out, skip_wide], 0)
    ssm, normed_out, d_z, d_y, d_state_local, dc_more, d_gain = pl.pallas_call(
        gate_kernel,
        grid=(length // block,),
        in_specs=[
            tall(inner),
            tall(inner),
            tall(inner),
            tall(inner),
            tall(2 * n_state),
            pl.BlockSpec((n_state, block), lambda g: (0, g)),
            pl.BlockSpec((None, block, TILE), lambda g: (3, g, 0)),
            whole((n_state, inner)),
            whole((2, inner)),
        ],
        out_specs=[
            tall(inner),
            tall(inner),
            tall(inner),
            tall(inner),
            whole((n_state, inner)),
            tall(n_state),
            whole((8, inner)),
        ],
        out_shape=[
            jax.ShapeDtypeStruct((length, inner), f32),
            jax.ShapeDtypeStruct((length, inner), bf16),
            jax.ShapeDtypeStruct((length, inner), bf16),
            jax.ShapeDtypeStruct((length, inner), bf16),
            jax.ShapeDtypeStruct((n_state, inner), bf16),
            jax.ShapeDtypeStruct((length, n_state), f32),
            jax.ShapeDtypeStruct((8, inner), f32),
        ],
        scratch_shapes=[
            pltpu.VMEM((block, inner), f32),
            pltpu.VMEM((block, inner), f32),
            pltpu.VMEM((block, inner), bf16),
            pltpu.VMEM((n_state, inner), f32),
        ],
        compiler_params=big,
        cost_estimate=pl.CostEstimate(
            flops=8 * length * n_state * inner, bytes_accessed=22 * length * inner, transcendentals=0
        ),
        name="mixer_gate",
    )(y_local, x_conv, gate_z, d_normed, bc, ct, per_head, state_in, gains)

    slices = to_slices(d_state_local, devices)
    sent = exchange(slices)
    normed_out, d_z = (after(normed_out, slices), after(d_z, slices))

    def both(value):
        return jnp.concatenate([value, other_core(value)], 0)

    def both_rows(value):
        own, rest = core_rows(value, core)
        return jnp.concatenate([own, other_core(rest)], 0)

    normed_pair = both_rows(normed_in)
    cot_pair = both(cotangent)
    out_pair = both_rows(normed_out)
    z_pair = both(d_z)
    if by_hand:
        block_out = out_forward(normed_out, hidden, g_out)
    else:
        block_out = (hidden.astype(f32) + mm(normed_out, w_out)).astype(bf16)
    grad_o = mm_tn(after(out_pair, block_out), cot_pair).astype(bf16)
    states = scan_devices(after(sent, grad_o), decays, me, True)
    returned = exchange(states)
    grad_z = mm_tn(normed_pair, after(z_pair, states)).astype(bf16)
    half_o, half_z = (width // 2, inner // 2)
    grad_o = after(grad_o, grad_z)
    sums_o = [RowSum(grad_o[:, :half_o], True), RowSum(grad_o[:, half_o:], False)]
    sums_z = [RowSum(grad_z[:, :half_z], True), RowSum(grad_z[:, half_z:], False)]
    x_conv = after(x_conv, grad_o, grad_z)

    dxs, db_in, dc_in = pl.pallas_call(
        inside_kernel,
        grid=(groups,),
        in_specs=[
            pl.BlockSpec((length, WIDE), lambda g: (0, g)),
            whole(flags.shape),
            whole((8, length)),
            whole(spreads.shape),
            pl.BlockSpec((1, length, GROUP), lambda g: (g, 0, 0)),
            pl.BlockSpec((1, GROUP, length), lambda g: (g, 0, 0)),
            whole((length, 2 * n_state)),
            whole((n_state, length)),
            pl.BlockSpec((length, WIDE), lambda g: (0, g)),
        ],
        out_specs=[
            pl.BlockSpec((length, WIDE), lambda g: (0, g)),
            whole((length, n_state)),
            whole((length, n_state)),
        ],
        out_shape=[
            jax.ShapeDtypeStruct((length, inner), f32),
            jax.ShapeDtypeStruct((length, n_state), f32),
            jax.ShapeDtypeStruct((length, n_state), f32),
        ],
        scratch_shapes=[
            pltpu.VMEM((length, length), f32),
            pltpu.VMEM((length, length), f32),
            pltpu.VMEM((length // half_t, GROUP * half_t, WIDE), bf16),
            pltpu.VMEM((length // half_t, length, GROUP * half_t), bf16),
            pltpu.VMEM((GROUP, length, WIDE), bf16),
            pltpu.VMEM((2, length, length), f32),
        ],
        compiler_params=big,
        cost_estimate=pl.CostEstimate(
            flops=8 * length * length * inner, bytes_accessed=10 * length * inner, transcendentals=0
        ),
        name="mixer_inside",
    )(x_conv, flags, seg_row, spreads, cum, sums_row, bc, ct, d_y)

    for chain in sums_o:
        chain.step(dxs)
    d_state = from_slices(after(returned, dxs), n_state, inner)
    taps8 = jnp.pad(taps8, ((0, 0), (0, WIDE)))

    def outside(first_group, count, final, grad, running):
        kept = lambda g: jnp.minimum(g, count - 1) + first_group
        steps = count + (2 if final else 0)
        columns = steps * WIDE
        tall = lambda: pl.BlockSpec((length, WIDE), lambda g: (0, kept(g)))
        flat = lambda: pl.BlockSpec((n_state, WIDE), lambda g: (0, kept(g)))
        return pl.pallas_call(
            lambda *refs: outside_kernel(first_group, count, final, *refs),
            grid=(steps,),
            in_specs=[
                pl.BlockSpec((length + HALO, WIDE), lambda g: (0, kept(g))),
                whole((length + HALO, WIDE)),
                pl.BlockSpec((8, WIDE), lambda g: (0, first_group + g)),
                whole(masks.shape),
                whole(spreads.shape),
                whole(per_head.shape),
                whole(rates.shape),
                whole((length, 2 * n_state)),
                tall(),
                tall(),
                tall(),
                flat(),
                flat(),
                whole((length, n_state)),
                whole((length, n_state)),
                whole((length, n_state)),
                whole((length, n_state)),
                whole((2, length, TILE)),
                whole((8, TILE)),
            ],
            out_specs=[
                pl.BlockSpec((length, WIDE), lambda g: (0, g)),
                pl.BlockSpec((HALO, WIDE), lambda g: (0, g)),
                pl.BlockSpec((HALO, WIDE), lambda g: (0, g)),
                pl.BlockSpec((8, WIDE), lambda g: (0, g)),
                whole((8, TILE)),
                whole((length, n_state)),
                whole((2, length, TILE)),
                whole((8, TILE)),
            ],
            out_shape=[
                jax.ShapeDtypeStruct((length, columns), bf16),
                jax.ShapeDtypeStruct((HALO, columns), f32),
                jax.ShapeDtypeStruct((HALO, columns), f32),
                jax.ShapeDtypeStruct((8, columns), f32),
                jax.ShapeDtypeStruct((8, TILE), f32),
                jax.ShapeDtypeStruct((length, n_state), f32),
                jax.ShapeDtypeStruct((2, length, TILE), f32),
                jax.ShapeDtypeStruct((8, TILE), f32),
            ],
            scratch_shapes=[
                pltpu.VMEM((length + HALO, WIDE), f32),
                pltpu.VMEM((length + HALO, WIDE), f32),
            ],
            compiler_params=big,
            cost_estimate=pl.CostEstimate(
                flops=8 * length * n_state * columns,
                bytes_accessed=16 * length * columns,
                transcendentals=0,
            ),
            name="mixer_outside",
        )(proj, proj_bc, taps8, masks, spreads, per_head, rates, bc, grad, ssm, dxs, d_state,
          state_in, db_in, dc_in, dc_more, *running)

    seg_end = near[length : length + 2 * HALO]

    def finish(grads, first, last, start):
        ahead = lax.ppermute(first, ALL, [(i + 1, i) for i in range(devices - 1)])
        joined = jnp.concatenate([jnp.zeros_like(first), ahead], 0)
        for tap in range(CONV - 1):
            lead = CONV - 1 - tap
            same = (seg_end[lead : lead + HALO] == seg_end[:HALO]).astype(f32)[:, None]
            here = taps8[tap, start : start + first.shape[1]]
            last = last + here[None, :] * joined[lead : lead + HALO] * same
        count = min(channels - start, first.shape[1])
        return lax.dynamic_update_slice(grads, last[:, :count].astype(bf16), (length - HALO, 0))

    running = (
        jnp.zeros((length, n_state), f32),
        jnp.zeros((2, length, TILE), f32),
        jnp.zeros((8, TILE), f32),
    )
    part = groups // 2
    half_x = part * WIDE

    values = lambda *chains: [chain.value for chain in chains]
    grad = after(d_y, *values(*sums_o))
    d_one, first, last, sums_one, _, *running = outside(0, part, False, grad, running)
    for chain in sums_z + sums_o:
        chain.step(d_one)
    d_one = finish(d_one, first, last, 0)
    one_pair = both(d_one)
    if by_hand:
        d_normed_in = back([after(d_z, d_one)], g_z, None)
    else:
        d_normed_in = stacked_back(d_z, stack_z, 0)
    grad_x = mm_tn(normed_pair, after(one_pair, d_normed_in)).astype(bf16)
    sum_a = RowSum(grad_x, True)
    grad = after(d_y, grad_x, *values(*sums_o, *sums_z))
    d_two, first, last, sums_two, head_sums, *_ = outside(part, groups - part, True, grad, running)
    sums = jnp.concatenate([sums_one, sums_two], 1)
    for chain in sums_z + sums_o + [sum_a]:
        chain.step(d_two)
    d_two = finish(d_two, first, last, half_x)
    two_pair = both(d_two)
    count = inner - half_x
    edge = after(d_two, *values(sum_a))[:, count : count + w_edge.shape[0]]
    d_normed_in = d_normed_in + mm(edge, w_edge)
    grad_y = mm_tn(normed_pair, after(two_pair, d_normed_in)).astype(bf16)
    half = grad_y.shape[1] // 2
    sums_b = [RowSum(grad_y[:, :half], True), RowSum(grad_y[:, half:], False)]
    for chain in sums_z + sums_o + [sum_a]:
        chain.step(grad_y)
    if by_hand:
        d_normed_in = back([d_one, after(d_two, grad_y)], g_x, d_normed_in)
    else:
        d_x = jnp.concatenate([d_one, d_two[:, :count]], 1)
        d_normed_in = d_normed_in + stacked_back(d_x, stack_x, 0)
    for chain in sums_b + [sum_a]:
        chain.step(d_normed_in)
    d_normed_in = after(d_normed_in, *values(sum_a, *sums_b))
    sums_x = [sum_a] + sums_b
    base = hidden_f[HALO:]
    scale = scale_in[HALO:]
    d_hat = d_normed_in * gain_in[None, :]
    mean = jnp.mean(d_hat * base, axis=1, keepdims=True)
    grad_hidden = cotangent.astype(f32) + scale * d_hat - base * (scale * scale * scale * mean)
    grad_gain_in = jnp.sum(d_normed_in * base * scale, 0)
    while any(chain.order for chain in sums_o + sums_z + sums_x):
        for chain in sums_x + sums_o + sums_z:
            chain.step(grad_gain_in)
    counts = [width // devices] + [channels // devices] * (CONV + 1) + [inner // devices]
    counts += [heads] * 3
    total = sum(counts)
    if by_hand:
        sizes = (width // devices, channels // devices, inner // devices, heads)
        packed = pl.pallas_call(
            lambda *refs: pack_kernel(sizes, *refs),
            out_shape=jax.ShapeDtypeStruct((devices, 1, total + -total % TILE), f32),
            name="pack",
        )(sums[:, :channels], grad_gain_in[None], d_gain, head_sums)
    else:
        slots = lambda v: v.reshape(-1, devices, v.shape[-1] // devices).transpose(1, 0, 2)
        same = jnp.broadcast_to(head_sums[:3, :heads].reshape(1, -1), (devices, 3 * heads))
        pieces = [slots(grad_gain_in), slots(sums[: CONV + 1, :channels])]
        pieces += [slots(jnp.sum(d_gain, 0)), same]
        packed = jnp.concatenate([p.reshape(devices, -1) for p in pieces], 1)[:, None]
    packed = lax.all_to_all(packed, ALL, split_axis=0, concat_axis=0, tiled=True).sum((0, 1))
    found, at = ([], 0)
    for size in counts:
        found.append(packed[at : at + size])
        at += size

    grads = [c.rows().astype(f32) for c in sums_z + sums_x]
    excess = sum(g.shape[1] for g in grads) - w_in.shape[0]
    grads[-1] = grads[-1][:, : grads[-1].shape[1] - excess]
    return (
        block_out,
        grad_hidden,
        found[0],
        jnp.concatenate(grads, 1),
        jnp.stack(found[1 : CONV + 1]),
        found[CONV + 1],
        found[CONV + 3],
        found[CONV + 4],
        found[CONV + 5],
        found[CONV + 2],
        jnp.concatenate([c.rows().astype(f32) for c in sums_o], 1),
    )


def solution(mesh):
    return jax.shard_map(
        on_device,
        mesh=mesh,
        in_specs=(
            P(ALL, None),
            P(ALL, None),
            P(),
            P("shard"),
            P("shard", None),
            P(None, "shard"),
            P("shard"),
            P(),
            P(),
            P(),
            P("shard"),
            P("shard", None),
        ),
        out_specs=(
            P(ALL, None),
            P(ALL, None),
            P(ALL),
            P(ALL, None),
            P(None, ALL),
            P(ALL),
            P(),
            P(),
            P(),
            P(ALL),
            P(ALL, None),
        ),
        check_vma=False,
    )
```

```python
import jax
import jax.numpy as jnp
from jax import lax
from jax.experimental import pallas as pl
from jax.experimental.pallas import tpu as pltpu
from jax.sharding import PartitionSpec as P

HEAD_DIM = 64
CONV = 4
EPS = 1e-05
HALO = 8
GROUP = 4
WIDE = GROUP * HEAD_DIM
TILE = 128
PIECE = 3 * WIDE
HIGH = lax.Precision.HIGHEST
ALL = ("shard", "seq")
f32 = jnp.float32
bf16 = jnp.bfloat16
CHEAP = pl.CostEstimate(flops=1, bytes_accessed=1, transcendentals=0)


def mm(a, b):
    return jnp.dot(a, b, preferred_element_type=f32)


def mm_nt(a, b):
    return lax.dot_general(a, b, (((1,), (1,)), ((), ())), preferred_element_type=f32)


def mm_tn(a, b):
    return lax.dot_general(a, b, (((0,), (0,)), ((), ())), preferred_element_type=f32)


def sigmoid(value):
    return 0.5 * jnp.tanh(0.5 * value) + 0.5


def head_lanes(group):
    lane = lax.rem(lax.broadcasted_iota(jnp.int32, (2 * TILE, WIDE), 0), TILE)
    owner = lax.broadcasted_iota(jnp.int32, (2 * TILE, WIDE), 1) // HEAD_DIM + GROUP * group
    return jnp.where(lane == owner, 1.0, 0.0).astype(bf16)


def two_parts(value):
    high = value.astype(bf16)
    low = (value - high.astype(f32)).astype(bf16)
    return high, low


def twice(value):
    return jnp.concatenate([value, value], 1)


def conv_rows(wide, taps, masks, start, rows):
    pre = taps[CONV : CONV + 1, :] + taps[CONV - 1 : CONV, :] * wide[pl.ds(HALO + start, rows), :]
    for tap in range(CONV - 1):
        shifted = wide[pl.ds(HALO - CONV + 1 + tap + start, rows), :]
        pre = pre + taps[tap : tap + 1, :] * shifted * twice(masks[tap, pl.ds(start, rows), :])
    return pre


def prepare_kernel(edge, rates, flags, out, spread_out, cum_out, row_out, masks_out):
    length = out.shape[1]
    shifted = edge[...].astype(f32) + rates[0:1, :]
    step = jax.nn.softplus(shifted)
    here = lax.broadcasted_iota(jnp.int32, (length, length), 0)
    there = lax.broadcasted_iota(jnp.int32, (length, length), 1)
    lower = jnp.where(here >= there, 1.0, 0.0)
    log_decay = -step * jnp.exp(rates[1:2, :])
    cum = lax.dot_general(
        lower, log_decay, (((1,), (0,)), ((), ())), precision=HIGH, preferred_element_type=f32
    )
    keep = jnp.exp(cum[length - 1 : length, :] - cum) * flags[:, 8:9]
    out[0] = cum
    out[1] = step
    out[2] = keep
    out[3] = jnp.exp(cum) * flags[:, 7:8]
    out[4] = sigmoid(shifted)
    for at, value in enumerate((step, keep)):
        high, low = two_parts(value)
        spread_out[at, :, :TILE] = high
        spread_out[at, :, TILE:] = low
    turned = cum.T
    for group in range(row_out.shape[0]):
        heads = slice(GROUP * group, GROUP * (group + 1))
        row_out[group] = turned[heads, :]
        cum_out[group] = cum[:, heads]
    for at in range(2 * (CONV - 1)):
        masks_out[at] = jnp.broadcast_to(flags[:, at : at + 1], (length, TILE))


def state_kernel(raw, raw_bc, taps, masks, spreads, x_out, state_out, bc_out, bt_out, ct_out, wide, bt):
    length = x_out.shape[0]
    n_state = bt.shape[0]
    step = pl.program_id(0)

    @pl.when(step == 0)
    def _():
        wide[...] = raw_bc[...].astype(f32)
        for start in range(0, length, TILE):
            rows = pl.ds(start, TILE)
            pre = conv_rows(wide, taps, masks, start, TILE)
            both = pre * sigmoid(pre)
            bc_out[rows, :] = both.astype(bf16)
            turned = both[:, :n_state].T.astype(bf16)
            bt[:, rows] = turned
            bt_out[:, rows] = turned
            ct_out[:, rows] = both[:, n_state:].T.astype(bf16)

    @pl.when(step > 0)
    def _():
        wide[...] = raw[...].astype(f32)
        lanes = head_lanes(step - 1)
        kept = []
        for start in range(0, length, TILE):
            rows = pl.ds(start, TILE)
            pre = conv_rows(wide, taps, masks, start, TILE)
            x = (pre * sigmoid(pre)).astype(bf16)
            x_out[rows, :] = x
            scaled = (x.astype(f32) * mm(spreads[0, rows, :], lanes)).astype(bf16)
            kept.append((scaled.astype(f32) * mm(spreads[1, rows, :], lanes)).astype(bf16))
        state_out[...] = mm(bt[...], jnp.concatenate(kept, 0)).astype(bf16)


def scored(first, second, flags, seg_row, score, later):
    length = score.shape[0]
    for start in range(0, length, TILE):
        rows = pl.ds(start, TILE)
        product = mm(first(rows), second[...])
        here = lax.broadcasted_iota(jnp.int32, (TILE, length), 0) + start
        there = lax.broadcasted_iota(jnp.int32, (TILE, length), 1)
        order = (here >= there) if later else (here <= there)
        seen = (flags[rows, 6:7] == seg_row[0:1, :]) & order
        score[rows, :] = jnp.where(seen, product, 0.0)


def by_head(value):
    owner = lax.broadcasted_iota(jnp.int32, value.shape, 1) // HEAD_DIM
    zero = jnp.zeros_like(value)
    return [jnp.where(owner == head, value, zero) for head in range(GROUP)]


def forward_kernel(x_in, flags, seg_row, spreads, cum, sums_row, bc, bt, y_out, score, apart, weights):
    length = y_out.shape[0]
    n_state = bt.shape[0]
    group = pl.program_id(0)
    big = weights.shape[2] // GROUP

    @pl.when(group == 0)
    def _():
        scored(lambda rows: bc[rows, n_state:], bt, flags, seg_row, score, True)
        weights[...] = jnp.zeros_like(weights)

    lanes = head_lanes(group)
    for start in range(0, length, TILE):
        rows = pl.ds(start, TILE)
        scaled = x_in[rows, :].astype(f32) * mm(spreads[0, rows, :], lanes)
        for head, value in enumerate(by_head(scaled)):
            apart[start // big, pl.ds(head * big + start % big, TILE), :] = value.astype(bf16)
    for head in range(GROUP):
        for start in range(0, length, TILE):
            rows = pl.ds(start, TILE)
            for at in range(0, start + TILE, big):
                end = min(at + big, start + TILE)
                gap = cum[0, rows, head : head + 1] - sums_row[0, head : head + 1, at:end]
                weight = jnp.exp(jnp.minimum(gap, 0.0)) * score[rows, at:end]
                weights[at // big, rows, head * big : head * big + end - at] = weight.astype(bf16)
    for at in range(0, length, big):
        part = mm(weights[at // big, at:, :], apart[at // big])
        if at == 0:
            y_out[...] = part
        else:
            y_out[at:, :] += part


def gate_kernel(
    y_in, x_in, z_in, dn_in, bc, ct, enter, state, gain, ssm_out, norm_out, dz_out, dy_out,
    ds_out, dc_out, dg_out, gated_s, sig_s, mo_s, ds_acc
):
    rows = y_in.shape[0]
    width = y_in.shape[1]
    n_state = state.shape[0]
    step = pl.program_id(0)
    lane = lax.broadcasted_iota(jnp.int32, (rows, 2 * HEAD_DIM), 1)
    c_mat = bc[:, n_state:]

    @pl.when(step == 0)
    def _():
        ds_acc[...] = jnp.zeros_like(ds_acc)
        dg_out[...] = jnp.zeros_like(dg_out)

    def entering(block):
        low = enter[:, 2 * block : 2 * block + 1]
        top = enter[:, 2 * block + 1 : 2 * block + 2]
        return jnp.where(lane < HEAD_DIM, low, top)

    square = jnp.zeros((rows, 2 * HEAD_DIM), f32)
    cross = jnp.zeros((rows, 2 * HEAD_DIM), f32)
    for block in range(width // (2 * HEAD_DIM)):
        lanes = slice(block * 2 * HEAD_DIM, (block + 1) * 2 * HEAD_DIM)
        ssm = y_in[:, lanes] + entering(block) * mm(c_mat, state[:, lanes])
        ssm_out[:, lanes] = ssm
        mo = (ssm + gain[1:2, lanes] * x_in[:, lanes].astype(f32)).astype(bf16)
        mo_s[:, lanes] = mo
        z = z_in[:, lanes].astype(f32)
        sig = sigmoid(z)
        gated = mo.astype(f32) * (z * sig)
        gated_s[:, lanes] = gated
        sig_s[:, lanes] = sig
        square = square + gated * gated
        cross = cross + gated * (dn_in[:, lanes] * gain[0:1, lanes])
    scale = lax.rsqrt(jnp.sum(square, axis=1, keepdims=True) * (1.0 / width) + EPS)
    pull = scale * scale * scale * (jnp.sum(cross, axis=1, keepdims=True) * (1.0 / width))
    dc = jnp.zeros((rows, n_state), f32)
    for block in range(width // (2 * HEAD_DIM)):
        lanes = slice(block * 2 * HEAD_DIM, (block + 1) * 2 * HEAD_DIM)
        gated = gated_s[:, lanes]
        sig = sig_s[:, lanes]
        silu = z_in[:, lanes].astype(f32) * sig
        dn = dn_in[:, lanes]
        hat = gated * scale
        norm_out[:, lanes] = (hat * gain[0:1, lanes]).astype(bf16)
        part = dn * hat
        total = part[0:8, :]
        for at in range(8, rows, 8):
            total = total + part[at : at + 8, :]
        dg_out[:, lanes] += total
        d_gated = scale * (dn * gain[0:1, lanes]) - gated * pull
        dy = (d_gated * silu).astype(bf16)
        dy_out[:, lanes] = dy
        mo = mo_s[:, lanes].astype(f32)
        dz_out[:, lanes] = (d_gated * mo * (sig + silu * (1.0 - sig))).astype(bf16)
        weighted = (dy.astype(f32) * entering(block)).astype(bf16)
        ds_acc[:, lanes] += mm(ct[...], weighted)
        dc = dc + mm_nt(weighted, state[:, lanes])
    dc_out[...] = dc

    @pl.when(step == pl.num_programs(0) - 1)
    def _():
        ds_out[...] = ds_acc[...].astype(bf16)


def inside_kernel(
    x_in, flags, seg_row, spreads, cum, sums_row, bc, ct, dy, dxs_out, db_out, dc_out, score, pair,
    apart, weights, xs, crossed
):
    length = dxs_out.shape[0]
    n_state = ct.shape[0]
    group = pl.program_id(0)
    big = weights.shape[2] // GROUP

    @pl.when(group == 0)
    def _():
        pair[...] = jnp.zeros_like(pair)
        weights[...] = jnp.zeros_like(weights)
        scored(lambda rows: bc[rows, :n_state], ct, flags, seg_row, score, False)

    lanes = head_lanes(group)
    for start in range(0, length, TILE):
        rows = pl.ds(start, TILE)
        scaled = x_in[rows, :].astype(f32) * mm(spreads[0, rows, :], lanes)
        for head, value in enumerate(by_head(scaled)):
            xs[head, rows, :] = value.astype(bf16)
        for head, value in enumerate(by_head(dy[rows, :].astype(f32))):
            apart[start // big, pl.ds(head * big + start % big, TILE), :] = value.astype(bf16)
    for head in range(GROUP):
        for at in range(0, length, big):
            end = at + big
            crossed[head % 2, :end, at:end] = mm_nt(xs[head, :end, :], dy[at:end, :])
        for start in range(0, length, TILE):
            rows = pl.ds(start, TILE)
            for at in range(start // big * big, length, big):
                first = max(at, start)
                end = at + big
                gap = sums_row[0, head : head + 1, first:end] - cum[0, rows, head : head + 1]
                decay = jnp.exp(jnp.minimum(gap, 0.0))
                weight = (decay * score[rows, first:end]).astype(bf16)
                weights[at // big, rows, head * big + first - at : (head + 1) * big] = weight
                pair[rows, first:end] += decay * crossed[head % 2, rows, first:end]
    for at in range(length - big, -1, -big):
        end = at + big
        part = mm(weights[at // big, :end, :], apart[at // big])
        if end == length:
            dxs_out[...] = part
        else:
            dxs_out[:end, :] += part

    @pl.when(group == pl.num_programs(0) - 1)
    def _():
        for start in range(0, length, TILE):
            rows = pl.ds(start, TILE)
            here = lax.broadcasted_iota(jnp.int32, (TILE, length), 0) + start
            there = lax.broadcasted_iota(jnp.int32, (TILE, length), 1)
            seen = (flags[rows, 6:7] == seg_row[0:1, :]) & (here <= there)
            part = jnp.where(seen, pair[rows, :], 0.0).astype(bf16)
            db_out[rows, :] = mm(part, bc[:, n_state:])
            if start == 0:
                dc_out[...] = mm_tn(part, bc[rows, :n_state])
            else:
                dc_out[...] += mm_tn(part, bc[rows, :n_state])


def split_mm(value, chosen):
    high, low = two_parts(value)
    return mm(high, chosen) + mm(low, chosen)


def outside_kernel(first_group, count, final, running, *refs):
    (raw, raw_bc, taps, masks, spreads, heads, rates, bc, dy, ssm, dxs_in, d_state, state, db_in,
     dc_in, dc_more, *started, d_out, first_out, last_out, sums_out,
     head_out, db_acc, found, totals_s, wide, d_pre) = refs
    length = d_out.shape[0]
    n_state = bc.shape[1] // 2
    step = pl.program_id(0)
    bc_step = count

    @pl.when(step == 0)
    def _():
        for at, ref in enumerate((db_acc, found, totals_s)):
            ref[...] = started[at][...] if running else jnp.zeros_like(ref)

    d_pre[pl.ds(length, HALO), :] = jnp.zeros((HALO, d_pre.shape[1]), f32)
    zero = jnp.zeros((1, d_pre.shape[1]), f32)

    @pl.when(step < bc_step)
    def _():
        wide[...] = raw[...].astype(f32)
        skip_sum, keep_sum = (zero, zero)
        ds = d_state[...]
        group = step + first_group
        lanes = head_lanes(group)
        owner = lax.broadcasted_iota(jnp.int32, (WIDE, TILE), 0) // HEAD_DIM + GROUP * group
        chosen = (owner == lax.broadcasted_iota(jnp.int32, (WIDE, TILE), 1)).astype(f32)
        chosen_b = chosen.astype(bf16)
        for start in range(0, length, TILE):
            rows = pl.ds(start, TILE)
            pre = conv_rows(wide, taps, masks, start, TILE)
            sig = sigmoid(pre)
            x = pre * sig
            stepped = mm(spreads[0, rows, :], lanes)
            scaled = (x.astype(bf16).astype(f32) * stepped).astype(bf16)
            keep = mm(spreads[1, rows, :], lanes)
            carried = keep * mm(bc[rows, :n_state], ds)
            dxs = dxs_in[rows, :] + carried
            scaled = scaled.astype(f32)
            db_acc[rows, :] += mm_nt((scaled * keep).astype(bf16), ds)
            grad = dy[rows, :].astype(f32)
            keep_sum = keep_sum + jnp.sum(scaled * carried, 0, keepdims=True)
            skip_sum = skip_sum + jnp.sum(grad * x, 0, keepdims=True)
            found[0, rows, :] += split_mm(grad * ssm[rows, :] - scaled * dxs, chosen_b)
            found[1, rows, :] += split_mm(x * dxs, chosen_b)
            d_x = taps[5:6, :] * grad + stepped * dxs
            d_pre[rows, :] = d_x * (sig + x * (1.0 - sig))
        met = jnp.sum(ds.astype(f32) * state[...].astype(f32), 0, keepdims=True)
        rest = jnp.zeros((5, WIDE), f32)
        totals_s[...] += lax.dot_general(
            jnp.concatenate([skip_sum, keep_sum, met, rest], 0),
            chosen,
            (((1,), (0,)), ((), ())),
            precision=HIGH,
            preferred_element_type=f32,
        )

    if final:

        @pl.when(step == bc_step)
        def _():
            wide[...] = raw_bc[...].astype(f32)
            for start in range(0, length, TILE):
                rows = pl.ds(start, TILE)
                pre = conv_rows(wide, taps, masks, start, TILE)
                sig = sigmoid(pre)
                slope = sig + pre * sig * (1.0 - sig)
                d_b = db_in[rows, :] + db_acc[rows, :]
                d_c = dc_in[rows, :] + dc_more[rows, :]
                d_pre[rows, :] = jnp.concatenate([d_b, d_c], 1) * slope

    @pl.when(step <= bc_step)
    def _():
        totals = [zero] * (CONV + 1)
        for start in range(0, length, TILE):
            rows = pl.ds(start, TILE)
            grad = d_pre[rows, :]
            totals[CONV] = totals[CONV] + jnp.sum(grad, 0, keepdims=True)
            here = wide[pl.ds(HALO + start, TILE), :]
            totals[CONV - 1] = totals[CONV - 1] + jnp.sum(grad * here, 0, keepdims=True)
            back = taps[CONV - 1 : CONV, :] * grad
            for tap in range(CONV - 1):
                shifted = wide[pl.ds(HALO - CONV + 1 + tap + start, TILE), :]
                masked = grad * twice(masks[tap, rows, :])
                totals[tap] = totals[tap] + jnp.sum(masked * shifted, 0, keepdims=True)
                ahead = d_pre[pl.ds(start + CONV - 1 - tap, TILE), :]
                back = back + taps[tap : tap + 1, :] * ahead * twice(masks[3 + tap, rows, :])
            d_out[rows, :] = back.astype(bf16)
            if start + TILE == length:
                last_out[...] = back[TILE - HALO :, :]
        first_out[...] = d_pre[pl.ds(0, HALO), :]
        for tap in range(CONV + 1):
            sums_out[tap : tap + 1, :] = totals[tap]
        sums_out[CONV + 1 : 8, :] = jnp.zeros((7 - CONV, d_pre.shape[1]), f32)

    if not final:
        head_out[...] = jnp.zeros_like(head_out)
        return

    @pl.when(step == bc_step + 1)
    def _():
        first_out[...] = jnp.zeros_like(first_out)
        last_out[...] = jnp.zeros_like(last_out)
        sums_out[...] = jnp.zeros_like(sums_out)
        rate = jnp.exp(rates[1:2, :])
        end = totals_s[1:2, :] + heads[3, pl.ds(length - 1, 1), :] * totals_s[2:3, :]
        here = lax.broadcasted_iota(jnp.int32, (length, length), 0)
        there = lax.broadcasted_iota(jnp.int32, (length, length), 1)
        upper = jnp.where(here <= there, 1.0, 0.0)
        d_log = lax.dot_general(
            upper, found[0], (((1,), (0,)), ((), ())), precision=HIGH, preferred_element_type=f32
        )
        d_log = d_log + end
        d_dt = (found[1] - rate * d_log) * heads[4]
        d_out[:, :TILE] = d_dt.astype(bf16)
        d_out[:, TILE:] = jnp.zeros((length, WIDE - TILE), bf16)
        head_out[0:1, :] = jnp.sum(d_dt, 0, keepdims=True)
        head_out[1:2, :] = jnp.sum(d_log * (-heads[1] * rate), 0, keepdims=True)
        head_out[2:3, :] = totals_s[0:1, :]
        head_out[3:8, :] = jnp.zeros((5, TILE), f32)


def pack_kernel(sizes, sums, gain_in, gain_out, head, out):
    devices = out.shape[0]
    gain_in = jnp.sum(gain_in[...], 0, keepdims=True)
    wide, channels, inner, heads = sizes
    gains = jnp.sum(gain_out[...], 0, keepdims=True)
    for at in range(devices):
        pieces = [gain_in[:, at * wide : (at + 1) * wide]]
        for tap in range(CONV + 1):
            pieces.append(sums[tap : tap + 1, at * channels : (at + 1) * channels])
        pieces.append(gains[:, at * inner : (at + 1) * inner])
        for row in range(3):
            pieces.append(head[row : row + 1, :heads])
        begin = 0
        for piece in pieces:
            out[at, :, begin : begin + piece.shape[1]] = piece
            begin += piece.shape[1]
        if begin < out.shape[2]:
            out[at, :, begin:] = jnp.zeros((1, out.shape[2] - begin), f32)


def scan_kernel(backward, place, mine, decay, out, wide):
    count = mine.shape[0]
    columns = out.shape[2]
    for at in range(2):
        for device in range(count):
            wide[at, device : device + 1, :] = decay[device, at : at + 1, :].astype(f32)
    lane = lax.broadcasted_iota(jnp.int32, (TILE, columns), 0)
    owner = lax.broadcasted_iota(jnp.int32, (TILE, columns), 1) // HEAD_DIM + place[0]
    chosen = jnp.where(lane == owner, 1.0, 0.0).astype(bf16)
    factor = mm(wide[0].astype(bf16), chosen) + mm(wide[1].astype(bf16), chosen)
    state = jnp.zeros(out.shape[1:], f32)
    for at in reversed(range(count)) if backward else range(count):
        out[at] = state.astype(bf16)
        state = factor[at : at + 1, :] * state + mine[at, :, :columns].astype(f32)


def to_slices(value, devices):
    n_state, inner = value.shape
    across = max(1, devices // 16)
    rows = n_state * across // devices
    value = value.reshape(n_state // rows, rows, across, inner // across)
    return value.transpose(0, 2, 1, 3).reshape(devices, rows, inner // across)


def from_slices(slices, n_state, inner):
    devices, rows, columns = slices.shape
    value = slices.reshape(n_state // rows, inner // columns, rows, columns)
    return value.transpose(0, 2, 1, 3).reshape(n_state, inner)


def exchange(slices):
    return lax.all_to_all(slices, ALL, split_axis=0, concat_axis=0, tiled=True)


def return_slices(states, n_state, inner):
    return from_slices(exchange(states), n_state, inner)


def with_decay(slices, end):
    devices, rows, _ = slices.shape
    more = jnp.pad(jnp.stack(end), ((0, rows - 2), (0, 0)))
    return jnp.concatenate([slices, jnp.broadcast_to(more[None], (devices, rows, TILE))], 2)


def scan_devices(mine, decay, columns, me, backward):
    devices, rows, _ = mine.shape
    across = max(1, devices // 16)
    place = jnp.reshape((me % across) * (columns // HEAD_DIM), (1,)).astype(jnp.int32)
    vmem = pl.BlockSpec(memory_space=pltpu.VMEM)
    return pl.pallas_call(
        lambda *refs: scan_kernel(backward, *refs),
        in_specs=[pl.BlockSpec(memory_space=pltpu.SMEM), vmem, vmem],
        out_specs=vmem,
        out_shape=jax.ShapeDtypeStruct((devices, rows, columns), bf16),
        scratch_shapes=[pltpu.VMEM((2, devices, TILE), f32)],
        compiler_params=pltpu.CompilerParams(vmem_limit_bytes=40 * 1024 * 1024),
        cost_estimate=CHEAP,
        name="scan_backward" if backward else "scan_forward",
    )(place, mine, decay)


def flip(axis, bit):
    count = lax.axis_size(axis)
    return [(i, i ^ bit) for i in range(count)]


def other_core(value):
    return lax.ppermute(value, "shard", flip("shard", 1))


class Gather:
    def __init__(self, own, other, base, half, chunks, *wait):
        self.own, self.other, self.base, self.half, self.chunks = (own, other, base, half, chunks)
        self.mine = lax.axis_index("seq") % 2
        self.size = half // chunks
        self.direct, self.passed = ([None] * chunks, [None] * chunks)
        self.parts = [None] * chunks
        for chunk in range(chunks):
            start = base + self.mine * half + chunk * self.size
            self.send = lax.dynamic_slice_in_dim(own, start, self.size, 0)
            if chunk:
                wait = (self.direct[chunk - 1],)
            if wait:
                self.send = after(self.send, *wait)
            self.direct[chunk] = lax.ppermute(self.send, "shard", flip("shard", 2))

    def share(self, *wait):
        for chunk in range(self.chunks):
            if chunk:
                wait = (self.passed[chunk - 1],)
            if wait:
                self.direct[chunk] = after(self.direct[chunk], *wait)
            self.passed[chunk] = lax.ppermute(self.direct[chunk], "seq", flip("seq", 1))

    def cross(self, *wait):
        for chunk in range(self.chunks):
            direct, passed = (self.direct[chunk], self.passed[chunk])
            if wait:
                direct, passed = lax.optimization_barrier((direct, passed) + wait)[:2]
            self.parts[chunk] = [direct, other_core(direct), passed, other_core(passed)]

    def turns(self):
        shard = lax.axis_index("shard")
        return [shard, shard ^ 1, shard ^ 2, shard ^ 3]


def project_kernel(table, *refs):
    lefts, (own, other, direct, direct_o, passed, passed_o) = (refs[:4], refs[4:10])
    out, left, weight = refs[-3:]
    step = pl.program_id(0)

    @pl.when(step == 0)
    def _():
        left[...] = jnp.concatenate([a[...] for a in lefts], 1)

    def fill(far, far_o):
        deep = own.shape[1]
        weight[:, :deep] = far[...]
        weight[:, deep:] = far_o[...]

    near = pl.num_programs(0) // 2
    pl.when(step < near)(lambda: fill(direct, direct_o))
    pl.when(step >= near)(lambda: fill(passed, passed_o))
    whole = jnp.concatenate([own[...], other[...], weight[...]], 1)
    out[...] = mm_nt(left[...], whole).astype(bf16)


def project(value, gather, chunk, result):
    rows = value.shape[0]
    deep = gather.own.shape[1]
    near = gather.size // PIECE
    first = chunk * near
    full = gather.half // PIECE
    base = gather.base // PIECE
    order = [full * gather.mine + first + at for at in range(near)]
    order += [full * (1 - gather.mine) + first + at for at in range(near)]
    table = jnp.stack(gather.turns() + order).astype(jnp.int32)
    block = lambda index: pl.BlockSpec((PIECE, deep), index)
    left = lambda k: pl.BlockSpec((rows, deep), lambda j, t: (0, t[k]))
    own = block(lambda j, t: (base + t[4 + j], 0))
    one = block(lambda j, t: (jnp.minimum(j, near - 1), 0))
    two = block(lambda j, t: (jnp.maximum(j - near, 0), 0))
    operands = [table, *([value] * 4), gather.own, gather.other, *gather.parts[chunk]]
    in_specs = [left(k) for k in range(4)] + [own, own, one, one, two, two]
    aliases = {}
    if result is not None:
        aliases = {len(operands): 0}
        operands.append(result)
        in_specs.append(pl.BlockSpec(memory_space=pl.ANY))
    return pl.pallas_call(
        project_kernel,
        grid_spec=pltpu.PrefetchScalarGridSpec(
            num_scalar_prefetch=1,
            grid=(2 * near,),
            in_specs=in_specs,
            out_specs=pl.BlockSpec((rows, PIECE), lambda j, t: (0, t[4 + j])),
            scratch_shapes=[
                pltpu.VMEM((rows, 4 * deep), bf16),
                pltpu.VMEM((PIECE, 2 * deep), bf16),
            ],
        ),
        out_shape=jax.ShapeDtypeStruct((rows, 2 * gather.half), bf16),
        input_output_aliases=aliases,
        compiler_params=pltpu.CompilerParams(vmem_limit_bytes=58 * 1024 * 1024),
        cost_estimate=CHEAP,
        name="project",
    )(*operands)


def back_kernel(values, chunks, norm, table, *refs):
    inputs, refs = (refs[:values], refs[values:])
    own, other = refs[:2]
    far, refs = (refs[2 : 2 + 4 * chunks], refs[2 + 4 * chunks :])
    total, value, weight = refs[-3:]
    refs = refs[:-3]
    if norm:
        hidden, cotangent, gain, out, gain_out = refs[-5:]
        start = refs[:-5]
    else:
        out, start = (refs[-1], refs[:-1])
    step = pl.program_id(0)
    last = pl.num_programs(0) - 1
    deep = own.shape[1]
    place = lambda k: pl.ds(pl.multiple_of(table[k] * deep, deep), deep)

    @pl.when(step == 0)
    def _():
        if start:
            for k in range(4):
                total[:, k * deep : (k + 1) * deep] = start[0][:, place(k)]
        else:
            total[...] = jnp.zeros_like(total)

    for at in range(values):

        @pl.when((step * values // (last + 1)) == at)
        def _(at=at):
            value[...] = inputs[at][...]

    for at in range(2 * chunks):

        @pl.when(table[4 + step] == at)
        def _(at=at):
            weight[:, :deep] = far[2 * at][...]
            weight[:, deep:] = far[2 * at + 1][...]

    total[...] += mm(value[...], jnp.concatenate([own[...], other[...], weight[...]], 1))

    @pl.when(step == last)
    def _():
        for k in range(4):
            out[:, place(k)] = total[:, k * deep : (k + 1) * deep]
        if norm:
            sums = jnp.zeros(gain_out.shape, f32)
            for at in range(0, out.shape[0], 64):
                rows = pl.ds(at, 64)
                base = hidden[rows, :].astype(f32)
                grad = out[rows, :]
                size = 1.0 / base.shape[1]
                scale = lax.rsqrt(jnp.sum(base * base, 1, keepdims=True) * size + EPS)
                hat = base * scale
                part = grad * hat
                for row in range(0, 64, 8):
                    sums = sums + part[row : row + 8, :]
                pull = jnp.sum(part * gain[...], 1, keepdims=True) * size
                inner = scale * (grad * gain[...] - hat * pull)
                out[rows, :] = cotangent[rows, :].astype(f32) + inner
            gain_out[...] = sums


def back(values, gather, start, norm=()):
    rows = values[0].shape[0]
    deep = gather.own.shape[1]
    count = 2 * gather.half // PIECE
    share = count // len(values)
    near = gather.half // PIECE
    each = near // gather.chunks
    base = gather.base // PIECE
    mine = gather.mine
    source, block = ([], [])
    for at in range(count):
        half, place = (at // near, at % near)
        source.append(2 * (place // each) + jnp.where(mine == half, 0, 1))
        block.append(place % each)
    table = jnp.stack([jnp.asarray(v, jnp.int32) for v in gather.turns() + source + block])
    whole = pl.BlockSpec((rows, 4 * deep), lambda j, t: (0, 0))
    own = pl.BlockSpec((PIECE, deep), lambda j, t: (base + j, 0))
    far = pl.BlockSpec((PIECE, deep), lambda j, t: (t[4 + count + j], 0))
    in_specs = [
        pl.BlockSpec((rows, PIECE), lambda j, t, k=k: (0, jnp.clip(j - k * share, 0, share - 1)))
        for k in range(len(values))
    ]
    started = [] if start is None else [start]
    parts = [piece for chunk in gather.parts for piece in chunk]
    in_specs += [own, own] + [far] * len(parts) + [whole] * len(started)
    out_specs, out_shape = (whole, jax.ShapeDtypeStruct((rows, 4 * deep), f32))
    if norm:
        narrow = lambda count: pl.BlockSpec((count, 4 * deep), lambda j, t: (0, 0))
        in_specs += [whole, whole, narrow(1)]
        out_specs = [whole, narrow(8)]
        out_shape = [out_shape, jax.ShapeDtypeStruct((8, 4 * deep), f32)]
    return pl.pallas_call(
        lambda *refs: back_kernel(len(values), gather.chunks, len(norm) > 0, *refs),
        grid_spec=pltpu.PrefetchScalarGridSpec(
            num_scalar_prefetch=1,
            grid=(count,),
            in_specs=in_specs,
            out_specs=out_specs,
            scratch_shapes=[
                pltpu.VMEM((rows, 4 * deep), f32),
                pltpu.VMEM((rows, PIECE), bf16),
                pltpu.VMEM((PIECE, 2 * deep), bf16),
            ],
        ),
        out_shape=out_shape,
        compiler_params=pltpu.CompilerParams(vmem_limit_bytes=58 * 1024 * 1024),
        cost_estimate=CHEAP,
        name="back",
    )(table, *values, gather.own, gather.other, *parts, *started, *norm)


def by_shard(gather):
    half, width = (gather.half, gather.own.shape[1])
    whole = pl.BlockSpec((2 * half, width), lambda g, t: (0, 0))
    part = pl.BlockSpec((half, width), lambda g, t: (0, 0))
    direct, direct_o, passed, passed_o = gather.parts[0]
    operands = [gather.own, gather.other, direct, passed, direct_o, passed_o]
    table = jnp.stack(gather.turns() + [gather.mine]).astype(jnp.int32)
    return operands, [whole] * 2 + [part] * 4, table


def out_back_kernel(table, value, own, other, direct, passed, direct_o, passed_o, out):
    step = pl.program_id(0)
    half = direct.shape[0]

    def two(near, far):
        out[:, pl.ds(pl.multiple_of(table[4] * half, half), half)] = mm_nt(value[...], near[...])
        far_at = pl.multiple_of((1 - table[4]) * half, half)
        out[:, pl.ds(far_at, half)] = mm_nt(value[...], far[...])

    for at, piece in enumerate((own, other)):

        @pl.when(step == at)
        def _(piece=piece):
            out[...] = mm_nt(value[...], piece[...])

    pl.when(step == 2)(lambda: two(direct, passed))
    pl.when(step == 3)(lambda: two(direct_o, passed_o))


def out_back(value, gather):
    rows, width = value.shape
    operands, specs, table = by_shard(gather)
    size = 2 * gather.half
    return pl.pallas_call(
        out_back_kernel,
        grid_spec=pltpu.PrefetchScalarGridSpec(
            num_scalar_prefetch=1,
            grid=(4,),
            in_specs=[pl.BlockSpec((rows, width), lambda g, t: (0, 0))] + specs,
            out_specs=pl.BlockSpec((rows, size), lambda g, t: (0, t[g])),
        ),
        out_shape=jax.ShapeDtypeStruct((rows, 4 * size), f32),
        compiler_params=pltpu.CompilerParams(vmem_limit_bytes=58 * 1024 * 1024),
        cost_estimate=CHEAP,
        name="out_back",
    )(table, value, *operands)


def out_forward_kernel(table, value, base, own, other, direct, passed, direct_o, passed_o, out, total):
    step = pl.program_id(0)
    half = direct.shape[0]

    def two(near, far):
        near_at = pl.multiple_of(table[4] * half, half)
        far_at = pl.multiple_of((1 - table[4]) * half, half)
        total[...] += mm(value[:, pl.ds(near_at, half)], near[...])
        total[...] += mm(value[:, pl.ds(far_at, half)], far[...])

    @pl.when(step == 0)
    def _():
        total[...] = base[...].astype(f32) + mm(value[...], own[...])

    @pl.when(step == 1)
    def _():
        total[...] += mm(value[...], other[...])

    pl.when(step == 2)(lambda: two(direct, passed))

    @pl.when(step == 3)
    def _():
        two(direct_o, passed_o)
        out[...] = total[...].astype(bf16)


def out_forward(value, base, gather):
    rows = value.shape[0]
    operands, specs, table = by_shard(gather)
    size = 2 * gather.half
    width = gather.own.shape[1]
    fixed = pl.BlockSpec((rows, width), lambda g, t: (0, 0))
    return pl.pallas_call(
        out_forward_kernel,
        grid_spec=pltpu.PrefetchScalarGridSpec(
            num_scalar_prefetch=1,
            grid=(4,),
            in_specs=[pl.BlockSpec((rows, size), lambda g, t: (0, t[g])), fixed] + specs,
            out_specs=fixed,
            scratch_shapes=[pltpu.VMEM((rows, width), f32)],
        ),
        out_shape=jax.ShapeDtypeStruct((rows, width), bf16),
        compiler_params=pltpu.CompilerParams(vmem_limit_bytes=58 * 1024 * 1024),
        cost_estimate=CHEAP,
        name="out_forward",
    )(table, value, base, *operands)


def stacked_project_kernel(value, *rest):
    weight = jnp.concatenate([w[...] for w in rest[:-1]], 1)
    rest[-1][...] = mm_nt(value[...], weight).astype(bf16)


def stacked_project(value, stack, base, count):
    rows = value.shape[0]
    shards, _, deep = stack.shape
    first = base // WIDE
    specs = [
        pl.BlockSpec((None, WIDE, deep), lambda j, k=k: (k, first + j, 0)) for k in range(shards)
    ]
    return pl.pallas_call(
        stacked_project_kernel,
        grid=(count // WIDE,),
        in_specs=[pl.BlockSpec((rows, shards * deep), lambda j: (0, 0))] + specs,
        out_specs=pl.BlockSpec((rows, WIDE), lambda j: (0, j)),
        out_shape=jax.ShapeDtypeStruct((rows, count), bf16),
        compiler_params=pltpu.CompilerParams(vmem_limit_bytes=58 * 1024 * 1024),
        cost_estimate=CHEAP,
        name="stacked_project",
    )(value, *([stack] * shards))


def stacked_back_kernel(value, *rest):
    out, total = rest[-2:]
    step = pl.program_id(0)

    @pl.when(step == 0)
    def _():
        total[...] = jnp.zeros_like(total)

    weight = jnp.concatenate([w[...] for w in rest[:-2]], 1)
    total[...] += mm(value[...], weight)

    @pl.when(step == pl.num_programs(0) - 1)
    def _():
        out[...] = total[...]


def stacked_back(value, stack, base):
    rows, count = value.shape
    shards, _, deep = stack.shape
    size = WIDE
    first = base // size
    specs = [
        pl.BlockSpec((None, size, deep), lambda j, k=k: (k, first + j, 0)) for k in range(shards)
    ]
    return pl.pallas_call(
        stacked_back_kernel,
        grid=(count // size,),
        in_specs=[pl.BlockSpec((rows, size), lambda j: (0, j))] + specs,
        out_specs=pl.BlockSpec((rows, shards * deep), lambda j: (0, 0)),
        out_shape=jax.ShapeDtypeStruct((rows, shards * deep), f32),
        scratch_shapes=[pltpu.VMEM((rows, shards * deep), f32)],
        compiler_params=pltpu.CompilerParams(vmem_limit_bytes=58 * 1024 * 1024),
        cost_estimate=CHEAP,
        name="stacked_back",
    )(value, *([stack] * shards))


def halve(value, dim, axis, bit, mine, wait):
    shape = value.shape
    value = value.reshape(shape[:dim] + (shape[dim] // 2, 2) + shape[dim + 1 :])
    send = lax.dynamic_index_in_dim(value, 1 - mine, dim + 1, False)
    kept = lax.dynamic_index_in_dim(value, mine, dim + 1, False)
    came = lax.ppermute(send, axis, flip(axis, bit))
    if wait:
        came = after(came, *wait)
    return (kept.astype(f32) + came.astype(f32)).astype(bf16), send


class RowSum:
    def __init__(self, partial, far_first):
        shards, places = (lax.axis_size("shard"), lax.axis_size("seq"))
        shard, place = (lax.axis_index("shard"), lax.axis_index("seq"))
        rows, columns = partial.shape
        chips = shards // 2
        self.value = partial.reshape(chips, places, rows // (chips * places), columns)
        far = [(0, "shard", 2 << k, (shard >> (k + 1)) & 1) for k in range(chips.bit_length() - 1)]
        near = [(1, "seq", 1 << k, (place >> k) & 1) for k in range(places.bit_length() - 1)]
        self.order = far + near if far_first else near[:1] + far + near[1:]

    def step(self, *wait):
        if not self.order:
            return
        dim, axis, bit, mine = self.order.pop(0)
        self.value, self.send = halve(self.value, dim, axis, bit, mine, wait)

    def rows(self):
        return self.value.reshape(self.value.shape[2:])


def core_rows(value, core):
    shards = lax.axis_size("shard")
    size = value.shape[1] // shards
    even = [value[:, at * size : (at + 1) * size] for at in range(0, shards, 2)]
    odd = [value[:, at * size : (at + 1) * size] for at in range(1, shards, 2)]
    own = [jnp.where(core == 0, a, b) for a, b in zip(even, odd)]
    rest = [jnp.where(core == 0, b, a) for a, b in zip(even, odd)]
    return jnp.concatenate(own, 1), jnp.concatenate(rest, 1)


def after(value, *others):
    return lax.optimization_barrier((value,) + others)[0]


def turn_blocks(value, shard):
    shards = lax.axis_size("shard")
    size = value.shape[1] // shards
    blocks = [
        lax.dynamic_slice_in_dim(value, (at ^ shard) * size, size, 1) for at in range(shards)
    ]
    return jnp.concatenate(blocks, 1)


def on_device(
    hidden,
    cotangent,
    seg_ids,
    norm_gain,
    in_weight,
    conv_weight,
    conv_bias,
    dt_bias,
    a_log,
    d_skip,
    out_gain,
    out_weight,
):
    shards, places = (lax.axis_size("shard"), lax.axis_size("seq"))
    shard, place = (lax.axis_index("shard"), lax.axis_index("seq"))
    devices = shards * places
    me = shard * places + place
    length, width = hidden.shape
    heads = dt_bias.shape[0]
    inner = out_weight.shape[0] * shards
    channels = conv_bias.shape[0] * shards
    n_state = (channels - inner) // 2
    groups = inner // WIDE
    start = me * length

    core = shard % 2
    w_in = in_weight.T
    by_hand = shards == 4 and places % 2 == 0
    edge_rows = w_in.shape[0] - 2 * inner
    small = jnp.concatenate([norm_gain, conv_weight.reshape(-1), conv_bias, out_gain])
    small_rows = pl.cdiv(small.shape[0], w_in.shape[1])
    small_rows += -(small_rows + edge_rows) % 16
    small = jnp.pad(small, (0, small_rows * w_in.shape[1] - small.shape[0]))
    edges = jnp.concatenate([w_in[2 * inner :], small.reshape(small_rows, w_in.shape[1])], 0)
    if by_hand:
        in_other = other_core(w_in)
        g_x = Gather(w_in, in_other, inner, inner // 2, 2, edges)
        edge_far = lax.ppermute(edges, "shard", flip("shard", 2))
        g_z = Gather(w_in, in_other, 0, inner // 2, 1, g_x.direct[1])
        pieces = [edges, other_core(edges), edge_far, other_core(edge_far)]
        edges = jnp.stack([after(piece, g_x.send) for piece in pieces])
        edges = jnp.stack([lax.dynamic_index_in_dim(edges, k ^ shard, 0, False) for k in range(4)])
    else:
        edges = lax.all_gather(edges, "shard")
    if by_hand:
        g_x.share()
        g_x.cross()
        out_other = other_core(after(out_weight, g_x.direct[0]))
    else:
        stack_x = lax.all_gather(w_in[inner : 2 * inner], "shard")
        stack_z = lax.all_gather(w_in[:inner], "shard")
        w_out = lax.all_gather(out_weight, "shard", axis=0, tiled=True)
    w_edge = edges[:, :edge_rows].transpose(1, 0, 2).reshape(edge_rows, width)
    w_edge = jnp.pad(w_edge, ((0, -edge_rows % TILE), (0, 0)))
    small = edges[:, edge_rows:].reshape(shards, -1)
    at = 0
    gain_in = small[:, at : at + norm_gain.shape[0]].reshape(-1).astype(f32)
    at += norm_gain.shape[0]
    taps = small[:, at : at + conv_weight.size].reshape(shards, CONV, -1)
    taps = taps.transpose(1, 0, 2).reshape(CONV, channels).astype(f32)
    at += conv_weight.size
    bias = small[:, at : at + conv_bias.shape[0]].reshape(-1).astype(f32)
    at += conv_bias.shape[0]
    gain_out = small[:, at : at + out_gain.shape[0]].reshape(-1).astype(f32)
    skip_wide = jnp.repeat(d_skip.astype(f32), HEAD_DIM)
    rows = jnp.concatenate([skip_wide, jnp.zeros((channels - inner,), f32)])
    taps8 = jnp.concatenate([taps, bias[None], rows[None], jnp.zeros((2, channels), f32)], 0)

    edge = jnp.full((HALO,), -1, jnp.int32)
    padded = jnp.concatenate([edge, seg_ids, edge - 1])
    near = lax.dynamic_slice_in_dim(padded, start, length + 2 * HALO)
    seg = near[HALO : HALO + length]
    fwd_masks = [near[HALO - CONV + 1 + k : HALO - CONV + 1 + k + length] == seg for k in range(3)]
    spot = jnp.arange(length, dtype=jnp.int32)
    bwd_masks = [
        (near[HALO + CONV - 1 - k : HALO + CONV - 1 - k + length] == seg)
        & (spot + CONV - 1 - k < length)
        for k in range(3)
    ]
    from_before = seg == near[HALO - 1]
    to_last = seg == seg[length - 1]
    flags = jnp.stack(
        [m.astype(f32) for m in fwd_masks + bwd_masks + [seg, from_before, to_last]], 1
    )
    flags = jnp.pad(flags, ((0, 0), (0, 16 - flags.shape[1])))
    seg_row = jnp.broadcast_to(seg.astype(f32)[None, :], (8, length))

    behind = lax.ppermute(
        hidden[length - HALO :], ALL, [(i, i + 1) for i in range(devices - 1)]
    )
    hidden_f = jnp.concatenate([behind, hidden], 0).astype(f32)
    scale_in = lax.rsqrt(jnp.mean(hidden_f * hidden_f, axis=1, keepdims=True) + EPS)
    normed_ext = (hidden_f * scale_in * gain_in[None, :]).astype(bf16)
    normed_in = normed_ext[HALO:]
    proj_edge = mm_nt(normed_ext, w_edge).astype(bf16)
    proj_bc = proj_edge[:, : 2 * n_state]
    rates = jnp.stack([dt_bias, a_log]).astype(f32)
    rates = jnp.pad(rates, ((0, 6), (0, TILE - heads)))
    big = pltpu.CompilerParams(vmem_limit_bytes=56 * 1024 * 1024)
    per_head, spreads, cum, sums_row, masks = pl.pallas_call(
        prepare_kernel,
        out_shape=[
            jax.ShapeDtypeStruct((5, length, TILE), f32),
            jax.ShapeDtypeStruct((2, length, 2 * TILE), bf16),
            jax.ShapeDtypeStruct((groups, length, GROUP), f32),
            jax.ShapeDtypeStruct((groups, GROUP, length), f32),
            jax.ShapeDtypeStruct((2 * (CONV - 1), length, TILE), f32),
        ],
        compiler_params=big,
        name="prepare",
    )(proj_edge[HALO:, 2 * n_state :], rates, flags)
    end = two_parts(per_head[3, length - 1])
    if by_hand:
        proj = project(after(normed_ext, per_head), g_x, 0, None)
        g_out = Gather(out_weight, out_other, 0, out_weight.shape[0] // 2, 1, proj, g_z.direct[0])
        g_z.share(proj)
        proj = project(normed_ext, g_x, 1, proj)
    else:
        proj = stacked_project(normed_ext, stack_x, 0, inner)

    def whole(shape):
        return pl.BlockSpec(shape, lambda g: (0,) * len(shape))

    def group_of(g):
        return jnp.maximum(g - 1, 0)

    order = lambda g: jnp.where(g == 0, groups, g - 1)
    x_conv, state_local, bc, bt, ct = pl.pallas_call(
        state_kernel,
        grid=(groups + 1,),
        in_specs=[
            pl.BlockSpec((length + HALO, WIDE), lambda g: (0, group_of(g))),
            whole((length + HALO, WIDE)),
            pl.BlockSpec((8, WIDE), lambda g: (0, order(g))),
            whole(masks.shape),
            whole(spreads.shape),
        ],
        out_specs=[
            pl.BlockSpec((length, WIDE), lambda g: (0, group_of(g))),
            pl.BlockSpec((n_state, WIDE), lambda g: (0, group_of(g))),
            whole((length, 2 * n_state)),
            whole((n_state, length)),
            whole((n_state, length)),
        ],
        out_shape=[
            jax.ShapeDtypeStruct((length, inner), bf16),
            jax.ShapeDtypeStruct((n_state, inner), bf16),
            jax.ShapeDtypeStruct((length, 2 * n_state), bf16),
            jax.ShapeDtypeStruct((n_state, length), bf16),
            jax.ShapeDtypeStruct((n_state, length), bf16),
        ],
        scratch_shapes=[
            pltpu.VMEM((length + HALO, WIDE), f32),
            pltpu.VMEM((n_state, length), bf16),
        ],
        compiler_params=big,
        cost_estimate=CHEAP,
        name="mixer_state",
    )(proj, proj_bc, taps8, masks, spreads)

    slices = with_decay(to_slices(state_local, devices), end)
    if by_hand:
        slices = after(slices, g_out.direct[0])
        g_out.share(slices)
        sent = exchange(slices)
        g_z.cross(slices)
        gate_z = project(after(normed_in, slices), g_z, 0, None)
        sent = after(sent, gate_z)
    else:
        sent = exchange(slices)
        gate_z = stacked_project(normed_in, stack_z, 0, inner)
    columns = slices.shape[2] - TILE
    decays = sent[:, :, columns:]
    states = scan_devices(sent, decays, columns, me, False)
    state_in = return_slices(states, n_state, inner)
    x_conv = after(x_conv, states)
    half_t = 2 * TILE
    y_local = pl.pallas_call(
        forward_kernel,
        grid=(groups,),
        in_specs=[
            pl.BlockSpec((length, WIDE), lambda g: (0, g)),
            whole(flags.shape),
            whole((8, length)),
            whole(spreads.shape),
            pl.BlockSpec((1, length, GROUP), lambda g: (g, 0, 0)),
            pl.BlockSpec((1, GROUP, length), lambda g: (g, 0, 0)),
            whole((length, 2 * n_state)),
            whole((n_state, length)),
        ],
        out_specs=pl.BlockSpec((length, WIDE), lambda g: (0, g)),
        out_shape=jax.ShapeDtypeStruct((length, inner), f32),
        scratch_shapes=[
            pltpu.VMEM((length, length), f32),
            pltpu.VMEM((length // half_t, GROUP * half_t, WIDE), bf16),
            pltpu.VMEM((length // half_t, length, GROUP * half_t), bf16),
        ],
        compiler_params=big,
        cost_estimate=CHEAP,
        name="mixer_forward",
    )(x_conv, flags, seg_row, spreads, cum, sums_row, bc, bt)
    if by_hand:
        g_out.cross(y_local)
        d_normed = out_back(after(cotangent, y_local), g_out)
    else:
        d_normed = mm_nt(cotangent, w_out)
    block = TILE
    tall = lambda dim: pl.BlockSpec((block, dim), lambda g: (g, 0))
    gains = jnp.stack([gain_out, skip_wide], 0)
    ssm, normed_out, d_z, d_y, d_state_local, dc_more, d_gain = pl.pallas_call(
        gate_kernel,
        grid=(length // block,),
        in_specs=[
            tall(inner),
            tall(inner),
            tall(inner),
            tall(inner),
            tall(2 * n_state),
            pl.BlockSpec((n_state, block), lambda g: (0, g)),
            pl.BlockSpec((None, block, TILE), lambda g: (3, g, 0)),
            whole((n_state, inner)),
            whole((2, inner)),
        ],
        out_specs=[
            tall(inner),
            tall(inner),
            tall(inner),
            tall(inner),
            whole((n_state, inner)),
            tall(n_state),
            whole((8, inner)),
        ],
        out_shape=[
            jax.ShapeDtypeStruct((length, inner), f32),
            jax.ShapeDtypeStruct((length, inner), bf16),
            jax.ShapeDtypeStruct((length, inner), bf16),
            jax.ShapeDtypeStruct((length, inner), bf16),
            jax.ShapeDtypeStruct((n_state, inner), bf16),
            jax.ShapeDtypeStruct((length, n_state), f32),
            jax.ShapeDtypeStruct((8, inner), f32),
        ],
        scratch_shapes=[
            pltpu.VMEM((block, inner), f32),
            pltpu.VMEM((block, inner), f32),
            pltpu.VMEM((block, inner), bf16),
            pltpu.VMEM((n_state, inner), f32),
        ],
        compiler_params=big,
        cost_estimate=CHEAP,
        name="mixer_gate",
    )(y_local, x_conv, gate_z, d_normed, bc, ct, per_head, state_in, gains)

    slices = to_slices(d_state_local, devices)
    sent = exchange(slices)
    normed_out, d_z = (after(normed_out, slices), after(d_z, slices))

    def both(value):
        return jnp.concatenate([value, other_core(value)], 0)

    def both_rows(value):
        own, rest = core_rows(value, core)
        return jnp.concatenate([own, other_core(rest)], 0)

    normed_pair = both_rows(normed_in)
    cot_pair = both(cotangent)
    out_pair = both_rows(normed_out)
    z_pair = both(d_z)
    if by_hand:
        block_out = out_forward(normed_out, hidden, g_out)
    else:
        block_out = (hidden.astype(f32) + mm(normed_out, w_out)).astype(bf16)
    grad_o = mm_tn(after(out_pair, block_out), cot_pair).astype(bf16)
    states = scan_devices(after(sent, grad_o), decays, columns, me, True)
    returned = exchange(states)
    grad_z = mm_tn(normed_pair, after(z_pair, states)).astype(bf16)
    x_conv = after(x_conv, grad_o, grad_z)

    dxs, db_in, dc_in = pl.pallas_call(
        inside_kernel,
        grid=(groups,),
        in_specs=[
            pl.BlockSpec((length, WIDE), lambda g: (0, g)),
            whole(flags.shape),
            whole((8, length)),
            whole(spreads.shape),
            pl.BlockSpec((1, length, GROUP), lambda g: (g, 0, 0)),
            pl.BlockSpec((1, GROUP, length), lambda g: (g, 0, 0)),
            whole((length, 2 * n_state)),
            whole((n_state, length)),
            pl.BlockSpec((length, WIDE), lambda g: (0, g)),
        ],
        out_specs=[
            pl.BlockSpec((length, WIDE), lambda g: (0, g)),
            whole((length, n_state)),
            whole((length, n_state)),
        ],
        out_shape=[
            jax.ShapeDtypeStruct((length, inner), f32),
            jax.ShapeDtypeStruct((length, n_state), f32),
            jax.ShapeDtypeStruct((length, n_state), f32),
        ],
        scratch_shapes=[
            pltpu.VMEM((length, length), f32),
            pltpu.VMEM((length, length), f32),
            pltpu.VMEM((length // half_t, GROUP * half_t, WIDE), bf16),
            pltpu.VMEM((length // half_t, length, GROUP * half_t), bf16),
            pltpu.VMEM((GROUP, length, WIDE), bf16),
            pltpu.VMEM((2, length, length), f32),
        ],
        compiler_params=big,
        cost_estimate=CHEAP,
        name="mixer_inside",
    )(x_conv, flags, seg_row, spreads, cum, sums_row, bc, ct, d_y)

    d_state = from_slices(after(returned, dxs), n_state, inner)
    grad_o, grad_z = lax.optimization_barrier((grad_o, grad_z, dxs))[:2]

    def halves(grad):
        half = grad.shape[1] // 2
        return [RowSum(grad[:, :half], True), RowSum(grad[:, half:], False)]

    def step(wait, *chains):
        for chain in chains:
            chain.step(wait)

    taps8 = jnp.pad(taps8, ((0, 0), (0, WIDE)))

    def outside(first_group, count, final, grad, running):
        kept = lambda g: jnp.minimum(g, count - 1) + first_group
        steps = count + (2 if final else 0)
        columns = steps * WIDE
        tall = lambda: pl.BlockSpec((length, WIDE), lambda g: (0, kept(g)))
        flat = lambda: pl.BlockSpec((n_state, WIDE), lambda g: (0, kept(g)))
        return pl.pallas_call(
            lambda *refs: outside_kernel(first_group, count, final, len(running) > 0, *refs),
            grid=(steps,),
            in_specs=[
                pl.BlockSpec((length + HALO, WIDE), lambda g: (0, kept(g))),
                whole((length + HALO, WIDE)),
                pl.BlockSpec((8, WIDE), lambda g: (0, first_group + g)),
                whole(masks.shape),
                whole(spreads.shape),
                whole(per_head.shape),
                whole(rates.shape),
                whole((length, 2 * n_state)),
                tall(),
                tall(),
                tall(),
                flat(),
                flat(),
                whole((length, n_state)),
                whole((length, n_state)),
                whole((length, n_state)),
                *[whole(value.shape) for value in running],
            ],
            out_specs=[
                pl.BlockSpec((length, WIDE), lambda g: (0, g)),
                pl.BlockSpec((HALO, WIDE), lambda g: (0, g)),
                pl.BlockSpec((HALO, WIDE), lambda g: (0, g)),
                pl.BlockSpec((8, WIDE), lambda g: (0, g)),
                whole((8, TILE)),
                whole((length, n_state)),
                whole((2, length, TILE)),
                whole((8, TILE)),
            ],
            out_shape=[
                jax.ShapeDtypeStruct((length, columns), bf16),
                jax.ShapeDtypeStruct((HALO, columns), f32),
                jax.ShapeDtypeStruct((HALO, columns), f32),
                jax.ShapeDtypeStruct((8, columns), f32),
                jax.ShapeDtypeStruct((8, TILE), f32),
                jax.ShapeDtypeStruct((length, n_state), f32),
                jax.ShapeDtypeStruct((2, length, TILE), f32),
                jax.ShapeDtypeStruct((8, TILE), f32),
            ],
            scratch_shapes=[
                pltpu.VMEM((length + HALO, WIDE), f32),
                pltpu.VMEM((length + HALO, WIDE), f32),
            ],
            compiler_params=big,
            cost_estimate=CHEAP,
            name="mixer_outside",
        )(proj, proj_bc, taps8, masks, spreads, per_head, rates, bc, grad, ssm, dxs, d_state,
          state_in, db_in, dc_in, dc_more, *running)

    seg_end = near[length : length + 2 * HALO]

    def finish(grads, first, last, start):
        ahead = lax.ppermute(first, ALL, [(i + 1, i) for i in range(devices - 1)])
        joined = jnp.concatenate([jnp.zeros_like(first), ahead], 0)
        for tap in range(CONV - 1):
            lead = CONV - 1 - tap
            same = (seg_end[lead : lead + HALO] == seg_end[:HALO]).astype(f32)[:, None]
            here = taps8[tap, start : start + first.shape[1]]
            last = last + here[None, :] * joined[lead : lead + HALO] * same
        count = min(channels - start, first.shape[1])
        return lax.dynamic_update_slice(grads, last[:, :count].astype(bf16), (length - HALO, 0))

    running = ()
    part = groups // 2
    half_x = part * WIDE

    values = lambda *chains: [chain.value for chain in chains]
    sums_o = halves(grad_o)
    d_one, first, last, sums_one, _, *running = outside(0, part, False, d_y, running)
    step(d_one, *sums_o)
    d_one = finish(d_one, first, last, 0)
    one_pair = both(d_one)
    if by_hand:
        d_normed_in = back([after(d_z, sums_one, *values(*sums_o))], g_z, None)
    else:
        d_normed_in = stacked_back(d_z, stack_z, 0)
    step(d_normed_in, *sums_o)
    sums_z = halves(after(grad_z, sums_one))
    grad_x = mm_tn(normed_pair, after(one_pair, d_normed_in)).astype(bf16)
    grad = after(d_y, grad_x, *values(*sums_o))
    d_two, first, last, sums_two, head_sums, *_ = outside(part, groups - part, True, grad, running)
    step(d_two, *sums_z, *sums_o)
    sum_a = RowSum(after(grad_x, d_two), True)
    sums = jnp.concatenate([sums_one, sums_two], 1)
    d_two = finish(d_two, first, last, half_x)
    two_pair = both(d_two)
    count = inner - half_x
    edge = d_two[:, count : count + w_edge.shape[0]]
    d_normed_in = d_normed_in + mm(edge, w_edge)
    grad_y = mm_tn(normed_pair, after(two_pair, d_normed_in, *values(*sums_z, *sums_o))).astype(bf16)
    step(grad_y, *sums_z, *sums_o)
    sums_b = halves(grad_y)
    if by_hand:
        last_values = [d_one, after(d_two, grad_y, *values(*sums_z))]
        norm = (hidden, cotangent, gain_in[None])
        grad_hidden, grad_gain_in = back(last_values, g_x, d_normed_in, norm)
    else:
        d_x = jnp.concatenate([d_one, d_two[:, :count]], 1)
        d_normed_in = d_normed_in + stacked_back(d_x, stack_x, 0)
        base = hidden.astype(f32)
        scale = scale_in[HALO:]
        d_hat = d_normed_in * gain_in[None, :]
        mean = jnp.mean(d_hat * base, axis=1, keepdims=True)
        grad_hidden = cotangent.astype(f32) + scale * d_hat - base * (scale * scale * scale * mean)
        grad_gain_in = (d_normed_in * base * scale).reshape(-1, 8, width).sum(0)
    step(grad_gain_in, *sums_b)
    sums_x = [sum_a] + sums_b
    step(sums_b[0].value, sum_a, *sums_z)
    step(sum_a.value, *sums_b)
    grad_gain_in = after(grad_gain_in, *values(*sums_b))
    step(sums_b[0].value, sum_a, *sums_z)
    while any(chain.order for chain in sums_o + sums_z + sums_x):
        step(grad_gain_in, *sums_b)
        step(sums_b[0].value, sum_a, *sums_z, *sums_o)
    counts = [width // devices] + [channels // devices] * (CONV + 1) + [inner // devices]
    counts += [heads] * 3
    total = sum(counts)
    if by_hand:
        sizes = (width // devices, channels // devices, inner // devices, heads)
        packed = pl.pallas_call(
            lambda *refs: pack_kernel(sizes, *refs),
            out_shape=jax.ShapeDtypeStruct((devices, 1, total + -total % TILE), f32),
            name="pack",
        )(sums[:, :channels], grad_gain_in, d_gain, head_sums)
    else:
        slots = lambda v: v.reshape(-1, devices, v.shape[-1] // devices).transpose(1, 0, 2)
        same = jnp.broadcast_to(head_sums[:3, :heads].reshape(1, -1), (devices, 3 * heads))
        pieces = [slots(grad_gain_in.sum(0)), slots(sums[: CONV + 1, :channels])]
        pieces += [slots(jnp.sum(d_gain, 0)), same]
        packed = jnp.concatenate([p.reshape(devices, -1) for p in pieces], 1)[:, None]
    packed = exchange(packed).sum((0, 1))
    found, at = ([], 0)
    for size in counts:
        found.append(packed[at : at + size])
        at += size

    grads = [c.rows().astype(f32) for c in sums_z + sums_x]
    excess = sum(g.shape[1] for g in grads) - w_in.shape[0]
    grads[-1] = grads[-1][:, : grads[-1].shape[1] - excess]
    return (
        block_out,
        grad_hidden,
        found[0],
        jnp.concatenate(grads, 1),
        jnp.stack(found[1 : CONV + 1]),
        found[CONV + 1],
        found[CONV + 3],
        found[CONV + 4],
        found[CONV + 5],
        found[CONV + 2],
        jnp.concatenate([c.rows().astype(f32) for c in sums_o], 1),
    )


def solution(mesh):
    return jax.shard_map(
        on_device,
        mesh=mesh,
        in_specs=(
            P(ALL, None),
            P(ALL, None),
            P(),
            P("shard"),
            P("shard", None),
            P(None, "shard"),
            P("shard"),
            P(),
            P(),
            P(),
            P("shard"),
            P("shard", None),
        ),
        out_specs=(
            P(ALL, None),
            P(ALL, None),
            P(ALL),
            P(ALL, None),
            P(None, ALL),
            P(ALL),
            P(),
            P(),
            P(),
            P(ALL),
            P(ALL, None),
        ),
        check_vma=False,
    )
```

```python
import jax
import jax.numpy as jnp
from jax import lax
from jax.experimental import pallas as pl
from jax.experimental.pallas import tpu as pltpu
from jax.sharding import PartitionSpec as P

HEAD_DIM = 64
CONV = 4
EPS = 1e-05
HALO = 8
GROUP = 4
WIDE = GROUP * HEAD_DIM
TILE = 128
PIECE = 3 * WIDE
SPAN = 2
HIGH = lax.Precision.HIGHEST
ALL = ("shard", "seq")
f32 = jnp.float32
bf16 = jnp.bfloat16
CHEAP = pl.CostEstimate(flops=1, bytes_accessed=1, transcendentals=0)


def mm(a, b):
    return jnp.dot(a, b, preferred_element_type=f32)


def mm_nt(a, b):
    return lax.dot_general(a, b, (((1,), (1,)), ((), ())), preferred_element_type=f32)


def mm_tn(a, b):
    return lax.dot_general(a, b, (((0,), (0,)), ((), ())), preferred_element_type=f32)


def sigmoid(value):
    return 0.5 * jnp.tanh(0.5 * value) + 0.5


def head_lanes(group):
    lane = lax.rem(lax.broadcasted_iota(jnp.int32, (2 * TILE, WIDE), 0), TILE)
    owner = lax.broadcasted_iota(jnp.int32, (2 * TILE, WIDE), 1) // HEAD_DIM + GROUP * group
    return jnp.where(lane == owner, 1.0, 0.0).astype(bf16)


def two_parts(value):
    high = value.astype(bf16)
    low = (value - high.astype(f32)).astype(bf16)
    return high, low


def twice(value):
    return jnp.concatenate([value, value], 1)


def conv_rows(wide, taps, masks, start, rows):
    pre = taps[CONV : CONV + 1, :] + taps[CONV - 1 : CONV, :] * wide[pl.ds(HALO + start, rows), :]
    for tap in range(CONV - 1):
        shifted = wide[pl.ds(HALO - CONV + 1 + tap + start, rows), :]
        pre = pre + taps[tap : tap + 1, :] * shifted * twice(masks[tap, pl.ds(start, rows), :])
    return pre


def prepare_kernel(edge, rates, flags, out, spread_out, cum_out, row_out, masks_out):
    length = out.shape[1]
    shifted = edge[...].astype(f32) + rates[0:1, :]
    step = jax.nn.softplus(shifted)
    here = lax.broadcasted_iota(jnp.int32, (length, length), 0)
    there = lax.broadcasted_iota(jnp.int32, (length, length), 1)
    lower = jnp.where(here >= there, 1.0, 0.0)
    log_decay = -step * jnp.exp(rates[1:2, :])
    cum = lax.dot_general(
        lower, log_decay, (((1,), (0,)), ((), ())), precision=HIGH, preferred_element_type=f32
    )
    keep = jnp.exp(cum[length - 1 : length, :] - cum) * flags[:, 8:9]
    out[0] = cum
    out[1] = step
    out[2] = keep
    out[3] = jnp.exp(cum) * flags[:, 7:8]
    out[4] = sigmoid(shifted)
    for at, value in enumerate((step, keep)):
        high, low = two_parts(value)
        spread_out[at, :, :TILE] = high
        spread_out[at, :, TILE:] = low
    turned = cum.T
    for group in range(row_out.shape[0]):
        heads = slice(GROUP * group, GROUP * (group + 1))
        row_out[group] = turned[heads, :]
        cum_out[group] = cum[:, heads]
    for at in range(2 * (CONV - 1)):
        masks_out[at] = jnp.broadcast_to(flags[:, at : at + 1], (length, TILE))


def span(sub):
    return pl.ds(pl.multiple_of(sub * WIDE, WIDE), WIDE)


def state_kernel(
    raw, raw_bc, taps, taps_bc, masks, spreads, x_out, state_out, bc_out, bt_out, ct_out, wide, bt
):
    length = x_out.shape[0]
    n_state = bt.shape[0]
    step = pl.program_id(0)

    @pl.when(step == 0)
    def _():
        wide[...] = raw_bc[...].astype(f32)
        tap = taps_bc[...]
        for start in range(0, length, TILE):
            rows = pl.ds(start, TILE)
            pre = conv_rows(wide, tap, masks, start, TILE)
            both = pre * sigmoid(pre)
            bc_out[rows, :] = both.astype(bf16)
            turned = both[:, :n_state].T.astype(bf16)
            bt[:, rows] = turned
            bt_out[:, rows] = turned
            ct_out[:, rows] = both[:, n_state:].T.astype(bf16)

    def one(sub, carry):
        columns = span(sub)
        wide[...] = raw[:, columns].astype(f32)
        tap = taps[:, columns]
        lanes = head_lanes(SPAN * step + sub)
        kept = []
        for start in range(0, length, TILE):
            rows = pl.ds(start, TILE)
            pre = conv_rows(wide, tap, masks, start, TILE)
            x = (pre * sigmoid(pre)).astype(bf16)
            x_out[rows, columns] = x
            scaled = (x.astype(f32) * mm(spreads[0, rows, :], lanes)).astype(bf16)
            kept.append((scaled.astype(f32) * mm(spreads[1, rows, :], lanes)).astype(bf16))
        state_out[:, columns] = mm(bt[...], jnp.concatenate(kept, 0)).astype(bf16)
        return carry

    lax.fori_loop(0, SPAN, one, 0)


def scored(first, second, flags, seg_row, score, later):
    length = score.shape[0]
    for start in range(0, length, TILE):
        rows = pl.ds(start, TILE)
        product = mm(first(rows), second[...])
        here = lax.broadcasted_iota(jnp.int32, (TILE, length), 0) + start
        there = lax.broadcasted_iota(jnp.int32, (TILE, length), 1)
        order = (here >= there) if later else (here <= there)
        seen = (flags[rows, 6:7] == seg_row[0:1, :]) & order
        score[rows, :] = jnp.where(seen, product, 0.0)


def by_head(value):
    owner = lax.broadcasted_iota(jnp.int32, value.shape, 1) // HEAD_DIM
    zero = jnp.zeros_like(value)
    return [jnp.where(owner == head, value, zero) for head in range(GROUP)]


def forward_kernel(x_in, flags, seg_row, spreads, cum, sums_row, bc, bt, y_out, score, apart, weights):
    length = y_out.shape[0]
    n_state = bt.shape[0]
    step = pl.program_id(0)
    big = weights.shape[2] // GROUP

    @pl.when(step == 0)
    def _():
        scored(lambda rows: bc[rows, n_state:], bt, flags, seg_row, score, True)
        weights[...] = jnp.zeros_like(weights)

    def one(sub, carry):
        columns = span(sub)
        lanes = head_lanes(SPAN * step + sub)
        for start in range(0, length, TILE):
            rows = pl.ds(start, TILE)
            scaled = x_in[rows, columns].astype(f32) * mm(spreads[0, rows, :], lanes)
            for head, value in enumerate(by_head(scaled)):
                apart[start // big, pl.ds(head * big + start % big, TILE), :] = value.astype(bf16)
        for head in range(GROUP):
            for start in range(0, length, TILE):
                rows = pl.ds(start, TILE)
                for at in range(0, start + TILE, big):
                    end = min(at + big, start + TILE)
                    gap = cum[sub, rows, head : head + 1] - sums_row[sub, head : head + 1, at:end]
                    weight = jnp.exp(jnp.minimum(gap, 0.0)) * score[rows, at:end]
                    weights[at // big, rows, head * big : head * big + end - at] = weight.astype(bf16)
        for at in range(0, length, big):
            part = mm(weights[at // big, at:, :], apart[at // big])
            if at == 0:
                y_out[:, columns] = part
            else:
                y_out[at:, columns] += part
        return carry

    lax.fori_loop(0, SPAN, one, 0)


def gate_kernel(
    shards, y_in, x_in, z_in, dn_in, bc, ct, enter, state, gain, ssm_out, norm_out, dz_out, dy_out,
    ds_out, dc_out, dg_out, gated_s, sig_s, mo_s, ds_acc
):
    rows = y_in.shape[0]
    width = y_in.shape[1]
    n_state = state.shape[0]
    step = pl.program_id(0)
    lane = lax.broadcasted_iota(jnp.int32, (rows, 2 * HEAD_DIM), 1)
    c_mat = bc[:, n_state:]

    @pl.when(step == 0)
    def _():
        ds_acc[...] = jnp.zeros_like(ds_acc)
        dg_out[...] = jnp.zeros_like(dg_out)

    def entering(block):
        low = enter[:, 2 * block : 2 * block + 1]
        top = enter[:, 2 * block + 1 : 2 * block + 2]
        return jnp.where(lane < HEAD_DIM, low, top)

    square = jnp.zeros((rows, 2 * HEAD_DIM), f32)
    cross = jnp.zeros((rows, 2 * HEAD_DIM), f32)
    for block in range(width // (2 * HEAD_DIM)):
        lanes = slice(block * 2 * HEAD_DIM, (block + 1) * 2 * HEAD_DIM)
        ssm = y_in[:, lanes] + entering(block) * mm(c_mat, state[:, lanes])
        ssm_out[:, lanes] = ssm
        mo = (ssm + gain[1:2, lanes] * x_in[:, lanes].astype(f32)).astype(bf16)
        mo_s[:, lanes] = mo
        z = z_in[:, lanes].astype(f32)
        sig = sigmoid(z)
        gated = mo.astype(f32) * (z * sig)
        gated_s[:, lanes] = gated
        sig_s[:, lanes] = sig
        square = square + gated * gated
        cross = cross + gated * (dn_in[:, lanes] * gain[0:1, lanes])
    scale = lax.rsqrt(jnp.sum(square, axis=1, keepdims=True) * (1.0 / width) + EPS)
    pull = scale * scale * scale * (jnp.sum(cross, axis=1, keepdims=True) * (1.0 / width))
    dc = jnp.zeros((rows, n_state), f32)
    for block in range(width // (2 * HEAD_DIM)):
        lanes = slice(block * 2 * HEAD_DIM, (block + 1) * 2 * HEAD_DIM)
        gated = gated_s[:, lanes]
        sig = sig_s[:, lanes]
        silu = z_in[:, lanes].astype(f32) * sig
        dn = dn_in[:, lanes]
        hat = gated * scale
        size = width // shards
        owner, at = divmod(block * 2 * HEAD_DIM, size)
        at += (owner // 2) * size
        norm_out[owner % 2, :, at : at + 2 * HEAD_DIM] = (hat * gain[0:1, lanes]).astype(bf16)
        part = dn * hat
        total = part[0:8, :]
        for at in range(8, rows, 8):
            total = total + part[at : at + 8, :]
        dg_out[:, lanes] += total
        d_gated = scale * (dn * gain[0:1, lanes]) - gated * pull
        dy = (d_gated * silu).astype(bf16)
        dy_out[:, lanes] = dy
        mo = mo_s[:, lanes].astype(f32)
        dz_out[:, lanes] = (d_gated * mo * (sig + silu * (1.0 - sig))).astype(bf16)
        weighted = (dy.astype(f32) * entering(block)).astype(bf16)
        ds_acc[:, lanes] += mm(ct[...], weighted)
        dc = dc + mm_nt(weighted, state[:, lanes])
    dc_out[...] = dc

    @pl.when(step == pl.num_programs(0) - 1)
    def _():
        ds_out[...] = ds_acc[...].astype(bf16)


def inside_kernel(
    x_in, flags, seg_row, spreads, cum, sums_row, bc, ct, dy, dxs_out, db_out, dc_out, score, pair,
    apart, weights, xs, crossed
):
    length = dxs_out.shape[0]
    n_state = ct.shape[0]
    group = pl.program_id(0)
    big = weights.shape[2] // GROUP

    @pl.when(group == 0)
    def _():
        pair[...] = jnp.zeros_like(pair)
        weights[...] = jnp.zeros_like(weights)
        scored(lambda rows: bc[rows, :n_state], ct, flags, seg_row, score, False)

    lanes = head_lanes(group)
    for start in range(0, length, TILE):
        rows = pl.ds(start, TILE)
        scaled = x_in[rows, :].astype(f32) * mm(spreads[0, rows, :], lanes)
        for head, value in enumerate(by_head(scaled)):
            xs[head, rows, :] = value.astype(bf16)
        for head, value in enumerate(by_head(dy[rows, :].astype(f32))):
            apart[start // big, pl.ds(head * big + start % big, TILE), :] = value.astype(bf16)
    for head in range(GROUP):
        for at in range(0, length, big):
            end = at + big
            crossed[head % 2, :end, at:end] = mm_nt(xs[head, :end, :], dy[at:end, :])
        for start in range(0, length, TILE):
            rows = pl.ds(start, TILE)
            for at in range(start // big * big, length, big):
                first = max(at, start)
                end = at + big
                gap = sums_row[0, head : head + 1, first:end] - cum[0, rows, head : head + 1]
                decay = jnp.exp(jnp.minimum(gap, 0.0))
                weight = (decay * score[rows, first:end]).astype(bf16)
                weights[at // big, rows, head * big + first - at : (head + 1) * big] = weight
                pair[rows, first:end] += decay * crossed[head % 2, rows, first:end]
    for at in range(length - big, -1, -big):
        end = at + big
        part = mm(weights[at // big, :end, :], apart[at // big])
        if end == length:
            dxs_out[...] = part
        else:
            dxs_out[:end, :] += part

    @pl.when(group == pl.num_programs(0) - 1)
    def _():
        for start in range(0, length, TILE):
            rows = pl.ds(start, TILE)
            here = lax.broadcasted_iota(jnp.int32, (TILE, length), 0) + start
            there = lax.broadcasted_iota(jnp.int32, (TILE, length), 1)
            seen = (flags[rows, 6:7] == seg_row[0:1, :]) & (here <= there)
            part = jnp.where(seen, pair[rows, :], 0.0).astype(bf16)
            db_out[rows, :] = mm(part, bc[:, n_state:])
            if start == 0:
                dc_out[...] = mm_tn(part, bc[rows, :n_state])
            else:
                dc_out[...] += mm_tn(part, bc[rows, :n_state])


def split_mm(value, chosen):
    high, low = two_parts(value)
    return mm(high, chosen) + mm(low, chosen)


def outside_kernel(first_group, count, final, running, *refs):
    (raw, raw_bc, taps, masks, spreads, heads, rates, bc, dy, ssm, dxs_in, d_state, state, db_in,
     dc_in, dc_more, *started, d_out, first_out, last_out, sums_out,
     head_out, db_acc, found, totals_s, wide, d_pre) = refs
    length = d_out.shape[0]
    n_state = bc.shape[1] // 2
    step = pl.program_id(0)
    bc_step = count

    @pl.when(step == 0)
    def _():
        for at, ref in enumerate((db_acc, found, totals_s)):
            ref[...] = started[at][...] if running else jnp.zeros_like(ref)

    d_pre[pl.ds(length, HALO), :] = jnp.zeros((HALO, d_pre.shape[1]), f32)
    zero = jnp.zeros((1, d_pre.shape[1]), f32)

    @pl.when(step < bc_step)
    def _():
        wide[...] = raw[...].astype(f32)
        skip_sum, keep_sum = (zero, zero)
        ds = d_state[...]
        group = step + first_group
        lanes = head_lanes(group)
        owner = lax.broadcasted_iota(jnp.int32, (WIDE, TILE), 0) // HEAD_DIM + GROUP * group
        chosen = (owner == lax.broadcasted_iota(jnp.int32, (WIDE, TILE), 1)).astype(f32)
        chosen_b = chosen.astype(bf16)
        for start in range(0, length, TILE):
            rows = pl.ds(start, TILE)
            pre = conv_rows(wide, taps, masks, start, TILE)
            sig = sigmoid(pre)
            x = pre * sig
            stepped = mm(spreads[0, rows, :], lanes)
            scaled = (x.astype(bf16).astype(f32) * stepped).astype(bf16)
            keep = mm(spreads[1, rows, :], lanes)
            carried = keep * mm(bc[rows, :n_state], ds)
            dxs = dxs_in[rows, :] + carried
            scaled = scaled.astype(f32)
            db_acc[rows, :] += mm_nt((scaled * keep).astype(bf16), ds)
            grad = dy[rows, :].astype(f32)
            keep_sum = keep_sum + jnp.sum(scaled * carried, 0, keepdims=True)
            skip_sum = skip_sum + jnp.sum(grad * x, 0, keepdims=True)
            found[0, rows, :] += split_mm(grad * ssm[rows, :] - scaled * dxs, chosen_b)
            found[1, rows, :] += split_mm(x * dxs, chosen_b)
            d_x = taps[5:6, :] * grad + stepped * dxs
            d_pre[rows, :] = d_x * (sig + x * (1.0 - sig))
        met = jnp.sum(ds.astype(f32) * state[...].astype(f32), 0, keepdims=True)
        rest = jnp.zeros((5, WIDE), f32)
        totals_s[...] += lax.dot_general(
            jnp.concatenate([skip_sum, keep_sum, met, rest], 0),
            chosen,
            (((1,), (0,)), ((), ())),
            precision=HIGH,
            preferred_element_type=f32,
        )

    if final:

        @pl.when(step == bc_step)
        def _():
            wide[...] = raw_bc[...].astype(f32)
            for start in range(0, length, TILE):
                rows = pl.ds(start, TILE)
                pre = conv_rows(wide, taps, masks, start, TILE)
                sig = sigmoid(pre)
                slope = sig + pre * sig * (1.0 - sig)
                d_b = db_in[rows, :] + db_acc[rows, :]
                d_c = dc_in[rows, :] + dc_more[rows, :]
                d_pre[rows, :] = jnp.concatenate([d_b, d_c], 1) * slope

    @pl.when(step <= bc_step)
    def _():
        totals = [zero] * (CONV + 1)
        for start in range(0, length, TILE):
            rows = pl.ds(start, TILE)
            grad = d_pre[rows, :]
            totals[CONV] = totals[CONV] + jnp.sum(grad, 0, keepdims=True)
            here = wide[pl.ds(HALO + start, TILE), :]
            totals[CONV - 1] = totals[CONV - 1] + jnp.sum(grad * here, 0, keepdims=True)
            back = taps[CONV - 1 : CONV, :] * grad
            for tap in range(CONV - 1):
                shifted = wide[pl.ds(HALO - CONV + 1 + tap + start, TILE), :]
                masked = grad * twice(masks[tap, rows, :])
                totals[tap] = totals[tap] + jnp.sum(masked * shifted, 0, keepdims=True)
                ahead = d_pre[pl.ds(start + CONV - 1 - tap, TILE), :]
                back = back + taps[tap : tap + 1, :] * ahead * twice(masks[3 + tap, rows, :])
            d_out[rows, :] = back.astype(bf16)
            if start + TILE == length:
                last_out[...] = back[TILE - HALO :, :]
        first_out[...] = d_pre[pl.ds(0, HALO), :]
        for tap in range(CONV + 1):
            sums_out[tap : tap + 1, :] = totals[tap]
        sums_out[CONV + 1 : 8, :] = jnp.zeros((7 - CONV, d_pre.shape[1]), f32)

    if not final:
        head_out[...] = jnp.zeros_like(head_out)
        return

    @pl.when(step == bc_step + 1)
    def _():
        first_out[...] = jnp.zeros_like(first_out)
        last_out[...] = jnp.zeros_like(last_out)
        sums_out[...] = jnp.zeros_like(sums_out)
        rate = jnp.exp(rates[1:2, :])
        end = totals_s[1:2, :] + heads[3, pl.ds(length - 1, 1), :] * totals_s[2:3, :]
        here = lax.broadcasted_iota(jnp.int32, (length, length), 0)
        there = lax.broadcasted_iota(jnp.int32, (length, length), 1)
        upper = jnp.where(here <= there, 1.0, 0.0)
        d_log = lax.dot_general(
            upper, found[0], (((1,), (0,)), ((), ())), precision=HIGH, preferred_element_type=f32
        )
        d_log = d_log + end
        d_dt = (found[1] - rate * d_log) * heads[4]
        d_out[:, :TILE] = d_dt.astype(bf16)
        d_out[:, TILE:] = jnp.zeros((length, WIDE - TILE), bf16)
        head_out[0:1, :] = jnp.sum(d_dt, 0, keepdims=True)
        head_out[1:2, :] = jnp.sum(d_log * (-heads[1] * rate), 0, keepdims=True)
        head_out[2:3, :] = totals_s[0:1, :]
        head_out[3:8, :] = jnp.zeros((5, TILE), f32)


def pack_kernel(sizes, sums, gain_in, gain_out, head, out):
    devices = out.shape[0]
    gain_in = jnp.sum(gain_in[...], 0, keepdims=True)
    wide, channels, inner, heads = sizes
    gains = jnp.sum(gain_out[...], 0, keepdims=True)
    for at in range(devices):
        pieces = [gain_in[:, at * wide : (at + 1) * wide]]
        for tap in range(CONV + 1):
            pieces.append(sums[tap : tap + 1, at * channels : (at + 1) * channels])
        pieces.append(gains[:, at * inner : (at + 1) * inner])
        for row in range(3):
            pieces.append(head[row : row + 1, :heads])
        begin = 0
        for piece in pieces:
            out[at, :, begin : begin + piece.shape[1]] = piece
            begin += piece.shape[1]
        if begin < out.shape[2]:
            out[at, :, begin:] = jnp.zeros((1, out.shape[2] - begin), f32)


def scan_kernel(backward, place, mine, decay, out, wide):
    count = mine.shape[0]
    columns = out.shape[2]
    for at in range(2):
        for device in range(count):
            wide[at, device : device + 1, :] = decay[device, at : at + 1, :].astype(f32)
    lane = lax.broadcasted_iota(jnp.int32, (TILE, columns), 0)
    owner = lax.broadcasted_iota(jnp.int32, (TILE, columns), 1) // HEAD_DIM + place[0]
    chosen = jnp.where(lane == owner, 1.0, 0.0).astype(bf16)
    factor = mm(wide[0].astype(bf16), chosen) + mm(wide[1].astype(bf16), chosen)
    state = jnp.zeros(out.shape[1:], f32)
    for at in reversed(range(count)) if backward else range(count):
        out[at] = state.astype(bf16)
        state = factor[at : at + 1, :] * state + mine[at, :, :columns].astype(f32)


def to_slices(value, devices):
    n_state, inner = value.shape
    across = max(1, devices // 16)
    rows = n_state * across // devices
    value = value.reshape(n_state // rows, rows, across, inner // across)
    return value.transpose(0, 2, 1, 3).reshape(devices, rows, inner // across)


def from_slices(slices, n_state, inner):
    devices, rows, columns = slices.shape
    value = slices.reshape(n_state // rows, inner // columns, rows, columns)
    return value.transpose(0, 2, 1, 3).reshape(n_state, inner)


def exchange(slices):
    return lax.all_to_all(slices, ALL, split_axis=0, concat_axis=0, tiled=True)


def return_slices(states, n_state, inner):
    return from_slices(exchange(states), n_state, inner)


def with_decay(slices, end):
    devices, rows, _ = slices.shape
    more = jnp.pad(jnp.stack(end), ((0, rows - 2), (0, 0)))
    return jnp.concatenate([slices, jnp.broadcast_to(more[None], (devices, rows, TILE))], 2)


def scan_devices(mine, decay, columns, me, backward):
    devices, rows, _ = mine.shape
    across = max(1, devices // 16)
    place = jnp.reshape((me % across) * (columns // HEAD_DIM), (1,)).astype(jnp.int32)
    vmem = pl.BlockSpec(memory_space=pltpu.VMEM)
    return pl.pallas_call(
        lambda *refs: scan_kernel(backward, *refs),
        in_specs=[pl.BlockSpec(memory_space=pltpu.SMEM), vmem, vmem],
        out_specs=vmem,
        out_shape=jax.ShapeDtypeStruct((devices, rows, columns), bf16),
        scratch_shapes=[pltpu.VMEM((2, devices, TILE), f32)],
        compiler_params=pltpu.CompilerParams(vmem_limit_bytes=40 * 1024 * 1024),
        cost_estimate=CHEAP,
        name="scan_backward" if backward else "scan_forward",
    )(place, mine, decay)


def flip(axis, bit):
    count = lax.axis_size(axis)
    return [(i, i ^ bit) for i in range(count)]


def other_core(value):
    return lax.ppermute(value, "shard", flip("shard", 1))


class Plan:
    def __init__(self):
        self.values, self.array = ([], None)

    def add(self, values):
        self.values += [jnp.asarray(value, jnp.int32) for value in values]
        return len(self.values) - len(values)

    def close(self):
        self.array = jnp.stack(self.values)


class Gather:
    def __init__(self, plan, own, other, base, half, chunks, *wait):
        self.own, self.other, self.base, self.half, self.chunks = (own, other, base, half, chunks)
        self.mine = lax.axis_index("seq") % 2
        self.size = half // chunks
        self.plan = plan
        if plan.array is None:
            full, near = (half // PIECE, self.size // PIECE)
            self.order = []
            for chunk in range(chunks):
                first = chunk * near
                order = [full * self.mine + first + at for at in range(near)]
                order += [full * (1 - self.mine) + first + at for at in range(near)]
                self.order.append(plan.add(order))
            source, block = ([], [])
            for at in range(2 * full):
                place = at % full
                source.append(2 * (place // near) + jnp.where(self.mine == at // full, 0, 1))
                block.append(place % near)
            self.source, self.block = (plan.add(source), plan.add(block))
        self.direct, self.passed = ([None] * chunks, [None] * chunks)
        self.parts = [None] * chunks
        for chunk in range(chunks):
            start = base + self.mine * half + chunk * self.size
            self.send = lax.dynamic_slice_in_dim(own, start, self.size, 0)
            if chunk:
                wait = (self.direct[chunk - 1],)
            if wait:
                self.send = after(self.send, *wait)
            self.direct[chunk] = lax.ppermute(self.send, "shard", flip("shard", 2))

    def share(self, *wait):
        for chunk in range(self.chunks):
            if chunk:
                wait = (self.passed[chunk - 1],)
            if wait:
                self.direct[chunk] = after(self.direct[chunk], *wait)
            self.passed[chunk] = lax.ppermute(self.direct[chunk], "seq", flip("seq", 1))

    def cross(self, chunk, *wait):
        direct, passed = (self.direct[chunk], self.passed[chunk])
        if wait:
            direct, passed = lax.optimization_barrier((direct, passed) + wait)[:2]
        self.parts[chunk] = [direct, other_core(direct), passed, other_core(passed)]


def project_kernel(table, *refs):
    lefts, (own, other, direct, direct_o, passed, passed_o) = (refs[:4], refs[4:10])
    out, left, weight = refs[-3:]
    step = pl.program_id(0)

    @pl.when(step == 0)
    def _():
        left[...] = jnp.concatenate([a[...] for a in lefts], 1)

    def fill(far, far_o):
        deep = own.shape[1]
        weight[:, :deep] = far[...]
        weight[:, deep:] = far_o[...]

    near = pl.num_programs(0) // 2
    pl.when(step < near)(lambda: fill(direct, direct_o))
    pl.when(step >= near)(lambda: fill(passed, passed_o))
    whole = jnp.concatenate([own[...], other[...], weight[...]], 1)
    out[...] = mm_nt(left[...], whole).astype(bf16)


def project(value, gather, chunk, result):
    rows = value.shape[0]
    deep = gather.own.shape[1]
    near = gather.size // PIECE
    base = gather.base // PIECE
    order = gather.order[chunk]
    table = gather.plan.array
    block = lambda index: pl.BlockSpec((PIECE, deep), index)
    left = lambda k: pl.BlockSpec((rows, deep), lambda j, t: (0, t[k]))
    own = block(lambda j, t: (base + t[order + j], 0))
    one = block(lambda j, t: (jnp.minimum(j, near - 1), 0))
    two = block(lambda j, t: (jnp.maximum(j - near, 0), 0))
    operands = [table, *([value] * 4), gather.own, gather.other, *gather.parts[chunk]]
    in_specs = [left(k) for k in range(4)] + [own, own, one, one, two, two]
    aliases = {}
    if result is not None:
        aliases = {len(operands): 0}
        operands.append(result)
        in_specs.append(pl.BlockSpec(memory_space=pl.ANY))
    return pl.pallas_call(
        project_kernel,
        grid_spec=pltpu.PrefetchScalarGridSpec(
            num_scalar_prefetch=1,
            grid=(2 * near,),
            in_specs=in_specs,
            out_specs=pl.BlockSpec((rows, PIECE), lambda j, t: (0, t[order + j])),
            scratch_shapes=[
                pltpu.VMEM((rows, 4 * deep), bf16),
                pltpu.VMEM((PIECE, 2 * deep), bf16),
            ],
        ),
        out_shape=jax.ShapeDtypeStruct((rows, 2 * gather.half), bf16),
        input_output_aliases=aliases,
        compiler_params=pltpu.CompilerParams(vmem_limit_bytes=58 * 1024 * 1024),
        cost_estimate=CHEAP,
        name="project",
    )(*operands)


def back_kernel(values, chunks, norm, source, table, *refs):
    inputs, refs = (refs[:values], refs[values:])
    own, other = refs[:2]
    far, refs = (refs[2 : 2 + 4 * chunks], refs[2 + 4 * chunks :])
    total, value, weight = refs[-3:]
    refs = refs[:-3]
    if norm:
        hidden, cotangent, gain, out, gain_out = refs[-5:]
        start = refs[:-5]
    else:
        out, start = (refs[-1], refs[:-1])
    step = pl.program_id(0)
    last = pl.num_programs(0) - 1
    deep = own.shape[1]
    place = lambda k: pl.ds(pl.multiple_of(table[k] * deep, deep), deep)

    @pl.when(step == 0)
    def _():
        if start:
            for k in range(4):
                total[:, k * deep : (k + 1) * deep] = start[0][:, place(k)]
        else:
            total[...] = jnp.zeros_like(total)

    for at in range(values):

        @pl.when((step * values // (last + 1)) == at)
        def _(at=at):
            value[...] = inputs[at][...]

    for at in range(2 * chunks):

        @pl.when(table[source + step] == at)
        def _(at=at):
            weight[:, :deep] = far[2 * at][...]
            weight[:, deep:] = far[2 * at + 1][...]

    total[...] += mm(value[...], jnp.concatenate([own[...], other[...], weight[...]], 1))

    @pl.when(step == last)
    def _():
        for k in range(4):
            out[:, place(k)] = total[:, k * deep : (k + 1) * deep]
        if norm:
            sums = jnp.zeros(gain_out.shape, f32)
            for at in range(0, out.shape[0], 64):
                rows = pl.ds(at, 64)
                base = hidden[rows, :].astype(f32)
                grad = out[rows, :]
                size = 1.0 / base.shape[1]
                scale = lax.rsqrt(jnp.sum(base * base, 1, keepdims=True) * size + EPS)
                hat = base * scale
                part = grad * hat
                for row in range(0, 64, 8):
                    sums = sums + part[row : row + 8, :]
                pull = jnp.sum(part * gain[...], 1, keepdims=True) * size
                inner = scale * (grad * gain[...] - hat * pull)
                out[rows, :] = cotangent[rows, :].astype(f32) + inner
            gain_out[...] = sums


def back(values, gather, start, norm=()):
    rows = values[0].shape[0]
    deep = gather.own.shape[1]
    count = 2 * gather.half // PIECE
    share = count // len(values)
    base = gather.base // PIECE
    table = gather.plan.array
    whole = pl.BlockSpec((rows, 4 * deep), lambda j, t: (0, 0))
    own = pl.BlockSpec((PIECE, deep), lambda j, t: (base + j, 0))
    far = pl.BlockSpec((PIECE, deep), lambda j, t: (t[gather.block + j], 0))
    in_specs = [
        pl.BlockSpec((rows, PIECE), lambda j, t, k=k: (0, jnp.clip(j - k * share, 0, share - 1)))
        for k in range(len(values))
    ]
    started = [] if start is None else [start]
    parts = [piece for chunk in gather.parts for piece in chunk]
    in_specs += [own, own] + [far] * len(parts) + [whole] * len(started)
    out_specs, out_shape = (whole, jax.ShapeDtypeStruct((rows, 4 * deep), f32))
    if norm:
        narrow = lambda count: pl.BlockSpec((count, 4 * deep), lambda j, t: (0, 0))
        in_specs += [whole, whole, narrow(1)]
        out_specs = [whole, narrow(8)]
        out_shape = [out_shape, jax.ShapeDtypeStruct((8, 4 * deep), f32)]
    return pl.pallas_call(
        lambda *refs: back_kernel(len(values), gather.chunks, len(norm) > 0, gather.source, *refs),
        grid_spec=pltpu.PrefetchScalarGridSpec(
            num_scalar_prefetch=1,
            grid=(count,),
            in_specs=in_specs,
            out_specs=out_specs,
            scratch_shapes=[
                pltpu.VMEM((rows, 4 * deep), f32),
                pltpu.VMEM((rows, PIECE), bf16),
                pltpu.VMEM((PIECE, 2 * deep), bf16),
            ],
        ),
        out_shape=out_shape,
        compiler_params=pltpu.CompilerParams(vmem_limit_bytes=58 * 1024 * 1024),
        cost_estimate=CHEAP,
        name="back",
    )(table, *values, gather.own, gather.other, *parts, *started, *norm)


def by_shard(gather):
    half, width = (gather.half, gather.own.shape[1])
    whole = pl.BlockSpec((2 * half, width), lambda g, t: (0, 0))
    part = pl.BlockSpec((half, width), lambda g, t: (0, 0))
    direct, direct_o, passed, passed_o = gather.parts[0]
    operands = [gather.own, gather.other, direct, passed, direct_o, passed_o]
    table = gather.plan.array
    return operands, [whole] * 2 + [part] * 4, table


def out_back_kernel(table, value, own, other, direct, passed, direct_o, passed_o, out):
    step = pl.program_id(0)
    half = direct.shape[0]

    def two(near, far):
        out[:, pl.ds(pl.multiple_of(table[4] * half, half), half)] = mm_nt(value[...], near[...])
        far_at = pl.multiple_of((1 - table[4]) * half, half)
        out[:, pl.ds(far_at, half)] = mm_nt(value[...], far[...])

    for at, piece in enumerate((own, other)):

        @pl.when(step == at)
        def _(piece=piece):
            out[...] = mm_nt(value[...], piece[...])

    pl.when(step == 2)(lambda: two(direct, passed))
    pl.when(step == 3)(lambda: two(direct_o, passed_o))


def out_back(value, gather):
    rows, width = value.shape
    operands, specs, table = by_shard(gather)
    size = 2 * gather.half
    return pl.pallas_call(
        out_back_kernel,
        grid_spec=pltpu.PrefetchScalarGridSpec(
            num_scalar_prefetch=1,
            grid=(4,),
            in_specs=[pl.BlockSpec((rows, width), lambda g, t: (0, 0))] + specs,
            out_specs=pl.BlockSpec((rows, size), lambda g, t: (0, t[g])),
        ),
        out_shape=jax.ShapeDtypeStruct((rows, 4 * size), f32),
        compiler_params=pltpu.CompilerParams(vmem_limit_bytes=58 * 1024 * 1024),
        cost_estimate=CHEAP,
        name="out_back",
    )(table, value, *operands)


def out_forward_kernel(table, value, base, own, other, direct, passed, direct_o, passed_o, out, total):
    step = pl.program_id(0)
    half = direct.shape[0]

    def two(near, far):
        near_at = pl.multiple_of(table[4] * half, half)
        far_at = pl.multiple_of((1 - table[4]) * half, half)
        total[...] += mm(value[:, pl.ds(near_at, half)], near[...])
        total[...] += mm(value[:, pl.ds(far_at, half)], far[...])

    @pl.when(step == 0)
    def _():
        total[...] = base[...].astype(f32) + mm(value[...], own[...])

    @pl.when(step == 1)
    def _():
        total[...] += mm(value[...], other[...])

    pl.when(step == 2)(lambda: two(direct, passed))

    @pl.when(step == 3)
    def _():
        two(direct_o, passed_o)
        out[...] = total[...].astype(bf16)


def out_forward(value, base, gather):
    rows = value.shape[1]
    operands, specs, table = by_shard(gather)
    size = 2 * gather.half
    width = gather.own.shape[1]
    fixed = pl.BlockSpec((rows, width), lambda g, t: (0, 0))
    return pl.pallas_call(
        out_forward_kernel,
        grid_spec=pltpu.PrefetchScalarGridSpec(
            num_scalar_prefetch=1,
            grid=(4,),
            in_specs=[
                pl.BlockSpec((None, rows, size), lambda g, t: (t[g] & 1, 0, t[g] >> 1)),
                fixed,
                *specs,
            ],
            out_specs=fixed,
            scratch_shapes=[pltpu.VMEM((rows, width), f32)],
        ),
        out_shape=jax.ShapeDtypeStruct((rows, width), bf16),
        compiler_params=pltpu.CompilerParams(vmem_limit_bytes=58 * 1024 * 1024),
        cost_estimate=CHEAP,
        name="out_forward",
    )(table, value, base, *operands)


def stacked_project_kernel(value, *rest):
    weight = jnp.concatenate([w[...] for w in rest[:-1]], 1)
    rest[-1][...] = mm_nt(value[...], weight).astype(bf16)


def stacked_project(value, stack, base, count):
    rows = value.shape[0]
    shards, _, deep = stack.shape
    first = base // WIDE
    specs = [
        pl.BlockSpec((None, WIDE, deep), lambda j, k=k: (k, first + j, 0)) for k in range(shards)
    ]
    return pl.pallas_call(
        stacked_project_kernel,
        grid=(count // WIDE,),
        in_specs=[pl.BlockSpec((rows, shards * deep), lambda j: (0, 0))] + specs,
        out_specs=pl.BlockSpec((rows, WIDE), lambda j: (0, j)),
        out_shape=jax.ShapeDtypeStruct((rows, count), bf16),
        compiler_params=pltpu.CompilerParams(vmem_limit_bytes=58 * 1024 * 1024),
        cost_estimate=CHEAP,
        name="stacked_project",
    )(value, *([stack] * shards))


def stacked_back_kernel(value, *rest):
    out, total = rest[-2:]
    step = pl.program_id(0)

    @pl.when(step == 0)
    def _():
        total[...] = jnp.zeros_like(total)

    weight = jnp.concatenate([w[...] for w in rest[:-2]], 1)
    total[...] += mm(value[...], weight)

    @pl.when(step == pl.num_programs(0) - 1)
    def _():
        out[...] = total[...]


def stacked_back(value, stack, base):
    rows, count = value.shape
    shards, _, deep = stack.shape
    size = WIDE
    first = base // size
    specs = [
        pl.BlockSpec((None, size, deep), lambda j, k=k: (k, first + j, 0)) for k in range(shards)
    ]
    return pl.pallas_call(
        stacked_back_kernel,
        grid=(count // size,),
        in_specs=[pl.BlockSpec((rows, size), lambda j: (0, j))] + specs,
        out_specs=pl.BlockSpec((rows, shards * deep), lambda j: (0, 0)),
        out_shape=jax.ShapeDtypeStruct((rows, shards * deep), f32),
        scratch_shapes=[pltpu.VMEM((rows, shards * deep), f32)],
        compiler_params=pltpu.CompilerParams(vmem_limit_bytes=58 * 1024 * 1024),
        cost_estimate=CHEAP,
        name="stacked_back",
    )(value, *([stack] * shards))


def halve(value, dim, axis, bit, mine, wait):
    shape = value.shape
    value = value.reshape(shape[:dim] + (shape[dim] // 2, 2) + shape[dim + 1 :])
    send = lax.dynamic_index_in_dim(value, 1 - mine, dim + 1, False)
    kept = lax.dynamic_index_in_dim(value, mine, dim + 1, False)
    came = lax.ppermute(send, axis, flip(axis, bit))
    if wait:
        came = after(came, *wait)
    return (kept.astype(f32) + came.astype(f32)).astype(bf16), send


class RowSum:
    def __init__(self, partial, far_first):
        shards, places = (lax.axis_size("shard"), lax.axis_size("seq"))
        shard, place = (lax.axis_index("shard"), lax.axis_index("seq"))
        rows, columns = partial.shape
        chips = shards // 2
        self.value = partial.reshape(chips, places, rows // (chips * places), columns)
        far = [(0, "shard", 2 << k, (shard >> (k + 1)) & 1) for k in range(chips.bit_length() - 1)]
        near = [(1, "seq", 1 << k, (place >> k) & 1) for k in range(places.bit_length() - 1)]
        self.order = far + near if far_first else near[:1] + far + near[1:]

    def step(self, *wait):
        if not self.order:
            return
        dim, axis, bit, mine = self.order.pop(0)
        self.value, self.send = halve(self.value, dim, axis, bit, mine, wait)

    def rows(self):
        return self.value.reshape(self.value.shape[2:])


def core_rows(value, core):
    shards = lax.axis_size("shard")
    size = value.shape[1] // shards
    even = [value[:, at * size : (at + 1) * size] for at in range(0, shards, 2)]
    odd = [value[:, at * size : (at + 1) * size] for at in range(1, shards, 2)]
    own = [jnp.where(core == 0, a, b) for a, b in zip(even, odd)]
    rest = [jnp.where(core == 0, b, a) for a, b in zip(even, odd)]
    return jnp.concatenate(own, 1), jnp.concatenate(rest, 1)


def after(value, *others):
    return lax.optimization_barrier((value,) + others)[0]


def turn_blocks(value, shard):
    shards = lax.axis_size("shard")
    size = value.shape[1] // shards
    blocks = [
        lax.dynamic_slice_in_dim(value, (at ^ shard) * size, size, 1) for at in range(shards)
    ]
    return jnp.concatenate(blocks, 1)


def on_device(
    hidden,
    cotangent,
    seg_ids,
    norm_gain,
    in_weight,
    conv_weight,
    conv_bias,
    dt_bias,
    a_log,
    d_skip,
    out_gain,
    out_weight,
):
    shards, places = (lax.axis_size("shard"), lax.axis_size("seq"))
    shard, place = (lax.axis_index("shard"), lax.axis_index("seq"))
    devices = shards * places
    me = shard * places + place
    length, width = hidden.shape
    heads = dt_bias.shape[0]
    inner = out_weight.shape[0] * shards
    channels = conv_bias.shape[0] * shards
    n_state = (channels - inner) // 2
    groups = inner // WIDE
    start = me * length

    core = shard % 2
    w_in = in_weight.T
    by_hand = shards == 4 and places % 2 == 0
    edge_rows = w_in.shape[0] - 2 * inner
    small = jnp.concatenate([norm_gain, conv_weight.reshape(-1), conv_bias, out_gain])
    small_rows = pl.cdiv(small.shape[0], w_in.shape[1])
    small_rows += -(small_rows + edge_rows) % 16
    small = jnp.pad(small, (0, small_rows * w_in.shape[1] - small.shape[0]))
    edges = jnp.concatenate([w_in[2 * inner :], small.reshape(small_rows, w_in.shape[1])], 0)
    if by_hand:
        in_other = other_core(w_in)
        plan = Plan()
        plan.add([shard, shard ^ 1, shard ^ 2, shard ^ 3, place % 2])
        g_x = Gather(plan, w_in, in_other, inner, inner // 2, 2, edges)
        edge_far = lax.ppermute(edges, "shard", flip("shard", 2))
        g_z = Gather(plan, w_in, in_other, 0, inner // 2, 1, g_x.direct[1])
        pieces = [edges, other_core(edges), edge_far, other_core(edge_far)]
        edges = jnp.stack([after(piece, g_x.send) for piece in pieces])
        edges = jnp.stack([lax.dynamic_index_in_dim(edges, k ^ shard, 0, False) for k in range(4)])
    else:
        edges = lax.all_gather(edges, "shard")
    if by_hand:
        plan.close()
        g_x.share()
        g_x.cross(0)
        out_other = other_core(after(out_weight, g_x.direct[0]))
    else:
        stack_x = lax.all_gather(w_in[inner : 2 * inner], "shard")
        stack_z = lax.all_gather(w_in[:inner], "shard")
        w_out = lax.all_gather(out_weight, "shard", axis=0, tiled=True)
    w_edge = edges[:, :edge_rows].transpose(1, 0, 2).reshape(edge_rows, width)
    w_edge = jnp.pad(w_edge, ((0, -edge_rows % TILE), (0, 0)))
    small = edges[:, edge_rows:].reshape(shards, -1)
    at = 0
    gain_in = small[:, at : at + norm_gain.shape[0]].reshape(-1).astype(f32)
    at += norm_gain.shape[0]
    taps = small[:, at : at + conv_weight.size].reshape(shards, CONV, -1)
    taps = taps.transpose(1, 0, 2).reshape(CONV, channels).astype(f32)
    at += conv_weight.size
    bias = small[:, at : at + conv_bias.shape[0]].reshape(-1).astype(f32)
    at += conv_bias.shape[0]
    gain_out = small[:, at : at + out_gain.shape[0]].reshape(-1).astype(f32)
    skip_wide = jnp.repeat(d_skip.astype(f32), HEAD_DIM)
    rows = jnp.concatenate([skip_wide, jnp.zeros((channels - inner,), f32)])
    taps8 = jnp.concatenate([taps, bias[None], rows[None], jnp.zeros((2, channels), f32)], 0)

    edge = jnp.full((HALO,), -1, jnp.int32)
    padded = jnp.concatenate([edge, seg_ids, edge - 1])
    near = lax.dynamic_slice_in_dim(padded, start, length + 2 * HALO)
    seg = near[HALO : HALO + length]
    fwd_masks = [near[HALO - CONV + 1 + k : HALO - CONV + 1 + k + length] == seg for k in range(3)]
    spot = jnp.arange(length, dtype=jnp.int32)
    bwd_masks = [
        (near[HALO + CONV - 1 - k : HALO + CONV - 1 - k + length] == seg)
        & (spot + CONV - 1 - k < length)
        for k in range(3)
    ]
    from_before = seg == near[HALO - 1]
    to_last = seg == seg[length - 1]
    flags = jnp.stack(
        [m.astype(f32) for m in fwd_masks + bwd_masks + [seg, from_before, to_last]], 1
    )
    flags = jnp.pad(flags, ((0, 0), (0, 16 - flags.shape[1])))
    seg_row = jnp.broadcast_to(seg.astype(f32)[None, :], (8, length))

    behind = lax.ppermute(
        hidden[length - HALO :], ALL, [(i, i + 1) for i in range(devices - 1)]
    )
    hidden_f = jnp.concatenate([behind, hidden], 0).astype(f32)
    scale_in = lax.rsqrt(jnp.mean(hidden_f * hidden_f, axis=1, keepdims=True) + EPS)
    normed_ext = (hidden_f * scale_in * gain_in[None, :]).astype(bf16)
    normed_in = normed_ext[HALO:]
    proj_edge = mm_nt(normed_ext, w_edge).astype(bf16)
    proj_bc = proj_edge[:, : 2 * n_state]
    rates = jnp.stack([dt_bias, a_log]).astype(f32)
    rates = jnp.pad(rates, ((0, 6), (0, TILE - heads)))
    big = pltpu.CompilerParams(vmem_limit_bytes=56 * 1024 * 1024)
    per_head, spreads, cum, sums_row, masks = pl.pallas_call(
        prepare_kernel,
        out_shape=[
            jax.ShapeDtypeStruct((5, length, TILE), f32),
            jax.ShapeDtypeStruct((2, length, 2 * TILE), bf16),
            jax.ShapeDtypeStruct((groups, length, GROUP), f32),
            jax.ShapeDtypeStruct((groups, GROUP, length), f32),
            jax.ShapeDtypeStruct((2 * (CONV - 1), length, TILE), f32),
        ],
        compiler_params=big,
        name="prepare",
    )(proj_edge[HALO:, 2 * n_state :], rates, flags)
    end = two_parts(per_head[3, length - 1])
    if by_hand:
        proj = project(after(normed_ext, per_head), g_x, 0, None)
        g_out = Gather(plan, out_weight, out_other, 0, out_weight.shape[0] // 2, 1, proj, g_z.direct[0])
        g_z.share(proj)
        g_x.cross(1, proj)
        proj = project(normed_ext, g_x, 1, proj)
    else:
        proj = stacked_project(normed_ext, stack_x, 0, inner)

    def whole(shape):
        return pl.BlockSpec(shape, lambda g: (0,) * len(shape))

    def group_of(g):
        return jnp.maximum(g - 1, 0)

    order = lambda g: jnp.where(g == 0, groups, g - 1)
    x_conv, state_local, bc, bt, ct = pl.pallas_call(
        state_kernel,
        grid=(groups // SPAN,),
        in_specs=[
            pl.BlockSpec((length + HALO, SPAN * WIDE), lambda g: (0, g)),
            whole((length + HALO, WIDE)),
            pl.BlockSpec((8, SPAN * WIDE), lambda g: (0, g)),
            whole((8, WIDE)),
            whole(masks.shape),
            whole(spreads.shape),
        ],
        out_specs=[
            pl.BlockSpec((length, SPAN * WIDE), lambda g: (0, g)),
            pl.BlockSpec((n_state, SPAN * WIDE), lambda g: (0, g)),
            whole((length, 2 * n_state)),
            whole((n_state, length)),
            whole((n_state, length)),
        ],
        out_shape=[
            jax.ShapeDtypeStruct((length, inner), bf16),
            jax.ShapeDtypeStruct((n_state, inner), bf16),
            jax.ShapeDtypeStruct((length, 2 * n_state), bf16),
            jax.ShapeDtypeStruct((n_state, length), bf16),
            jax.ShapeDtypeStruct((n_state, length), bf16),
        ],
        scratch_shapes=[
            pltpu.VMEM((length + HALO, WIDE), f32),
            pltpu.VMEM((n_state, length), bf16),
        ],
        compiler_params=big,
        cost_estimate=CHEAP,
        name="mixer_state",
    )(proj, proj_bc, taps8, taps8[:, inner:], masks, spreads)

    slices = with_decay(to_slices(state_local, devices), end)
    if by_hand:
        slices = after(slices, g_out.direct[0])
        g_out.share(slices)
        sent = exchange(slices)
        g_z.cross(0, slices)
        gate_z = project(after(normed_in, slices), g_z, 0, None)
        sent = after(sent, gate_z)
    else:
        sent = exchange(slices)
        gate_z = stacked_project(normed_in, stack_z, 0, inner)
    columns = slices.shape[2] - TILE
    decays = sent[:, :, columns:]
    states = scan_devices(sent, decays, columns, me, False)
    state_in = return_slices(states, n_state, inner)
    x_conv = after(x_conv, states)
    half_t = 2 * TILE
    y_local = pl.pallas_call(
        forward_kernel,
        grid=(groups // SPAN,),
        in_specs=[
            pl.BlockSpec((length, SPAN * WIDE), lambda g: (0, g)),
            whole(flags.shape),
            whole((8, length)),
            whole(spreads.shape),
            pl.BlockSpec((SPAN, length, GROUP), lambda g: (g, 0, 0)),
            pl.BlockSpec((SPAN, GROUP, length), lambda g: (g, 0, 0)),
            whole((length, 2 * n_state)),
            whole((n_state, length)),
        ],
        out_specs=pl.BlockSpec((length, SPAN * WIDE), lambda g: (0, g)),
        out_shape=jax.ShapeDtypeStruct((length, inner), f32),
        scratch_shapes=[
            pltpu.VMEM((length, length), f32),
            pltpu.VMEM((length // half_t, GROUP * half_t, WIDE), bf16),
            pltpu.VMEM((length // half_t, length, GROUP * half_t), bf16),
        ],
        compiler_params=big,
        cost_estimate=CHEAP,
        name="mixer_forward",
    )(x_conv, flags, seg_row, spreads, cum, sums_row, bc, bt)
    if by_hand:
        g_out.cross(0, y_local)
        d_normed = out_back(after(cotangent, y_local), g_out)
    else:
        d_normed = mm_nt(cotangent, w_out)
    block = TILE
    tall = lambda dim: pl.BlockSpec((block, dim), lambda g: (g, 0))
    gains = jnp.stack([gain_out, skip_wide], 0)
    ssm, normed_out, d_z, d_y, d_state_local, dc_more, d_gain = pl.pallas_call(
        lambda *refs: gate_kernel(shards, *refs),
        grid=(length // block,),
        in_specs=[
            tall(inner),
            tall(inner),
            tall(inner),
            tall(inner),
            tall(2 * n_state),
            pl.BlockSpec((n_state, block), lambda g: (0, g)),
            pl.BlockSpec((None, block, TILE), lambda g: (3, g, 0)),
            whole((n_state, inner)),
            whole((2, inner)),
        ],
        out_specs=[
            tall(inner),
            pl.BlockSpec((2, block, inner // 2), lambda g: (0, g, 0)),
            tall(inner),
            tall(inner),
            whole((n_state, inner)),
            tall(n_state),
            whole((8, inner)),
        ],
        out_shape=[
            jax.ShapeDtypeStruct((length, inner), f32),
            jax.ShapeDtypeStruct((2, length, inner // 2), bf16),
            jax.ShapeDtypeStruct((length, inner), bf16),
            jax.ShapeDtypeStruct((length, inner), bf16),
            jax.ShapeDtypeStruct((n_state, inner), bf16),
            jax.ShapeDtypeStruct((length, n_state), f32),
            jax.ShapeDtypeStruct((8, inner), f32),
        ],
        scratch_shapes=[
            pltpu.VMEM((block, inner), f32),
            pltpu.VMEM((block, inner), f32),
            pltpu.VMEM((block, inner), bf16),
            pltpu.VMEM((n_state, inner), f32),
        ],
        compiler_params=big,
        cost_estimate=CHEAP,
        name="mixer_gate",
    )(y_local, x_conv, gate_z, d_normed, bc, ct, per_head, state_in, gains)

    slices = to_slices(d_state_local, devices)
    sent = exchange(slices)
    normed_out, d_z = (after(normed_out, slices), after(d_z, slices))

    def both(value):
        return jnp.concatenate([value, other_core(value)], 0)

    def both_rows(value):
        own, rest = core_rows(value, core)
        return jnp.concatenate([own, other_core(rest)], 0)

    normed_pair = both_rows(normed_in)
    cot_pair = both(cotangent)
    pick = lambda at: lax.dynamic_index_in_dim(normed_out, at, 0, False)
    out_pair = jnp.concatenate([pick(core), other_core(pick(1 - core))], 0)
    z_pair = both(d_z)
    if by_hand:
        block_out = out_forward(normed_out, hidden, g_out)
    else:
        size = inner // shards
        parts = [
            normed_out[at % 2, :, (at // 2) * size : (at // 2 + 1) * size] for at in range(shards)
        ]
        block_out = (hidden.astype(f32) + mm(jnp.concatenate(parts, 1), w_out)).astype(bf16)
    grad_o = mm_tn(after(out_pair, block_out), cot_pair).astype(bf16)
    states = scan_devices(after(sent, grad_o), decays, columns, me, True)
    returned = exchange(states)
    z_pair = after(z_pair, states)
    half_z = inner // 2
    grad_z = [mm_tn(normed_pair, z).astype(bf16) for z in (z_pair[:, :half_z], z_pair[:, half_z:])]
    x_conv = after(x_conv, grad_o, *grad_z)

    dxs, db_in, dc_in = pl.pallas_call(
        inside_kernel,
        grid=(groups,),
        in_specs=[
            pl.BlockSpec((length, WIDE), lambda g: (0, g)),
            whole(flags.shape),
            whole((8, length)),
            whole(spreads.shape),
            pl.BlockSpec((1, length, GROUP), lambda g: (g, 0, 0)),
            pl.BlockSpec((1, GROUP, length), lambda g: (g, 0, 0)),
            whole((length, 2 * n_state)),
            whole((n_state, length)),
            pl.BlockSpec((length, WIDE), lambda g: (0, g)),
        ],
        out_specs=[
            pl.BlockSpec((length, WIDE), lambda g: (0, g)),
            whole((length, n_state)),
            whole((length, n_state)),
        ],
        out_shape=[
            jax.ShapeDtypeStruct((length, inner), f32),
            jax.ShapeDtypeStruct((length, n_state), f32),
            jax.ShapeDtypeStruct((length, n_state), f32),
        ],
        scratch_shapes=[
            pltpu.VMEM((length, length), f32),
            pltpu.VMEM((length, length), f32),
            pltpu.VMEM((length // half_t, GROUP * half_t, WIDE), bf16),
            pltpu.VMEM((length // half_t, length, GROUP * half_t), bf16),
            pltpu.VMEM((GROUP, length, WIDE), bf16),
            pltpu.VMEM((2, length, length), f32),
        ],
        compiler_params=big,
        cost_estimate=CHEAP,
        name="mixer_inside",
    )(x_conv, flags, seg_row, spreads, cum, sums_row, bc, ct, d_y)

    d_state = from_slices(after(returned, dxs), n_state, inner)
    grad_o, *grad_z = lax.optimization_barrier((grad_o, *grad_z, dxs))[:3]

    def halves(grad):
        half = grad.shape[1] // 2
        return [RowSum(grad[:, :half], True), RowSum(grad[:, half:], False)]

    def step(wait, *chains):
        for chain in chains:
            chain.step(wait)

    taps8 = jnp.pad(taps8, ((0, 0), (0, WIDE)))

    def outside(first_group, count, final, grad, running):
        kept = lambda g: jnp.minimum(g, count - 1) + first_group
        steps = count + (2 if final else 0)
        columns = steps * WIDE
        tall = lambda: pl.BlockSpec((length, WIDE), lambda g: (0, kept(g)))
        flat = lambda: pl.BlockSpec((n_state, WIDE), lambda g: (0, kept(g)))
        return pl.pallas_call(
            lambda *refs: outside_kernel(first_group, count, final, len(running) > 0, *refs),
            grid=(steps,),
            in_specs=[
                pl.BlockSpec((length + HALO, WIDE), lambda g: (0, kept(g))),
                whole((length + HALO, WIDE)),
                pl.BlockSpec((8, WIDE), lambda g: (0, first_group + g)),
                whole(masks.shape),
                whole(spreads.shape),
                whole(per_head.shape),
                whole(rates.shape),
                whole((length, 2 * n_state)),
                tall(),
                tall(),
                tall(),
                flat(),
                flat(),
                whole((length, n_state)),
                whole((length, n_state)),
                whole((length, n_state)),
                *[whole(value.shape) for value in running],
            ],
            out_specs=[
                pl.BlockSpec((length, WIDE), lambda g: (0, g)),
                pl.BlockSpec((HALO, WIDE), lambda g: (0, g)),
                pl.BlockSpec((HALO, WIDE), lambda g: (0, g)),
                pl.BlockSpec((8, WIDE), lambda g: (0, g)),
                whole((8, TILE)),
                whole((length, n_state)),
                whole((2, length, TILE)),
                whole((8, TILE)),
            ],
            out_shape=[
                jax.ShapeDtypeStruct((length, columns), bf16),
                jax.ShapeDtypeStruct((HALO, columns), f32),
                jax.ShapeDtypeStruct((HALO, columns), f32),
                jax.ShapeDtypeStruct((8, columns), f32),
                jax.ShapeDtypeStruct((8, TILE), f32),
                jax.ShapeDtypeStruct((length, n_state), f32),
                jax.ShapeDtypeStruct((2, length, TILE), f32),
                jax.ShapeDtypeStruct((8, TILE), f32),
            ],
            scratch_shapes=[
                pltpu.VMEM((length + HALO, WIDE), f32),
                pltpu.VMEM((length + HALO, WIDE), f32),
            ],
            compiler_params=big,
            cost_estimate=CHEAP,
            name="mixer_outside",
        )(proj, proj_bc, taps8, masks, spreads, per_head, rates, bc, grad, ssm, dxs, d_state,
          state_in, db_in, dc_in, dc_more, *running)

    seg_end = near[length : length + 2 * HALO]

    def finish(grads, first, last, start):
        ahead = lax.ppermute(first, ALL, [(i + 1, i) for i in range(devices - 1)])
        joined = jnp.concatenate([jnp.zeros_like(first), ahead], 0)
        for tap in range(CONV - 1):
            lead = CONV - 1 - tap
            same = (seg_end[lead : lead + HALO] == seg_end[:HALO]).astype(f32)[:, None]
            here = taps8[tap, start : start + first.shape[1]]
            last = last + here[None, :] * joined[lead : lead + HALO] * same
        count = min(channels - start, first.shape[1])
        return lax.dynamic_update_slice(grads, last[:, :count].astype(bf16), (length - HALO, 0))

    running = ()
    part = groups // 2
    half_x = part * WIDE

    values = lambda *chains: [chain.value for chain in chains]
    sums_o = halves(grad_o)
    d_one, first, last, sums_one, _, *running = outside(0, part, False, d_y, running)
    step(d_one, *sums_o)
    d_one = finish(d_one, first, last, 0)
    one_pair = both(d_one)
    if by_hand:
        d_normed_in = back([after(d_z, sums_one, *values(*sums_o))], g_z, None)
    else:
        d_normed_in = stacked_back(d_z, stack_z, 0)
    step(d_normed_in, *sums_o)
    grad_z = lax.optimization_barrier((*grad_z, sums_one))[:2]
    sums_z = [RowSum(grad_z[0], True), RowSum(grad_z[1], False)]
    grad_x = mm_tn(normed_pair, after(one_pair, d_normed_in)).astype(bf16)
    grad = after(d_y, grad_x, *values(*sums_o))
    d_two, first, last, sums_two, head_sums, *_ = outside(part, groups - part, True, grad, running)
    sum_a = RowSum(grad_x, True)
    step(d_two, sum_a)
    d_two, first, last = lax.optimization_barrier((d_two, first, last, sum_a.value))[:3]
    step(d_two, *sums_z, *sums_o)
    sums = jnp.concatenate([sums_one, sums_two], 1)
    d_two = finish(d_two, first, last, half_x)
    two_pair = both(d_two)
    count = inner - half_x
    edge = d_two[:, count : count + w_edge.shape[0]]
    d_normed_in = d_normed_in + mm(edge, w_edge)
    grad_y = mm_tn(normed_pair, after(two_pair, d_normed_in, *values(*sums_z, *sums_o))).astype(bf16)
    step(grad_y, *sums_z, *sums_o)
    sums_b = halves(grad_y)
    if by_hand:
        last_values = [d_one, after(d_two, grad_y, *values(*sums_z))]
        norm = (hidden, cotangent, gain_in[None])
        grad_hidden, grad_gain_in = back(last_values, g_x, d_normed_in, norm)
    else:
        d_x = jnp.concatenate([d_one, d_two[:, :count]], 1)
        d_normed_in = d_normed_in + stacked_back(d_x, stack_x, 0)
        base = hidden.astype(f32)
        scale = scale_in[HALO:]
        d_hat = d_normed_in * gain_in[None, :]
        mean = jnp.mean(d_hat * base, axis=1, keepdims=True)
        grad_hidden = cotangent.astype(f32) + scale * d_hat - base * (scale * scale * scale * mean)
        grad_gain_in = (d_normed_in * base * scale).reshape(-1, 8, width).sum(0)
    step(grad_gain_in, *sums_b)
    sums_x = [sum_a] + sums_b
    step(sums_b[0].value, sum_a, *sums_z)
    step(sum_a.value, *sums_b)
    grad_gain_in = after(grad_gain_in, *values(*sums_b))
    step(sums_b[0].value, sum_a, *sums_z)
    while any(chain.order for chain in sums_o + sums_z + sums_x):
        step(grad_gain_in, *sums_b)
        step(sums_b[0].value, sum_a, *sums_z, *sums_o)
    counts = [width // devices] + [channels // devices] * (CONV + 1) + [inner // devices]
    counts += [heads] * 3
    total = sum(counts)
    if by_hand:
        sizes = (width // devices, channels // devices, inner // devices, heads)
        packed = pl.pallas_call(
            lambda *refs: pack_kernel(sizes, *refs),
            out_shape=jax.ShapeDtypeStruct((devices, 1, total + -total % TILE), f32),
            name="pack",
        )(sums[:, :channels], grad_gain_in, d_gain, head_sums)
    else:
        slots = lambda v: v.reshape(-1, devices, v.shape[-1] // devices).transpose(1, 0, 2)
        same = jnp.broadcast_to(head_sums[:3, :heads].reshape(1, -1), (devices, 3 * heads))
        pieces = [slots(grad_gain_in.sum(0)), slots(sums[: CONV + 1, :channels])]
        pieces += [slots(jnp.sum(d_gain, 0)), same]
        packed = jnp.concatenate([p.reshape(devices, -1) for p in pieces], 1)[:, None]
    packed = exchange(packed).sum((0, 1))
    found, at = ([], 0)
    for size in counts:
        found.append(packed[at : at + size])
        at += size

    grads = [c.rows().astype(f32) for c in sums_z + sums_x]
    excess = sum(g.shape[1] for g in grads) - w_in.shape[0]
    grads[-1] = grads[-1][:, : grads[-1].shape[1] - excess]
    return (
        block_out,
        grad_hidden,
        found[0],
        jnp.concatenate(grads, 1),
        jnp.stack(found[1 : CONV + 1]),
        found[CONV + 1],
        found[CONV + 3],
        found[CONV + 4],
        found[CONV + 5],
        found[CONV + 2],
        jnp.concatenate([c.rows().astype(f32) for c in sums_o], 1),
    )


def solution(mesh):
    return jax.shard_map(
        on_device,
        mesh=mesh,
        in_specs=(
            P(ALL, None),
            P(ALL, None),
            P(),
            P("shard"),
            P("shard", None),
            P(None, "shard"),
            P("shard"),
            P(),
            P(),
            P(),
            P("shard"),
            P("shard", None),
        ),
        out_specs=(
            P(ALL, None),
            P(ALL, None),
            P(ALL),
            P(ALL, None),
            P(None, ALL),
            P(ALL),
            P(),
            P(),
            P(),
            P(ALL),
            P(ALL, None),
        ),
        check_vma=False,
    )
```

```python
import jax
import jax.numpy as jnp
from jax import lax
from jax.experimental import pallas as pl
from jax.experimental.pallas import tpu as pltpu
from jax.sharding import PartitionSpec as P

HEAD_DIM = 64
CONV = 4
EPS = 1e-05
HALO = 8
GROUP = 4
WIDE = GROUP * HEAD_DIM
TILE = 128
PIECE = 3 * WIDE
SPAN = 2
HIGH = lax.Precision.HIGHEST
ALL = ("shard", "seq")
f32 = jnp.float32
bf16 = jnp.bfloat16
CHEAP = pl.CostEstimate(flops=1, bytes_accessed=1, transcendentals=0)


def mm(a, b):
    return jnp.dot(a, b, preferred_element_type=f32)


def mm_nt(a, b):
    return lax.dot_general(a, b, (((1,), (1,)), ((), ())), preferred_element_type=f32)


def mm_tn(a, b):
    return lax.dot_general(a, b, (((0,), (0,)), ((), ())), preferred_element_type=f32)


def sigmoid(value):
    return 0.5 * jnp.tanh(0.5 * value) + 0.5


def head_lanes(group):
    lane = lax.rem(lax.broadcasted_iota(jnp.int32, (2 * TILE, WIDE), 0), TILE)
    owner = lax.broadcasted_iota(jnp.int32, (2 * TILE, WIDE), 1) // HEAD_DIM + GROUP * group
    return jnp.where(lane == owner, 1.0, 0.0).astype(bf16)


def two_parts(value):
    high = value.astype(bf16)
    low = (value - high.astype(f32)).astype(bf16)
    return high, low


def twice(value):
    return jnp.concatenate([value, value], 1)


def conv_rows(wide, taps, masks, start, rows):
    pre = taps[CONV : CONV + 1, :] + taps[CONV - 1 : CONV, :] * wide[pl.ds(HALO + start, rows), :]
    for tap in range(CONV - 1):
        shifted = wide[pl.ds(HALO - CONV + 1 + tap + start, rows), :]
        pre = pre + taps[tap : tap + 1, :] * shifted * twice(masks[tap, pl.ds(start, rows), :])
    return pre


def prepare_kernel(edge, rates, flags, out, spread_out, cum_out, row_out, masks_out):
    length = out.shape[1]
    shifted = edge[...].astype(f32) + rates[0:1, :]
    step = jax.nn.softplus(shifted)
    here = lax.broadcasted_iota(jnp.int32, (length, length), 0)
    there = lax.broadcasted_iota(jnp.int32, (length, length), 1)
    lower = jnp.where(here >= there, 1.0, 0.0)
    log_decay = -step * jnp.exp(rates[1:2, :])
    cum = lax.dot_general(
        lower, log_decay, (((1,), (0,)), ((), ())), precision=HIGH, preferred_element_type=f32
    )
    keep = jnp.exp(cum[length - 1 : length, :] - cum) * flags[:, 8:9]
    out[0] = cum
    out[1] = step
    out[2] = keep
    out[3] = jnp.exp(cum) * flags[:, 7:8]
    out[4] = sigmoid(shifted)
    for at, value in enumerate((step, keep)):
        high, low = two_parts(value)
        spread_out[at, :, :TILE] = high
        spread_out[at, :, TILE:] = low
    turned = cum.T
    for group in range(row_out.shape[0]):
        heads = slice(GROUP * group, GROUP * (group + 1))
        row_out[group] = turned[heads, :]
        cum_out[group] = cum[:, heads]
    for at in range(2 * (CONV - 1)):
        masks_out[at] = jnp.broadcast_to(flags[:, at : at + 1], (length, TILE))


def span(sub):
    return pl.ds(pl.multiple_of(sub * WIDE, WIDE), WIDE)


def state_kernel(
    raw, raw_bc, taps, taps_bc, masks, spreads, x_out, state_out, bc_out, bt_out, ct_out, wide, bt
):
    length = x_out.shape[0]
    n_state = bt.shape[0]
    step = pl.program_id(0)

    @pl.when(step == 0)
    def _():
        wide[...] = raw_bc[...].astype(f32)
        tap = taps_bc[...]
        for start in range(0, length, TILE):
            rows = pl.ds(start, TILE)
            pre = conv_rows(wide, tap, masks, start, TILE)
            both = pre * sigmoid(pre)
            bc_out[rows, :] = both.astype(bf16)
            turned = both[:, :n_state].T.astype(bf16)
            bt[:, rows] = turned
            bt_out[:, rows] = turned
            ct_out[:, rows] = both[:, n_state:].T.astype(bf16)

    def one(sub, carry):
        columns = span(sub)
        wide[...] = raw[:, columns].astype(f32)
        tap = taps[:, columns]
        lanes = head_lanes(SPAN * step + sub)
        kept = []
        for start in range(0, length, TILE):
            rows = pl.ds(start, TILE)
            pre = conv_rows(wide, tap, masks, start, TILE)
            x = (pre * sigmoid(pre)).astype(bf16)
            x_out[rows, columns] = x
            scaled = (x.astype(f32) * mm(spreads[0, rows, :], lanes)).astype(bf16)
            kept.append((scaled.astype(f32) * mm(spreads[1, rows, :], lanes)).astype(bf16))
        state_out[:, columns] = mm(bt[...], jnp.concatenate(kept, 0)).astype(bf16)
        return carry

    lax.fori_loop(0, SPAN, one, 0)


def scored(first, second, flags, seg_row, score, later):
    length = score.shape[0]
    for start in range(0, length, TILE):
        rows = pl.ds(start, TILE)
        product = mm(first(rows), second[...])
        here = lax.broadcasted_iota(jnp.int32, (TILE, length), 0) + start
        there = lax.broadcasted_iota(jnp.int32, (TILE, length), 1)
        order = (here >= there) if later else (here <= there)
        seen = (flags[rows, 6:7] == seg_row[0:1, :]) & order
        score[rows, :] = jnp.where(seen, product, 0.0)


def by_head(value):
    owner = lax.broadcasted_iota(jnp.int32, value.shape, 1) // HEAD_DIM
    zero = jnp.zeros_like(value)
    return [jnp.where(owner == head, value, zero) for head in range(GROUP)]


def forward_kernel(x_in, flags, seg_row, spreads, cum, sums_row, bc, bt, y_out, score, apart, weights):
    length = y_out.shape[0]
    n_state = bt.shape[0]
    step = pl.program_id(0)
    big = weights.shape[2] // GROUP

    @pl.when(step == 0)
    def _():
        scored(lambda rows: bc[rows, n_state:], bt, flags, seg_row, score, True)
        weights[...] = jnp.zeros_like(weights)

    def one(sub, carry):
        columns = span(sub)
        lanes = head_lanes(SPAN * step + sub)
        for start in range(0, length, TILE):
            rows = pl.ds(start, TILE)
            scaled = x_in[rows, columns].astype(f32) * mm(spreads[0, rows, :], lanes)
            for head, value in enumerate(by_head(scaled)):
                apart[start // big, pl.ds(head * big + start % big, TILE), :] = value.astype(bf16)
        for head in range(GROUP):
            for start in range(0, length, TILE):
                rows = pl.ds(start, TILE)
                for at in range(0, start + TILE, big):
                    end = min(at + big, start + TILE)
                    gap = cum[sub, rows, head : head + 1] - sums_row[sub, head : head + 1, at:end]
                    weight = jnp.exp(jnp.minimum(gap, 0.0)) * score[rows, at:end]
                    weights[at // big, rows, head * big : head * big + end - at] = weight.astype(bf16)
        for at in range(0, length, big):
            part = mm(weights[at // big, at:, :], apart[at // big])
            if at == 0:
                y_out[:, columns] = part
            else:
                y_out[at:, columns] += part
        return carry

    lax.fori_loop(0, SPAN, one, 0)


def gate_kernel(
    shards, y_in, x_in, z_in, dn_in, bc, ct, enter, state, gain, ssm_out, norm_out, dz_out, dy_out,
    ds_out, dc_out, dg_out, gated_s, sig_s, mo_s, ds_acc
):
    rows = y_in.shape[0]
    width = y_in.shape[1]
    n_state = state.shape[0]
    step = pl.program_id(0)
    lane = lax.broadcasted_iota(jnp.int32, (rows, 2 * HEAD_DIM), 1)
    c_mat = bc[:, n_state:]

    @pl.when(step == 0)
    def _():
        ds_acc[...] = jnp.zeros_like(ds_acc)
        dg_out[...] = jnp.zeros_like(dg_out)

    def entering(block):
        low = enter[:, 2 * block : 2 * block + 1]
        top = enter[:, 2 * block + 1 : 2 * block + 2]
        return jnp.where(lane < HEAD_DIM, low, top)

    square = jnp.zeros((rows, 2 * HEAD_DIM), f32)
    cross = jnp.zeros((rows, 2 * HEAD_DIM), f32)
    for block in range(width // (2 * HEAD_DIM)):
        lanes = slice(block * 2 * HEAD_DIM, (block + 1) * 2 * HEAD_DIM)
        ssm = y_in[:, lanes] + entering(block) * mm(c_mat, state[:, lanes])
        ssm_out[:, lanes] = ssm
        mo = (ssm + gain[1:2, lanes] * x_in[:, lanes].astype(f32)).astype(bf16)
        mo_s[:, lanes] = mo
        z = z_in[:, lanes].astype(f32)
        sig = sigmoid(z)
        gated = mo.astype(f32) * (z * sig)
        gated_s[:, lanes] = gated
        sig_s[:, lanes] = sig
        square = square + gated * gated
        cross = cross + gated * (dn_in[:, lanes].astype(f32) * gain[0:1, lanes])
    scale = lax.rsqrt(jnp.sum(square, axis=1, keepdims=True) * (1.0 / width) + EPS)
    pull = scale * scale * scale * (jnp.sum(cross, axis=1, keepdims=True) * (1.0 / width))
    dc = jnp.zeros((rows, n_state), f32)
    for block in range(width // (2 * HEAD_DIM)):
        lanes = slice(block * 2 * HEAD_DIM, (block + 1) * 2 * HEAD_DIM)
        gated = gated_s[:, lanes]
        sig = sig_s[:, lanes]
        silu = z_in[:, lanes].astype(f32) * sig
        dn = dn_in[:, lanes].astype(f32)
        hat = gated * scale
        size = width // shards
        owner, at = divmod(block * 2 * HEAD_DIM, size)
        at += (owner // 2) * size
        norm_out[owner % 2, :, at : at + 2 * HEAD_DIM] = (hat * gain[0:1, lanes]).astype(bf16)
        part = dn * hat
        total = part[0:8, :]
        for at in range(8, rows, 8):
            total = total + part[at : at + 8, :]
        dg_out[:, lanes] += total
        d_gated = scale * (dn * gain[0:1, lanes]) - gated * pull
        dy = (d_gated * silu).astype(bf16)
        dy_out[:, lanes] = dy
        mo = mo_s[:, lanes].astype(f32)
        dz_out[:, lanes] = (d_gated * mo * (sig + silu * (1.0 - sig))).astype(bf16)
        weighted = (dy.astype(f32) * entering(block)).astype(bf16)
        ds_acc[:, lanes] += mm(ct[...], weighted)
        dc = dc + mm_nt(weighted, state[:, lanes])
    dc_out[...] = dc

    @pl.when(step == pl.num_programs(0) - 1)
    def _():
        ds_out[...] = ds_acc[...].astype(bf16)


def inside_kernel(
    x_in, flags, seg_row, spreads, cum, sums_row, bc, ct, dy, dxs_out, db_out, dc_out, score, pair,
    apart, weights, xs, crossed
):
    length = dxs_out.shape[0]
    n_state = ct.shape[0]
    group = pl.program_id(0)
    big = weights.shape[2] // GROUP

    @pl.when(group == 0)
    def _():
        pair[...] = jnp.zeros_like(pair)
        weights[...] = jnp.zeros_like(weights)
        scored(lambda rows: bc[rows, :n_state], ct, flags, seg_row, score, False)

    lanes = head_lanes(group)
    for start in range(0, length, TILE):
        rows = pl.ds(start, TILE)
        scaled = x_in[rows, :].astype(f32) * mm(spreads[0, rows, :], lanes)
        for head, value in enumerate(by_head(scaled)):
            xs[head, rows, :] = value.astype(bf16)
        for head, value in enumerate(by_head(dy[rows, :].astype(f32))):
            apart[start // big, pl.ds(head * big + start % big, TILE), :] = value.astype(bf16)
    for head in range(GROUP):
        for at in range(0, length, big):
            end = at + big
            crossed[head % 2, :end, at:end] = mm_nt(xs[head, :end, :], dy[at:end, :])
        for start in range(0, length, TILE):
            rows = pl.ds(start, TILE)
            for at in range(start // big * big, length, big):
                first = max(at, start)
                end = at + big
                gap = sums_row[0, head : head + 1, first:end] - cum[0, rows, head : head + 1]
                decay = jnp.exp(jnp.minimum(gap, 0.0))
                weight = (decay * score[rows, first:end]).astype(bf16)
                weights[at // big, rows, head * big + first - at : (head + 1) * big] = weight
                pair[rows, first:end] += decay * crossed[head % 2, rows, first:end]
    for at in range(length - big, -1, -big):
        end = at + big
        part = mm(weights[at // big, :end, :], apart[at // big])
        if end == length:
            dxs_out[...] = part
        else:
            dxs_out[:end, :] += part

    @pl.when(group == pl.num_programs(0) - 1)
    def _():
        for start in range(0, length, TILE):
            rows = pl.ds(start, TILE)
            here = lax.broadcasted_iota(jnp.int32, (TILE, length), 0) + start
            there = lax.broadcasted_iota(jnp.int32, (TILE, length), 1)
            seen = (flags[rows, 6:7] == seg_row[0:1, :]) & (here <= there)
            part = jnp.where(seen, pair[rows, :], 0.0).astype(bf16)
            db_out[rows, :] = mm(part, bc[:, n_state:])
            if start == 0:
                dc_out[...] = mm_tn(part, bc[rows, :n_state])
            else:
                dc_out[...] += mm_tn(part, bc[rows, :n_state])


def split_mm(value, chosen):
    high, low = two_parts(value)
    return mm(high, chosen) + mm(low, chosen)


def outside_kernel(first_group, count, final, running, *refs):
    (raw, raw_bc, taps, masks, spreads, heads, rates, bc, dy, ssm, dxs_in, d_state, state, db_in,
     dc_in, dc_more, *started, d_out, first_out, last_out, sums_out,
     head_out, db_acc, found, totals_s, wide, d_pre) = refs
    length = d_out.shape[0]
    n_state = bc.shape[1] // 2
    step = pl.program_id(0)
    bc_step = count

    @pl.when(step == 0)
    def _():
        for at, ref in enumerate((db_acc, found, totals_s)):
            ref[...] = started[at][...] if running else jnp.zeros_like(ref)

    d_pre[pl.ds(length, HALO), :] = jnp.zeros((HALO, d_pre.shape[1]), f32)
    zero = jnp.zeros((1, d_pre.shape[1]), f32)

    @pl.when(step < bc_step)
    def _():
        wide[...] = raw[...].astype(f32)
        skip_sum, keep_sum = (zero, zero)
        ds = d_state[...]
        group = step + first_group
        lanes = head_lanes(group)
        owner = lax.broadcasted_iota(jnp.int32, (WIDE, TILE), 0) // HEAD_DIM + GROUP * group
        chosen = (owner == lax.broadcasted_iota(jnp.int32, (WIDE, TILE), 1)).astype(f32)
        chosen_b = chosen.astype(bf16)
        for start in range(0, length, TILE):
            rows = pl.ds(start, TILE)
            pre = conv_rows(wide, taps, masks, start, TILE)
            sig = sigmoid(pre)
            x = pre * sig
            stepped = mm(spreads[0, rows, :], lanes)
            scaled = (x.astype(bf16).astype(f32) * stepped).astype(bf16)
            keep = mm(spreads[1, rows, :], lanes)
            carried = keep * mm(bc[rows, :n_state], ds)
            dxs = dxs_in[rows, :] + carried
            scaled = scaled.astype(f32)
            db_acc[rows, :] += mm_nt((scaled * keep).astype(bf16), ds)
            grad = dy[rows, :].astype(f32)
            keep_sum = keep_sum + jnp.sum(scaled * carried, 0, keepdims=True)
            skip_sum = skip_sum + jnp.sum(grad * x, 0, keepdims=True)
            found[0, rows, :] += split_mm(grad * ssm[rows, :] - scaled * dxs, chosen_b)
            found[1, rows, :] += split_mm(x * dxs, chosen_b)
            d_x = taps[5:6, :] * grad + stepped * dxs
            d_pre[rows, :] = d_x * (sig + x * (1.0 - sig))
        met = jnp.sum(ds.astype(f32) * state[...].astype(f32), 0, keepdims=True)
        rest = jnp.zeros((5, WIDE), f32)
        totals_s[...] += lax.dot_general(
            jnp.concatenate([skip_sum, keep_sum, met, rest], 0),
            chosen,
            (((1,), (0,)), ((), ())),
            precision=HIGH,
            preferred_element_type=f32,
        )

    if final:

        @pl.when(step == bc_step)
        def _():
            wide[...] = raw_bc[...].astype(f32)
            for start in range(0, length, TILE):
                rows = pl.ds(start, TILE)
                pre = conv_rows(wide, taps, masks, start, TILE)
                sig = sigmoid(pre)
                slope = sig + pre * sig * (1.0 - sig)
                d_b = db_in[rows, :] + db_acc[rows, :]
                d_c = dc_in[rows, :] + dc_more[rows, :]
                d_pre[rows, :] = jnp.concatenate([d_b, d_c], 1) * slope

    @pl.when(step <= bc_step)
    def _():
        totals = [zero] * (CONV + 1)
        for start in range(0, length, TILE):
            rows = pl.ds(start, TILE)
            grad = d_pre[rows, :]
            totals[CONV] = totals[CONV] + jnp.sum(grad, 0, keepdims=True)
            here = wide[pl.ds(HALO + start, TILE), :]
            totals[CONV - 1] = totals[CONV - 1] + jnp.sum(grad * here, 0, keepdims=True)
            back = taps[CONV - 1 : CONV, :] * grad
            for tap in range(CONV - 1):
                shifted = wide[pl.ds(HALO - CONV + 1 + tap + start, TILE), :]
                masked = grad * twice(masks[tap, rows, :])
                totals[tap] = totals[tap] + jnp.sum(masked * shifted, 0, keepdims=True)
                ahead = d_pre[pl.ds(start + CONV - 1 - tap, TILE), :]
                back = back + taps[tap : tap + 1, :] * ahead * twice(masks[3 + tap, rows, :])
            d_out[rows, :] = back.astype(bf16)
            if start + TILE == length:
                last_out[...] = back[TILE - HALO :, :]
        first_out[...] = d_pre[pl.ds(0, HALO), :]
        for tap in range(CONV + 1):
            sums_out[tap : tap + 1, :] = totals[tap]
        sums_out[CONV + 1 : 8, :] = jnp.zeros((7 - CONV, d_pre.shape[1]), f32)

    if not final:
        head_out[...] = jnp.zeros_like(head_out)
        return

    @pl.when(step == bc_step + 1)
    def _():
        first_out[...] = jnp.zeros_like(first_out)
        last_out[...] = jnp.zeros_like(last_out)
        sums_out[...] = jnp.zeros_like(sums_out)
        rate = jnp.exp(rates[1:2, :])
        end = totals_s[1:2, :] + heads[3, pl.ds(length - 1, 1), :] * totals_s[2:3, :]
        here = lax.broadcasted_iota(jnp.int32, (length, length), 0)
        there = lax.broadcasted_iota(jnp.int32, (length, length), 1)
        upper = jnp.where(here <= there, 1.0, 0.0)
        d_log = lax.dot_general(
            upper, found[0], (((1,), (0,)), ((), ())), precision=HIGH, preferred_element_type=f32
        )
        d_log = d_log + end
        d_dt = (found[1] - rate * d_log) * heads[4]
        d_out[:, :TILE] = d_dt.astype(bf16)
        d_out[:, TILE:] = jnp.zeros((length, WIDE - TILE), bf16)
        head_out[0:1, :] = jnp.sum(d_dt, 0, keepdims=True)
        head_out[1:2, :] = jnp.sum(d_log * (-heads[1] * rate), 0, keepdims=True)
        head_out[2:3, :] = totals_s[0:1, :]
        head_out[3:8, :] = jnp.zeros((5, TILE), f32)


def pack_kernel(sizes, sums, gain_in, gain_out, head, out):
    devices = out.shape[0]
    gain_in = jnp.sum(gain_in[...], 0, keepdims=True)
    wide, channels, inner, heads = sizes
    gains = jnp.sum(gain_out[...], 0, keepdims=True)
    for at in range(devices):
        pieces = [gain_in[:, at * wide : (at + 1) * wide]]
        for tap in range(CONV + 1):
            pieces.append(sums[tap : tap + 1, at * channels : (at + 1) * channels])
        pieces.append(gains[:, at * inner : (at + 1) * inner])
        for row in range(3):
            pieces.append(head[row : row + 1, :heads])
        begin = 0
        for piece in pieces:
            out[at, :, begin : begin + piece.shape[1]] = piece
            begin += piece.shape[1]
        if begin < out.shape[2]:
            out[at, :, begin:] = jnp.zeros((1, out.shape[2] - begin), f32)


def scan_kernel(backward, place, mine, decay, out, wide):
    count = mine.shape[0]
    columns = out.shape[2]
    for at in range(2):
        for device in range(count):
            wide[at, device : device + 1, :] = decay[device, at : at + 1, :].astype(f32)
    lane = lax.broadcasted_iota(jnp.int32, (TILE, columns), 0)
    owner = lax.broadcasted_iota(jnp.int32, (TILE, columns), 1) // HEAD_DIM + place[0]
    chosen = jnp.where(lane == owner, 1.0, 0.0).astype(bf16)
    factor = mm(wide[0].astype(bf16), chosen) + mm(wide[1].astype(bf16), chosen)
    state = jnp.zeros(out.shape[1:], f32)
    for at in reversed(range(count)) if backward else range(count):
        out[at] = state.astype(bf16)
        state = factor[at : at + 1, :] * state + mine[at, :, :columns].astype(f32)


def to_slices(value, devices):
    n_state, inner = value.shape
    across = max(1, devices // 16)
    rows = n_state * across // devices
    value = value.reshape(n_state // rows, rows, across, inner // across)
    return value.transpose(0, 2, 1, 3).reshape(devices, rows, inner // across)


def from_slices(slices, n_state, inner):
    devices, rows, columns = slices.shape
    value = slices.reshape(n_state // rows, inner // columns, rows, columns)
    return value.transpose(0, 2, 1, 3).reshape(n_state, inner)


def exchange(slices):
    return lax.all_to_all(slices, ALL, split_axis=0, concat_axis=0, tiled=True)


def return_slices(states, n_state, inner):
    return from_slices(exchange(states), n_state, inner)


def with_decay(slices, end):
    devices, rows, _ = slices.shape
    more = jnp.pad(jnp.stack(end), ((0, rows - 2), (0, 0)))
    return jnp.concatenate([slices, jnp.broadcast_to(more[None], (devices, rows, TILE))], 2)


def scan_devices(mine, decay, columns, me, backward):
    devices, rows, _ = mine.shape
    across = max(1, devices // 16)
    place = jnp.reshape((me % across) * (columns // HEAD_DIM), (1,)).astype(jnp.int32)
    vmem = pl.BlockSpec(memory_space=pltpu.VMEM)
    return pl.pallas_call(
        lambda *refs: scan_kernel(backward, *refs),
        in_specs=[pl.BlockSpec(memory_space=pltpu.SMEM), vmem, vmem],
        out_specs=vmem,
        out_shape=jax.ShapeDtypeStruct((devices, rows, columns), bf16),
        scratch_shapes=[pltpu.VMEM((2, devices, TILE), f32)],
        compiler_params=pltpu.CompilerParams(vmem_limit_bytes=40 * 1024 * 1024),
        cost_estimate=CHEAP,
        name="scan_backward" if backward else "scan_forward",
    )(place, mine, decay)


def flip(axis, bit):
    count = lax.axis_size(axis)
    return [(i, i ^ bit) for i in range(count)]


def other_core(value):
    return lax.ppermute(value, "shard", flip("shard", 1))


def turn_kernel(count, *refs):
    for at in range(count):
        refs[count + at][...] = refs[at][...].astype(f32).T.astype(bf16)


def turned(*values):
    shape = values[0].shape
    whole = pl.BlockSpec(memory_space=pltpu.VMEM)
    return pl.pallas_call(
        lambda *refs: turn_kernel(len(values), *refs),
        in_specs=[whole] * len(values),
        out_specs=[whole] * len(values),
        out_shape=[jax.ShapeDtypeStruct(shape[::-1], bf16)] * len(values),
        compiler_params=pltpu.CompilerParams(vmem_limit_bytes=40 * 1024 * 1024),
        cost_estimate=CHEAP,
        name="turn",
    )(*values)


def pair_kernel(left, left_other, value, value_other, out):
    out[...] = (mm(left[...], value[...]) + mm(left_other[...], value_other[...])).astype(bf16)


def pair_grad(lefts, value, value_other, first, count):
    rows, tokens = lefts[0].shape
    size = 2 * WIDE
    whole = pl.BlockSpec((rows, tokens), lambda g: (0, 0))
    block = pl.BlockSpec((tokens, size), lambda g: (0, first + g))
    return pl.pallas_call(
        pair_kernel,
        grid=(count,),
        in_specs=[whole, whole, block, block],
        out_specs=pl.BlockSpec((rows, size), lambda g: (0, g)),
        out_shape=jax.ShapeDtypeStruct((rows, count * size), bf16),
        compiler_params=pltpu.CompilerParams(vmem_limit_bytes=58 * 1024 * 1024),
        cost_estimate=CHEAP,
        name="pair_grad",
    )(*lefts, value, value_other)


class Plan:
    def __init__(self):
        self.values, self.array = ([], None)

    def add(self, values):
        self.values += [jnp.asarray(value, jnp.int32) for value in values]
        return len(self.values) - len(values)

    def close(self):
        self.array = jnp.stack(self.values)


class Gather:
    def __init__(self, plan, own, other, base, half, chunks, *wait):
        self.own, self.other, self.base, self.half, self.chunks = (own, other, base, half, chunks)
        self.mine = lax.axis_index("seq") % 2
        self.size = half // chunks
        self.plan = plan
        if plan.array is None:
            full, near = (half // PIECE, self.size // PIECE)
            self.order = []
            for chunk in range(chunks):
                first = chunk * near
                order = [full * self.mine + first + at for at in range(near)]
                order += [full * (1 - self.mine) + first + at for at in range(near)]
                self.order.append(plan.add(order))
            source, block = ([], [])
            for at in range(2 * full):
                place = at % full
                source.append(2 * (place // near) + jnp.where(self.mine == at // full, 0, 1))
                block.append(place % near)
            self.source, self.block = (plan.add(source), plan.add(block))
        self.direct, self.passed = ([None] * chunks, [None] * chunks)
        self.parts = [None] * chunks
        for chunk in range(chunks):
            start = base + self.mine * half + chunk * self.size
            self.send = lax.dynamic_slice_in_dim(own, start, self.size, 0)
            if chunk:
                wait = (self.direct[chunk - 1],)
            if wait:
                self.send = after(self.send, *wait)
            self.direct[chunk] = lax.ppermute(self.send, "shard", flip("shard", 2))

    def share(self, *wait):
        for chunk in range(self.chunks):
            if chunk:
                wait = (self.passed[chunk - 1],)
            if wait:
                self.direct[chunk] = after(self.direct[chunk], *wait)
            self.passed[chunk] = lax.ppermute(self.direct[chunk], "seq", flip("seq", 1))

    def cross(self, chunk, *wait):
        direct, passed = (self.direct[chunk], self.passed[chunk])
        if wait:
            direct, passed = lax.optimization_barrier((direct, passed) + wait)[:2]
        self.parts[chunk] = [direct, other_core(direct), passed, other_core(passed)]


def project_kernel(table, *refs):
    lefts, (own, other, direct, direct_o, passed, passed_o) = (refs[:4], refs[4:10])
    out, left, weight = refs[-3:]
    step = pl.program_id(0)

    @pl.when(step == 0)
    def _():
        left[...] = jnp.concatenate([a[...] for a in lefts], 1)

    def fill(far, far_o):
        deep = own.shape[1]
        weight[:, :deep] = far[...]
        weight[:, deep:] = far_o[...]

    near = pl.num_programs(0) // 2
    pl.when(step < near)(lambda: fill(direct, direct_o))
    pl.when(step >= near)(lambda: fill(passed, passed_o))
    whole = jnp.concatenate([own[...], other[...], weight[...]], 1)
    out[...] = mm_nt(left[...], whole).astype(bf16)


def project(value, gather, chunk, result):
    rows = value.shape[0]
    deep = gather.own.shape[1]
    near = gather.size // PIECE
    base = gather.base // PIECE
    order = gather.order[chunk]
    table = gather.plan.array
    block = lambda index: pl.BlockSpec((PIECE, deep), index)
    left = lambda k: pl.BlockSpec((rows, deep), lambda j, t: (0, t[k]))
    own = block(lambda j, t: (base + t[order + j], 0))
    one = block(lambda j, t: (jnp.minimum(j, near - 1), 0))
    two = block(lambda j, t: (jnp.maximum(j - near, 0), 0))
    operands = [table, *([value] * 4), gather.own, gather.other, *gather.parts[chunk]]
    in_specs = [left(k) for k in range(4)] + [own, own, one, one, two, two]
    aliases = {}
    if result is not None:
        aliases = {len(operands): 0}
        operands.append(result)
        in_specs.append(pl.BlockSpec(memory_space=pl.ANY))
    return pl.pallas_call(
        project_kernel,
        grid_spec=pltpu.PrefetchScalarGridSpec(
            num_scalar_prefetch=1,
            grid=(2 * near,),
            in_specs=in_specs,
            out_specs=pl.BlockSpec((rows, PIECE), lambda j, t: (0, t[order + j])),
            scratch_shapes=[
                pltpu.VMEM((rows, 4 * deep), bf16),
                pltpu.VMEM((PIECE, 2 * deep), bf16),
            ],
        ),
        out_shape=jax.ShapeDtypeStruct((rows, 2 * gather.half), bf16),
        input_output_aliases=aliases,
        compiler_params=pltpu.CompilerParams(vmem_limit_bytes=58 * 1024 * 1024),
        cost_estimate=CHEAP,
        name="project",
    )(*operands)


def back_kernel(values, chunks, norm, source, table, *refs):
    inputs, refs = (refs[:values], refs[values:])
    own, other = refs[:2]
    far, refs = (refs[2 : 2 + 4 * chunks], refs[2 + 4 * chunks :])
    total, value, weight = refs[-3:]
    refs = refs[:-3]
    if norm:
        hidden, cotangent, gain, out, gain_out = refs[-5:]
        start = refs[:-5]
    else:
        out, start = (refs[-1], refs[:-1])
    step = pl.program_id(0)
    last = pl.num_programs(0) - 1
    deep = own.shape[1]
    place = lambda k: pl.ds(pl.multiple_of(table[k] * deep, deep), deep)

    @pl.when(step == 0)
    def _():
        if start:
            for k in range(4):
                total[:, k * deep : (k + 1) * deep] = start[0][:, place(k)]
        else:
            total[...] = jnp.zeros_like(total)

    for at in range(values):

        @pl.when((step * values // (last + 1)) == at)
        def _(at=at):
            value[...] = inputs[at][...]

    for at in range(2 * chunks):

        @pl.when(table[source + step] == at)
        def _(at=at):
            weight[:, :deep] = far[2 * at][...]
            weight[:, deep:] = far[2 * at + 1][...]

    total[...] += mm(value[...], jnp.concatenate([own[...], other[...], weight[...]], 1))

    @pl.when(step == last)
    def _():
        for k in range(4):
            out[:, place(k)] = total[:, k * deep : (k + 1) * deep]
        if norm:
            sums = jnp.zeros(gain_out.shape, f32)
            for at in range(0, out.shape[0], 64):
                rows = pl.ds(at, 64)
                base = hidden[rows, :].astype(f32)
                grad = out[rows, :]
                size = 1.0 / base.shape[1]
                scale = lax.rsqrt(jnp.sum(base * base, 1, keepdims=True) * size + EPS)
                hat = base * scale
                part = grad * hat
                for row in range(0, 64, 8):
                    sums = sums + part[row : row + 8, :]
                pull = jnp.sum(part * gain[...], 1, keepdims=True) * size
                inner = scale * (grad * gain[...] - hat * pull)
                out[rows, :] = cotangent[rows, :].astype(f32) + inner
            gain_out[...] = sums


def back(values, gather, start, norm=()):
    rows = values[0].shape[0]
    deep = gather.own.shape[1]
    count = 2 * gather.half // PIECE
    share = count // len(values)
    base = gather.base // PIECE
    table = gather.plan.array
    whole = pl.BlockSpec((rows, 4 * deep), lambda j, t: (0, 0))
    own = pl.BlockSpec((PIECE, deep), lambda j, t: (base + j, 0))
    far = pl.BlockSpec((PIECE, deep), lambda j, t: (t[gather.block + j], 0))
    in_specs = [
        pl.BlockSpec((rows, PIECE), lambda j, t, k=k: (0, jnp.clip(j - k * share, 0, share - 1)))
        for k in range(len(values))
    ]
    started = [] if start is None else [start]
    parts = [piece for chunk in gather.parts for piece in chunk]
    in_specs += [own, own] + [far] * len(parts) + [whole] * len(started)
    out_specs, out_shape = (whole, jax.ShapeDtypeStruct((rows, 4 * deep), f32))
    if norm:
        narrow = lambda count: pl.BlockSpec((count, 4 * deep), lambda j, t: (0, 0))
        in_specs += [whole, whole, narrow(1)]
        out_specs = [whole, narrow(8)]
        out_shape = [out_shape, jax.ShapeDtypeStruct((8, 4 * deep), f32)]
    return pl.pallas_call(
        lambda *refs: back_kernel(len(values), gather.chunks, len(norm) > 0, gather.source, *refs),
        grid_spec=pltpu.PrefetchScalarGridSpec(
            num_scalar_prefetch=1,
            grid=(count,),
            in_specs=in_specs,
            out_specs=out_specs,
            scratch_shapes=[
                pltpu.VMEM((rows, 4 * deep), f32),
                pltpu.VMEM((rows, PIECE), bf16),
                pltpu.VMEM((PIECE, 2 * deep), bf16),
            ],
        ),
        out_shape=out_shape,
        compiler_params=pltpu.CompilerParams(vmem_limit_bytes=58 * 1024 * 1024),
        cost_estimate=CHEAP,
        name="back",
    )(table, *values, gather.own, gather.other, *parts, *started, *norm)


def by_shard(gather):
    half, width = (gather.half, gather.own.shape[1])
    whole = pl.BlockSpec((2 * half, width), lambda g, t: (0, 0))
    part = pl.BlockSpec((half, width), lambda g, t: (0, 0))
    direct, direct_o, passed, passed_o = gather.parts[0]
    operands = [gather.own, gather.other, direct, passed, direct_o, passed_o]
    table = gather.plan.array
    return operands, [whole] * 2 + [part] * 4, table


def out_back_kernel(table, value, own, other, direct, passed, direct_o, passed_o, out):
    step = pl.program_id(0)
    half = direct.shape[0]

    def two(near, far):
        out[:, pl.ds(pl.multiple_of(table[4] * half, half), half)] = mm_nt(value[...], near[...]).astype(bf16)
        far_at = pl.multiple_of((1 - table[4]) * half, half)
        out[:, pl.ds(far_at, half)] = mm_nt(value[...], far[...]).astype(bf16)

    for at, piece in enumerate((own, other)):

        @pl.when(step == at)
        def _(piece=piece):
            out[...] = mm_nt(value[...], piece[...]).astype(bf16)

    pl.when(step == 2)(lambda: two(direct, passed))
    pl.when(step == 3)(lambda: two(direct_o, passed_o))


def out_back(value, gather):
    rows, width = value.shape
    operands, specs, table = by_shard(gather)
    size = 2 * gather.half
    return pl.pallas_call(
        out_back_kernel,
        grid_spec=pltpu.PrefetchScalarGridSpec(
            num_scalar_prefetch=1,
            grid=(4,),
            in_specs=[pl.BlockSpec((rows, width), lambda g, t: (0, 0))] + specs,
            out_specs=pl.BlockSpec((rows, size), lambda g, t: (0, t[g])),
        ),
        out_shape=jax.ShapeDtypeStruct((rows, 4 * size), bf16),
        compiler_params=pltpu.CompilerParams(vmem_limit_bytes=58 * 1024 * 1024),
        cost_estimate=CHEAP,
        name="out_back",
    )(table, value, *operands)


def out_forward_kernel(table, value, base, own, other, direct, passed, direct_o, passed_o, out, total):
    step = pl.program_id(0)
    half = direct.shape[0]

    def two(near, far):
        near_at = pl.multiple_of(table[4] * half, half)
        far_at = pl.multiple_of((1 - table[4]) * half, half)
        total[...] += mm(value[:, pl.ds(near_at, half)], near[...])
        total[...] += mm(value[:, pl.ds(far_at, half)], far[...])

    @pl.when(step == 0)
    def _():
        total[...] = base[...].astype(f32) + mm(value[...], own[...])

    @pl.when(step == 1)
    def _():
        total[...] += mm(value[...], other[...])

    pl.when(step == 2)(lambda: two(direct, passed))

    @pl.when(step == 3)
    def _():
        two(direct_o, passed_o)
        out[...] = total[...].astype(bf16)


def out_forward(value, base, gather):
    rows = value.shape[1]
    operands, specs, table = by_shard(gather)
    size = 2 * gather.half
    width = gather.own.shape[1]
    fixed = pl.BlockSpec((rows, width), lambda g, t: (0, 0))
    return pl.pallas_call(
        out_forward_kernel,
        grid_spec=pltpu.PrefetchScalarGridSpec(
            num_scalar_prefetch=1,
            grid=(4,),
            in_specs=[
                pl.BlockSpec((None, rows, size), lambda g, t: (t[g] & 1, 0, t[g] >> 1)),
                fixed,
                *specs,
            ],
            out_specs=fixed,
            scratch_shapes=[pltpu.VMEM((rows, width), f32)],
        ),
        out_shape=jax.ShapeDtypeStruct((rows, width), bf16),
        compiler_params=pltpu.CompilerParams(vmem_limit_bytes=58 * 1024 * 1024),
        cost_estimate=CHEAP,
        name="out_forward",
    )(table, value, base, *operands)


def stacked_project_kernel(value, *rest):
    weight = jnp.concatenate([w[...] for w in rest[:-1]], 1)
    rest[-1][...] = mm_nt(value[...], weight).astype(bf16)


def stacked_project(value, stack, base, count):
    rows = value.shape[0]
    shards, _, deep = stack.shape
    first = base // WIDE
    specs = [
        pl.BlockSpec((None, WIDE, deep), lambda j, k=k: (k, first + j, 0)) for k in range(shards)
    ]
    return pl.pallas_call(
        stacked_project_kernel,
        grid=(count // WIDE,),
        in_specs=[pl.BlockSpec((rows, shards * deep), lambda j: (0, 0))] + specs,
        out_specs=pl.BlockSpec((rows, WIDE), lambda j: (0, j)),
        out_shape=jax.ShapeDtypeStruct((rows, count), bf16),
        compiler_params=pltpu.CompilerParams(vmem_limit_bytes=58 * 1024 * 1024),
        cost_estimate=CHEAP,
        name="stacked_project",
    )(value, *([stack] * shards))


def stacked_back_kernel(value, *rest):
    out, total = rest[-2:]
    step = pl.program_id(0)

    @pl.when(step == 0)
    def _():
        total[...] = jnp.zeros_like(total)

    weight = jnp.concatenate([w[...] for w in rest[:-2]], 1)
    total[...] += mm(value[...], weight)

    @pl.when(step == pl.num_programs(0) - 1)
    def _():
        out[...] = total[...]


def stacked_back(value, stack, base):
    rows, count = value.shape
    shards, _, deep = stack.shape
    size = WIDE
    first = base // size
    specs = [
        pl.BlockSpec((None, size, deep), lambda j, k=k: (k, first + j, 0)) for k in range(shards)
    ]
    return pl.pallas_call(
        stacked_back_kernel,
        grid=(count // size,),
        in_specs=[pl.BlockSpec((rows, size), lambda j: (0, j))] + specs,
        out_specs=pl.BlockSpec((rows, shards * deep), lambda j: (0, 0)),
        out_shape=jax.ShapeDtypeStruct((rows, shards * deep), f32),
        scratch_shapes=[pltpu.VMEM((rows, shards * deep), f32)],
        compiler_params=pltpu.CompilerParams(vmem_limit_bytes=58 * 1024 * 1024),
        cost_estimate=CHEAP,
        name="stacked_back",
    )(value, *([stack] * shards))


def halve(value, dim, axis, bit, mine, wait):
    shape = value.shape
    value = value.reshape(shape[:dim] + (shape[dim] // 2, 2) + shape[dim + 1 :])
    send = lax.dynamic_index_in_dim(value, 1 - mine, dim + 1, False)
    kept = lax.dynamic_index_in_dim(value, mine, dim + 1, False)
    came = lax.ppermute(send, axis, flip(axis, bit))
    if wait:
        came = after(came, *wait)
    return (kept.astype(f32) + came.astype(f32)).astype(bf16), send


class RowSum:
    def __init__(self, partial, far_first):
        shards, places = (lax.axis_size("shard"), lax.axis_size("seq"))
        shard, place = (lax.axis_index("shard"), lax.axis_index("seq"))
        rows, columns = partial.shape
        chips = shards // 2
        self.value = partial.reshape(chips, places, rows // (chips * places), columns)
        far = [(0, "shard", 2 << k, (shard >> (k + 1)) & 1) for k in range(chips.bit_length() - 1)]
        near = [(1, "seq", 1 << k, (place >> k) & 1) for k in range(places.bit_length() - 1)]
        self.order = far + near if far_first else near[:1] + far + near[1:]

    def step(self, *wait):
        if not self.order:
            return
        dim, axis, bit, mine = self.order.pop(0)
        self.value, self.send = halve(self.value, dim, axis, bit, mine, wait)

    def rows(self):
        return self.value.reshape(self.value.shape[2:])


def core_rows(value, core):
    shards = lax.axis_size("shard")
    size = value.shape[1] // shards
    even = [value[:, at * size : (at + 1) * size] for at in range(0, shards, 2)]
    odd = [value[:, at * size : (at + 1) * size] for at in range(1, shards, 2)]
    own = [jnp.where(core == 0, a, b) for a, b in zip(even, odd)]
    rest = [jnp.where(core == 0, b, a) for a, b in zip(even, odd)]
    return jnp.concatenate(own, 1), jnp.concatenate(rest, 1)


def after(value, *others):
    return lax.optimization_barrier((value,) + others)[0]


def turn_blocks(value, shard):
    shards = lax.axis_size("shard")
    size = value.shape[1] // shards
    blocks = [
        lax.dynamic_slice_in_dim(value, (at ^ shard) * size, size, 1) for at in range(shards)
    ]
    return jnp.concatenate(blocks, 1)


def on_device(
    hidden,
    cotangent,
    seg_ids,
    norm_gain,
    in_weight,
    conv_weight,
    conv_bias,
    dt_bias,
    a_log,
    d_skip,
    out_gain,
    out_weight,
):
    shards, places = (lax.axis_size("shard"), lax.axis_size("seq"))
    shard, place = (lax.axis_index("shard"), lax.axis_index("seq"))
    devices = shards * places
    me = shard * places + place
    length, width = hidden.shape
    heads = dt_bias.shape[0]
    inner = out_weight.shape[0] * shards
    channels = conv_bias.shape[0] * shards
    n_state = (channels - inner) // 2
    groups = inner // WIDE
    start = me * length

    core = shard % 2
    w_in = in_weight.T
    by_hand = shards == 4 and places % 2 == 0
    edge_rows = w_in.shape[0] - 2 * inner
    small = jnp.concatenate([norm_gain, conv_weight.reshape(-1), conv_bias, out_gain])
    small_rows = pl.cdiv(small.shape[0], w_in.shape[1])
    small_rows += -(small_rows + edge_rows) % 16
    small = jnp.pad(small, (0, small_rows * w_in.shape[1] - small.shape[0]))
    edges = jnp.concatenate([w_in[2 * inner :], small.reshape(small_rows, w_in.shape[1])], 0)
    if by_hand:
        in_other = other_core(w_in)
        plan = Plan()
        plan.add([shard, shard ^ 1, shard ^ 2, shard ^ 3, place % 2])
        g_x = Gather(plan, w_in, in_other, inner, inner // 2, 2, edges)
        edge_far = lax.ppermute(edges, "shard", flip("shard", 2))
        g_z = Gather(plan, w_in, in_other, 0, inner // 2, 1, g_x.direct[1])
        pieces = [edges, other_core(edges), edge_far, other_core(edge_far)]
        edges = jnp.stack([after(piece, g_x.send) for piece in pieces])
        edges = jnp.stack([lax.dynamic_index_in_dim(edges, k ^ shard, 0, False) for k in range(4)])
    else:
        edges = lax.all_gather(edges, "shard")
    if by_hand:
        plan.close()
        g_x.share()
        g_x.cross(0)
        out_other = other_core(after(out_weight, g_x.direct[0]))
    else:
        stack_x = lax.all_gather(w_in[inner : 2 * inner], "shard")
        stack_z = lax.all_gather(w_in[:inner], "shard")
        w_out = lax.all_gather(out_weight, "shard", axis=0, tiled=True)
    w_edge = edges[:, :edge_rows].transpose(1, 0, 2).reshape(edge_rows, width)
    w_edge = jnp.pad(w_edge, ((0, -edge_rows % TILE), (0, 0)))
    small = edges[:, edge_rows:].reshape(shards, -1)
    at = 0
    gain_in = small[:, at : at + norm_gain.shape[0]].reshape(-1).astype(f32)
    at += norm_gain.shape[0]
    taps = small[:, at : at + conv_weight.size].reshape(shards, CONV, -1)
    taps = taps.transpose(1, 0, 2).reshape(CONV, channels).astype(f32)
    at += conv_weight.size
    bias = small[:, at : at + conv_bias.shape[0]].reshape(-1).astype(f32)
    at += conv_bias.shape[0]
    gain_out = small[:, at : at + out_gain.shape[0]].reshape(-1).astype(f32)
    skip_wide = jnp.repeat(d_skip.astype(f32), HEAD_DIM)
    rows = jnp.concatenate([skip_wide, jnp.zeros((channels - inner,), f32)])
    taps8 = jnp.concatenate([taps, bias[None], rows[None], jnp.zeros((2, channels), f32)], 0)

    edge = jnp.full((HALO,), -1, jnp.int32)
    padded = jnp.concatenate([edge, seg_ids, edge - 1])
    near = lax.dynamic_slice_in_dim(padded, start, length + 2 * HALO)
    seg = near[HALO : HALO + length]
    fwd_masks = [near[HALO - CONV + 1 + k : HALO - CONV + 1 + k + length] == seg for k in range(3)]
    spot = jnp.arange(length, dtype=jnp.int32)
    bwd_masks = [
        (near[HALO + CONV - 1 - k : HALO + CONV - 1 - k + length] == seg)
        & (spot + CONV - 1 - k < length)
        for k in range(3)
    ]
    from_before = seg == near[HALO - 1]
    to_last = seg == seg[length - 1]
    flags = jnp.stack(
        [m.astype(f32) for m in fwd_masks + bwd_masks + [seg, from_before, to_last]], 1
    )
    flags = jnp.pad(flags, ((0, 0), (0, 16 - flags.shape[1])))
    seg_row = jnp.broadcast_to(seg.astype(f32)[None, :], (8, length))

    behind = lax.ppermute(
        hidden[length - HALO :], ALL, [(i, i + 1) for i in range(devices - 1)]
    )
    hidden_f = jnp.concatenate([behind, hidden], 0).astype(f32)
    scale_in = lax.rsqrt(jnp.mean(hidden_f * hidden_f, axis=1, keepdims=True) + EPS)
    normed_ext = (hidden_f * scale_in * gain_in[None, :]).astype(bf16)
    normed_in = normed_ext[HALO:]
    proj_edge = mm_nt(normed_ext, w_edge).astype(bf16)
    proj_bc = proj_edge[:, : 2 * n_state]
    rates = jnp.stack([dt_bias, a_log]).astype(f32)
    rates = jnp.pad(rates, ((0, 6), (0, TILE - heads)))
    big = pltpu.CompilerParams(vmem_limit_bytes=56 * 1024 * 1024)
    per_head, spreads, cum, sums_row, masks = pl.pallas_call(
        prepare_kernel,
        out_shape=[
            jax.ShapeDtypeStruct((5, length, TILE), f32),
            jax.ShapeDtypeStruct((2, length, 2 * TILE), bf16),
            jax.ShapeDtypeStruct((groups, length, GROUP), f32),
            jax.ShapeDtypeStruct((groups, GROUP, length), f32),
            jax.ShapeDtypeStruct((2 * (CONV - 1), length, TILE), f32),
        ],
        compiler_params=big,
        name="prepare",
    )(proj_edge[HALO:, 2 * n_state :], rates, flags)
    end = two_parts(per_head[3, length - 1])
    if by_hand:
        proj = project(after(normed_ext, per_head), g_x, 0, None)
        g_out = Gather(plan, out_weight, out_other, 0, out_weight.shape[0] // 2, 1, proj, g_z.direct[0])
        g_z.share(proj)
        g_x.cross(1, proj)
        proj = project(normed_ext, g_x, 1, proj)
    else:
        proj = stacked_project(normed_ext, stack_x, 0, inner)

    def whole(shape):
        return pl.BlockSpec(shape, lambda g: (0,) * len(shape))

    def group_of(g):
        return jnp.maximum(g - 1, 0)

    order = lambda g: jnp.where(g == 0, groups, g - 1)
    x_conv, state_local, bc, bt, ct = pl.pallas_call(
        state_kernel,
        grid=(groups // SPAN,),
        in_specs=[
            pl.BlockSpec((length + HALO, SPAN * WIDE), lambda g: (0, g)),
            whole((length + HALO, WIDE)),
            pl.BlockSpec((8, SPAN * WIDE), lambda g: (0, g)),
            whole((8, WIDE)),
            whole(masks.shape),
            whole(spreads.shape),
        ],
        out_specs=[
            pl.BlockSpec((length, SPAN * WIDE), lambda g: (0, g)),
            pl.BlockSpec((n_state, SPAN * WIDE), lambda g: (0, g)),
            whole((length, 2 * n_state)),
            whole((n_state, length)),
            whole((n_state, length)),
        ],
        out_shape=[
            jax.ShapeDtypeStruct((length, inner), bf16),
            jax.ShapeDtypeStruct((n_state, inner), bf16),
            jax.ShapeDtypeStruct((length, 2 * n_state), bf16),
            jax.ShapeDtypeStruct((n_state, length), bf16),
            jax.ShapeDtypeStruct((n_state, length), bf16),
        ],
        scratch_shapes=[
            pltpu.VMEM((length + HALO, WIDE), f32),
            pltpu.VMEM((n_state, length), bf16),
        ],
        compiler_params=big,
        cost_estimate=CHEAP,
        name="mixer_state",
    )(proj, proj_bc, taps8, taps8[:, inner:], masks, spreads)

    slices = with_decay(to_slices(state_local, devices), end)
    if by_hand:
        slices = after(slices, g_out.direct[0])
        g_out.share(slices)
        sent = exchange(slices)
        g_z.cross(0, slices)
        gate_z = project(after(normed_in, slices), g_z, 0, None)
        own, rest = core_rows(after(normed_in, slices), core)
        lefts = turned(after(own, gate_z), after(other_core(rest), gate_z))
        sent = after(sent, gate_z, *lefts)
    else:
        sent = exchange(slices)
        own, rest = core_rows(normed_in, core)
        lefts = turned(own, other_core(rest))
        gate_z = stacked_project(normed_in, stack_z, 0, inner)
    columns = slices.shape[2] - TILE
    decays = sent[:, :, columns:]
    states = scan_devices(sent, decays, columns, me, False)
    state_in = return_slices(states, n_state, inner)
    x_conv = after(x_conv, states)
    half_t = 2 * TILE
    y_local = pl.pallas_call(
        forward_kernel,
        grid=(groups // SPAN,),
        in_specs=[
            pl.BlockSpec((length, SPAN * WIDE), lambda g: (0, g)),
            whole(flags.shape),
            whole((8, length)),
            whole(spreads.shape),
            pl.BlockSpec((SPAN, length, GROUP), lambda g: (g, 0, 0)),
            pl.BlockSpec((SPAN, GROUP, length), lambda g: (g, 0, 0)),
            whole((length, 2 * n_state)),
            whole((n_state, length)),
        ],
        out_specs=pl.BlockSpec((length, SPAN * WIDE), lambda g: (0, g)),
        out_shape=jax.ShapeDtypeStruct((length, inner), f32),
        scratch_shapes=[
            pltpu.VMEM((length, length), f32),
            pltpu.VMEM((length // half_t, GROUP * half_t, WIDE), bf16),
            pltpu.VMEM((length // half_t, length, GROUP * half_t), bf16),
        ],
        compiler_params=big,
        cost_estimate=CHEAP,
        name="mixer_forward",
    )(x_conv, flags, seg_row, spreads, cum, sums_row, bc, bt)
    if by_hand:
        g_out.cross(0, y_local)
        d_normed = out_back(after(cotangent, y_local), g_out)
    else:
        d_normed = mm_nt(cotangent, w_out).astype(bf16)
    block = TILE
    tall = lambda dim: pl.BlockSpec((block, dim), lambda g: (g, 0))
    gains = jnp.stack([gain_out, skip_wide], 0)
    ssm, normed_out, d_z, d_y, d_state_local, dc_more, d_gain = pl.pallas_call(
        lambda *refs: gate_kernel(shards, *refs),
        grid=(length // block,),
        in_specs=[
            tall(inner),
            tall(inner),
            tall(inner),
            tall(inner),
            tall(2 * n_state),
            pl.BlockSpec((n_state, block), lambda g: (0, g)),
            pl.BlockSpec((None, block, TILE), lambda g: (3, g, 0)),
            whole((n_state, inner)),
            whole((2, inner)),
        ],
        out_specs=[
            tall(inner),
            pl.BlockSpec((2, block, inner // 2), lambda g: (0, g, 0)),
            tall(inner),
            tall(inner),
            whole((n_state, inner)),
            tall(n_state),
            whole((8, inner)),
        ],
        out_shape=[
            jax.ShapeDtypeStruct((length, inner), f32),
            jax.ShapeDtypeStruct((2, length, inner // 2), bf16),
            jax.ShapeDtypeStruct((length, inner), bf16),
            jax.ShapeDtypeStruct((length, inner), bf16),
            jax.ShapeDtypeStruct((n_state, inner), bf16),
            jax.ShapeDtypeStruct((length, n_state), f32),
            jax.ShapeDtypeStruct((8, inner), f32),
        ],
        scratch_shapes=[
            pltpu.VMEM((block, inner), f32),
            pltpu.VMEM((block, inner), f32),
            pltpu.VMEM((block, inner), bf16),
            pltpu.VMEM((n_state, inner), f32),
        ],
        compiler_params=big,
        cost_estimate=CHEAP,
        name="mixer_gate",
    )(y_local, x_conv, gate_z, d_normed, bc, ct, per_head, state_in, gains)

    slices = to_slices(d_state_local, devices)
    sent = exchange(slices)
    normed_out, d_z = (after(normed_out, slices), after(d_z, slices))

    def both(value):
        return jnp.concatenate([value, other_core(value)], 0)

    def both_rows(value):
        own, rest = core_rows(value, core)
        return jnp.concatenate([own, other_core(rest)], 0)

    cot_pair = both(cotangent)
    pick = lambda at: lax.dynamic_index_in_dim(normed_out, at, 0, False)
    out_pair = jnp.concatenate([pick(core), other_core(pick(1 - core))], 0)
    z_other = other_core(d_z)
    if by_hand:
        block_out = out_forward(normed_out, hidden, g_out)
    else:
        size = inner // shards
        parts = [
            normed_out[at % 2, :, (at // 2) * size : (at // 2 + 1) * size] for at in range(shards)
        ]
        block_out = (hidden.astype(f32) + mm(jnp.concatenate(parts, 1), w_out)).astype(bf16)
    grad_o = mm_tn(after(out_pair, block_out), cot_pair).astype(bf16)
    states = scan_devices(after(sent, grad_o), decays, columns, me, True)
    returned = exchange(states)
    z_other = after(z_other, states)
    blocks = inner // (4 * WIDE)
    grad_z = [pair_grad(lefts, d_z, z_other, at, blocks) for at in (0, blocks)]
    x_conv = after(x_conv, grad_o, *grad_z)

    dxs, db_in, dc_in = pl.pallas_call(
        inside_kernel,
        grid=(groups,),
        in_specs=[
            pl.BlockSpec((length, WIDE), lambda g: (0, g)),
            whole(flags.shape),
            whole((8, length)),
            whole(spreads.shape),
            pl.BlockSpec((1, length, GROUP), lambda g: (g, 0, 0)),
            pl.BlockSpec((1, GROUP, length), lambda g: (g, 0, 0)),
            whole((length, 2 * n_state)),
            whole((n_state, length)),
            pl.BlockSpec((length, WIDE), lambda g: (0, g)),
        ],
        out_specs=[
            pl.BlockSpec((length, WIDE), lambda g: (0, g)),
            whole((length, n_state)),
            whole((length, n_state)),
        ],
        out_shape=[
            jax.ShapeDtypeStruct((length, inner), f32),
            jax.ShapeDtypeStruct((length, n_state), f32),
            jax.ShapeDtypeStruct((length, n_state), f32),
        ],
        scratch_shapes=[
            pltpu.VMEM((length, length), f32),
            pltpu.VMEM((length, length), f32),
            pltpu.VMEM((length // half_t, GROUP * half_t, WIDE), bf16),
            pltpu.VMEM((length // half_t, length, GROUP * half_t), bf16),
            pltpu.VMEM((GROUP, length, WIDE), bf16),
            pltpu.VMEM((2, length, length), f32),
        ],
        compiler_params=big,
        cost_estimate=CHEAP,
        name="mixer_inside",
    )(x_conv, flags, seg_row, spreads, cum, sums_row, bc, ct, d_y)

    d_state = from_slices(after(returned, dxs), n_state, inner)
    grad_o, *grad_z = lax.optimization_barrier((grad_o, *grad_z, dxs))[:3]

    def halves(grad):
        half = grad.shape[1] // 2
        return [RowSum(grad[:, :half], True), RowSum(grad[:, half:], False)]

    def step(wait, *chains):
        for chain in chains:
            chain.step(wait)

    taps8 = jnp.pad(taps8, ((0, 0), (0, WIDE)))

    def outside(first_group, count, final, grad, running):
        kept = lambda g: jnp.minimum(g, count - 1) + first_group
        steps = count + (2 if final else 0)
        columns = steps * WIDE
        tall = lambda: pl.BlockSpec((length, WIDE), lambda g: (0, kept(g)))
        flat = lambda: pl.BlockSpec((n_state, WIDE), lambda g: (0, kept(g)))
        return pl.pallas_call(
            lambda *refs: outside_kernel(first_group, count, final, len(running) > 0, *refs),
            grid=(steps,),
            in_specs=[
                pl.BlockSpec((length + HALO, WIDE), lambda g: (0, kept(g))),
                whole((length + HALO, WIDE)),
                pl.BlockSpec((8, WIDE), lambda g: (0, first_group + g)),
                whole(masks.shape),
                whole(spreads.shape),
                whole(per_head.shape),
                whole(rates.shape),
                whole((length, 2 * n_state)),
                tall(),
                tall(),
                tall(),
                flat(),
                flat(),
                whole((length, n_state)),
                whole((length, n_state)),
                whole((length, n_state)),
                *[whole(value.shape) for value in running],
            ],
            out_specs=[
                pl.BlockSpec((length, WIDE), lambda g: (0, g)),
                pl.BlockSpec((HALO, WIDE), lambda g: (0, g)),
                pl.BlockSpec((HALO, WIDE), lambda g: (0, g)),
                pl.BlockSpec((8, WIDE), lambda g: (0, g)),
                whole((8, TILE)),
                whole((length, n_state)),
                whole((2, length, TILE)),
                whole((8, TILE)),
            ],
            out_shape=[
                jax.ShapeDtypeStruct((length, columns), bf16),
                jax.ShapeDtypeStruct((HALO, columns), f32),
                jax.ShapeDtypeStruct((HALO, columns), f32),
                jax.ShapeDtypeStruct((8, columns), f32),
                jax.ShapeDtypeStruct((8, TILE), f32),
                jax.ShapeDtypeStruct((length, n_state), f32),
                jax.ShapeDtypeStruct((2, length, TILE), f32),
                jax.ShapeDtypeStruct((8, TILE), f32),
            ],
            scratch_shapes=[
                pltpu.VMEM((length + HALO, WIDE), f32),
                pltpu.VMEM((length + HALO, WIDE), f32),
            ],
            compiler_params=big,
            cost_estimate=CHEAP,
            name="mixer_outside",
        )(proj, proj_bc, taps8, masks, spreads, per_head, rates, bc, grad, ssm, dxs, d_state,
          state_in, db_in, dc_in, dc_more, *running)

    seg_end = near[length : length + 2 * HALO]

    def finish(grads, first, last, start):
        ahead = lax.ppermute(first, ALL, [(i + 1, i) for i in range(devices - 1)])
        joined = jnp.concatenate([jnp.zeros_like(first), ahead], 0)
        for tap in range(CONV - 1):
            lead = CONV - 1 - tap
            same = (seg_end[lead : lead + HALO] == seg_end[:HALO]).astype(f32)[:, None]
            here = taps8[tap, start : start + first.shape[1]]
            last = last + here[None, :] * joined[lead : lead + HALO] * same
        count = min(channels - start, first.shape[1])
        return lax.dynamic_update_slice(grads, last[:, :count].astype(bf16), (length - HALO, 0))

    running = ()
    part = groups // 2
    half_x = part * WIDE

    values = lambda *chains: [chain.value for chain in chains]
    sums_o = halves(grad_o)
    d_one, first, last, sums_one, _, *running = outside(0, part, False, d_y, running)
    step(d_one, *sums_o)
    d_one = finish(d_one, first, last, 0)
    one_other = other_core(d_one)
    if by_hand:
        d_normed_in = back([after(d_z, sums_one, *values(*sums_o))], g_z, None)
    else:
        d_normed_in = stacked_back(d_z, stack_z, 0)
    step(d_normed_in, *sums_o)
    grad_z = lax.optimization_barrier((*grad_z, sums_one))[:2]
    sums_z = [RowSum(grad_z[0], True), RowSum(grad_z[1], False)]
    one_other = after(one_other, d_normed_in)
    blocks = d_one.shape[1] // (2 * WIDE)
    more = (blocks + 1) // 2
    grad_x = [
        pair_grad(lefts, d_one, one_other, 0, more),
        pair_grad(lefts, d_one, one_other, more, blocks - more),
    ]
    grad = after(d_y, *grad_x, *values(*sums_o))
    d_two, first, last, sums_two, head_sums, *_ = outside(part, groups - part, True, grad, running)
    sums_a = [RowSum(grad_x[0], True), RowSum(grad_x[1], False)]
    step(d_two, *sums_a)
    ready = values(*sums_a)
    d_two, first, last = lax.optimization_barrier((d_two, first, last, *ready))[:3]
    step(d_two, *sums_z, *sums_o)
    sums = jnp.concatenate([sums_one, sums_two], 1)
    d_two = finish(d_two, first, last, half_x)
    two_other = other_core(d_two)
    count = inner - half_x
    edge = d_two[:, count : count + w_edge.shape[0]]
    d_normed_in = d_normed_in + mm(edge, w_edge)
    two_other = after(two_other, d_normed_in, *values(*sums_z, *sums_o))
    blocks = d_two.shape[1] // (4 * WIDE)
    grad_y = [pair_grad(lefts, d_two, two_other, at, blocks) for at in (0, blocks)]
    step(grad_y[1], *sums_z, *sums_o)
    sums_b = [RowSum(grad_y[0], True), RowSum(grad_y[1], False)]
    if by_hand:
        last_values = [d_one, after(d_two, *grad_y, *values(*sums_z))]
        norm = (hidden, cotangent, gain_in[None])
        grad_hidden, grad_gain_in = back(last_values, g_x, d_normed_in, norm)
    else:
        d_x = jnp.concatenate([d_one, d_two[:, :count]], 1)
        d_normed_in = d_normed_in + stacked_back(d_x, stack_x, 0)
        base = hidden.astype(f32)
        scale = scale_in[HALO:]
        d_hat = d_normed_in * gain_in[None, :]
        mean = jnp.mean(d_hat * base, axis=1, keepdims=True)
        grad_hidden = cotangent.astype(f32) + scale * d_hat - base * (scale * scale * scale * mean)
        grad_gain_in = (d_normed_in * base * scale).reshape(-1, 8, width).sum(0)
    step(grad_gain_in, *sums_b)
    sums_x = sums_a + sums_b
    step(sums_b[0].value, *sums_a, *sums_z)
    step(sums_a[0].value, *sums_b)
    grad_gain_in = after(grad_gain_in, *values(*sums_b))
    step(sums_b[0].value, *sums_a, *sums_z)
    while any(chain.order for chain in sums_o + sums_z + sums_x):
        step(grad_gain_in, *sums_b)
        step(sums_b[0].value, *sums_a, *sums_z, *sums_o)
    counts = [width // devices] + [channels // devices] * (CONV + 1) + [inner // devices]
    counts += [heads] * 3
    total = sum(counts)
    if by_hand:
        sizes = (width // devices, channels // devices, inner // devices, heads)
        packed = pl.pallas_call(
            lambda *refs: pack_kernel(sizes, *refs),
            out_shape=jax.ShapeDtypeStruct((devices, 1, total + -total % TILE), f32),
            name="pack",
        )(sums[:, :channels], grad_gain_in, d_gain, head_sums)
    else:
        slots = lambda v: v.reshape(-1, devices, v.shape[-1] // devices).transpose(1, 0, 2)
        same = jnp.broadcast_to(head_sums[:3, :heads].reshape(1, -1), (devices, 3 * heads))
        pieces = [slots(grad_gain_in.sum(0)), slots(sums[: CONV + 1, :channels])]
        pieces += [slots(jnp.sum(d_gain, 0)), same]
        packed = jnp.concatenate([p.reshape(devices, -1) for p in pieces], 1)[:, None]
    packed = exchange(packed).sum((0, 1))
    found, at = ([], 0)
    for size in counts:
        found.append(packed[at : at + size])
        at += size

    grads = [c.rows().astype(f32) for c in sums_z + sums_x]
    excess = sum(g.shape[1] for g in grads) - w_in.shape[0]
    grads[-1] = grads[-1][:, : grads[-1].shape[1] - excess]
    return (
        block_out,
        grad_hidden,
        found[0],
        jnp.concatenate(grads, 1),
        jnp.stack(found[1 : CONV + 1]),
        found[CONV + 1],
        found[CONV + 3],
        found[CONV + 4],
        found[CONV + 5],
        found[CONV + 2],
        jnp.concatenate([c.rows().astype(f32) for c in sums_o], 1),
    )


def solution(mesh):
    return jax.shard_map(
        on_device,
        mesh=mesh,
        in_specs=(
            P(ALL, None),
            P(ALL, None),
            P(),
            P("shard"),
            P("shard", None),
            P(None, "shard"),
            P("shard"),
            P(),
            P(),
            P(),
            P("shard"),
            P("shard", None),
        ),
        out_specs=(
            P(ALL, None),
            P(ALL, None),
            P(ALL),
            P(ALL, None),
            P(None, ALL),
            P(ALL),
            P(),
            P(),
            P(),
            P(ALL),
            P(ALL, None),
        ),
        check_vma=False,
    )
```

```python
import jax
import jax.numpy as jnp
from jax import lax
from jax.experimental import pallas as pl
from jax.experimental.pallas import tpu as pltpu
from jax.sharding import PartitionSpec as P

HEAD_DIM = 64
CONV = 4
EPS = 1e-05
HALO = 8
GROUP = 4
WIDE = GROUP * HEAD_DIM
TILE = 128
PIECE = 3 * WIDE
SPAN = 2
HIGH = lax.Precision.HIGHEST
ALL = ("shard", "seq")
f32 = jnp.float32
bf16 = jnp.bfloat16
CHEAP = pl.CostEstimate(flops=1, bytes_accessed=1, transcendentals=0)


def mm(a, b):
    return jnp.dot(a, b, preferred_element_type=f32)


def mm_nt(a, b):
    return lax.dot_general(a, b, (((1,), (1,)), ((), ())), preferred_element_type=f32)


def mm_tn(a, b):
    return lax.dot_general(a, b, (((0,), (0,)), ((), ())), preferred_element_type=f32)


def sigmoid(value):
    return 0.5 * jnp.tanh(0.5 * value) + 0.5


def head_lanes(group):
    lane = lax.rem(lax.broadcasted_iota(jnp.int32, (2 * TILE, WIDE), 0), TILE)
    owner = lax.broadcasted_iota(jnp.int32, (2 * TILE, WIDE), 1) // HEAD_DIM + GROUP * group
    return jnp.where(lane == owner, 1.0, 0.0).astype(bf16)


def two_parts(value):
    high = value.astype(bf16)
    low = (value - high.astype(f32)).astype(bf16)
    return high, low


def twice(value):
    return jnp.concatenate([value, value], 1)


def conv_rows(wide, taps, masks, start, rows):
    pre = taps[CONV : CONV + 1, :] + taps[CONV - 1 : CONV, :] * wide[pl.ds(HALO + start, rows), :]
    for tap in range(CONV - 1):
        shifted = wide[pl.ds(HALO - CONV + 1 + tap + start, rows), :]
        pre = pre + taps[tap : tap + 1, :] * shifted * twice(masks[tap, pl.ds(start, rows), :])
    return pre


def prepare_kernel(edge, rates, flags, out, spread_out, cum_out, row_out, masks_out):
    length = out.shape[1]
    shifted = edge[...].astype(f32) + rates[0:1, :]
    step = jax.nn.softplus(shifted)
    here = lax.broadcasted_iota(jnp.int32, (length, length), 0)
    there = lax.broadcasted_iota(jnp.int32, (length, length), 1)
    lower = jnp.where(here >= there, 1.0, 0.0)
    log_decay = -step * jnp.exp(rates[1:2, :])
    cum = lax.dot_general(
        lower, log_decay, (((1,), (0,)), ((), ())), precision=HIGH, preferred_element_type=f32
    )
    keep = jnp.exp(cum[length - 1 : length, :] - cum) * flags[:, 8:9]
    out[0] = cum
    out[1] = step
    out[2] = keep
    out[3] = jnp.exp(cum) * flags[:, 7:8]
    out[4] = sigmoid(shifted)
    for at, value in enumerate((step, keep)):
        high, low = two_parts(value)
        spread_out[at, :, :TILE] = high
        spread_out[at, :, TILE:] = low
    turned = cum.T
    for group in range(row_out.shape[0]):
        heads = slice(GROUP * group, GROUP * (group + 1))
        row_out[group] = turned[heads, :]
        cum_out[group] = cum[:, heads]
    for at in range(2 * (CONV - 1)):
        masks_out[at] = jnp.broadcast_to(flags[:, at : at + 1], (length, TILE))


def span(sub):
    return pl.ds(pl.multiple_of(sub * WIDE, WIDE), WIDE)


def state_kernel(
    raw, raw_bc, taps, taps_bc, masks, spreads, x_out, state_out, bc_out, bt_out, ct_out, wide, bt
):
    length = x_out.shape[0]
    n_state = bt.shape[0]
    step = pl.program_id(0)

    @pl.when(step == 0)
    def _():
        wide[...] = raw_bc[...].astype(f32)
        tap = taps_bc[...]
        for start in range(0, length, TILE):
            rows = pl.ds(start, TILE)
            pre = conv_rows(wide, tap, masks, start, TILE)
            both = pre * sigmoid(pre)
            bc_out[rows, :] = both.astype(bf16)
            turned = both[:, :n_state].T.astype(bf16)
            bt[:, rows] = turned
            bt_out[:, rows] = turned
            ct_out[:, rows] = both[:, n_state:].T.astype(bf16)

    def one(sub, carry):
        columns = span(sub)
        wide[...] = raw[:, columns].astype(f32)
        tap = taps[:, columns]
        lanes = head_lanes(SPAN * step + sub)
        kept = []
        for start in range(0, length, TILE):
            rows = pl.ds(start, TILE)
            pre = conv_rows(wide, tap, masks, start, TILE)
            x = (pre * sigmoid(pre)).astype(bf16)
            x_out[rows, columns] = x
            scaled = (x.astype(f32) * mm(spreads[0, rows, :], lanes)).astype(bf16)
            kept.append((scaled.astype(f32) * mm(spreads[1, rows, :], lanes)).astype(bf16))
        state_out[:, columns] = mm(bt[...], jnp.concatenate(kept, 0)).astype(bf16)
        return carry

    lax.fori_loop(0, SPAN, one, 0)


def scored(first, second, flags, seg_row, score, later):
    length = score.shape[0]
    for start in range(0, length, TILE):
        rows = pl.ds(start, TILE)
        product = mm(first(rows), second[...])
        here = lax.broadcasted_iota(jnp.int32, (TILE, length), 0) + start
        there = lax.broadcasted_iota(jnp.int32, (TILE, length), 1)
        order = (here >= there) if later else (here <= there)
        seen = (flags[rows, 6:7] == seg_row[0:1, :]) & order
        score[rows, :] = jnp.where(seen, product, 0.0)


def by_head(value):
    owner = lax.broadcasted_iota(jnp.int32, value.shape, 1) // HEAD_DIM
    zero = jnp.zeros_like(value)
    return [jnp.where(owner == head, value, zero) for head in range(GROUP)]


def forward_kernel(x_in, flags, seg_row, spreads, cum, sums_row, bc, bt, y_out, score, apart, weights):
    length = y_out.shape[0]
    n_state = bt.shape[0]
    step = pl.program_id(0)
    big = weights.shape[2] // GROUP

    @pl.when(step == 0)
    def _():
        scored(lambda rows: bc[rows, n_state:], bt, flags, seg_row, score, True)
        weights[...] = jnp.zeros_like(weights)

    def one(sub, carry):
        columns = span(sub)
        lanes = head_lanes(SPAN * step + sub)
        for start in range(0, length, TILE):
            rows = pl.ds(start, TILE)
            scaled = x_in[rows, columns].astype(f32) * mm(spreads[0, rows, :], lanes)
            for head, value in enumerate(by_head(scaled)):
                apart[start // big, pl.ds(head * big + start % big, TILE), :] = value.astype(bf16)
        for head in range(GROUP):
            for start in range(0, length, TILE):
                rows = pl.ds(start, TILE)
                for at in range(0, start + TILE, big):
                    end = min(at + big, start + TILE)
                    gap = cum[sub, rows, head : head + 1] - sums_row[sub, head : head + 1, at:end]
                    weight = jnp.exp(jnp.minimum(gap, 0.0)) * score[rows, at:end]
                    weights[at // big, rows, head * big : head * big + end - at] = weight.astype(bf16)
        for at in range(0, length, big):
            part = mm(weights[at // big, at:, :], apart[at // big])
            if at == 0:
                y_out[:, columns] = part
            else:
                y_out[at:, columns] += part
        return carry

    lax.fori_loop(0, SPAN, one, 0)


def gate_kernel(
    shards, y_in, x_in, z_in, dn_in, bc, ct, enter, state, gain, ssm_out, norm_out, dz_out, dy_out,
    ds_out, dc_out, dg_out, gated_s, sig_s, mo_s, ds_acc
):
    rows = y_in.shape[0]
    width = y_in.shape[1]
    n_state = state.shape[0]
    step = pl.program_id(0)
    lane = lax.broadcasted_iota(jnp.int32, (rows, 2 * HEAD_DIM), 1)
    c_mat = bc[:, n_state:]

    @pl.when(step == 0)
    def _():
        ds_acc[...] = jnp.zeros_like(ds_acc)
        dg_out[...] = jnp.zeros_like(dg_out)

    def entering(block):
        low = enter[:, 2 * block : 2 * block + 1]
        top = enter[:, 2 * block + 1 : 2 * block + 2]
        return jnp.where(lane < HEAD_DIM, low, top)

    square = jnp.zeros((rows, 2 * HEAD_DIM), f32)
    cross = jnp.zeros((rows, 2 * HEAD_DIM), f32)
    for block in range(width // (2 * HEAD_DIM)):
        lanes = slice(block * 2 * HEAD_DIM, (block + 1) * 2 * HEAD_DIM)
        ssm = y_in[:, lanes] + entering(block) * mm(c_mat, state[:, lanes])
        ssm_out[:, lanes] = ssm
        mo = (ssm + gain[1:2, lanes] * x_in[:, lanes].astype(f32)).astype(bf16)
        mo_s[:, lanes] = mo
        z = z_in[:, lanes].astype(f32)
        sig = sigmoid(z)
        gated = mo.astype(f32) * (z * sig)
        gated_s[:, lanes] = gated
        sig_s[:, lanes] = sig
        square = square + gated * gated
        cross = cross + gated * (dn_in[:, lanes].astype(f32) * gain[0:1, lanes])
    scale = lax.rsqrt(jnp.sum(square, axis=1, keepdims=True) * (1.0 / width) + EPS)
    pull = scale * scale * scale * (jnp.sum(cross, axis=1, keepdims=True) * (1.0 / width))
    dc = jnp.zeros((rows, n_state), f32)
    for block in range(width // (2 * HEAD_DIM)):
        lanes = slice(block * 2 * HEAD_DIM, (block + 1) * 2 * HEAD_DIM)
        gated = gated_s[:, lanes]
        sig = sig_s[:, lanes]
        silu = z_in[:, lanes].astype(f32) * sig
        dn = dn_in[:, lanes].astype(f32)
        hat = gated * scale
        size = width // shards
        owner, at = divmod(block * 2 * HEAD_DIM, size)
        at += (owner // 2) * size
        norm_out[owner % 2, :, at : at + 2 * HEAD_DIM] = (hat * gain[0:1, lanes]).astype(bf16)
        part = dn * hat
        total = part[0:8, :]
        for at in range(8, rows, 8):
            total = total + part[at : at + 8, :]
        dg_out[:, lanes] += total
        d_gated = scale * (dn * gain[0:1, lanes]) - gated * pull
        dy = (d_gated * silu).astype(bf16)
        dy_out[:, lanes] = dy
        mo = mo_s[:, lanes].astype(f32)
        dz_out[:, lanes] = (d_gated * mo * (sig + silu * (1.0 - sig))).astype(bf16)
        weighted = (dy.astype(f32) * entering(block)).astype(bf16)
        ds_acc[:, lanes] += mm(ct[...], weighted)
        dc = dc + mm_nt(weighted, state[:, lanes])
    dc_out[...] = dc

    @pl.when(step == pl.num_programs(0) - 1)
    def _():
        ds_out[...] = ds_acc[...].astype(bf16)


def inside_kernel(
    x_in, flags, seg_row, spreads, cum, sums_row, bc, ct, dy, dxs_out, db_out, dc_out, score, pair,
    apart, weights, xs, crossed
):
    length = dxs_out.shape[0]
    n_state = ct.shape[0]
    group = pl.program_id(0)
    big = weights.shape[2] // GROUP

    @pl.when(group == 0)
    def _():
        pair[...] = jnp.zeros_like(pair)
        weights[...] = jnp.zeros_like(weights)
        scored(lambda rows: bc[rows, :n_state], ct, flags, seg_row, score, False)

    lanes = head_lanes(group)
    for start in range(0, length, TILE):
        rows = pl.ds(start, TILE)
        scaled = x_in[rows, :].astype(f32) * mm(spreads[0, rows, :], lanes)
        for head, value in enumerate(by_head(scaled)):
            xs[head, rows, :] = value.astype(bf16)
        for head, value in enumerate(by_head(dy[rows, :].astype(f32))):
            apart[start // big, pl.ds(head * big + start % big, TILE), :] = value.astype(bf16)
    for head in range(GROUP):
        for at in range(0, length, big):
            end = at + big
            crossed[head % 2, :end, at:end] = mm_nt(xs[head, :end, :], dy[at:end, :])
        for start in range(0, length, TILE):
            rows = pl.ds(start, TILE)
            for at in range(start // big * big, length, big):
                first = max(at, start)
                end = at + big
                gap = sums_row[0, head : head + 1, first:end] - cum[0, rows, head : head + 1]
                decay = jnp.exp(jnp.minimum(gap, 0.0))
                weight = (decay * score[rows, first:end]).astype(bf16)
                weights[at // big, rows, head * big + first - at : (head + 1) * big] = weight
                pair[rows, first:end] += decay * crossed[head % 2, rows, first:end]
    for at in range(length - big, -1, -big):
        end = at + big
        part = mm(weights[at // big, :end, :], apart[at // big])
        if end == length:
            dxs_out[...] = part
        else:
            dxs_out[:end, :] += part

    @pl.when(group == pl.num_programs(0) - 1)
    def _():
        for start in range(0, length, TILE):
            rows = pl.ds(start, TILE)
            here = lax.broadcasted_iota(jnp.int32, (TILE, length), 0) + start
            there = lax.broadcasted_iota(jnp.int32, (TILE, length), 1)
            seen = (flags[rows, 6:7] == seg_row[0:1, :]) & (here <= there)
            part = jnp.where(seen, pair[rows, :], 0.0).astype(bf16)
            db_out[rows, :] = mm(part, bc[:, n_state:])
            if start == 0:
                dc_out[...] = mm_tn(part, bc[rows, :n_state])
            else:
                dc_out[...] += mm_tn(part, bc[rows, :n_state])


def split_mm(value, chosen):
    high, low = two_parts(value)
    return mm(high, chosen) + mm(low, chosen)


def outside_kernel(first_group, count, final, running, *refs):
    (raw, raw_bc, taps, masks, spreads, heads, rates, bc, dy, ssm, dxs_in, d_state, state, db_in,
     dc_in, dc_more, *started, d_out, first_out, last_out, sums_out,
     head_out, db_acc, found, totals_s, wide, d_pre) = refs
    length = d_out.shape[0]
    n_state = bc.shape[1] // 2
    step = pl.program_id(0)
    bc_step = count

    @pl.when(step == 0)
    def _():
        for at, ref in enumerate((db_acc, found, totals_s)):
            ref[...] = started[at][...] if running else jnp.zeros_like(ref)

    d_pre[pl.ds(length, HALO), :] = jnp.zeros((HALO, d_pre.shape[1]), f32)
    zero = jnp.zeros((1, d_pre.shape[1]), f32)

    @pl.when(step < bc_step)
    def _():
        wide[...] = raw[...].astype(f32)
        skip_sum, keep_sum = (zero, zero)
        ds = d_state[...]
        group = step + first_group
        lanes = head_lanes(group)
        owner = lax.broadcasted_iota(jnp.int32, (WIDE, TILE), 0) // HEAD_DIM + GROUP * group
        chosen = (owner == lax.broadcasted_iota(jnp.int32, (WIDE, TILE), 1)).astype(f32)
        chosen_b = chosen.astype(bf16)
        for start in range(0, length, TILE):
            rows = pl.ds(start, TILE)
            pre = conv_rows(wide, taps, masks, start, TILE)
            sig = sigmoid(pre)
            x = pre * sig
            stepped = mm(spreads[0, rows, :], lanes)
            scaled = (x.astype(bf16).astype(f32) * stepped).astype(bf16)
            keep = mm(spreads[1, rows, :], lanes)
            carried = keep * mm(bc[rows, :n_state], ds)
            dxs = dxs_in[rows, :] + carried
            scaled = scaled.astype(f32)
            db_acc[rows, :] += mm_nt((scaled * keep).astype(bf16), ds)
            grad = dy[rows, :].astype(f32)
            keep_sum = keep_sum + jnp.sum(scaled * carried, 0, keepdims=True)
            skip_sum = skip_sum + jnp.sum(grad * x, 0, keepdims=True)
            found[0, rows, :] += split_mm(grad * ssm[rows, :] - scaled * dxs, chosen_b)
            found[1, rows, :] += split_mm(x * dxs, chosen_b)
            d_x = taps[5:6, :] * grad + stepped * dxs
            d_pre[rows, :] = d_x * (sig + x * (1.0 - sig))
        met = jnp.sum(ds.astype(f32) * state[...].astype(f32), 0, keepdims=True)
        rest = jnp.zeros((5, WIDE), f32)
        totals_s[...] += lax.dot_general(
            jnp.concatenate([skip_sum, keep_sum, met, rest], 0),
            chosen,
            (((1,), (0,)), ((), ())),
            precision=HIGH,
            preferred_element_type=f32,
        )

    if final:

        @pl.when(step == bc_step)
        def _():
            wide[...] = raw_bc[...].astype(f32)
            for start in range(0, length, TILE):
                rows = pl.ds(start, TILE)
                pre = conv_rows(wide, taps, masks, start, TILE)
                sig = sigmoid(pre)
                slope = sig + pre * sig * (1.0 - sig)
                d_b = db_in[rows, :] + db_acc[rows, :]
                d_c = dc_in[rows, :] + dc_more[rows, :]
                d_pre[rows, :] = jnp.concatenate([d_b, d_c], 1) * slope

    @pl.when(step <= bc_step)
    def _():
        totals = [zero] * (CONV + 1)
        for start in range(0, length, TILE):
            rows = pl.ds(start, TILE)
            grad = d_pre[rows, :]
            totals[CONV] = totals[CONV] + jnp.sum(grad, 0, keepdims=True)
            here = wide[pl.ds(HALO + start, TILE), :]
            totals[CONV - 1] = totals[CONV - 1] + jnp.sum(grad * here, 0, keepdims=True)
            back = taps[CONV - 1 : CONV, :] * grad
            for tap in range(CONV - 1):
                shifted = wide[pl.ds(HALO - CONV + 1 + tap + start, TILE), :]
                masked = grad * twice(masks[tap, rows, :])
                totals[tap] = totals[tap] + jnp.sum(masked * shifted, 0, keepdims=True)
                ahead = d_pre[pl.ds(start + CONV - 1 - tap, TILE), :]
                back = back + taps[tap : tap + 1, :] * ahead * twice(masks[3 + tap, rows, :])
            d_out[rows, :] = back.astype(bf16)
            if start + TILE == length:
                last_out[...] = back[TILE - HALO :, :]
        first_out[...] = d_pre[pl.ds(0, HALO), :]
        for tap in range(CONV + 1):
            sums_out[tap : tap + 1, :] = totals[tap]
        sums_out[CONV + 1 : 8, :] = jnp.zeros((7 - CONV, d_pre.shape[1]), f32)

    if not final:
        head_out[...] = jnp.zeros_like(head_out)
        return

    @pl.when(step == bc_step + 1)
    def _():
        first_out[...] = jnp.zeros_like(first_out)
        last_out[...] = jnp.zeros_like(last_out)
        sums_out[...] = jnp.zeros_like(sums_out)
        rate = jnp.exp(rates[1:2, :])
        end = totals_s[1:2, :] + heads[3, pl.ds(length - 1, 1), :] * totals_s[2:3, :]
        here = lax.broadcasted_iota(jnp.int32, (length, length), 0)
        there = lax.broadcasted_iota(jnp.int32, (length, length), 1)
        upper = jnp.where(here <= there, 1.0, 0.0)
        d_log = lax.dot_general(
            upper, found[0], (((1,), (0,)), ((), ())), precision=HIGH, preferred_element_type=f32
        )
        d_log = d_log + end
        d_dt = (found[1] - rate * d_log) * heads[4]
        d_out[:, :TILE] = d_dt.astype(bf16)
        d_out[:, TILE:] = jnp.zeros((length, WIDE - TILE), bf16)
        head_out[0:1, :] = jnp.sum(d_dt, 0, keepdims=True)
        head_out[1:2, :] = jnp.sum(d_log * (-heads[1] * rate), 0, keepdims=True)
        head_out[2:3, :] = totals_s[0:1, :]
        head_out[3:8, :] = jnp.zeros((5, TILE), f32)


def pack_kernel(sizes, sums, gain_in, gain_out, head, out):
    devices = out.shape[0]
    gain_in = jnp.sum(gain_in[...], 0, keepdims=True)
    wide, channels, inner, heads = sizes
    gains = jnp.sum(gain_out[...], 0, keepdims=True)
    for at in range(devices):
        pieces = [gain_in[:, at * wide : (at + 1) * wide]]
        for tap in range(CONV + 1):
            pieces.append(sums[tap : tap + 1, at * channels : (at + 1) * channels])
        pieces.append(gains[:, at * inner : (at + 1) * inner])
        for row in range(3):
            pieces.append(head[row : row + 1, :heads])
        begin = 0
        for piece in pieces:
            out[at, :, begin : begin + piece.shape[1]] = piece
            begin += piece.shape[1]
        if begin < out.shape[2]:
            out[at, :, begin:] = jnp.zeros((1, out.shape[2] - begin), f32)


def scan_kernel(backward, place, mine, decay, out, wide):
    count = mine.shape[0]
    columns = out.shape[2]
    for at in range(2):
        for device in range(count):
            wide[at, device : device + 1, :] = decay[device, at : at + 1, :].astype(f32)
    lane = lax.broadcasted_iota(jnp.int32, (TILE, columns), 0)
    owner = lax.broadcasted_iota(jnp.int32, (TILE, columns), 1) // HEAD_DIM + place[0]
    chosen = jnp.where(lane == owner, 1.0, 0.0).astype(bf16)
    factor = mm(wide[0].astype(bf16), chosen) + mm(wide[1].astype(bf16), chosen)
    state = jnp.zeros(out.shape[1:], f32)
    for at in reversed(range(count)) if backward else range(count):
        out[at] = state.astype(bf16)
        state = factor[at : at + 1, :] * state + mine[at, :, :columns].astype(f32)


def to_slices(value, devices):
    n_state, inner = value.shape
    across = max(1, devices // 16)
    rows = n_state * across // devices
    value = value.reshape(n_state // rows, rows, across, inner // across)
    return value.transpose(0, 2, 1, 3).reshape(devices, rows, inner // across)


def from_slices(slices, n_state, inner):
    devices, rows, columns = slices.shape
    value = slices.reshape(n_state // rows, inner // columns, rows, columns)
    return value.transpose(0, 2, 1, 3).reshape(n_state, inner)


def exchange(slices):
    return lax.all_to_all(slices, ALL, split_axis=0, concat_axis=0, tiled=True)


def return_slices(states, n_state, inner):
    return from_slices(exchange(states), n_state, inner)


def with_decay(slices, end):
    devices, rows, _ = slices.shape
    more = jnp.pad(jnp.stack(end), ((0, rows - 2), (0, 0)))
    return jnp.concatenate([slices, jnp.broadcast_to(more[None], (devices, rows, TILE))], 2)


def scan_devices(mine, decay, columns, me, backward):
    devices, rows, _ = mine.shape
    across = max(1, devices // 16)
    place = jnp.reshape((me % across) * (columns // HEAD_DIM), (1,)).astype(jnp.int32)
    vmem = pl.BlockSpec(memory_space=pltpu.VMEM)
    return pl.pallas_call(
        lambda *refs: scan_kernel(backward, *refs),
        in_specs=[pl.BlockSpec(memory_space=pltpu.SMEM), vmem, vmem],
        out_specs=vmem,
        out_shape=jax.ShapeDtypeStruct((devices, rows, columns), bf16),
        scratch_shapes=[pltpu.VMEM((2, devices, TILE), f32)],
        compiler_params=pltpu.CompilerParams(vmem_limit_bytes=40 * 1024 * 1024),
        cost_estimate=CHEAP,
        name="scan_backward" if backward else "scan_forward",
    )(place, mine, decay)


def flip(axis, bit):
    count = lax.axis_size(axis)
    return [(i, i ^ bit) for i in range(count)]


def other_core(value):
    return lax.ppermute(value, "shard", flip("shard", 1))


def turn_kernel(count, *refs):
    for at in range(count):
        refs[count + at][...] = refs[at][...].astype(f32).T.astype(bf16)


def turned(*values):
    shape = values[0].shape
    whole = pl.BlockSpec(memory_space=pltpu.VMEM)
    return pl.pallas_call(
        lambda *refs: turn_kernel(len(values), *refs),
        in_specs=[whole] * len(values),
        out_specs=[whole] * len(values),
        out_shape=[jax.ShapeDtypeStruct(shape[::-1], bf16)] * len(values),
        compiler_params=pltpu.CompilerParams(vmem_limit_bytes=40 * 1024 * 1024),
        cost_estimate=CHEAP,
        name="turn",
    )(*values)


def pair_kernel(left, left_other, value, value_other, out):
    out[...] = (mm(left[...], value[...]) + mm(left_other[...], value_other[...])).astype(bf16)


def pair_grad(lefts, value, value_other, first, count):
    rows, tokens = lefts[0].shape
    size = 2 * WIDE
    whole = pl.BlockSpec((rows, tokens), lambda g: (0, 0))
    block = pl.BlockSpec((tokens, size), lambda g: (0, first + g))
    return pl.pallas_call(
        pair_kernel,
        grid=(count,),
        in_specs=[whole, whole, block, block],
        out_specs=pl.BlockSpec((rows, size), lambda g: (0, g)),
        out_shape=jax.ShapeDtypeStruct((rows, count * size), bf16),
        compiler_params=pltpu.CompilerParams(vmem_limit_bytes=58 * 1024 * 1024),
        cost_estimate=CHEAP,
        name="pair_grad",
    )(*lefts, value, value_other)


class Plan:
    def __init__(self):
        self.values, self.array = ([], None)

    def add(self, values):
        self.values += [jnp.asarray(value, jnp.int32) for value in values]
        return len(self.values) - len(values)

    def close(self):
        self.array = jnp.stack(self.values)


class Gather:
    def __init__(self, plan, own, other, base, half, chunks, *wait):
        self.own, self.other, self.base, self.half, self.chunks = (own, other, base, half, chunks)
        self.mine = lax.axis_index("seq") % 2
        self.size = half // chunks
        self.plan = plan
        if plan.array is None:
            full, near = (half // PIECE, self.size // PIECE)
            self.order = []
            for chunk in range(chunks):
                first = chunk * near
                order = [full * self.mine + first + at for at in range(near)]
                order += [full * (1 - self.mine) + first + at for at in range(near)]
                self.order.append(plan.add(order))
            source, block = ([], [])
            for at in range(2 * full):
                place = at % full
                source.append(2 * (place // near) + jnp.where(self.mine == at // full, 0, 1))
                block.append(place % near)
            self.source, self.block = (plan.add(source), plan.add(block))
        self.direct, self.passed = ([None] * chunks, [None] * chunks)
        self.parts = [None] * chunks
        for chunk in range(chunks):
            start = base + self.mine * half + chunk * self.size
            self.send = lax.dynamic_slice_in_dim(own, start, self.size, 0)
            if chunk:
                wait = (self.direct[chunk - 1],)
            if wait:
                self.send = after(self.send, *wait)
            self.direct[chunk] = lax.ppermute(self.send, "shard", flip("shard", 2))

    def share(self, *wait):
        for chunk in range(self.chunks):
            if chunk:
                wait = (self.passed[chunk - 1],)
            if wait:
                self.direct[chunk] = after(self.direct[chunk], *wait)
            self.passed[chunk] = lax.ppermute(self.direct[chunk], "seq", flip("seq", 1))

    def cross(self, chunk, *wait):
        direct, passed = (self.direct[chunk], self.passed[chunk])
        if wait:
            direct, passed = lax.optimization_barrier((direct, passed) + wait)[:2]
        self.parts[chunk] = [direct, other_core(direct), passed, other_core(passed)]


def project_kernel(table, *refs):
    lefts, (own, other, direct, direct_o, passed, passed_o) = (refs[:4], refs[4:10])
    out, left, weight = refs[-3:]
    step = pl.program_id(0)

    @pl.when(step == 0)
    def _():
        left[...] = jnp.concatenate([a[...] for a in lefts], 1)

    def fill(far, far_o):
        deep = own.shape[1]
        weight[:, :deep] = far[...]
        weight[:, deep:] = far_o[...]

    near = pl.num_programs(0) // 2
    pl.when(step < near)(lambda: fill(direct, direct_o))
    pl.when(step >= near)(lambda: fill(passed, passed_o))
    whole = jnp.concatenate([own[...], other[...], weight[...]], 1)
    out[...] = mm_nt(left[...], whole).astype(bf16)


def project(value, gather, chunk, result):
    rows = value.shape[0]
    deep = gather.own.shape[1]
    near = gather.size // PIECE
    base = gather.base // PIECE
    order = gather.order[chunk]
    table = gather.plan.array
    block = lambda index: pl.BlockSpec((PIECE, deep), index)
    left = lambda k: pl.BlockSpec((rows, deep), lambda j, t: (0, t[k]))
    own = block(lambda j, t: (base + t[order + j], 0))
    one = block(lambda j, t: (jnp.minimum(j, near - 1), 0))
    two = block(lambda j, t: (jnp.maximum(j - near, 0), 0))
    operands = [table, *([value] * 4), gather.own, gather.other, *gather.parts[chunk]]
    in_specs = [left(k) for k in range(4)] + [own, own, one, one, two, two]
    aliases = {}
    if result is not None:
        aliases = {len(operands): 0}
        operands.append(result)
        in_specs.append(pl.BlockSpec(memory_space=pl.ANY))
    return pl.pallas_call(
        project_kernel,
        grid_spec=pltpu.PrefetchScalarGridSpec(
            num_scalar_prefetch=1,
            grid=(2 * near,),
            in_specs=in_specs,
            out_specs=pl.BlockSpec((rows, PIECE), lambda j, t: (0, t[order + j])),
            scratch_shapes=[
                pltpu.VMEM((rows, 4 * deep), bf16),
                pltpu.VMEM((PIECE, 2 * deep), bf16),
            ],
        ),
        out_shape=jax.ShapeDtypeStruct((rows, 2 * gather.half), bf16),
        input_output_aliases=aliases,
        compiler_params=pltpu.CompilerParams(vmem_limit_bytes=58 * 1024 * 1024),
        cost_estimate=CHEAP,
        name="project",
    )(*operands)


def back_kernel(values, chunks, norm, source, table, *refs):
    inputs, refs = (refs[:values], refs[values:])
    own, other = refs[:2]
    far, refs = (refs[2 : 2 + 4 * chunks], refs[2 + 4 * chunks :])
    total, value, weight = refs[-3:]
    refs = refs[:-3]
    if norm:
        hidden, cotangent, gain, out, gain_out = refs[-5:]
        start = refs[:-5]
    else:
        out, start = (refs[-1], refs[:-1])
    step = pl.program_id(0)
    last = pl.num_programs(0) - 1
    deep = own.shape[1]
    place = lambda k: pl.ds(pl.multiple_of(table[k] * deep, deep), deep)

    @pl.when(step == 0)
    def _():
        if start:
            for k in range(4):
                total[:, k * deep : (k + 1) * deep] = start[0][:, place(k)]
        else:
            total[...] = jnp.zeros_like(total)

    for at in range(values):

        @pl.when((step * values // (last + 1)) == at)
        def _(at=at):
            value[...] = inputs[at][...]

    for at in range(2 * chunks):

        @pl.when(table[source + step] == at)
        def _(at=at):
            weight[:, :deep] = far[2 * at][...]
            weight[:, deep:] = far[2 * at + 1][...]

    total[...] += mm(value[...], jnp.concatenate([own[...], other[...], weight[...]], 1))

    @pl.when(step == last)
    def _():
        for k in range(4):
            out[:, place(k)] = total[:, k * deep : (k + 1) * deep]
        if norm:
            sums = jnp.zeros(gain_out.shape, f32)
            for at in range(0, out.shape[0], 64):
                rows = pl.ds(at, 64)
                base = hidden[rows, :].astype(f32)
                grad = out[rows, :]
                size = 1.0 / base.shape[1]
                scale = lax.rsqrt(jnp.sum(base * base, 1, keepdims=True) * size + EPS)
                hat = base * scale
                part = grad * hat
                for row in range(0, 64, 8):
                    sums = sums + part[row : row + 8, :]
                pull = jnp.sum(part * gain[...], 1, keepdims=True) * size
                inner = scale * (grad * gain[...] - hat * pull)
                out[rows, :] = cotangent[rows, :].astype(f32) + inner
            gain_out[...] = sums


def back(values, gather, start, norm=()):
    rows = values[0].shape[0]
    deep = gather.own.shape[1]
    count = 2 * gather.half // PIECE
    share = count // len(values)
    base = gather.base // PIECE
    table = gather.plan.array
    whole = pl.BlockSpec((rows, 4 * deep), lambda j, t: (0, 0))
    own = pl.BlockSpec((PIECE, deep), lambda j, t: (base + j, 0))
    far = pl.BlockSpec((PIECE, deep), lambda j, t: (t[gather.block + j], 0))
    in_specs = [
        pl.BlockSpec((rows, PIECE), lambda j, t, k=k: (0, jnp.clip(j - k * share, 0, share - 1)))
        for k in range(len(values))
    ]
    started = [] if start is None else [start]
    parts = [piece for chunk in gather.parts for piece in chunk]
    in_specs += [own, own] + [far] * len(parts) + [whole] * len(started)
    out_specs, out_shape = (whole, jax.ShapeDtypeStruct((rows, 4 * deep), f32))
    if norm:
        narrow = lambda count: pl.BlockSpec((count, 4 * deep), lambda j, t: (0, 0))
        in_specs += [whole, whole, narrow(1)]
        out_specs = [whole, narrow(8)]
        out_shape = [out_shape, jax.ShapeDtypeStruct((8, 4 * deep), f32)]
    return pl.pallas_call(
        lambda *refs: back_kernel(len(values), gather.chunks, len(norm) > 0, gather.source, *refs),
        grid_spec=pltpu.PrefetchScalarGridSpec(
            num_scalar_prefetch=1,
            grid=(count,),
            in_specs=in_specs,
            out_specs=out_specs,
            scratch_shapes=[
                pltpu.VMEM((rows, 4 * deep), f32),
                pltpu.VMEM((rows, PIECE), bf16),
                pltpu.VMEM((PIECE, 2 * deep), bf16),
            ],
        ),
        out_shape=out_shape,
        compiler_params=pltpu.CompilerParams(vmem_limit_bytes=58 * 1024 * 1024),
        cost_estimate=CHEAP,
        name="back",
    )(table, *values, gather.own, gather.other, *parts, *started, *norm)


def by_shard(gather):
    half, width = (gather.half, gather.own.shape[1])
    whole = pl.BlockSpec((2 * half, width), lambda g, t: (0, 0))
    part = pl.BlockSpec((half, width), lambda g, t: (0, 0))
    direct, direct_o, passed, passed_o = gather.parts[0]
    operands = [gather.own, gather.other, direct, passed, direct_o, passed_o]
    table = gather.plan.array
    return operands, [whole] * 2 + [part] * 4, table


def out_back_kernel(table, value, own, other, direct, passed, direct_o, passed_o, out):
    step = pl.program_id(0)
    half = direct.shape[0]

    def two(near, far):
        out[:, pl.ds(pl.multiple_of(table[4] * half, half), half)] = mm_nt(value[...], near[...]).astype(bf16)
        far_at = pl.multiple_of((1 - table[4]) * half, half)
        out[:, pl.ds(far_at, half)] = mm_nt(value[...], far[...]).astype(bf16)

    for at, piece in enumerate((own, other)):

        @pl.when(step == at)
        def _(piece=piece):
            out[...] = mm_nt(value[...], piece[...]).astype(bf16)

    pl.when(step == 2)(lambda: two(direct, passed))
    pl.when(step == 3)(lambda: two(direct_o, passed_o))


def out_back(value, gather):
    rows, width = value.shape
    operands, specs, table = by_shard(gather)
    size = 2 * gather.half
    return pl.pallas_call(
        out_back_kernel,
        grid_spec=pltpu.PrefetchScalarGridSpec(
            num_scalar_prefetch=1,
            grid=(4,),
            in_specs=[pl.BlockSpec((rows, width), lambda g, t: (0, 0))] + specs,
            out_specs=pl.BlockSpec((rows, size), lambda g, t: (0, t[g])),
        ),
        out_shape=jax.ShapeDtypeStruct((rows, 4 * size), bf16),
        compiler_params=pltpu.CompilerParams(vmem_limit_bytes=58 * 1024 * 1024),
        cost_estimate=CHEAP,
        name="out_back",
    )(table, value, *operands)


def out_forward_kernel(table, value, base, own, other, direct, passed, direct_o, passed_o, out, total):
    step = pl.program_id(0)
    half = direct.shape[0]

    def two(near, far):
        near_at = pl.multiple_of(table[4] * half, half)
        far_at = pl.multiple_of((1 - table[4]) * half, half)
        total[...] += mm(value[:, pl.ds(near_at, half)], near[...])
        total[...] += mm(value[:, pl.ds(far_at, half)], far[...])

    @pl.when(step == 0)
    def _():
        total[...] = base[...].astype(f32) + mm(value[...], own[...])

    @pl.when(step == 1)
    def _():
        total[...] += mm(value[...], other[...])

    pl.when(step == 2)(lambda: two(direct, passed))

    @pl.when(step == 3)
    def _():
        two(direct_o, passed_o)
        out[...] = total[...].astype(bf16)


def out_forward(value, base, gather):
    rows = value.shape[1]
    operands, specs, table = by_shard(gather)
    size = 2 * gather.half
    width = gather.own.shape[1]
    fixed = pl.BlockSpec((rows, width), lambda g, t: (0, 0))
    return pl.pallas_call(
        out_forward_kernel,
        grid_spec=pltpu.PrefetchScalarGridSpec(
            num_scalar_prefetch=1,
            grid=(4,),
            in_specs=[
                pl.BlockSpec((None, rows, size), lambda g, t: (t[g] & 1, 0, t[g] >> 1)),
                fixed,
                *specs,
            ],
            out_specs=fixed,
            scratch_shapes=[pltpu.VMEM((rows, width), f32)],
        ),
        out_shape=jax.ShapeDtypeStruct((rows, width), bf16),
        compiler_params=pltpu.CompilerParams(vmem_limit_bytes=58 * 1024 * 1024),
        cost_estimate=CHEAP,
        name="out_forward",
    )(table, value, base, *operands)


def stacked_project_kernel(value, *rest):
    weight = jnp.concatenate([w[...] for w in rest[:-1]], 1)
    rest[-1][...] = mm_nt(value[...], weight).astype(bf16)


def stacked_project(value, stack, base, count):
    rows = value.shape[0]
    shards, _, deep = stack.shape
    first = base // WIDE
    specs = [
        pl.BlockSpec((None, WIDE, deep), lambda j, k=k: (k, first + j, 0)) for k in range(shards)
    ]
    return pl.pallas_call(
        stacked_project_kernel,
        grid=(count // WIDE,),
        in_specs=[pl.BlockSpec((rows, shards * deep), lambda j: (0, 0))] + specs,
        out_specs=pl.BlockSpec((rows, WIDE), lambda j: (0, j)),
        out_shape=jax.ShapeDtypeStruct((rows, count), bf16),
        compiler_params=pltpu.CompilerParams(vmem_limit_bytes=58 * 1024 * 1024),
        cost_estimate=CHEAP,
        name="stacked_project",
    )(value, *([stack] * shards))


def stacked_back_kernel(value, *rest):
    out, total = rest[-2:]
    step = pl.program_id(0)

    @pl.when(step == 0)
    def _():
        total[...] = jnp.zeros_like(total)

    weight = jnp.concatenate([w[...] for w in rest[:-2]], 1)
    total[...] += mm(value[...], weight)

    @pl.when(step == pl.num_programs(0) - 1)
    def _():
        out[...] = total[...]


def stacked_back(value, stack, base):
    rows, count = value.shape
    shards, _, deep = stack.shape
    size = WIDE
    first = base // size
    specs = [
        pl.BlockSpec((None, size, deep), lambda j, k=k: (k, first + j, 0)) for k in range(shards)
    ]
    return pl.pallas_call(
        stacked_back_kernel,
        grid=(count // size,),
        in_specs=[pl.BlockSpec((rows, size), lambda j: (0, j))] + specs,
        out_specs=pl.BlockSpec((rows, shards * deep), lambda j: (0, 0)),
        out_shape=jax.ShapeDtypeStruct((rows, shards * deep), f32),
        scratch_shapes=[pltpu.VMEM((rows, shards * deep), f32)],
        compiler_params=pltpu.CompilerParams(vmem_limit_bytes=58 * 1024 * 1024),
        cost_estimate=CHEAP,
        name="stacked_back",
    )(value, *([stack] * shards))


def halve(value, dim, axis, bit, mine, wait):
    shape = value.shape
    value = value.reshape(shape[:dim] + (shape[dim] // 2, 2) + shape[dim + 1 :])
    send = lax.dynamic_index_in_dim(value, 1 - mine, dim + 1, False)
    kept = lax.dynamic_index_in_dim(value, mine, dim + 1, False)
    came = lax.ppermute(send, axis, flip(axis, bit))
    if wait:
        came = after(came, *wait)
    return (kept.astype(f32) + came.astype(f32)).astype(bf16), send


class RowSum:
    def __init__(self, partial, far_first):
        shards, places = (lax.axis_size("shard"), lax.axis_size("seq"))
        shard, place = (lax.axis_index("shard"), lax.axis_index("seq"))
        rows, columns = partial.shape
        chips = shards // 2
        self.value = partial.reshape(chips, places, rows // (chips * places), columns)
        far = [(0, "shard", 2 << k, (shard >> (k + 1)) & 1) for k in range(chips.bit_length() - 1)]
        near = [(1, "seq", 1 << k, (place >> k) & 1) for k in range(places.bit_length() - 1)]
        self.order = far + near if far_first else near[:1] + far + near[1:]

    def step(self, *wait):
        if not self.order:
            return
        dim, axis, bit, mine = self.order.pop(0)
        self.value, self.send = halve(self.value, dim, axis, bit, mine, wait)

    def rows(self):
        return self.value.reshape(self.value.shape[2:])


def core_rows(value, core):
    shards = lax.axis_size("shard")
    size = value.shape[1] // shards
    even = [value[:, at * size : (at + 1) * size] for at in range(0, shards, 2)]
    odd = [value[:, at * size : (at + 1) * size] for at in range(1, shards, 2)]
    own = [jnp.where(core == 0, a, b) for a, b in zip(even, odd)]
    rest = [jnp.where(core == 0, b, a) for a, b in zip(even, odd)]
    return jnp.concatenate(own, 1), jnp.concatenate(rest, 1)


def after(value, *others):
    return lax.optimization_barrier((value,) + others)[0]


def turn_blocks(value, shard):
    shards = lax.axis_size("shard")
    size = value.shape[1] // shards
    blocks = [
        lax.dynamic_slice_in_dim(value, (at ^ shard) * size, size, 1) for at in range(shards)
    ]
    return jnp.concatenate(blocks, 1)


def on_device(
    hidden,
    cotangent,
    seg_ids,
    norm_gain,
    in_weight,
    conv_weight,
    conv_bias,
    dt_bias,
    a_log,
    d_skip,
    out_gain,
    out_weight,
):
    shards, places = (lax.axis_size("shard"), lax.axis_size("seq"))
    shard, place = (lax.axis_index("shard"), lax.axis_index("seq"))
    devices = shards * places
    me = shard * places + place
    length, width = hidden.shape
    heads = dt_bias.shape[0]
    inner = out_weight.shape[0] * shards
    channels = conv_bias.shape[0] * shards
    n_state = (channels - inner) // 2
    groups = inner // WIDE
    start = me * length

    core = shard % 2
    w_in = in_weight.T
    by_hand = shards == 4 and places % 2 == 0
    edge_rows = w_in.shape[0] - 2 * inner
    small = jnp.concatenate([norm_gain, conv_weight.reshape(-1), conv_bias, out_gain])
    small_rows = pl.cdiv(small.shape[0], w_in.shape[1])
    small_rows += -(small_rows + edge_rows) % 16
    small = jnp.pad(small, (0, small_rows * w_in.shape[1] - small.shape[0]))
    edges = jnp.concatenate([w_in[2 * inner :], small.reshape(small_rows, w_in.shape[1])], 0)
    if by_hand:
        in_other = other_core(w_in)
        plan = Plan()
        plan.add([shard, shard ^ 1, shard ^ 2, shard ^ 3, place % 2])
        g_x = Gather(plan, w_in, in_other, inner, inner // 2, 2, edges)
        edge_far = lax.ppermute(edges, "shard", flip("shard", 2))
        g_z = Gather(plan, w_in, in_other, 0, inner // 2, 1, g_x.direct[1])
        pieces = [edges, other_core(edges), edge_far, other_core(edge_far)]
        edges = jnp.stack([after(piece, g_x.send) for piece in pieces])
        edges = jnp.stack([lax.dynamic_index_in_dim(edges, k ^ shard, 0, False) for k in range(4)])
    else:
        edges = lax.all_gather(edges, "shard")
    if by_hand:
        plan.close()
        g_x.share()
        g_x.cross(0)
        out_other = other_core(after(out_weight, g_x.direct[0]))
    else:
        stack_x = lax.all_gather(w_in[inner : 2 * inner], "shard")
        stack_z = lax.all_gather(w_in[:inner], "shard")
        w_out = lax.all_gather(out_weight, "shard", axis=0, tiled=True)
    w_edge = edges[:, :edge_rows].transpose(1, 0, 2).reshape(edge_rows, width)
    w_edge = jnp.pad(w_edge, ((0, -edge_rows % TILE), (0, 0)))
    small = edges[:, edge_rows:].reshape(shards, -1)
    at = 0
    gain_in = small[:, at : at + norm_gain.shape[0]].reshape(-1).astype(f32)
    at += norm_gain.shape[0]
    taps = small[:, at : at + conv_weight.size].reshape(shards, CONV, -1)
    taps = taps.transpose(1, 0, 2).reshape(CONV, channels).astype(f32)
    at += conv_weight.size
    bias = small[:, at : at + conv_bias.shape[0]].reshape(-1).astype(f32)
    at += conv_bias.shape[0]
    gain_out = small[:, at : at + out_gain.shape[0]].reshape(-1).astype(f32)
    skip_wide = jnp.repeat(d_skip.astype(f32), HEAD_DIM)
    rows = jnp.concatenate([skip_wide, jnp.zeros((channels - inner,), f32)])
    taps8 = jnp.concatenate([taps, bias[None], rows[None], jnp.zeros((2, channels), f32)], 0)

    edge = jnp.full((HALO,), -1, jnp.int32)
    padded = jnp.concatenate([edge, seg_ids, edge - 1])
    near = lax.dynamic_slice_in_dim(padded, start, length + 2 * HALO)
    seg = near[HALO : HALO + length]
    fwd_masks = [near[HALO - CONV + 1 + k : HALO - CONV + 1 + k + length] == seg for k in range(3)]
    spot = jnp.arange(length, dtype=jnp.int32)
    bwd_masks = [
        (near[HALO + CONV - 1 - k : HALO + CONV - 1 - k + length] == seg)
        & (spot + CONV - 1 - k < length)
        for k in range(3)
    ]
    from_before = seg == near[HALO - 1]
    to_last = seg == seg[length - 1]
    flags = jnp.stack(
        [m.astype(f32) for m in fwd_masks + bwd_masks + [seg, from_before, to_last]], 1
    )
    flags = jnp.pad(flags, ((0, 0), (0, 16 - flags.shape[1])))
    seg_row = jnp.broadcast_to(seg.astype(f32)[None, :], (8, length))

    behind = lax.ppermute(
        hidden[length - HALO :], ALL, [(i, i + 1) for i in range(devices - 1)]
    )
    hidden_f = jnp.concatenate([behind, hidden], 0).astype(f32)
    scale_in = lax.rsqrt(jnp.mean(hidden_f * hidden_f, axis=1, keepdims=True) + EPS)
    normed_ext = (hidden_f * scale_in * gain_in[None, :]).astype(bf16)
    normed_in = normed_ext[HALO:]
    proj_edge = mm_nt(normed_ext, w_edge).astype(bf16)
    proj_bc = proj_edge[:, : 2 * n_state]
    rates = jnp.stack([dt_bias, a_log]).astype(f32)
    rates = jnp.pad(rates, ((0, 6), (0, TILE - heads)))
    big = pltpu.CompilerParams(vmem_limit_bytes=56 * 1024 * 1024)
    per_head, spreads, cum, sums_row, masks = pl.pallas_call(
        prepare_kernel,
        out_shape=[
            jax.ShapeDtypeStruct((5, length, TILE), f32),
            jax.ShapeDtypeStruct((2, length, 2 * TILE), bf16),
            jax.ShapeDtypeStruct((groups, length, GROUP), f32),
            jax.ShapeDtypeStruct((groups, GROUP, length), f32),
            jax.ShapeDtypeStruct((2 * (CONV - 1), length, TILE), f32),
        ],
        compiler_params=big,
        name="prepare",
    )(proj_edge[HALO:, 2 * n_state :], rates, flags)
    end = two_parts(per_head[3, length - 1])
    if by_hand:
        proj = project(after(normed_ext, per_head), g_x, 0, None)
        g_out = Gather(plan, out_weight, out_other, 0, out_weight.shape[0] // 2, 1, proj, g_z.direct[0])
        g_z.share(proj)
        g_x.cross(1, proj)
        proj = project(normed_ext, g_x, 1, proj)
    else:
        proj = stacked_project(normed_ext, stack_x, 0, inner)

    def whole(shape):
        return pl.BlockSpec(shape, lambda g: (0,) * len(shape))

    def group_of(g):
        return jnp.maximum(g - 1, 0)

    order = lambda g: jnp.where(g == 0, groups, g - 1)
    x_conv, state_local, bc, bt, ct = pl.pallas_call(
        state_kernel,
        grid=(groups // SPAN,),
        in_specs=[
            pl.BlockSpec((length + HALO, SPAN * WIDE), lambda g: (0, g)),
            whole((length + HALO, WIDE)),
            pl.BlockSpec((8, SPAN * WIDE), lambda g: (0, g)),
            whole((8, WIDE)),
            whole(masks.shape),
            whole(spreads.shape),
        ],
        out_specs=[
            pl.BlockSpec((length, SPAN * WIDE), lambda g: (0, g)),
            pl.BlockSpec((n_state, SPAN * WIDE), lambda g: (0, g)),
            whole((length, 2 * n_state)),
            whole((n_state, length)),
            whole((n_state, length)),
        ],
        out_shape=[
            jax.ShapeDtypeStruct((length, inner), bf16),
            jax.ShapeDtypeStruct((n_state, inner), bf16),
            jax.ShapeDtypeStruct((length, 2 * n_state), bf16),
            jax.ShapeDtypeStruct((n_state, length), bf16),
            jax.ShapeDtypeStruct((n_state, length), bf16),
        ],
        scratch_shapes=[
            pltpu.VMEM((length + HALO, WIDE), f32),
            pltpu.VMEM((n_state, length), bf16),
        ],
        compiler_params=big,
        cost_estimate=CHEAP,
        name="mixer_state",
    )(proj, proj_bc, taps8, taps8[:, inner:], masks, spreads)

    slices = with_decay(to_slices(state_local, devices), end)
    if by_hand:
        slices = after(slices, g_out.direct[0])
        g_out.share(slices)
        sent = exchange(slices)
        g_z.cross(0, slices)
        gate_z = project(after(normed_in, slices), g_z, 0, None)
        own, rest = core_rows(after(normed_in, slices), core)
        lefts = turned(after(own, gate_z), after(other_core(rest), gate_z))
        sent = after(sent, gate_z, *lefts)
    else:
        sent = exchange(slices)
        own, rest = core_rows(normed_in, core)
        lefts = turned(own, other_core(rest))
        gate_z = stacked_project(normed_in, stack_z, 0, inner)
    columns = slices.shape[2] - TILE
    decays = sent[:, :, columns:]
    states = scan_devices(sent, decays, columns, me, False)
    state_in = return_slices(states, n_state, inner)
    x_conv = after(x_conv, states)
    half_t = 2 * TILE
    y_local = pl.pallas_call(
        forward_kernel,
        grid=(groups // SPAN,),
        in_specs=[
            pl.BlockSpec((length, SPAN * WIDE), lambda g: (0, g)),
            whole(flags.shape),
            whole((8, length)),
            whole(spreads.shape),
            pl.BlockSpec((SPAN, length, GROUP), lambda g: (g, 0, 0)),
            pl.BlockSpec((SPAN, GROUP, length), lambda g: (g, 0, 0)),
            whole((length, 2 * n_state)),
            whole((n_state, length)),
        ],
        out_specs=pl.BlockSpec((length, SPAN * WIDE), lambda g: (0, g)),
        out_shape=jax.ShapeDtypeStruct((length, inner), f32),
        scratch_shapes=[
            pltpu.VMEM((length, length), f32),
            pltpu.VMEM((length // half_t, GROUP * half_t, WIDE), bf16),
            pltpu.VMEM((length // half_t, length, GROUP * half_t), bf16),
        ],
        compiler_params=big,
        cost_estimate=CHEAP,
        name="mixer_forward",
    )(x_conv, flags, seg_row, spreads, cum, sums_row, bc, bt)
    if by_hand:
        g_out.cross(0, y_local)
        d_normed = out_back(after(cotangent, y_local), g_out)
    else:
        d_normed = mm_nt(cotangent, w_out).astype(bf16)
    block = TILE
    tall = lambda dim: pl.BlockSpec((block, dim), lambda g: (g, 0))
    gains = jnp.stack([gain_out, skip_wide], 0)
    ssm, normed_out, d_z, d_y, d_state_local, dc_more, d_gain = pl.pallas_call(
        lambda *refs: gate_kernel(shards, *refs),
        grid=(length // block,),
        in_specs=[
            tall(inner),
            tall(inner),
            tall(inner),
            tall(inner),
            tall(2 * n_state),
            pl.BlockSpec((n_state, block), lambda g: (0, g)),
            pl.BlockSpec((None, block, TILE), lambda g: (3, g, 0)),
            whole((n_state, inner)),
            whole((2, inner)),
        ],
        out_specs=[
            tall(inner),
            pl.BlockSpec((2, block, inner // 2), lambda g: (0, g, 0)),
            tall(inner),
            tall(inner),
            whole((n_state, inner)),
            tall(n_state),
            whole((8, inner)),
        ],
        out_shape=[
            jax.ShapeDtypeStruct((length, inner), f32),
            jax.ShapeDtypeStruct((2, length, inner // 2), bf16),
            jax.ShapeDtypeStruct((length, inner), bf16),
            jax.ShapeDtypeStruct((length, inner), bf16),
            jax.ShapeDtypeStruct((n_state, inner), bf16),
            jax.ShapeDtypeStruct((length, n_state), f32),
            jax.ShapeDtypeStruct((8, inner), f32),
        ],
        scratch_shapes=[
            pltpu.VMEM((block, inner), f32),
            pltpu.VMEM((block, inner), f32),
            pltpu.VMEM((block, inner), bf16),
            pltpu.VMEM((n_state, inner), f32),
        ],
        compiler_params=big,
        cost_estimate=CHEAP,
        name="mixer_gate",
    )(y_local, x_conv, gate_z, d_normed, bc, ct, per_head, state_in, gains)

    slices = to_slices(d_state_local, devices)
    sent = exchange(slices)
    normed_out, d_z = (after(normed_out, slices), after(d_z, slices))

    def both(value):
        return jnp.concatenate([value, other_core(value)], 0)

    def both_rows(value):
        own, rest = core_rows(value, core)
        return jnp.concatenate([own, other_core(rest)], 0)

    cot_pair = both(cotangent)
    pick = lambda at: lax.dynamic_index_in_dim(normed_out, at, 0, False)
    out_pair = jnp.concatenate([pick(core), other_core(pick(1 - core))], 0)
    z_other = other_core(d_z)
    if by_hand:
        block_out = out_forward(normed_out, hidden, g_out)
    else:
        size = inner // shards
        parts = [
            normed_out[at % 2, :, (at // 2) * size : (at // 2 + 1) * size] for at in range(shards)
        ]
        block_out = (hidden.astype(f32) + mm(jnp.concatenate(parts, 1), w_out)).astype(bf16)
    grad_o = mm_tn(after(out_pair, block_out), cot_pair).astype(bf16)
    states = scan_devices(after(sent, grad_o), decays, columns, me, True)
    returned = exchange(states)
    z_other = after(z_other, states)
    blocks = inner // (4 * WIDE)
    grad_z = [pair_grad(lefts, d_z, z_other, at, blocks) for at in (0, blocks)]
    x_conv = after(x_conv, grad_o, *grad_z)

    dxs, db_in, dc_in = pl.pallas_call(
        inside_kernel,
        grid=(groups,),
        in_specs=[
            pl.BlockSpec((length, WIDE), lambda g: (0, g)),
            whole(flags.shape),
            whole((8, length)),
            whole(spreads.shape),
            pl.BlockSpec((1, length, GROUP), lambda g: (g, 0, 0)),
            pl.BlockSpec((1, GROUP, length), lambda g: (g, 0, 0)),
            whole((length, 2 * n_state)),
            whole((n_state, length)),
            pl.BlockSpec((length, WIDE), lambda g: (0, g)),
        ],
        out_specs=[
            pl.BlockSpec((length, WIDE), lambda g: (0, g)),
            whole((length, n_state)),
            whole((length, n_state)),
        ],
        out_shape=[
            jax.ShapeDtypeStruct((length, inner), f32),
            jax.ShapeDtypeStruct((length, n_state), f32),
            jax.ShapeDtypeStruct((length, n_state), f32),
        ],
        scratch_shapes=[
            pltpu.VMEM((length, length), f32),
            pltpu.VMEM((length, length), f32),
            pltpu.VMEM((length // half_t, GROUP * half_t, WIDE), bf16),
            pltpu.VMEM((length // half_t, length, GROUP * half_t), bf16),
            pltpu.VMEM((GROUP, length, WIDE), bf16),
            pltpu.VMEM((2, length, length), f32),
        ],
        compiler_params=big,
        cost_estimate=CHEAP,
        name="mixer_inside",
    )(x_conv, flags, seg_row, spreads, cum, sums_row, bc, ct, d_y)

    d_state = from_slices(after(returned, dxs), n_state, inner)
    grad_o, *grad_z = lax.optimization_barrier((grad_o, *grad_z, dxs))[:3]

    def halves(grad):
        half = grad.shape[1] // 2
        return [RowSum(grad[:, :half], True), RowSum(grad[:, half:], False)]

    def step(wait, *chains):
        for chain in chains:
            chain.step(wait)

    taps8 = jnp.pad(taps8, ((0, 0), (0, WIDE)))

    def outside(first_group, count, final, grad, running):
        kept = lambda g: jnp.minimum(g, count - 1) + first_group
        steps = count + (2 if final else 0)
        columns = steps * WIDE
        tall = lambda: pl.BlockSpec((length, WIDE), lambda g: (0, kept(g)))
        flat = lambda: pl.BlockSpec((n_state, WIDE), lambda g: (0, kept(g)))
        return pl.pallas_call(
            lambda *refs: outside_kernel(first_group, count, final, len(running) > 0, *refs),
            grid=(steps,),
            in_specs=[
                pl.BlockSpec((length + HALO, WIDE), lambda g: (0, kept(g))),
                whole((length + HALO, WIDE)),
                pl.BlockSpec((8, WIDE), lambda g: (0, first_group + g)),
                whole(masks.shape),
                whole(spreads.shape),
                whole(per_head.shape),
                whole(rates.shape),
                whole((length, 2 * n_state)),
                tall(),
                tall(),
                tall(),
                flat(),
                flat(),
                whole((length, n_state)),
                whole((length, n_state)),
                whole((length, n_state)),
                *[whole(value.shape) for value in running],
            ],
            out_specs=[
                pl.BlockSpec((length, WIDE), lambda g: (0, g)),
                pl.BlockSpec((HALO, WIDE), lambda g: (0, g)),
                pl.BlockSpec((HALO, WIDE), lambda g: (0, g)),
                pl.BlockSpec((8, WIDE), lambda g: (0, g)),
                whole((8, TILE)),
                whole((length, n_state)),
                whole((2, length, TILE)),
                whole((8, TILE)),
            ],
            out_shape=[
                jax.ShapeDtypeStruct((length, columns), bf16),
                jax.ShapeDtypeStruct((HALO, columns), f32),
                jax.ShapeDtypeStruct((HALO, columns), f32),
                jax.ShapeDtypeStruct((8, columns), f32),
                jax.ShapeDtypeStruct((8, TILE), f32),
                jax.ShapeDtypeStruct((length, n_state), f32),
                jax.ShapeDtypeStruct((2, length, TILE), f32),
                jax.ShapeDtypeStruct((8, TILE), f32),
            ],
            scratch_shapes=[
                pltpu.VMEM((length + HALO, WIDE), f32),
                pltpu.VMEM((length + HALO, WIDE), f32),
            ],
            compiler_params=big,
            cost_estimate=CHEAP,
            name="mixer_outside",
        )(proj, proj_bc, taps8, masks, spreads, per_head, rates, bc, grad, ssm, dxs, d_state,
          state_in, db_in, dc_in, dc_more, *running)

    seg_end = near[length : length + 2 * HALO]

    def finish(grads, first, last, start):
        ahead = lax.ppermute(first, ALL, [(i + 1, i) for i in range(devices - 1)])
        joined = jnp.concatenate([jnp.zeros_like(first), ahead], 0)
        for tap in range(CONV - 1):
            lead = CONV - 1 - tap
            same = (seg_end[lead : lead + HALO] == seg_end[:HALO]).astype(f32)[:, None]
            here = taps8[tap, start : start + first.shape[1]]
            last = last + here[None, :] * joined[lead : lead + HALO] * same
        count = min(channels - start, first.shape[1])
        return lax.dynamic_update_slice(grads, last[:, :count].astype(bf16), (length - HALO, 0))

    running = ()
    part = groups // 2
    half_x = part * WIDE

    values = lambda *chains: [chain.value for chain in chains]
    sums_o = halves(grad_o)
    d_one, first, last, sums_one, _, *running = outside(0, part, False, d_y, running)
    step(d_one, *sums_o)
    d_one = finish(d_one, first, last, 0)
    one_other = other_core(d_one)
    if by_hand:
        d_normed_in = back([after(d_z, sums_one, *values(*sums_o))], g_z, None)
    else:
        d_normed_in = stacked_back(d_z, stack_z, 0)
    step(d_normed_in, *sums_o)
    grad_z = lax.optimization_barrier((*grad_z, sums_one))[:2]
    sums_z = [RowSum(grad_z[0], True), RowSum(grad_z[1], False)]
    one_other = after(one_other, d_normed_in)
    blocks = d_one.shape[1] // (2 * WIDE)
    more = (blocks + 1) // 2
    grad_x = [
        pair_grad(lefts, d_one, one_other, 0, more),
        pair_grad(lefts, d_one, one_other, more, blocks - more),
    ]
    grad = after(d_y, *grad_x, *values(*sums_o))
    d_two, first, last, sums_two, head_sums, *_ = outside(part, groups - part, True, grad, running)
    sums_a = [RowSum(grad_x[0], True), RowSum(grad_x[1], False)]
    step(d_two, *sums_a)
    ready = values(*sums_a)
    d_two, first, last = lax.optimization_barrier((d_two, first, last, *ready))[:3]
    step(d_two, *sums_z, *sums_o)
    sums = jnp.concatenate([sums_one, sums_two], 1)
    d_two = finish(d_two, first, last, half_x)
    two_other = other_core(d_two)
    count = inner - half_x
    edge = d_two[:, count : count + w_edge.shape[0]]
    d_normed_in = d_normed_in + mm(edge, w_edge)
    two_other = after(two_other, d_normed_in, *values(*sums_z, *sums_o))
    blocks = d_two.shape[1] // (4 * WIDE)
    grad_y = [pair_grad(lefts, d_two, two_other, at, blocks) for at in (0, blocks)]
    step(grad_y[1], *sums_z, *sums_o)
    sums_b = [RowSum(grad_y[0], True), RowSum(grad_y[1], False)]
    if by_hand:
        last_values = [d_one, after(d_two, *grad_y, *values(*sums_z))]
        norm = (hidden, cotangent, gain_in[None])
        grad_hidden, grad_gain_in = back(last_values, g_x, d_normed_in, norm)
    else:
        d_x = jnp.concatenate([d_one, d_two[:, :count]], 1)
        d_normed_in = d_normed_in + stacked_back(d_x, stack_x, 0)
        base = hidden.astype(f32)
        scale = scale_in[HALO:]
        d_hat = d_normed_in * gain_in[None, :]
        mean = jnp.mean(d_hat * base, axis=1, keepdims=True)
        grad_hidden = cotangent.astype(f32) + scale * d_hat - base * (scale * scale * scale * mean)
        grad_gain_in = (d_normed_in * base * scale).reshape(-1, 8, width).sum(0)
    step(grad_gain_in, *sums_b)
    sums_x = sums_a + sums_b
    step(sums_b[0].value, *sums_a, *sums_z)
    step(sums_a[0].value, *sums_b)
    step(sums_b[0].value, *sums_b)
    grad_gain_in = after(grad_gain_in, *[chain.send for chain in sums_b])
    step(sums_b[0].send, *sums_a, *sums_z)
    while any(chain.order for chain in sums_o + sums_z + sums_x):
        step(grad_gain_in, *sums_b)
        step(sums_b[0].value, *sums_a, *sums_z, *sums_o)
    counts = [width // devices] + [channels // devices] * (CONV + 1) + [inner // devices]
    counts += [heads] * 3
    total = sum(counts)
    if by_hand:
        sizes = (width // devices, channels // devices, inner // devices, heads)
        packed = pl.pallas_call(
            lambda *refs: pack_kernel(sizes, *refs),
            out_shape=jax.ShapeDtypeStruct((devices, 1, total + -total % TILE), f32),
            name="pack",
        )(sums[:, :channels], grad_gain_in, d_gain, head_sums)
    else:
        slots = lambda v: v.reshape(-1, devices, v.shape[-1] // devices).transpose(1, 0, 2)
        same = jnp.broadcast_to(head_sums[:3, :heads].reshape(1, -1), (devices, 3 * heads))
        pieces = [slots(grad_gain_in.sum(0)), slots(sums[: CONV + 1, :channels])]
        pieces += [slots(jnp.sum(d_gain, 0)), same]
        packed = jnp.concatenate([p.reshape(devices, -1) for p in pieces], 1)[:, None]
    packed = exchange(packed).sum((0, 1))
    found, at = ([], 0)
    for size in counts:
        found.append(packed[at : at + size])
        at += size

    grads = [c.rows().astype(f32) for c in sums_z + sums_x]
    excess = sum(g.shape[1] for g in grads) - w_in.shape[0]
    grads[-1] = grads[-1][:, : grads[-1].shape[1] - excess]
    return (
        block_out,
        grad_hidden,
        found[0],
        jnp.concatenate(grads, 1),
        jnp.stack(found[1 : CONV + 1]),
        found[CONV + 1],
        found[CONV + 3],
        found[CONV + 4],
        found[CONV + 5],
        found[CONV + 2],
        jnp.concatenate([c.rows().astype(f32) for c in sums_o], 1),
    )


def solution(mesh):
    return jax.shard_map(
        on_device,
        mesh=mesh,
        in_specs=(
            P(ALL, None),
            P(ALL, None),
            P(),
            P("shard"),
            P("shard", None),
            P(None, "shard"),
            P("shard"),
            P(),
            P(),
            P(),
            P("shard"),
            P("shard", None),
        ),
        out_specs=(
            P(ALL, None),
            P(ALL, None),
            P(ALL),
            P(ALL, None),
            P(None, ALL),
            P(ALL),
            P(),
            P(),
            P(),
            P(ALL),
            P(ALL, None),
        ),
        check_vma=False,
    )
```

```python
import jax
import jax.numpy as jnp
from jax import lax
from jax.experimental import pallas as pl
from jax.experimental.pallas import tpu as pltpu
from jax.sharding import PartitionSpec as P

HEAD_DIM = 64
CONV = 4
EPS = 1e-05
HALO = 8
GROUP = 4
WIDE = GROUP * HEAD_DIM
TILE = 128
PIECE = 3 * WIDE
SPAN = 2
HIGH = lax.Precision.HIGHEST
ALL = ("shard", "seq")
f32 = jnp.float32
bf16 = jnp.bfloat16
CHEAP = pl.CostEstimate(flops=1, bytes_accessed=1, transcendentals=0)


def mm(a, b):
    return jnp.dot(a, b, preferred_element_type=f32)


def mm_nt(a, b):
    return lax.dot_general(a, b, (((1,), (1,)), ((), ())), preferred_element_type=f32)


def mm_tn(a, b):
    return lax.dot_general(a, b, (((0,), (0,)), ((), ())), preferred_element_type=f32)


def sigmoid(value):
    return 0.5 * jnp.tanh(0.5 * value) + 0.5


def head_lanes(group):
    lane = lax.rem(lax.broadcasted_iota(jnp.int32, (2 * TILE, WIDE), 0), TILE)
    owner = lax.broadcasted_iota(jnp.int32, (2 * TILE, WIDE), 1) // HEAD_DIM + GROUP * group
    return jnp.where(lane == owner, 1.0, 0.0).astype(bf16)


def two_parts(value):
    high = value.astype(bf16)
    low = (value - high.astype(f32)).astype(bf16)
    return high, low


def twice(value):
    return jnp.concatenate([value, value], 1)


def conv_rows(wide, taps, masks, start, rows):
    pre = taps[CONV : CONV + 1, :] + taps[CONV - 1 : CONV, :] * wide[pl.ds(HALO + start, rows), :]
    for tap in range(CONV - 1):
        shifted = wide[pl.ds(HALO - CONV + 1 + tap + start, rows), :]
        pre = pre + taps[tap : tap + 1, :] * shifted * twice(masks[tap, pl.ds(start, rows), :])
    return pre


def prepare_kernel(edge, rates, flags, out, spread_out, cum_out, row_out, masks_out):
    length = out.shape[1]
    shifted = edge[...].astype(f32) + rates[0:1, :]
    step = jax.nn.softplus(shifted)
    here = lax.broadcasted_iota(jnp.int32, (length, length), 0)
    there = lax.broadcasted_iota(jnp.int32, (length, length), 1)
    lower = jnp.where(here >= there, 1.0, 0.0)
    log_decay = -step * jnp.exp(rates[1:2, :])
    cum = lax.dot_general(
        lower, log_decay, (((1,), (0,)), ((), ())), precision=HIGH, preferred_element_type=f32
    )
    keep = jnp.exp(cum[length - 1 : length, :] - cum) * flags[:, 8:9]
    out[0] = cum
    out[1] = step
    out[2] = keep
    out[3] = jnp.exp(cum) * flags[:, 7:8]
    out[4] = sigmoid(shifted)
    for at, value in enumerate((step, keep)):
        high, low = two_parts(value)
        spread_out[at, :, :TILE] = high
        spread_out[at, :, TILE:] = low
    turned = cum.T
    for group in range(row_out.shape[0]):
        heads = slice(GROUP * group, GROUP * (group + 1))
        row_out[group] = turned[heads, :]
        cum_out[group] = cum[:, heads]
    for at in range(2 * (CONV - 1)):
        masks_out[at] = jnp.broadcast_to(flags[:, at : at + 1], (length, TILE))


def span(sub):
    return pl.ds(pl.multiple_of(sub * WIDE, WIDE), WIDE)


def state_kernel(
    raw, raw_bc, taps, taps_bc, masks, spreads, x_out, state_out, bc_out, bt_out, ct_out, wide, bt
):
    length = x_out.shape[0]
    n_state = bt.shape[0]
    step = pl.program_id(0)

    @pl.when(step == 0)
    def _():
        wide[...] = raw_bc[...].astype(f32)
        tap = taps_bc[...]
        for start in range(0, length, TILE):
            rows = pl.ds(start, TILE)
            pre = conv_rows(wide, tap, masks, start, TILE)
            both = pre * sigmoid(pre)
            bc_out[rows, :] = both.astype(bf16)
            turned = both[:, :n_state].T.astype(bf16)
            bt[:, rows] = turned
            bt_out[:, rows] = turned
            ct_out[:, rows] = both[:, n_state:].T.astype(bf16)

    def one(sub, carry):
        columns = span(sub)
        wide[...] = raw[:, columns].astype(f32)
        tap = taps[:, columns]
        lanes = head_lanes(SPAN * step + sub)
        kept = []
        for start in range(0, length, TILE):
            rows = pl.ds(start, TILE)
            pre = conv_rows(wide, tap, masks, start, TILE)
            x = (pre * sigmoid(pre)).astype(bf16)
            x_out[rows, columns] = x
            scaled = (x.astype(f32) * mm(spreads[0, rows, :], lanes)).astype(bf16)
            kept.append((scaled.astype(f32) * mm(spreads[1, rows, :], lanes)).astype(bf16))
        state_out[:, columns] = mm(bt[...], jnp.concatenate(kept, 0)).astype(bf16)
        return carry

    lax.fori_loop(0, SPAN, one, 0)


def scored(first, second, flags, seg_row, score, later):
    length = score.shape[0]
    for start in range(0, length, TILE):
        rows = pl.ds(start, TILE)
        product = mm(first(rows), second[...])
        here = lax.broadcasted_iota(jnp.int32, (TILE, length), 0) + start
        there = lax.broadcasted_iota(jnp.int32, (TILE, length), 1)
        order = (here >= there) if later else (here <= there)
        seen = (flags[rows, 6:7] == seg_row[0:1, :]) & order
        score[rows, :] = jnp.where(seen, product, 0.0)


def by_head(value):
    owner = lax.broadcasted_iota(jnp.int32, value.shape, 1) // HEAD_DIM
    zero = jnp.zeros_like(value)
    return [jnp.where(owner == head, value, zero) for head in range(GROUP)]


def forward_kernel(x_in, flags, seg_row, spreads, cum, sums_row, bc, bt, y_out, score, apart, weights):
    length = y_out.shape[0]
    n_state = bt.shape[0]
    step = pl.program_id(0)
    big = weights.shape[2] // GROUP

    @pl.when(step == 0)
    def _():
        scored(lambda rows: bc[rows, n_state:], bt, flags, seg_row, score, True)
        weights[...] = jnp.zeros_like(weights)

    def one(sub, carry):
        columns = span(sub)
        lanes = head_lanes(SPAN * step + sub)
        for start in range(0, length, TILE):
            rows = pl.ds(start, TILE)
            scaled = x_in[rows, columns].astype(f32) * mm(spreads[0, rows, :], lanes)
            for head, value in enumerate(by_head(scaled)):
                apart[start // big, pl.ds(head * big + start % big, TILE), :] = value.astype(bf16)
        for head in range(GROUP):
            for start in range(0, length, TILE):
                rows = pl.ds(start, TILE)
                for at in range(0, start + TILE, big):
                    end = min(at + big, start + TILE)
                    gap = cum[sub, rows, head : head + 1] - sums_row[sub, head : head + 1, at:end]
                    weight = jnp.exp(jnp.minimum(gap, 0.0)) * score[rows, at:end]
                    weights[at // big, rows, head * big : head * big + end - at] = weight.astype(bf16)
        for at in range(0, length, big):
            part = mm(weights[at // big, at:, :], apart[at // big])
            if at == 0:
                y_out[:, columns] = part
            else:
                y_out[at:, columns] += part
        return carry

    lax.fori_loop(0, SPAN, one, 0)


def gate_kernel(
    shards, y_in, x_in, z_in, dn_in, bc, ct, enter, state, gain, ssm_out, norm_out, dz_out, dy_out,
    ds_out, dc_out, dg_out, gated_s, sig_s, mo_s, ds_acc
):
    rows = y_in.shape[0]
    width = y_in.shape[1]
    n_state = state.shape[0]
    step = pl.program_id(0)
    lane = lax.broadcasted_iota(jnp.int32, (rows, 2 * HEAD_DIM), 1)
    c_mat = bc[:, n_state:]

    @pl.when(step == 0)
    def _():
        ds_acc[...] = jnp.zeros_like(ds_acc)
        dg_out[...] = jnp.zeros_like(dg_out)

    def entering(block):
        low = enter[:, 2 * block : 2 * block + 1]
        top = enter[:, 2 * block + 1 : 2 * block + 2]
        return jnp.where(lane < HEAD_DIM, low, top)

    square = jnp.zeros((rows, 2 * HEAD_DIM), f32)
    cross = jnp.zeros((rows, 2 * HEAD_DIM), f32)
    for block in range(width // (2 * HEAD_DIM)):
        lanes = slice(block * 2 * HEAD_DIM, (block + 1) * 2 * HEAD_DIM)
        ssm = y_in[:, lanes] + entering(block) * mm(c_mat, state[:, lanes])
        ssm_out[:, lanes] = ssm
        mo = (ssm + gain[1:2, lanes] * x_in[:, lanes].astype(f32)).astype(bf16)
        mo_s[:, lanes] = mo
        z = z_in[:, lanes].astype(f32)
        sig = sigmoid(z)
        gated = mo.astype(f32) * (z * sig)
        gated_s[:, lanes] = gated
        sig_s[:, lanes] = sig
        square = square + gated * gated
        cross = cross + gated * (dn_in[:, lanes].astype(f32) * gain[0:1, lanes])
    scale = lax.rsqrt(jnp.sum(square, axis=1, keepdims=True) * (1.0 / width) + EPS)
    pull = scale * scale * scale * (jnp.sum(cross, axis=1, keepdims=True) * (1.0 / width))
    dc = jnp.zeros((rows, n_state), f32)
    for block in range(width // (2 * HEAD_DIM)):
        lanes = slice(block * 2 * HEAD_DIM, (block + 1) * 2 * HEAD_DIM)
        gated = gated_s[:, lanes]
        sig = sig_s[:, lanes]
        silu = z_in[:, lanes].astype(f32) * sig
        dn = dn_in[:, lanes].astype(f32)
        hat = gated * scale
        size = width // shards
        owner, at = divmod(block * 2 * HEAD_DIM, size)
        at += (owner // 2) * size
        norm_out[owner % 2, :, at : at + 2 * HEAD_DIM] = (hat * gain[0:1, lanes]).astype(bf16)
        part = dn * hat
        total = part[0:8, :]
        for at in range(8, rows, 8):
            total = total + part[at : at + 8, :]
        dg_out[:, lanes] += total
        d_gated = scale * (dn * gain[0:1, lanes]) - gated * pull
        dy = (d_gated * silu).astype(bf16)
        dy_out[:, lanes] = dy
        mo = mo_s[:, lanes].astype(f32)
        dz_out[:, lanes] = (d_gated * mo * (sig + silu * (1.0 - sig))).astype(bf16)
        weighted = (dy.astype(f32) * entering(block)).astype(bf16)
        ds_acc[:, lanes] += mm(ct[...], weighted)
        dc = dc + mm_nt(weighted, state[:, lanes])
    dc_out[...] = dc

    @pl.when(step == pl.num_programs(0) - 1)
    def _():
        ds_out[...] = ds_acc[...].astype(bf16)


def inside_kernel(
    x_in, flags, seg_row, spreads, cum, sums_row, bc, ct, dy, dxs_out, db_out, dc_out, score, pair,
    apart, weights, xs, crossed
):
    length = dxs_out.shape[0]
    n_state = ct.shape[0]
    group = pl.program_id(0)
    big = weights.shape[2] // GROUP

    @pl.when(group == 0)
    def _():
        pair[...] = jnp.zeros_like(pair)
        weights[...] = jnp.zeros_like(weights)
        scored(lambda rows: bc[rows, :n_state], ct, flags, seg_row, score, False)

    lanes = head_lanes(group)
    for start in range(0, length, TILE):
        rows = pl.ds(start, TILE)
        scaled = x_in[rows, :].astype(f32) * mm(spreads[0, rows, :], lanes)
        for head, value in enumerate(by_head(scaled)):
            xs[head, rows, :] = value.astype(bf16)
        for head, value in enumerate(by_head(dy[rows, :].astype(f32))):
            apart[start // big, pl.ds(head * big + start % big, TILE), :] = value.astype(bf16)
    for head in range(GROUP):
        for at in range(0, length, big):
            end = at + big
            crossed[head % 2, :end, at:end] = mm_nt(xs[head, :end, :], dy[at:end, :])
        for start in range(0, length, TILE):
            rows = pl.ds(start, TILE)
            for at in range(start // big * big, length, big):
                first = max(at, start)
                end = at + big
                gap = sums_row[0, head : head + 1, first:end] - cum[0, rows, head : head + 1]
                decay = jnp.exp(jnp.minimum(gap, 0.0))
                weight = (decay * score[rows, first:end]).astype(bf16)
                weights[at // big, rows, head * big + first - at : (head + 1) * big] = weight
                pair[rows, first:end] += decay * crossed[head % 2, rows, first:end]
    for at in range(length - big, -1, -big):
        end = at + big
        part = mm(weights[at // big, :end, :], apart[at // big])
        if end == length:
            dxs_out[...] = part
        else:
            dxs_out[:end, :] += part

    @pl.when(group == pl.num_programs(0) - 1)
    def _():
        for start in range(0, length, TILE):
            rows = pl.ds(start, TILE)
            here = lax.broadcasted_iota(jnp.int32, (TILE, length), 0) + start
            there = lax.broadcasted_iota(jnp.int32, (TILE, length), 1)
            seen = (flags[rows, 6:7] == seg_row[0:1, :]) & (here <= there)
            part = jnp.where(seen, pair[rows, :], 0.0).astype(bf16)
            db_out[rows, :] = mm(part, bc[:, n_state:])
            if start == 0:
                dc_out[...] = mm_tn(part, bc[rows, :n_state])
            else:
                dc_out[...] += mm_tn(part, bc[rows, :n_state])


def split_mm(value, chosen):
    high, low = two_parts(value)
    return mm(high, chosen) + mm(low, chosen)


def outside_kernel(first_group, count, final, running, *refs):
    (raw, raw_bc, taps, masks, spreads, heads, rates, bc, dy, ssm, dxs_in, d_state, state, db_in,
     dc_in, dc_more, *started, d_out, first_out, last_out, sums_out,
     head_out, db_acc, found, totals_s, wide, d_pre) = refs
    length = d_out.shape[0]
    n_state = bc.shape[1] // 2
    step = pl.program_id(0)
    bc_step = count

    @pl.when(step == 0)
    def _():
        for at, ref in enumerate((db_acc, found, totals_s)):
            ref[...] = started[at][...] if running else jnp.zeros_like(ref)

    d_pre[pl.ds(length, HALO), :] = jnp.zeros((HALO, d_pre.shape[1]), f32)
    zero = jnp.zeros((1, d_pre.shape[1]), f32)

    @pl.when(step < bc_step)
    def _():
        wide[...] = raw[...].astype(f32)
        skip_sum, keep_sum = (zero, zero)
        ds = d_state[...]
        group = step + first_group
        lanes = head_lanes(group)
        owner = lax.broadcasted_iota(jnp.int32, (WIDE, TILE), 0) // HEAD_DIM + GROUP * group
        chosen = (owner == lax.broadcasted_iota(jnp.int32, (WIDE, TILE), 1)).astype(f32)
        chosen_b = chosen.astype(bf16)
        for start in range(0, length, TILE):
            rows = pl.ds(start, TILE)
            pre = conv_rows(wide, taps, masks, start, TILE)
            sig = sigmoid(pre)
            x = pre * sig
            stepped = mm(spreads[0, rows, :], lanes)
            scaled = (x.astype(bf16).astype(f32) * stepped).astype(bf16)
            keep = mm(spreads[1, rows, :], lanes)
            carried = keep * mm(bc[rows, :n_state], ds)
            dxs = dxs_in[rows, :] + carried
            scaled = scaled.astype(f32)
            db_acc[rows, :] += mm_nt((scaled * keep).astype(bf16), ds)
            grad = dy[rows, :].astype(f32)
            keep_sum = keep_sum + jnp.sum(scaled * carried, 0, keepdims=True)
            skip_sum = skip_sum + jnp.sum(grad * x, 0, keepdims=True)
            found[0, rows, :] += split_mm(grad * ssm[rows, :] - scaled * dxs, chosen_b)
            found[1, rows, :] += split_mm(x * dxs, chosen_b)
            d_x = taps[5:6, :] * grad + stepped * dxs
            d_pre[rows, :] = d_x * (sig + x * (1.0 - sig))
        met = jnp.sum(ds.astype(f32) * state[...].astype(f32), 0, keepdims=True)
        rest = jnp.zeros((5, WIDE), f32)
        totals_s[...] += lax.dot_general(
            jnp.concatenate([skip_sum, keep_sum, met, rest], 0),
            chosen,
            (((1,), (0,)), ((), ())),
            precision=HIGH,
            preferred_element_type=f32,
        )

    if final:

        @pl.when(step == bc_step)
        def _():
            wide[...] = raw_bc[...].astype(f32)
            for start in range(0, length, TILE):
                rows = pl.ds(start, TILE)
                pre = conv_rows(wide, taps, masks, start, TILE)
                sig = sigmoid(pre)
                slope = sig + pre * sig * (1.0 - sig)
                d_b = db_in[rows, :] + db_acc[rows, :]
                d_c = dc_in[rows, :] + dc_more[rows, :]
                d_pre[rows, :] = jnp.concatenate([d_b, d_c], 1) * slope

    @pl.when(step <= bc_step)
    def _():
        totals = [zero] * (CONV + 1)
        for start in range(0, length, TILE):
            rows = pl.ds(start, TILE)
            grad = d_pre[rows, :]
            totals[CONV] = totals[CONV] + jnp.sum(grad, 0, keepdims=True)
            here = wide[pl.ds(HALO + start, TILE), :]
            totals[CONV - 1] = totals[CONV - 1] + jnp.sum(grad * here, 0, keepdims=True)
            back = taps[CONV - 1 : CONV, :] * grad
            for tap in range(CONV - 1):
                shifted = wide[pl.ds(HALO - CONV + 1 + tap + start, TILE), :]
                masked = grad * twice(masks[tap, rows, :])
                totals[tap] = totals[tap] + jnp.sum(masked * shifted, 0, keepdims=True)
                ahead = d_pre[pl.ds(start + CONV - 1 - tap, TILE), :]
                back = back + taps[tap : tap + 1, :] * ahead * twice(masks[3 + tap, rows, :])
            d_out[rows, :] = back.astype(bf16)
            if start + TILE == length:
                last_out[...] = back[TILE - HALO :, :]
        first_out[...] = d_pre[pl.ds(0, HALO), :]
        for tap in range(CONV + 1):
            sums_out[tap : tap + 1, :] = totals[tap]
        sums_out[CONV + 1 : 8, :] = jnp.zeros((7 - CONV, d_pre.shape[1]), f32)

    if not final:
        head_out[...] = jnp.zeros_like(head_out)
        return

    @pl.when(step == bc_step + 1)
    def _():
        first_out[...] = jnp.zeros_like(first_out)
        last_out[...] = jnp.zeros_like(last_out)
        sums_out[...] = jnp.zeros_like(sums_out)
        rate = jnp.exp(rates[1:2, :])
        end = totals_s[1:2, :] + heads[3, pl.ds(length - 1, 1), :] * totals_s[2:3, :]
        here = lax.broadcasted_iota(jnp.int32, (length, length), 0)
        there = lax.broadcasted_iota(jnp.int32, (length, length), 1)
        upper = jnp.where(here <= there, 1.0, 0.0)
        d_log = lax.dot_general(
            upper, found[0], (((1,), (0,)), ((), ())), precision=HIGH, preferred_element_type=f32
        )
        d_log = d_log + end
        d_dt = (found[1] - rate * d_log) * heads[4]
        d_out[:, :TILE] = d_dt.astype(bf16)
        d_out[:, TILE:] = jnp.zeros((length, WIDE - TILE), bf16)
        head_out[0:1, :] = jnp.sum(d_dt, 0, keepdims=True)
        head_out[1:2, :] = jnp.sum(d_log * (-heads[1] * rate), 0, keepdims=True)
        head_out[2:3, :] = totals_s[0:1, :]
        head_out[3:8, :] = jnp.zeros((5, TILE), f32)


def pack_kernel(sizes, sums, gain_in, gain_out, head, out):
    devices = out.shape[0]
    gain_in = jnp.sum(gain_in[...], 0, keepdims=True)
    wide, channels, inner, heads = sizes
    gains = jnp.sum(gain_out[...], 0, keepdims=True)
    for at in range(devices):
        pieces = [gain_in[:, at * wide : (at + 1) * wide]]
        for tap in range(CONV + 1):
            pieces.append(sums[tap : tap + 1, at * channels : (at + 1) * channels])
        pieces.append(gains[:, at * inner : (at + 1) * inner])
        for row in range(3):
            pieces.append(head[row : row + 1, :heads])
        begin = 0
        for piece in pieces:
            out[at, :, begin : begin + piece.shape[1]] = piece
            begin += piece.shape[1]
        if begin < out.shape[2]:
            out[at, :, begin:] = jnp.zeros((1, out.shape[2] - begin), f32)


def scan_kernel(backward, place, mine, decay, out, wide):
    count = mine.shape[0]
    columns = out.shape[2]
    for at in range(2):
        for device in range(count):
            wide[at, device : device + 1, :] = decay[device, at : at + 1, :].astype(f32)
    lane = lax.broadcasted_iota(jnp.int32, (TILE, columns), 0)
    owner = lax.broadcasted_iota(jnp.int32, (TILE, columns), 1) // HEAD_DIM + place[0]
    chosen = jnp.where(lane == owner, 1.0, 0.0).astype(bf16)
    factor = mm(wide[0].astype(bf16), chosen) + mm(wide[1].astype(bf16), chosen)
    state = jnp.zeros(out.shape[1:], f32)
    for at in reversed(range(count)) if backward else range(count):
        out[at] = state.astype(bf16)
        state = factor[at : at + 1, :] * state + mine[at, :, :columns].astype(f32)


def to_slices(value, devices):
    n_state, inner = value.shape
    across = max(1, devices // 16)
    rows = n_state * across // devices
    value = value.reshape(n_state // rows, rows, across, inner // across)
    return value.transpose(0, 2, 1, 3).reshape(devices, rows, inner // across)


def from_slices(slices, n_state, inner):
    devices, rows, columns = slices.shape
    value = slices.reshape(n_state // rows, inner // columns, rows, columns)
    return value.transpose(0, 2, 1, 3).reshape(n_state, inner)


def exchange(slices):
    return lax.all_to_all(slices, ALL, split_axis=0, concat_axis=0, tiled=True)


def return_slices(states, n_state, inner):
    return from_slices(exchange(states), n_state, inner)


def with_decay(slices, end):
    devices, rows, _ = slices.shape
    more = jnp.pad(jnp.stack(end), ((0, rows - 2), (0, 0)))
    return jnp.concatenate([slices, jnp.broadcast_to(more[None], (devices, rows, TILE))], 2)


def scan_devices(mine, decay, columns, me, backward):
    devices, rows, _ = mine.shape
    across = max(1, devices // 16)
    place = jnp.reshape((me % across) * (columns // HEAD_DIM), (1,)).astype(jnp.int32)
    vmem = pl.BlockSpec(memory_space=pltpu.VMEM)
    return pl.pallas_call(
        lambda *refs: scan_kernel(backward, *refs),
        in_specs=[pl.BlockSpec(memory_space=pltpu.SMEM), vmem, vmem],
        out_specs=vmem,
        out_shape=jax.ShapeDtypeStruct((devices, rows, columns), bf16),
        scratch_shapes=[pltpu.VMEM((2, devices, TILE), f32)],
        compiler_params=pltpu.CompilerParams(vmem_limit_bytes=40 * 1024 * 1024),
        cost_estimate=CHEAP,
        name="scan_backward" if backward else "scan_forward",
    )(place, mine, decay)


def flip(axis, bit):
    count = lax.axis_size(axis)
    return [(i, i ^ bit) for i in range(count)]


def other_core(value):
    return lax.ppermute(value, "shard", flip("shard", 1))


def turn_kernel(count, *refs):
    for at in range(count):
        refs[count + at][...] = refs[at][...].astype(f32).T.astype(bf16)


def turned(*values):
    shape = values[0].shape
    whole = pl.BlockSpec(memory_space=pltpu.VMEM)
    return pl.pallas_call(
        lambda *refs: turn_kernel(len(values), *refs),
        in_specs=[whole] * len(values),
        out_specs=[whole] * len(values),
        out_shape=[jax.ShapeDtypeStruct(shape[::-1], bf16)] * len(values),
        compiler_params=pltpu.CompilerParams(vmem_limit_bytes=40 * 1024 * 1024),
        cost_estimate=CHEAP,
        name="turn",
    )(*values)


def pair_kernel(left, left_other, value, value_other, out):
    out[...] = (mm(left[...], value[...]) + mm(left_other[...], value_other[...])).astype(bf16)


def pair_grad(lefts, value, value_other, first, count):
    rows, tokens = lefts[0].shape
    size = 2 * WIDE
    whole = pl.BlockSpec((rows, tokens), lambda g: (0, 0))
    block = pl.BlockSpec((tokens, size), lambda g: (0, first + g))
    return pl.pallas_call(
        pair_kernel,
        grid=(count,),
        in_specs=[whole, whole, block, block],
        out_specs=pl.BlockSpec((rows, size), lambda g: (0, g)),
        out_shape=jax.ShapeDtypeStruct((rows, count * size), bf16),
        compiler_params=pltpu.CompilerParams(vmem_limit_bytes=58 * 1024 * 1024),
        cost_estimate=CHEAP,
        name="pair_grad",
    )(*lefts, value, value_other)


class Plan:
    def __init__(self):
        self.values, self.array = ([], None)

    def add(self, values):
        self.values += [jnp.asarray(value, jnp.int32) for value in values]
        return len(self.values) - len(values)

    def close(self):
        self.array = jnp.stack(self.values)


class Gather:
    def __init__(self, plan, own, other, base, half, chunks, *wait):
        self.own, self.other, self.base, self.half, self.chunks = (own, other, base, half, chunks)
        self.mine = lax.axis_index("seq") % 2
        self.size = half // chunks
        self.plan = plan
        if plan.array is None:
            full, near = (half // PIECE, self.size // PIECE)
            self.order = []
            for chunk in range(chunks):
                first = chunk * near
                order = [full * self.mine + first + at for at in range(near)]
                order += [full * (1 - self.mine) + first + at for at in range(near)]
                self.order.append(plan.add(order))
            source, block = ([], [])
            for at in range(2 * full):
                place = at % full
                source.append(2 * (place // near) + jnp.where(self.mine == at // full, 0, 1))
                block.append(place % near)
            self.source, self.block = (plan.add(source), plan.add(block))
        self.direct, self.passed = ([None] * chunks, [None] * chunks)
        self.parts = [None] * chunks
        for chunk in range(chunks):
            start = base + self.mine * half + chunk * self.size
            self.send = lax.dynamic_slice_in_dim(own, start, self.size, 0)
            if chunk:
                wait = (self.direct[chunk - 1],)
            if wait:
                self.send = after(self.send, *wait)
            self.direct[chunk] = lax.ppermute(self.send, "shard", flip("shard", 2))

    def share(self, *wait):
        for chunk in range(self.chunks):
            if chunk:
                wait = (self.passed[chunk - 1],)
            if wait:
                self.direct[chunk] = after(self.direct[chunk], *wait)
            self.passed[chunk] = lax.ppermute(self.direct[chunk], "seq", flip("seq", 1))

    def cross(self, chunk, *wait):
        direct, passed = (self.direct[chunk], self.passed[chunk])
        if wait:
            direct, passed = lax.optimization_barrier((direct, passed) + wait)[:2]
        self.parts[chunk] = [direct, other_core(direct), passed, other_core(passed)]


def project_kernel(table, *refs):
    lefts, (own, other, direct, direct_o, passed, passed_o) = (refs[:4], refs[4:10])
    out, left, weight = refs[-3:]
    step = pl.program_id(0)

    @pl.when(step == 0)
    def _():
        left[...] = jnp.concatenate([a[...] for a in lefts], 1)

    def fill(far, far_o):
        deep = own.shape[1]
        weight[:, :deep] = far[...]
        weight[:, deep:] = far_o[...]

    near = pl.num_programs(0) // 2
    pl.when(step < near)(lambda: fill(direct, direct_o))
    pl.when(step >= near)(lambda: fill(passed, passed_o))
    whole = jnp.concatenate([own[...], other[...], weight[...]], 1)
    out[...] = mm_nt(left[...], whole).astype(bf16)


def project(value, gather, chunk, result):
    rows = value.shape[0]
    deep = gather.own.shape[1]
    near = gather.size // PIECE
    base = gather.base // PIECE
    order = gather.order[chunk]
    table = gather.plan.array
    block = lambda index: pl.BlockSpec((PIECE, deep), index)
    left = lambda k: pl.BlockSpec((rows, deep), lambda j, t: (0, t[k]))
    own = block(lambda j, t: (base + t[order + j], 0))
    one = block(lambda j, t: (jnp.minimum(j, near - 1), 0))
    two = block(lambda j, t: (jnp.maximum(j - near, 0), 0))
    operands = [table, *([value] * 4), gather.own, gather.other, *gather.parts[chunk]]
    in_specs = [left(k) for k in range(4)] + [own, own, one, one, two, two]
    aliases = {}
    if result is not None:
        aliases = {len(operands): 0}
        operands.append(result)
        in_specs.append(pl.BlockSpec(memory_space=pl.ANY))
    return pl.pallas_call(
        project_kernel,
        grid_spec=pltpu.PrefetchScalarGridSpec(
            num_scalar_prefetch=1,
            grid=(2 * near,),
            in_specs=in_specs,
            out_specs=pl.BlockSpec((rows, PIECE), lambda j, t: (0, t[order + j])),
            scratch_shapes=[
                pltpu.VMEM((rows, 4 * deep), bf16),
                pltpu.VMEM((PIECE, 2 * deep), bf16),
            ],
        ),
        out_shape=jax.ShapeDtypeStruct((rows, 2 * gather.half), bf16),
        input_output_aliases=aliases,
        compiler_params=pltpu.CompilerParams(vmem_limit_bytes=58 * 1024 * 1024),
        cost_estimate=CHEAP,
        name="project",
    )(*operands)


def back_kernel(values, chunks, norm, source, table, *refs):
    inputs, refs = (refs[:values], refs[values:])
    own, other = refs[:2]
    far, refs = (refs[2 : 2 + 4 * chunks], refs[2 + 4 * chunks :])
    total, value, weight = refs[-3:]
    refs = refs[:-3]
    if norm:
        hidden, cotangent, gain, out, gain_out = refs[-5:]
        start = refs[:-5]
    else:
        out, start = (refs[-1], refs[:-1])
    step = pl.program_id(0)
    last = pl.num_programs(0) - 1
    deep = own.shape[1]
    place = lambda k: pl.ds(pl.multiple_of(table[k] * deep, deep), deep)

    @pl.when(step == 0)
    def _():
        if start:
            for k in range(4):
                total[:, k * deep : (k + 1) * deep] = start[0][:, place(k)]
        else:
            total[...] = jnp.zeros_like(total)

    for at in range(values):

        @pl.when((step * values // (last + 1)) == at)
        def _(at=at):
            value[...] = inputs[at][...]

    for at in range(2 * chunks):

        @pl.when(table[source + step] == at)
        def _(at=at):
            weight[:, :deep] = far[2 * at][...]
            weight[:, deep:] = far[2 * at + 1][...]

    total[...] += mm(value[...], jnp.concatenate([own[...], other[...], weight[...]], 1))

    @pl.when(step == last)
    def _():
        for k in range(4):
            out[:, place(k)] = total[:, k * deep : (k + 1) * deep]
        if norm:
            sums = jnp.zeros(gain_out.shape, f32)
            for at in range(0, out.shape[0], 64):
                rows = pl.ds(at, 64)
                base = hidden[rows, :].astype(f32)
                grad = out[rows, :]
                size = 1.0 / base.shape[1]
                scale = lax.rsqrt(jnp.sum(base * base, 1, keepdims=True) * size + EPS)
                hat = base * scale
                part = grad * hat
                for row in range(0, 64, 8):
                    sums = sums + part[row : row + 8, :]
                pull = jnp.sum(part * gain[...], 1, keepdims=True) * size
                inner = scale * (grad * gain[...] - hat * pull)
                out[rows, :] = cotangent[rows, :].astype(f32) + inner
            gain_out[...] = sums


def back(values, gather, start, norm=()):
    rows = values[0].shape[0]
    deep = gather.own.shape[1]
    count = 2 * gather.half // PIECE
    share = count // len(values)
    base = gather.base // PIECE
    table = gather.plan.array
    whole = pl.BlockSpec((rows, 4 * deep), lambda j, t: (0, 0))
    own = pl.BlockSpec((PIECE, deep), lambda j, t: (base + j, 0))
    far = pl.BlockSpec((PIECE, deep), lambda j, t: (t[gather.block + j], 0))
    in_specs = [
        pl.BlockSpec((rows, PIECE), lambda j, t, k=k: (0, jnp.clip(j - k * share, 0, share - 1)))
        for k in range(len(values))
    ]
    started = [] if start is None else [start]
    parts = [piece for chunk in gather.parts for piece in chunk]
    in_specs += [own, own] + [far] * len(parts) + [whole] * len(started)
    out_specs, out_shape = (whole, jax.ShapeDtypeStruct((rows, 4 * deep), f32))
    if norm:
        narrow = lambda count: pl.BlockSpec((count, 4 * deep), lambda j, t: (0, 0))
        in_specs += [whole, whole, narrow(1)]
        out_specs = [whole, narrow(8)]
        out_shape = [out_shape, jax.ShapeDtypeStruct((8, 4 * deep), f32)]
    return pl.pallas_call(
        lambda *refs: back_kernel(len(values), gather.chunks, len(norm) > 0, gather.source, *refs),
        grid_spec=pltpu.PrefetchScalarGridSpec(
            num_scalar_prefetch=1,
            grid=(count,),
            in_specs=in_specs,
            out_specs=out_specs,
            scratch_shapes=[
                pltpu.VMEM((rows, 4 * deep), f32),
                pltpu.VMEM((rows, PIECE), bf16),
                pltpu.VMEM((PIECE, 2 * deep), bf16),
            ],
        ),
        out_shape=out_shape,
        compiler_params=pltpu.CompilerParams(vmem_limit_bytes=58 * 1024 * 1024),
        cost_estimate=CHEAP,
        name="back",
    )(table, *values, gather.own, gather.other, *parts, *started, *norm)


def by_shard(gather):
    half, width = (gather.half, gather.own.shape[1])
    whole = pl.BlockSpec((2 * half, width), lambda g, t: (0, 0))
    part = pl.BlockSpec((half, width), lambda g, t: (0, 0))
    direct, direct_o, passed, passed_o = gather.parts[0]
    operands = [gather.own, gather.other, direct, passed, direct_o, passed_o]
    table = gather.plan.array
    return operands, [whole] * 2 + [part] * 4, table


def out_back_kernel(table, value, own, other, direct, passed, direct_o, passed_o, out):
    step = pl.program_id(0)
    half = direct.shape[0]

    def two(near, far):
        out[:, pl.ds(pl.multiple_of(table[4] * half, half), half)] = mm_nt(value[...], near[...]).astype(bf16)
        far_at = pl.multiple_of((1 - table[4]) * half, half)
        out[:, pl.ds(far_at, half)] = mm_nt(value[...], far[...]).astype(bf16)

    for at, piece in enumerate((own, other)):

        @pl.when(step == at)
        def _(piece=piece):
            out[...] = mm_nt(value[...], piece[...]).astype(bf16)

    pl.when(step == 2)(lambda: two(direct, passed))
    pl.when(step == 3)(lambda: two(direct_o, passed_o))


def out_back(value, gather):
    rows, width = value.shape
    operands, specs, table = by_shard(gather)
    size = 2 * gather.half
    return pl.pallas_call(
        out_back_kernel,
        grid_spec=pltpu.PrefetchScalarGridSpec(
            num_scalar_prefetch=1,
            grid=(4,),
            in_specs=[pl.BlockSpec((rows, width), lambda g, t: (0, 0))] + specs,
            out_specs=pl.BlockSpec((rows, size), lambda g, t: (0, t[g])),
        ),
        out_shape=jax.ShapeDtypeStruct((rows, 4 * size), bf16),
        compiler_params=pltpu.CompilerParams(vmem_limit_bytes=58 * 1024 * 1024),
        cost_estimate=CHEAP,
        name="out_back",
    )(table, value, *operands)


def out_forward_kernel(table, value, base, own, other, direct, passed, direct_o, passed_o, out, total):
    step = pl.program_id(0)
    half = direct.shape[0]

    def two(near, far):
        near_at = pl.multiple_of(table[4] * half, half)
        far_at = pl.multiple_of((1 - table[4]) * half, half)
        total[...] += mm(value[:, pl.ds(near_at, half)], near[...])
        total[...] += mm(value[:, pl.ds(far_at, half)], far[...])

    @pl.when(step == 0)
    def _():
        total[...] = base[...].astype(f32) + mm(value[...], own[...])

    @pl.when(step == 1)
    def _():
        total[...] += mm(value[...], other[...])

    pl.when(step == 2)(lambda: two(direct, passed))

    @pl.when(step == 3)
    def _():
        two(direct_o, passed_o)
        out[...] = total[...].astype(bf16)


def out_forward(value, base, gather):
    rows = value.shape[1]
    operands, specs, table = by_shard(gather)
    size = 2 * gather.half
    width = gather.own.shape[1]
    fixed = pl.BlockSpec((rows, width), lambda g, t: (0, 0))
    return pl.pallas_call(
        out_forward_kernel,
        grid_spec=pltpu.PrefetchScalarGridSpec(
            num_scalar_prefetch=1,
            grid=(4,),
            in_specs=[
                pl.BlockSpec((None, rows, size), lambda g, t: (t[g] & 1, 0, t[g] >> 1)),
                fixed,
                *specs,
            ],
            out_specs=fixed,
            scratch_shapes=[pltpu.VMEM((rows, width), f32)],
        ),
        out_shape=jax.ShapeDtypeStruct((rows, width), bf16),
        compiler_params=pltpu.CompilerParams(vmem_limit_bytes=58 * 1024 * 1024),
        cost_estimate=CHEAP,
        name="out_forward",
    )(table, value, base, *operands)


def stacked_project_kernel(value, *rest):
    weight = jnp.concatenate([w[...] for w in rest[:-1]], 1)
    rest[-1][...] = mm_nt(value[...], weight).astype(bf16)


def stacked_project(value, stack, base, count):
    rows = value.shape[0]
    shards, _, deep = stack.shape
    first = base // WIDE
    specs = [
        pl.BlockSpec((None, WIDE, deep), lambda j, k=k: (k, first + j, 0)) for k in range(shards)
    ]
    return pl.pallas_call(
        stacked_project_kernel,
        grid=(count // WIDE,),
        in_specs=[pl.BlockSpec((rows, shards * deep), lambda j: (0, 0))] + specs,
        out_specs=pl.BlockSpec((rows, WIDE), lambda j: (0, j)),
        out_shape=jax.ShapeDtypeStruct((rows, count), bf16),
        compiler_params=pltpu.CompilerParams(vmem_limit_bytes=58 * 1024 * 1024),
        cost_estimate=CHEAP,
        name="stacked_project",
    )(value, *([stack] * shards))


def stacked_back_kernel(value, *rest):
    out, total = rest[-2:]
    step = pl.program_id(0)

    @pl.when(step == 0)
    def _():
        total[...] = jnp.zeros_like(total)

    weight = jnp.concatenate([w[...] for w in rest[:-2]], 1)
    total[...] += mm(value[...], weight)

    @pl.when(step == pl.num_programs(0) - 1)
    def _():
        out[...] = total[...]


def stacked_back(value, stack, base):
    rows, count = value.shape
    shards, _, deep = stack.shape
    size = WIDE
    first = base // size
    specs = [
        pl.BlockSpec((None, size, deep), lambda j, k=k: (k, first + j, 0)) for k in range(shards)
    ]
    return pl.pallas_call(
        stacked_back_kernel,
        grid=(count // size,),
        in_specs=[pl.BlockSpec((rows, size), lambda j: (0, j))] + specs,
        out_specs=pl.BlockSpec((rows, shards * deep), lambda j: (0, 0)),
        out_shape=jax.ShapeDtypeStruct((rows, shards * deep), f32),
        scratch_shapes=[pltpu.VMEM((rows, shards * deep), f32)],
        compiler_params=pltpu.CompilerParams(vmem_limit_bytes=58 * 1024 * 1024),
        cost_estimate=CHEAP,
        name="stacked_back",
    )(value, *([stack] * shards))


def halve(value, dim, axis, bit, mine, wait):
    shape = value.shape
    value = value.reshape(shape[:dim] + (shape[dim] // 2, 2) + shape[dim + 1 :])
    send = lax.dynamic_index_in_dim(value, 1 - mine, dim + 1, False)
    kept = lax.dynamic_index_in_dim(value, mine, dim + 1, False)
    came = lax.ppermute(send, axis, flip(axis, bit))
    if wait:
        came = after(came, *wait)
    return (kept.astype(f32) + came.astype(f32)).astype(bf16), send


class RowSum:
    def __init__(self, partial, far_first):
        shards, places = (lax.axis_size("shard"), lax.axis_size("seq"))
        shard, place = (lax.axis_index("shard"), lax.axis_index("seq"))
        rows, columns = partial.shape
        chips = shards // 2
        self.value = partial.reshape(chips, places, rows // (chips * places), columns)
        far = [(0, "shard", 2 << k, (shard >> (k + 1)) & 1) for k in range(chips.bit_length() - 1)]
        near = [(1, "seq", 1 << k, (place >> k) & 1) for k in range(places.bit_length() - 1)]
        self.order = far + near if far_first else near[:1] + far + near[1:]

    def step(self, *wait):
        if not self.order:
            return
        dim, axis, bit, mine = self.order.pop(0)
        self.value, self.send = halve(self.value, dim, axis, bit, mine, wait)

    def rows(self):
        return self.value.reshape(self.value.shape[2:])


def core_rows(value, core):
    shards = lax.axis_size("shard")
    size = value.shape[1] // shards
    even = [value[:, at * size : (at + 1) * size] for at in range(0, shards, 2)]
    odd = [value[:, at * size : (at + 1) * size] for at in range(1, shards, 2)]
    own = [jnp.where(core == 0, a, b) for a, b in zip(even, odd)]
    rest = [jnp.where(core == 0, b, a) for a, b in zip(even, odd)]
    return jnp.concatenate(own, 1), jnp.concatenate(rest, 1)


def after(value, *others):
    return lax.optimization_barrier((value,) + others)[0]


def turn_blocks(value, shard):
    shards = lax.axis_size("shard")
    size = value.shape[1] // shards
    blocks = [
        lax.dynamic_slice_in_dim(value, (at ^ shard) * size, size, 1) for at in range(shards)
    ]
    return jnp.concatenate(blocks, 1)


def on_device(
    hidden,
    cotangent,
    seg_ids,
    norm_gain,
    in_weight,
    conv_weight,
    conv_bias,
    dt_bias,
    a_log,
    d_skip,
    out_gain,
    out_weight,
):
    shards, places = (lax.axis_size("shard"), lax.axis_size("seq"))
    shard, place = (lax.axis_index("shard"), lax.axis_index("seq"))
    devices = shards * places
    me = shard * places + place
    length, width = hidden.shape
    heads = dt_bias.shape[0]
    inner = out_weight.shape[0] * shards
    channels = conv_bias.shape[0] * shards
    n_state = (channels - inner) // 2
    groups = inner // WIDE
    start = me * length

    core = shard % 2
    w_in = in_weight.T
    by_hand = shards == 4 and places % 2 == 0
    edge_rows = w_in.shape[0] - 2 * inner
    small = jnp.concatenate([norm_gain, conv_weight.reshape(-1), conv_bias, out_gain])
    small_rows = pl.cdiv(small.shape[0], w_in.shape[1])
    small_rows += -(small_rows + edge_rows) % 16
    small = jnp.pad(small, (0, small_rows * w_in.shape[1] - small.shape[0]))
    edges = jnp.concatenate([w_in[2 * inner :], small.reshape(small_rows, w_in.shape[1])], 0)
    if by_hand:
        in_other = other_core(w_in)
        plan = Plan()
        plan.add([shard, shard ^ 1, shard ^ 2, shard ^ 3, place % 2])
        g_x = Gather(plan, w_in, in_other, inner, inner // 2, 2, edges)
        edge_far = lax.ppermute(edges, "shard", flip("shard", 2))
        g_z = Gather(plan, w_in, in_other, 0, inner // 2, 1, g_x.direct[1])
        pieces = [edges, other_core(edges), edge_far, other_core(edge_far)]
        edges = jnp.stack([after(piece, g_x.send) for piece in pieces])
        edges = jnp.stack([lax.dynamic_index_in_dim(edges, k ^ shard, 0, False) for k in range(4)])
    else:
        edges = lax.all_gather(edges, "shard")
    if by_hand:
        plan.close()
        g_x.share()
        g_x.cross(0)
        out_other = other_core(after(out_weight, g_x.direct[0]))
    else:
        stack_x = lax.all_gather(w_in[inner : 2 * inner], "shard")
        stack_z = lax.all_gather(w_in[:inner], "shard")
        w_out = lax.all_gather(out_weight, "shard", axis=0, tiled=True)
    w_edge = edges[:, :edge_rows].transpose(1, 0, 2).reshape(edge_rows, width)
    w_edge = jnp.pad(w_edge, ((0, -edge_rows % TILE), (0, 0)))
    small = edges[:, edge_rows:].reshape(shards, -1)
    at = 0
    gain_in = small[:, at : at + norm_gain.shape[0]].reshape(-1).astype(f32)
    at += norm_gain.shape[0]
    taps = small[:, at : at + conv_weight.size].reshape(shards, CONV, -1)
    taps = taps.transpose(1, 0, 2).reshape(CONV, channels).astype(f32)
    at += conv_weight.size
    bias = small[:, at : at + conv_bias.shape[0]].reshape(-1).astype(f32)
    at += conv_bias.shape[0]
    gain_out = small[:, at : at + out_gain.shape[0]].reshape(-1).astype(f32)
    skip_wide = jnp.repeat(d_skip.astype(f32), HEAD_DIM)
    rows = jnp.concatenate([skip_wide, jnp.zeros((channels - inner,), f32)])
    taps8 = jnp.concatenate([taps, bias[None], rows[None], jnp.zeros((2, channels), f32)], 0)

    edge = jnp.full((HALO,), -1, jnp.int32)
    padded = jnp.concatenate([edge, seg_ids, edge - 1])
    near = lax.dynamic_slice_in_dim(padded, start, length + 2 * HALO)
    seg = near[HALO : HALO + length]
    fwd_masks = [near[HALO - CONV + 1 + k : HALO - CONV + 1 + k + length] == seg for k in range(3)]
    spot = jnp.arange(length, dtype=jnp.int32)
    bwd_masks = [
        (near[HALO + CONV - 1 - k : HALO + CONV - 1 - k + length] == seg)
        & (spot + CONV - 1 - k < length)
        for k in range(3)
    ]
    from_before = seg == near[HALO - 1]
    to_last = seg == seg[length - 1]
    flags = jnp.stack(
        [m.astype(f32) for m in fwd_masks + bwd_masks + [seg, from_before, to_last]], 1
    )
    flags = jnp.pad(flags, ((0, 0), (0, 16 - flags.shape[1])))
    seg_row = jnp.broadcast_to(seg.astype(f32)[None, :], (8, length))

    behind = lax.ppermute(
        hidden[length - HALO :], ALL, [(i, i + 1) for i in range(devices - 1)]
    )
    hidden_f = jnp.concatenate([behind, hidden], 0).astype(f32)
    scale_in = lax.rsqrt(jnp.mean(hidden_f * hidden_f, axis=1, keepdims=True) + EPS)
    normed_ext = (hidden_f * scale_in * gain_in[None, :]).astype(bf16)
    normed_in = normed_ext[HALO:]
    proj_edge = mm_nt(normed_ext, w_edge).astype(bf16)
    proj_bc = proj_edge[:, : 2 * n_state]
    rates = jnp.stack([dt_bias, a_log]).astype(f32)
    rates = jnp.pad(rates, ((0, 6), (0, TILE - heads)))
    big = pltpu.CompilerParams(vmem_limit_bytes=56 * 1024 * 1024)
    per_head, spreads, cum, sums_row, masks = pl.pallas_call(
        prepare_kernel,
        out_shape=[
            jax.ShapeDtypeStruct((5, length, TILE), f32),
            jax.ShapeDtypeStruct((2, length, 2 * TILE), bf16),
            jax.ShapeDtypeStruct((groups, length, GROUP), f32),
            jax.ShapeDtypeStruct((groups, GROUP, length), f32),
            jax.ShapeDtypeStruct((2 * (CONV - 1), length, TILE), f32),
        ],
        compiler_params=big,
        name="prepare",
    )(proj_edge[HALO:, 2 * n_state :], rates, flags)
    end = two_parts(per_head[3, length - 1])
    if by_hand:
        proj = project(after(normed_ext, per_head), g_x, 0, None)
        g_out = Gather(plan, out_weight, out_other, 0, out_weight.shape[0] // 2, 1, proj, g_z.direct[0])
        g_z.share(proj)
        g_x.cross(1, proj)
        proj = project(normed_ext, g_x, 1, proj)
    else:
        proj = stacked_project(normed_ext, stack_x, 0, inner)

    def whole(shape):
        return pl.BlockSpec(shape, lambda g: (0,) * len(shape))

    def group_of(g):
        return jnp.maximum(g - 1, 0)

    order = lambda g: jnp.where(g == 0, groups, g - 1)
    x_conv, state_local, bc, bt, ct = pl.pallas_call(
        state_kernel,
        grid=(groups // SPAN,),
        in_specs=[
            pl.BlockSpec((length + HALO, SPAN * WIDE), lambda g: (0, g)),
            whole((length + HALO, WIDE)),
            pl.BlockSpec((8, SPAN * WIDE), lambda g: (0, g)),
            whole((8, WIDE)),
            whole(masks.shape),
            whole(spreads.shape),
        ],
        out_specs=[
            pl.BlockSpec((length, SPAN * WIDE), lambda g: (0, g)),
            pl.BlockSpec((n_state, SPAN * WIDE), lambda g: (0, g)),
            whole((length, 2 * n_state)),
            whole((n_state, length)),
            whole((n_state, length)),
        ],
        out_shape=[
            jax.ShapeDtypeStruct((length, inner), bf16),
            jax.ShapeDtypeStruct((n_state, inner), bf16),
            jax.ShapeDtypeStruct((length, 2 * n_state), bf16),
            jax.ShapeDtypeStruct((n_state, length), bf16),
            jax.ShapeDtypeStruct((n_state, length), bf16),
        ],
        scratch_shapes=[
            pltpu.VMEM((length + HALO, WIDE), f32),
            pltpu.VMEM((n_state, length), bf16),
        ],
        compiler_params=big,
        cost_estimate=CHEAP,
        name="mixer_state",
    )(proj, proj_bc, taps8, taps8[:, inner:], masks, spreads)

    slices = with_decay(to_slices(state_local, devices), end)
    if by_hand:
        slices = after(slices, g_out.direct[0])
        g_out.share(slices)
        sent = exchange(slices)
        g_z.cross(0, slices)
        gate_z = project(after(normed_in, slices), g_z, 0, None)
        out_early = other_core(after(g_out.direct[0], gate_z))
        own, rest = core_rows(after(normed_in, slices), core)
        lefts = turned(after(own, gate_z), after(other_core(rest), gate_z))
        sent = after(sent, gate_z, *lefts)
    else:
        sent = exchange(slices)
        own, rest = core_rows(normed_in, core)
        lefts = turned(own, other_core(rest))
        gate_z = stacked_project(normed_in, stack_z, 0, inner)
    columns = slices.shape[2] - TILE
    decays = sent[:, :, columns:]
    states = scan_devices(sent, decays, columns, me, False)
    state_in = return_slices(states, n_state, inner)
    x_conv = after(x_conv, states)
    half_t = 2 * TILE
    y_local = pl.pallas_call(
        forward_kernel,
        grid=(groups // SPAN,),
        in_specs=[
            pl.BlockSpec((length, SPAN * WIDE), lambda g: (0, g)),
            whole(flags.shape),
            whole((8, length)),
            whole(spreads.shape),
            pl.BlockSpec((SPAN, length, GROUP), lambda g: (g, 0, 0)),
            pl.BlockSpec((SPAN, GROUP, length), lambda g: (g, 0, 0)),
            whole((length, 2 * n_state)),
            whole((n_state, length)),
        ],
        out_specs=pl.BlockSpec((length, SPAN * WIDE), lambda g: (0, g)),
        out_shape=jax.ShapeDtypeStruct((length, inner), f32),
        scratch_shapes=[
            pltpu.VMEM((length, length), f32),
            pltpu.VMEM((length // half_t, GROUP * half_t, WIDE), bf16),
            pltpu.VMEM((length // half_t, length, GROUP * half_t), bf16),
        ],
        compiler_params=big,
        cost_estimate=CHEAP,
        name="mixer_forward",
    )(x_conv, flags, seg_row, spreads, cum, sums_row, bc, bt)
    if by_hand:
        g_out.cross(0, y_local)
        g_out.parts[0][1] = out_early
        d_normed = out_back(after(cotangent, y_local), g_out)
    else:
        d_normed = mm_nt(cotangent, w_out).astype(bf16)
    block = TILE
    tall = lambda dim: pl.BlockSpec((block, dim), lambda g: (g, 0))
    gains = jnp.stack([gain_out, skip_wide], 0)
    ssm, normed_out, d_z, d_y, d_state_local, dc_more, d_gain = pl.pallas_call(
        lambda *refs: gate_kernel(shards, *refs),
        grid=(length // block,),
        in_specs=[
            tall(inner),
            tall(inner),
            tall(inner),
            tall(inner),
            tall(2 * n_state),
            pl.BlockSpec((n_state, block), lambda g: (0, g)),
            pl.BlockSpec((None, block, TILE), lambda g: (3, g, 0)),
            whole((n_state, inner)),
            whole((2, inner)),
        ],
        out_specs=[
            tall(inner),
            pl.BlockSpec((2, block, inner // 2), lambda g: (0, g, 0)),
            tall(inner),
            tall(inner),
            whole((n_state, inner)),
            tall(n_state),
            whole((8, inner)),
        ],
        out_shape=[
            jax.ShapeDtypeStruct((length, inner), f32),
            jax.ShapeDtypeStruct((2, length, inner // 2), bf16),
            jax.ShapeDtypeStruct((length, inner), bf16),
            jax.ShapeDtypeStruct((length, inner), bf16),
            jax.ShapeDtypeStruct((n_state, inner), bf16),
            jax.ShapeDtypeStruct((length, n_state), f32),
            jax.ShapeDtypeStruct((8, inner), f32),
        ],
        scratch_shapes=[
            pltpu.VMEM((block, inner), f32),
            pltpu.VMEM((block, inner), f32),
            pltpu.VMEM((block, inner), bf16),
            pltpu.VMEM((n_state, inner), f32),
        ],
        compiler_params=big,
        cost_estimate=CHEAP,
        name="mixer_gate",
    )(y_local, x_conv, gate_z, d_normed, bc, ct, per_head, state_in, gains)

    slices = to_slices(d_state_local, devices)
    sent = exchange(slices)
    normed_out, d_z = (after(normed_out, slices), after(d_z, slices))

    def both(value):
        return jnp.concatenate([value, other_core(value)], 0)

    def both_rows(value):
        own, rest = core_rows(value, core)
        return jnp.concatenate([own, other_core(rest)], 0)

    cot_pair = both(cotangent)
    pick = lambda at: lax.dynamic_index_in_dim(normed_out, at, 0, False)
    out_pair = jnp.concatenate([pick(core), other_core(pick(1 - core))], 0)
    z_other = other_core(d_z)
    if by_hand:
        block_out = out_forward(normed_out, hidden, g_out)
    else:
        size = inner // shards
        parts = [
            normed_out[at % 2, :, (at // 2) * size : (at // 2 + 1) * size] for at in range(shards)
        ]
        block_out = (hidden.astype(f32) + mm(jnp.concatenate(parts, 1), w_out)).astype(bf16)
    grad_o = mm_tn(after(out_pair, block_out), cot_pair).astype(bf16)
    states = scan_devices(after(sent, grad_o), decays, columns, me, True)
    returned = exchange(states)
    z_other = after(z_other, states)
    blocks = inner // (4 * WIDE)
    grad_z = [pair_grad(lefts, d_z, z_other, at, blocks) for at in (0, blocks)]
    x_conv = after(x_conv, grad_o, *grad_z)

    dxs, db_in, dc_in = pl.pallas_call(
        inside_kernel,
        grid=(groups,),
        in_specs=[
            pl.BlockSpec((length, WIDE), lambda g: (0, g)),
            whole(flags.shape),
            whole((8, length)),
            whole(spreads.shape),
            pl.BlockSpec((1, length, GROUP), lambda g: (g, 0, 0)),
            pl.BlockSpec((1, GROUP, length), lambda g: (g, 0, 0)),
            whole((length, 2 * n_state)),
            whole((n_state, length)),
            pl.BlockSpec((length, WIDE), lambda g: (0, g)),
        ],
        out_specs=[
            pl.BlockSpec((length, WIDE), lambda g: (0, g)),
            whole((length, n_state)),
            whole((length, n_state)),
        ],
        out_shape=[
            jax.ShapeDtypeStruct((length, inner), f32),
            jax.ShapeDtypeStruct((length, n_state), f32),
            jax.ShapeDtypeStruct((length, n_state), f32),
        ],
        scratch_shapes=[
            pltpu.VMEM((length, length), f32),
            pltpu.VMEM((length, length), f32),
            pltpu.VMEM((length // half_t, GROUP * half_t, WIDE), bf16),
            pltpu.VMEM((length // half_t, length, GROUP * half_t), bf16),
            pltpu.VMEM((GROUP, length, WIDE), bf16),
            pltpu.VMEM((2, length, length), f32),
        ],
        compiler_params=big,
        cost_estimate=CHEAP,
        name="mixer_inside",
    )(x_conv, flags, seg_row, spreads, cum, sums_row, bc, ct, d_y)

    d_state = from_slices(after(returned, dxs), n_state, inner)
    grad_o, *grad_z = lax.optimization_barrier((grad_o, *grad_z, dxs))[:3]

    def halves(grad):
        half = grad.shape[1] // 2
        return [RowSum(grad[:, :half], True), RowSum(grad[:, half:], False)]

    def step(wait, *chains):
        for chain in chains:
            chain.step(wait)

    taps8 = jnp.pad(taps8, ((0, 0), (0, WIDE)))

    def outside(first_group, count, final, grad, running):
        kept = lambda g: jnp.minimum(g, count - 1) + first_group
        steps = count + (2 if final else 0)
        columns = steps * WIDE
        tall = lambda: pl.BlockSpec((length, WIDE), lambda g: (0, kept(g)))
        flat = lambda: pl.BlockSpec((n_state, WIDE), lambda g: (0, kept(g)))
        return pl.pallas_call(
            lambda *refs: outside_kernel(first_group, count, final, len(running) > 0, *refs),
            grid=(steps,),
            in_specs=[
                pl.BlockSpec((length + HALO, WIDE), lambda g: (0, kept(g))),
                whole((length + HALO, WIDE)),
                pl.BlockSpec((8, WIDE), lambda g: (0, first_group + g)),
                whole(masks.shape),
                whole(spreads.shape),
                whole(per_head.shape),
                whole(rates.shape),
                whole((length, 2 * n_state)),
                tall(),
                tall(),
                tall(),
                flat(),
                flat(),
                whole((length, n_state)),
                whole((length, n_state)),
                whole((length, n_state)),
                *[whole(value.shape) for value in running],
            ],
            out_specs=[
                pl.BlockSpec((length, WIDE), lambda g: (0, g)),
                pl.BlockSpec((HALO, WIDE), lambda g: (0, g)),
                pl.BlockSpec((HALO, WIDE), lambda g: (0, g)),
                pl.BlockSpec((8, WIDE), lambda g: (0, g)),
                whole((8, TILE)),
                whole((length, n_state)),
                whole((2, length, TILE)),
                whole((8, TILE)),
            ],
            out_shape=[
                jax.ShapeDtypeStruct((length, columns), bf16),
                jax.ShapeDtypeStruct((HALO, columns), f32),
                jax.ShapeDtypeStruct((HALO, columns), f32),
                jax.ShapeDtypeStruct((8, columns), f32),
                jax.ShapeDtypeStruct((8, TILE), f32),
                jax.ShapeDtypeStruct((length, n_state), f32),
                jax.ShapeDtypeStruct((2, length, TILE), f32),
                jax.ShapeDtypeStruct((8, TILE), f32),
            ],
            scratch_shapes=[
                pltpu.VMEM((length + HALO, WIDE), f32),
                pltpu.VMEM((length + HALO, WIDE), f32),
            ],
            compiler_params=big,
            cost_estimate=CHEAP,
            name="mixer_outside",
        )(proj, proj_bc, taps8, masks, spreads, per_head, rates, bc, grad, ssm, dxs, d_state,
          state_in, db_in, dc_in, dc_more, *running)

    seg_end = near[length : length + 2 * HALO]

    def finish(grads, first, last, start):
        ahead = lax.ppermute(first, ALL, [(i + 1, i) for i in range(devices - 1)])
        joined = jnp.concatenate([jnp.zeros_like(first), ahead], 0)
        for tap in range(CONV - 1):
            lead = CONV - 1 - tap
            same = (seg_end[lead : lead + HALO] == seg_end[:HALO]).astype(f32)[:, None]
            here = taps8[tap, start : start + first.shape[1]]
            last = last + here[None, :] * joined[lead : lead + HALO] * same
        count = min(channels - start, first.shape[1])
        return lax.dynamic_update_slice(grads, last[:, :count].astype(bf16), (length - HALO, 0))

    running = ()
    part = groups // 2
    half_x = part * WIDE

    values = lambda *chains: [chain.value for chain in chains]
    sums_o = halves(grad_o)
    d_one, first, last, sums_one, _, *running = outside(0, part, False, d_y, running)
    step(d_one, *sums_o)
    d_one = finish(d_one, first, last, 0)
    one_other = other_core(d_one)
    if by_hand:
        d_normed_in = back([after(d_z, sums_one, *values(*sums_o))], g_z, None)
    else:
        d_normed_in = stacked_back(d_z, stack_z, 0)
    step(d_normed_in, *sums_o)
    grad_z = lax.optimization_barrier((*grad_z, sums_one))[:2]
    sums_z = [RowSum(grad_z[0], True), RowSum(grad_z[1], False)]
    one_other = after(one_other, d_normed_in)
    blocks = d_one.shape[1] // (2 * WIDE)
    more = (blocks + 1) // 2
    grad_x = [
        pair_grad(lefts, d_one, one_other, 0, more),
        pair_grad(lefts, d_one, one_other, more, blocks - more),
    ]
    grad = after(d_y, *grad_x, *values(*sums_o))
    d_two, first, last, sums_two, head_sums, *_ = outside(part, groups - part, True, grad, running)
    sums_a = [RowSum(grad_x[0], True), RowSum(grad_x[1], False)]
    step(d_two, *sums_a)
    ready = values(*sums_a)
    d_two, first, last = lax.optimization_barrier((d_two, first, last, *ready))[:3]
    step(d_two, *sums_z, *sums_o)
    sums = jnp.concatenate([sums_one, sums_two], 1)
    d_two = finish(d_two, first, last, half_x)
    two_other = other_core(d_two)
    count = inner - half_x
    edge = d_two[:, count : count + w_edge.shape[0]]
    d_normed_in = d_normed_in + mm(edge, w_edge)
    two_other = after(two_other, d_normed_in, *values(*sums_z, *sums_o))
    blocks = d_two.shape[1] // (4 * WIDE)
    grad_y = [pair_grad(lefts, d_two, two_other, at, blocks) for at in (0, blocks)]
    step(grad_y[1], *sums_z, *sums_o)
    sums_b = [RowSum(grad_y[0], True), RowSum(grad_y[1], False)]
    if by_hand:
        last_values = [d_one, after(d_two, *grad_y, *values(*sums_z))]
        norm = (hidden, cotangent, gain_in[None])
        grad_hidden, grad_gain_in = back(last_values, g_x, d_normed_in, norm)
    else:
        d_x = jnp.concatenate([d_one, d_two[:, :count]], 1)
        d_normed_in = d_normed_in + stacked_back(d_x, stack_x, 0)
        base = hidden.astype(f32)
        scale = scale_in[HALO:]
        d_hat = d_normed_in * gain_in[None, :]
        mean = jnp.mean(d_hat * base, axis=1, keepdims=True)
        grad_hidden = cotangent.astype(f32) + scale * d_hat - base * (scale * scale * scale * mean)
        grad_gain_in = (d_normed_in * base * scale).reshape(-1, 8, width).sum(0)
    step(grad_gain_in, *sums_b)
    sums_x = sums_a + sums_b
    step(sums_b[0].value, *sums_a, *sums_z)
    step(sums_a[0].value, *sums_b)
    step(sums_b[0].value, *sums_b)
    grad_gain_in = after(grad_gain_in, *[chain.send for chain in sums_b])
    step(sums_b[0].send, *sums_a, *sums_z)
    while any(chain.order for chain in sums_o + sums_z + sums_x):
        step(grad_gain_in, *sums_b)
        step(sums_b[0].value, *sums_a, *sums_z, *sums_o)
    counts = [width // devices] + [channels // devices] * (CONV + 1) + [inner // devices]
    counts += [heads] * 3
    total = sum(counts)
    if by_hand:
        sizes = (width // devices, channels // devices, inner // devices, heads)
        packed = pl.pallas_call(
            lambda *refs: pack_kernel(sizes, *refs),
            out_shape=jax.ShapeDtypeStruct((devices, 1, total + -total % TILE), f32),
            name="pack",
        )(sums[:, :channels], grad_gain_in, d_gain, head_sums)
    else:
        slots = lambda v: v.reshape(-1, devices, v.shape[-1] // devices).transpose(1, 0, 2)
        same = jnp.broadcast_to(head_sums[:3, :heads].reshape(1, -1), (devices, 3 * heads))
        pieces = [slots(grad_gain_in.sum(0)), slots(sums[: CONV + 1, :channels])]
        pieces += [slots(jnp.sum(d_gain, 0)), same]
        packed = jnp.concatenate([p.reshape(devices, -1) for p in pieces], 1)[:, None]
    packed = exchange(packed).sum((0, 1))
    found, at = ([], 0)
    for size in counts:
        found.append(packed[at : at + size])
        at += size

    grads = [c.rows().astype(f32) for c in sums_z + sums_x]
    excess = sum(g.shape[1] for g in grads) - w_in.shape[0]
    grads[-1] = grads[-1][:, : grads[-1].shape[1] - excess]
    return (
        block_out,
        grad_hidden,
        found[0],
        jnp.concatenate(grads, 1),
        jnp.stack(found[1 : CONV + 1]),
        found[CONV + 1],
        found[CONV + 3],
        found[CONV + 4],
        found[CONV + 5],
        found[CONV + 2],
        jnp.concatenate([c.rows().astype(f32) for c in sums_o], 1),
    )


def solution(mesh):
    return jax.shard_map(
        on_device,
        mesh=mesh,
        in_specs=(
            P(ALL, None),
            P(ALL, None),
            P(),
            P("shard"),
            P("shard", None),
            P(None, "shard"),
            P("shard"),
            P(),
            P(),
            P(),
            P("shard"),
            P("shard", None),
        ),
        out_specs=(
            P(ALL, None),
            P(ALL, None),
            P(ALL),
            P(ALL, None),
            P(None, ALL),
            P(ALL),
            P(),
            P(),
            P(),
            P(ALL),
            P(ALL, None),
        ),
        check_vma=False,
    )
```
